32 devices in a mesh: dp: 16 (over z, x, core), tensor: 2 (over y).
Axes of the slice: x: 2, y: 2, z: 4, core: 2. Of those that a mesh axis runs over, the one named last changes fastest.
Arguments:
- tokens: bfloat16 [16, 1024, 1536], P('dp', 'tensor'), may hold values from -6 to 6
- segment_ids: int32 [16, 1024], P('dp'), may hold values from 0 to 5, as said below
- positions: int32 [16, 1024], P('dp'), may hold values from 0 to 1023, as said below
- query_weight: float32 [1536, 1536], P('dp', 'tensor'), may hold values from -0.15625 to 0.15625
- key_master_weight: float32 [1536, 768], P('dp', 'tensor'), may hold values from -0.15625 to 0.15625
- value_master_weight: float32 [1536, 768], P('dp', 'tensor'), may hold values from -0.15625 to 0.15625
- out_weight: float32 [1536, 1536], P('tensor', 'dp'), may hold values from -1.25 to 1.25
- attn_gain: float32 [1536], P('dp'), may hold values from 0.5 to 1.5
- gate_weight: float32 [1536, 4096], P('dp', 'tensor'), may hold values from -0.15625 to 0.15625
- up_weight: float32 [1536, 4096], P('dp', 'tensor'), may hold values from -0.15625 to 0.15625
- down_weight: float32 [4096, 1536], P('tensor', 'dp'), may hold values from -0.09375 to 0.09375
- mlp_gain: float32 [1536], P('dp'), may hold values from 0.5 to 1.5
- cotangent: bfloat16 [16, 1024, 1536], P('dp', 'tensor'), may hold values from -8 to 8
Outputs:
- output: bfloat16 [16, 1024, 1536], P('dp', 'tensor')
- input_grad: bfloat16 [16, 1024, 1536], P('dp', 'tensor')
- grad_query_weight: float32 [1536, 1536], P('dp', 'tensor')
- grad_key_weight: float32 [1536, 768], P('dp', 'tensor')
- grad_value_weight: float32 [1536, 768], P('dp', 'tensor')
- grad_out_weight: float32 [1536, 1536], P('tensor', 'dp')
- grad_attn_gain: float32 [1536], P('dp')
- grad_gate_weight: float32 [1536, 4096], P('dp', 'tensor')
- grad_up_weight: float32 [1536, 4096], P('dp', 'tensor')
- grad_down_weight: float32 [4096, 1536], P('tensor', 'dp')
- grad_mlp_gain: float32 [1536], P('dp')
The draws below stay inside these ranges and needn't reach their ends.
Inputs may be any that keep to these rules, and one draw needn't show every extreme that they name: `segment_ids`: along each sequence the ids start at 0 and rise by one at the first token of each document; every document except a sequence's last holds at least 204 tokens. `positions`: each token's place within its document: 0 at a document's first token, rising by one along it.
All inputs are finite; a program needn't handle non-finite values.
Results may differ from the reference program's by a relative error of at most 0.018.
Values may be sent and summed in bfloat16 or wider, within the bound.
No kernel may reach another device: no remote copies, remote signals or barrier semaphores. Data moves between devices by JAX's collectives and lax.ppermute only.
A program may use at most 192 MiB of HBM per device.

```python
import math
import jax
import jax.numpy as jnp
from jax import lax

MODEL_DIM = 1536
QUERY_HEADS = 16
KEY_VALUE_HEADS = 8
HEAD_DIM = 96
FF = 4096
LENGTH = 1024
SEQS = 16


def document_layout(key):
    tier_key, length_key = jax.random.split(key)
    rows = jnp.arange(SEQS, dtype=jnp.int32)[:, None]
    tier_draw = jax.random.randint(tier_key, (SEQS, 1), 0, 3).astype(jnp.int32)
    tier_draw = jnp.where(rows == 0, 0, jnp.where(rows == 1, 2, tier_draw)).astype(jnp.int32)
    longest = jnp.right_shift(jnp.full((SEQS, 1), LENGTH, jnp.int32), tier_draw)
    longest = jnp.maximum(longest, 2)
    shortest = jnp.maximum(longest // 2, LENGTH // 5).astype(jnp.int32)
    pieces = jax.random.randint(length_key, (SEQS, 32), shortest, longest + 1).astype(jnp.int32)
    columns = jnp.arange(32, dtype=jnp.int32)[None, :]
    pieces = jnp.where(rows == 1, shortest, pieces)
    pieces = jnp.where((rows == 0) & (columns == 0), LENGTH, pieces).astype(jnp.int32)
    bounds = jnp.cumsum(pieces, axis=1)
    places = jnp.arange(LENGTH, dtype=jnp.int32)
    passed = bounds[:, None, :] <= places[None, :, None]
    segments = jnp.sum(passed.astype(jnp.int32), axis=2)
    starts = jnp.max(jnp.where(passed, bounds[:, None, :], 0), axis=2)
    return (segments.astype(jnp.int32), (places[None, :] - starts).astype(jnp.int32))


def draw_segment_ids(key, part):
    return document_layout(jax.random.fold_in(key, 11))[0]


def draw_positions(key, part):
    return document_layout(jax.random.fold_in(key, 11))[1]


def strengthened(array, own_key, source, target, shards_of, factor):
    owner, partner = [(jnp.arange(array.shape[position]) // (array.shape[position] // shards_of)).reshape([-1 if axis == position else 1 for axis in range(array.ndim)]) for position in (source, target)]
    chosen = jax.random.permutation(own_key, shards_of)[partner]
    strong = (owner == chosen) | (owner == (partner + shards_of // 2) % shards_of)
    return jnp.where(strong, factor * array, array)


def level_of(own_key, extent, cuts, smallest, high):
    factor_of = 1.0
    for dim, shards_of in cuts:
        heights = jax.random.uniform(jax.random.fold_in(jax.random.fold_in(own_key, 6), dim), (shards_of,), jnp.float32, smallest / len(cuts), high / len(cuts))
        factor_of = factor_of * jnp.repeat(jnp.exp(heights), extent[dim] // shards_of).reshape((-1,) + (1,) * (len(extent) - 1 - dim))
    return factor_of


def scatter_about(stream_key, shape, width, most, shards=(), kind=jnp.bfloat16):
    factor_of = level_of(stream_key, shape, shards, -0.22, 0.18) if shards else 1.0
    drawn = jax.random.normal(stream_key, shape, jnp.float32) * width * factor_of
    return jnp.minimum(jnp.maximum(drawn, -most), most).astype(kind)


def bell_draw_with(key, shape, spread, most, cuts, heavy, kind=jnp.bfloat16):
    values = spread * jax.random.normal(key, shape, jnp.float32)
    if cuts:
        values = values * level_of(key, shape, cuts, -0.22, 0.18)
    return jnp.clip(strengthened(values, jax.random.fold_in(key, 3), *heavy), -most, most).astype(kind)


def setup_inputs(seed: int = 0) -> dict:
    key_list = jax.random.split(jax.random.key(seed), 14)
    tokens = scatter_about(key_list[0], (SEQS, LENGTH, MODEL_DIM), 1.0, 6.0, ((0, 16), (1, 2)))
    segment_ids = draw_segment_ids(jax.random.fold_in(key_list[13], 71), 0)
    positions = draw_positions(jax.random.fold_in(key_list[13], 71), 0)
    query_weight = scatter_about(key_list[3], (MODEL_DIM, QUERY_HEADS * HEAD_DIM), MODEL_DIM ** -0.5, 0.15625, ((0, 16), (1, 2)), jnp.float32)
    key_master_weight = scatter_about(key_list[4], (MODEL_DIM, KEY_VALUE_HEADS * HEAD_DIM), MODEL_DIM ** -0.5, 0.15625, ((0, 16), (1, 2)), jnp.float32)
    value_master_weight = scatter_about(key_list[5], (MODEL_DIM, KEY_VALUE_HEADS * HEAD_DIM), MODEL_DIM ** -0.5, 0.15625, ((0, 16), (1, 2)), jnp.float32)
    out_weight = scatter_about(key_list[6], (QUERY_HEADS * HEAD_DIM, MODEL_DIM), (max(QUERY_HEADS * HEAD_DIM // 64, 1)) ** -0.5, 1.25, ((0, 2), (1, 16)), jnp.float32)
    attn_gain = jnp.clip(1.0 + 0.1 * jax.random.normal(key_list[7], (MODEL_DIM,), jnp.float32), 0.5, 1.5)
    gate_weight = scatter_about(key_list[8], (MODEL_DIM, FF), MODEL_DIM ** -0.5, 0.15625, ((0, 16), (1, 2)), jnp.float32)
    up_weight = scatter_about(key_list[9], (MODEL_DIM, FF), MODEL_DIM ** -0.5, 0.15625, ((0, 16), (1, 2)), jnp.float32)
    down_weight = scatter_about(key_list[10], (FF, MODEL_DIM), FF ** -0.5, 0.09375, ((0, 2), (1, 16)), jnp.float32)
    mlp_gain = jnp.clip(1.0 + 0.1 * jax.random.normal(key_list[11], (MODEL_DIM,), jnp.float32), 0.5, 1.5)
    cotangent = bell_draw_with(key_list[12], (SEQS, LENGTH, MODEL_DIM), 1.0, 8.0, ((0, 16), (1, 2)), (0, 2, 16, 2.0))
    return dict(tokens=tokens, segment_ids=segment_ids, positions=positions, query_weight=query_weight, key_master_weight=key_master_weight, value_master_weight=value_master_weight, out_weight=out_weight, attn_gain=attn_gain, gate_weight=gate_weight, up_weight=up_weight, down_weight=down_weight, mlp_gain=mlp_gain, cotangent=cotangent)


EPSILON = 1e-05
ROPE_BASE = 100000.0
MASKED = -1000000000.0
PRECISE = lax.Precision.HIGHEST

@jax.custom_vjp
def lower_precision(v):
    return lax.optimization_barrier(v.astype(jnp.bfloat16)).astype(jnp.float32)

@jax.custom_vjp
def lower_precision_back(v):
    return v

def low_keep(v):
    return (lower_precision(v), None)

def low_pass(kept, grad):
    return (grad,)

def back_keep(v):
    return (v, None)

def back_low(kept, grad):
    return (lower_precision(grad),)
lower_precision.defvjp(low_keep, low_pass)
lower_precision_back.defvjp(back_keep, back_low)

def round_operands(value_tensor):
    return lower_precision(lower_precision_back(value_tensor))

def matrix_product(left, right):
    return jnp.dot(left, right, precision=PRECISE, preferred_element_type=jnp.float32)

def rope_tables(places, head_width):
    half_width = head_width // 2
    ladder = jnp.arange(half_width, dtype=jnp.float32)
    inverse = jnp.power(jnp.float32(ROPE_BASE), -2.0 * ladder / head_width)
    angles = places.astype(jnp.float32)[..., None] * inverse
    cosine_table = jnp.cos(angles)
    sine_table = jnp.sin(angles)
    return (jnp.concatenate([cosine_table, cosine_table], -1), jnp.concatenate([sine_table, sine_table], -1))

def rotate_pairs(value_tensor):
    half_width = value_tensor.shape[-1] // 2
    return jnp.concatenate([-value_tensor[..., half_width:], value_tensor[..., :half_width]], -1)

def rms_normed(value_tensor, gain_vec):
    return value_tensor * lax.rsqrt(lax.optimization_barrier(jnp.mean(value_tensor * value_tensor, -1, keepdims=True)) + EPSILON) * gain_vec

def decoder_layer(seq_tokens, segments, places, query_mat, key_matrix, value_matrix, out_mat, attn_vec, gate_mat, up_mat, down_mat, mlp_vec):
    token_length = seq_tokens.shape[0]
    cosine_table, sine_table = rope_tables(places, HEAD_DIM)
    cosine_table = cosine_table[:, None, :]
    sine_table = sine_table[:, None, :]
    normed_input = lower_precision(rms_normed(seq_tokens, attn_vec))
    query_tensor = lower_precision_back(matrix_product(normed_input, query_mat)).reshape(token_length, QUERY_HEADS, HEAD_DIM)
    key_tensor = lower_precision_back(matrix_product(normed_input, key_matrix)).reshape(token_length, KEY_VALUE_HEADS, HEAD_DIM)
    value_tensor = round_operands(matrix_product(normed_input, value_matrix)).reshape(token_length, KEY_VALUE_HEADS, HEAD_DIM)
    query_tensor = lower_precision(query_tensor * cosine_table + rotate_pairs(query_tensor) * sine_table).reshape(token_length, KEY_VALUE_HEADS, QUERY_HEADS // KEY_VALUE_HEADS, HEAD_DIM)
    key_tensor = lower_precision(key_tensor * cosine_table + rotate_pairs(key_tensor) * sine_table)
    scores = lower_precision_back(jnp.einsum('qgrd,kgd->grqk', query_tensor, key_tensor, precision=PRECISE) * (1.0 / math.sqrt(HEAD_DIM)))
    ladder = jnp.arange(token_length)
    allowed = (segments[:, None] == segments[None, :]) & (ladder[:, None] >= ladder[None, :])
    scores = jnp.where(allowed, scores, MASKED)
    probabilities = lower_precision(jax.nn.softmax(scores, axis=-1))
    attended = round_operands(jnp.einsum('grqk,kgd->qgrd', probabilities, value_tensor, precision=PRECISE)).reshape(token_length, QUERY_HEADS * HEAD_DIM)
    middle = seq_tokens + lower_precision_back(matrix_product(attended, out_mat))
    normed_two = lower_precision(rms_normed(middle, mlp_vec))
    gate_rows = lower_precision_back(matrix_product(normed_two, gate_mat))
    up_rows = lower_precision_back(matrix_product(normed_two, up_mat))
    hidden = lower_precision(jax.nn.silu(gate_rows) * up_rows)
    return middle + lower_precision_back(matrix_product(hidden, down_mat))

def reference(tokens, segment_ids, positions, query_weight, key_master_weight, value_master_weight, out_weight, attn_gain, gate_weight, up_weight, down_weight, mlp_gain, cotangent):
    masters = (query_weight, key_master_weight, value_master_weight, out_weight, attn_gain, gate_weight, up_weight, down_weight, mlp_gain)

    def forward(inputs, params):
        lowered = tuple((lower_precision(master) for master in params))

        def per_sequence(entries):
            return decoder_layer(entries[0], entries[1], entries[2], *lowered)
        return lax.map(jax.checkpoint(per_sequence), (inputs, segment_ids, positions))
    outputs, pullback = jax.vjp(forward, tokens.astype(jnp.float32), masters)
    input_grad, weight_grads = pullback(cotangent.astype(jnp.float32))
    return (outputs.astype(jnp.bfloat16), input_grad.astype(jnp.bfloat16), weight_grads[0], weight_grads[1], weight_grads[2], weight_grads[3], weight_grads[4], weight_grads[5], weight_grads[6], weight_grads[7], weight_grads[8])
```

```python
import functools
import math

import jax
import jax.numpy as jnp
from jax import lax
from jax.experimental import pallas as pl
from jax.experimental.pallas import tpu as pltpu
from jax.sharding import PartitionSpec as P

HEAD_DIM = 96
PAD_DIM = 128
BLOCK = 256
DOCS = 16
EPSILON = 1e-05
ROPE_BASE = 100000.0
FAR = float(2**30)
RING_LIMIT = 16
SCALE = 1.0 / math.sqrt(HEAD_DIM)
LOG2E = math.log2(math.e)

F32 = jnp.float32
BF16 = jnp.bfloat16


def mm(left, right, left_dim, right_dim, dtype=F32):
    return lax.dot_general(
        left, right, (((left_dim,), (right_dim,)), ((), ())), preferred_element_type=F32
    ).astype(dtype)


def swap_halves(value):
    return lax.ppermute(value, "tensor", [(0, 1), (1, 0)])


def ring_of(dp):
    chips = dp // 2
    order = list(range(0, chips, 2)) + list(range(chips - 1 - chips % 2, 0, -2))
    place = [0] * chips
    for spot, chip in enumerate(order):
        place[chip] = spot
    pairs = []
    for spot in range(chips):
        here, after = order[spot], order[(spot + 1) % chips]
        pairs.append((2 * here, 2 * after))
        pairs.append((2 * after + 1, 2 * here + 1))
    return order, place, pairs


def ring_state(dp):
    order, place, pairs = ring_of(dp)
    chips = dp // 2
    me = lax.axis_index("dp")
    core = me % 2
    spot = jnp.asarray(place, jnp.int32)[me // 2]
    order = jnp.asarray(order, jnp.int32)

    def chip_at(steps, which):
        shift = jnp.where(which == 0, steps, -steps)
        return order[(spot + shift + 2 * chips) % chips]

    return me, core, chip_at, pairs


def gather_rows(shard, dp):
    if dp > RING_LIMIT or dp < 4:
        return lax.all_gather(shard, "dp", axis=0, tiled=True)
    rows = shard.shape[0]
    me, core, chip_at, pairs = ring_state(dp)
    swap = [(i, i ^ 1) for i in range(dp)]
    whole = jnp.zeros((dp * rows, shard.shape[1]), shard.dtype)

    def put(whole, piece, device):
        return lax.dynamic_update_slice(whole, piece, (device * rows, 0))

    held = shard
    for step in range(dp // 2):
        if step:
            held = lax.ppermute(held, "dp", pairs)
        other = lax.ppermute(held, "dp", swap)
        whole = put(whole, held, 2 * chip_at(-step, core) + core)
        whole = put(whole, other, 2 * chip_at(-step, 1 - core) + 1 - core)
    return whole


def scatter_rows(full, dp):
    if dp > RING_LIMIT or dp < 4:
        return lax.psum_scatter(full, "dp", scatter_dimension=0, tiled=True).astype(F32)
    rows = full.shape[0] // dp
    width = full.shape[1]
    chips = dp // 2
    me, core, chip_at, pairs = ring_state(dp)
    swap = [(i, i ^ 1) for i in range(dp)]
    parts = full.reshape(chips, 2, rows, width)
    mine = lax.dynamic_slice(parts, (0, core, 0, 0), (chips, 1, rows, width))[:, 0]
    theirs = lax.dynamic_slice(parts, (0, 1 - core, 0, 0), (chips, 1, rows, width))[:, 0]
    got = lax.ppermute(theirs, "dp", swap)

    def local(steps):
        chip = chip_at(steps, core)
        both = [lax.dynamic_slice(a, (chip, 0, 0), (1, rows, width))[0] for a in (mine, got)]
        return both[0].astype(F32) + both[1].astype(F32)

    total = local(-1)
    for step in range(2, chips + 1):
        held = lax.ppermute(total.astype(BF16), "dp", pairs)
        total = held.astype(F32) + local(-step)
    return total


def place_of(natural, side, length):
    return pl.multiple_of((natural + side * (length // 2)) % length, BLOCK)


def rope_rows(top, bottom, cos, sin):
    return top * cos - bottom * sin, bottom * cos + top * sin


def diagonal():
    keys = lax.broadcasted_iota(jnp.int32, (BLOCK, BLOCK), 0)
    queries = lax.broadcasted_iota(jnp.int32, (BLOCK, BLOCK), 1)
    return keys <= queries


def forward_kernel(
    side_ref, q_in, k_in, v_in, cos_ref, sin_ref, oq_ref, ok_ref,
    att_ref, q_out, k_out, v_out, lse_ref, q_scr, kt_scr, k_scr,
):
    length = q_in.shape[1]
    half = HEAD_DIM // 2
    side = side_ref[0]
    blocks = length // BLOCK
    kt_scr[HEAD_DIM:, :] = jnp.zeros((PAD_DIM - HEAD_DIM, length), BF16)
    kt_scr[HEAD_DIM : HEAD_DIM + DOCS, :] = ok_ref[...]
    for h in range(2):
        q_scr[h, HEAD_DIM:, :] = jnp.zeros((PAD_DIM - HEAD_DIM, length), BF16)
        q_scr[h, HEAD_DIM : HEAD_DIM + DOCS, :] = oq_ref[...]
    for b in range(blocks):
        here = pl.ds(b * BLOCK, BLOCK)
        there = pl.ds(place_of(b * BLOCK, side, length), BLOCK)
        cos, sin = cos_ref[:, there], sin_ref[:, there]
        for source, row, target in (
            (q_in, 0, q_scr.at[0]),
            (q_in, HEAD_DIM, q_scr.at[1]),
            (k_in, 0, kt_scr),
        ):
            top, bottom = rope_rows(
                source[row : row + half, there], source[row + half : row + HEAD_DIM, there], cos, sin
            )
            target[:half, here] = top.astype(BF16)
            target[half:HEAD_DIM, here] = bottom.astype(BF16)
        v_out[:, here] = v_in[:, there].astype(BF16)
    for h in range(2):
        q_out[h * HEAD_DIM : (h + 1) * HEAD_DIM, :] = q_scr[h, :HEAD_DIM, :]
    k_out[...] = kt_scr[:HEAD_DIM, :]
    k_scr[...] = kt_scr[...].T
    causal = diagonal()
    for h in range(2):
        for b in range(blocks):
            here = pl.ds(b * BLOCK, BLOCK)
            keys = (b + 1) * BLOCK
            query = q_scr[h, :, here]
            last = mm(k_scr[b * BLOCK : keys, :], query, 1, 0)
            last = jnp.where(causal, last, -FAR)
            top = jnp.max(last, 0, keepdims=True)
            if b:
                early = mm(k_scr[: b * BLOCK, :], query, 1, 0)
                top = jnp.maximum(top, jnp.max(early, 0, keepdims=True))
            top = top * (SCALE * LOG2E)
            weight = jnp.exp2(last * (SCALE * LOG2E) - top)
            total = jnp.sum(weight, 0, keepdims=True)
            out = mm(v_out[:, b * BLOCK : keys], weight.astype(BF16), 1, 0)
            if b:
                weight = jnp.exp2(early * (SCALE * LOG2E) - top)
                total = total + jnp.sum(weight, 0, keepdims=True)
                out = out + mm(v_out[:, : b * BLOCK], weight.astype(BF16), 1, 0)
            out = out / total
            there = pl.ds(place_of(b * BLOCK, side, length), BLOCK)
            att_ref[h * HEAD_DIM : (h + 1) * HEAD_DIM, there] = out.astype(BF16)
            lse_ref[0, h : h + 1, here] = top + jnp.log2(total)


def attend(side, qkv, cos, sin, doc_q, doc_k):
    hidden, length = qkv.shape
    groups = hidden // (4 * HEAD_DIM)
    whole = lambda g, s: (0, 0)
    spec = pl.BlockSpec
    return pl.pallas_call(
        forward_kernel,
        grid_spec=pltpu.PrefetchScalarGridSpec(
            num_scalar_prefetch=1,
            grid=(groups,),
            in_specs=[
                spec((2 * HEAD_DIM, length), lambda g, s: (g, 0)),
                spec((HEAD_DIM, length), lambda g, s: (2 * groups + g, 0)),
                spec((HEAD_DIM, length), lambda g, s: (3 * groups + g, 0)),
                spec((HEAD_DIM // 2, length), whole),
                spec((HEAD_DIM // 2, length), whole),
                spec((DOCS, length), whole),
                spec((DOCS, length), whole),
            ],
            out_specs=[
                spec((2 * HEAD_DIM, length), lambda g, s: (g, 0)),
                spec((2 * HEAD_DIM, length), lambda g, s: (g, 0)),
                spec((HEAD_DIM, length), lambda g, s: (g, 0)),
                spec((HEAD_DIM, length), lambda g, s: (g, 0)),
                spec((1, 2, length), lambda g, s: (g, 0, 0)),
            ],
            scratch_shapes=[
                pltpu.VMEM((2, PAD_DIM, length), BF16),
                pltpu.VMEM((PAD_DIM, length), BF16),
                pltpu.VMEM((length, PAD_DIM), BF16),
            ],
        ),
        out_shape=[
            jax.ShapeDtypeStruct((2 * groups * HEAD_DIM, length), BF16),
            jax.ShapeDtypeStruct((2 * groups * HEAD_DIM, length), BF16),
            jax.ShapeDtypeStruct((groups * HEAD_DIM, length), BF16),
            jax.ShapeDtypeStruct((groups * HEAD_DIM, length), BF16),
            jax.ShapeDtypeStruct((groups, 2, length), F32),
        ],
        compiler_params=pltpu.CompilerParams(vmem_limit_bytes=48 * 2**20),
        cost_estimate=pl.CostEstimate(
            flops=groups * 4 * length * length * 192, bytes_accessed=12 * 2**20,
            transcendentals=groups * length * length,
        ),
        name="attend",
    )(side, qkv, qkv, qkv, cos, sin, doc_q, doc_k)


def backward_kernel(
    side_ref, q_ref, k_ref, v_ref, att_ref, datt_ref, lse_ref, cos_ref, sin_ref, oq_ref, ok_ref,
    dq_ref, dk_ref, dv_ref, q_scr, kt_scr, k_scr, vt_scr, v_scr, do_scr, dq_scr, dk_scr, dv_scr,
):
    length = q_ref.shape[1]
    half = HEAD_DIM // 2
    side = side_ref[0]
    blocks = length // BLOCK
    blank = jnp.zeros((PAD_DIM - HEAD_DIM, length), BF16)
    kt_scr[:HEAD_DIM, :] = k_ref[...]
    kt_scr[HEAD_DIM:, :] = blank
    kt_scr[HEAD_DIM : HEAD_DIM + DOCS, :] = ok_ref[...]
    vt_scr[:HEAD_DIM, :] = v_ref[...]
    vt_scr[HEAD_DIM:, :] = blank
    k_scr[...] = kt_scr[...].T
    v_scr[...] = vt_scr[...].T
    causal = diagonal()
    for h in range(2):
        rows = slice(h * HEAD_DIM, (h + 1) * HEAD_DIM)
        q_scr[:HEAD_DIM, :] = q_ref[rows, :]
        q_scr[HEAD_DIM:, :] = blank
        q_scr[HEAD_DIM : HEAD_DIM + DOCS, :] = oq_ref[...]
        do_scr[HEAD_DIM:, :] = blank
        for b in range(blocks):
            here = pl.ds(b * BLOCK, BLOCK)
            there = pl.ds(place_of(b * BLOCK, side, length), BLOCK)
            do_scr[:HEAD_DIM, here] = datt_ref[rows, there]
            base = jnp.sum(
                datt_ref[rows, there].astype(F32) * att_ref[rows, there].astype(F32), 0, keepdims=True
            )
            keys = (b + 1) * BLOCK
            query, upstream = q_scr[:, here], do_scr[:, here]
            level = lse_ref[0, h : h + 1, here]
            dq = None
            for start, stop in ((b * BLOCK, keys), (0, b * BLOCK)):
                if start == stop:
                    continue
                span = slice(start, stop)
                score = mm(k_scr[span, :], query, 1, 0)
                prob = jnp.exp2(score * (SCALE * LOG2E) - level)
                if start:
                    prob = jnp.where(causal, prob, 0.0)
                elif stop == keys:
                    prob = jnp.where(causal, prob, 0.0)
                slope = mm(v_scr[span, :], upstream, 1, 0)
                ds = (prob * (slope - base)).astype(BF16)
                part = mm(kt_scr[:HEAD_DIM, span], ds, 1, 0)
                dq = part if dq is None else dq + part
                dk = mm(query[:HEAD_DIM, :], ds, 1, 1)
                dv = mm(upstream[:HEAD_DIM, :], prob.astype(BF16), 1, 1)
                if h == 0 and start == b * BLOCK:
                    dk_scr[:, span] = dk
                    dv_scr[:, span] = dv
                else:
                    dk_scr[:, span] += dk
                    dv_scr[:, span] += dv
            cos, sin = cos_ref[:, there], sin_ref[:, there]
            dq = dq * SCALE
            top, bottom = rope_rows(dq[:half, :], dq[half:, :], cos, -sin)
            dq_ref[h * HEAD_DIM : h * HEAD_DIM + half, there] = top.astype(BF16)
            dq_ref[h * HEAD_DIM + half : (h + 1) * HEAD_DIM, there] = bottom.astype(BF16)
    for b in range(blocks):
        here = pl.ds(b * BLOCK, BLOCK)
        there = pl.ds(place_of(b * BLOCK, side, length), BLOCK)
        cos, sin = cos_ref[:, there], sin_ref[:, there]
        dk = dk_scr[:, here] * SCALE
        top, bottom = rope_rows(dk[:half, :], dk[half:, :], cos, -sin)
        dk_ref[:half, there] = top.astype(BF16)
        dk_ref[half:, there] = bottom.astype(BF16)
        dv_ref[:, there] = dv_scr[:, here].astype(BF16)


def attend_back(side, q, k, v, att, datt, lse, cos, sin, doc_q, doc_k):
    length = q.shape[1]
    groups = k.shape[0] // HEAD_DIM
    whole = lambda g, s: (0, 0)
    spec = pl.BlockSpec
    wide = spec((2 * HEAD_DIM, length), lambda g, s: (g, 0))
    narrow = spec((HEAD_DIM, length), lambda g, s: (g, 0))
    table = spec((HEAD_DIM // 2, length), whole)
    docs = spec((DOCS, length), whole)
    return pl.pallas_call(
        backward_kernel,
        grid_spec=pltpu.PrefetchScalarGridSpec(
            num_scalar_prefetch=1,
            grid=(groups,),
            in_specs=[
                wide, narrow, narrow, wide, wide, spec((1, 2, length), lambda g, s: (g, 0, 0)),
                table, table, docs, docs,
            ],
            out_specs=[wide, narrow, narrow],
            scratch_shapes=[
                pltpu.VMEM((PAD_DIM, length), BF16),
                pltpu.VMEM((PAD_DIM, length), BF16),
                pltpu.VMEM((length, PAD_DIM), BF16),
                pltpu.VMEM((PAD_DIM, length), BF16),
                pltpu.VMEM((length, PAD_DIM), BF16),
                pltpu.VMEM((PAD_DIM, length), BF16),
                pltpu.VMEM((HEAD_DIM, length), F32),
                pltpu.VMEM((HEAD_DIM, length), F32),
                pltpu.VMEM((HEAD_DIM, length), F32),
            ],
        ),
        out_shape=[
            jax.ShapeDtypeStruct(q.shape, BF16),
            jax.ShapeDtypeStruct(k.shape, BF16),
            jax.ShapeDtypeStruct(v.shape, BF16),
        ],
        compiler_params=pltpu.CompilerParams(vmem_limit_bytes=48 * 2**20),
        cost_estimate=pl.CostEstimate(
            flops=groups * 10 * length * length * 192, bytes_accessed=12 * 2**20,
            transcendentals=groups * length * length,
        ),
        name="attend_back",
    )(side, q, k, v, att, datt, lse, cos, sin, doc_q, doc_k)


def rms_inverse(value):
    return lax.rsqrt(jnp.mean(value * value, -1, keepdims=True) + EPSILON)


def norm_back(upstream, value, inverse, gain):
    scaled = upstream * gain
    inner = jnp.mean(scaled * value, -1, keepdims=True)
    return inverse * (scaled - value * inverse * inverse * inner)


def layer(
    dp, tokens, segment_ids, positions, query_weight, key_weight, value_weight, out_weight,
    attn_gain, gate_weight, up_weight, down_weight, mlp_gain, cotangent,
):
    seqs, own_rows, model = tokens.shape
    length = segment_ids.shape[1]
    heads = query_weight.shape[1]
    qkv_width = 2 * heads
    ff = gate_weight.shape[1]
    side_index = lax.axis_index("tensor").astype(jnp.int32)
    side = side_index[None]

    x_own = tokens.reshape(own_rows, model)
    e_own = cotangent.reshape(own_rows, model)
    x_par = swap_halves(x_own)
    e_par = swap_halves(e_own)

    low = lambda w: w.astype(BF16)
    gains = jnp.pad(jnp.stack([low(attn_gain), low(mlp_gain)], 1), ((0, 0), (0, 126)))
    first = gather_rows(
        jnp.concatenate(
            [low(query_weight), low(key_weight), low(value_weight), low(out_weight).T, gains], 1
        ),
        dp,
    )
    second = gather_rows(
        jnp.concatenate([low(gate_weight), low(up_weight), low(down_weight).T], 1), dp
    )
    qkv_full = first[:, :qkv_width]
    out_full = first[:, qkv_width : qkv_width + heads]
    gain_one = first[:, qkv_width + heads].astype(F32)
    gain_two = first[:, qkv_width + heads + 1].astype(F32)
    gate_full, up_full, down_full = (second[:, i * ff : (i + 1) * ff] for i in range(3))

    x = jnp.concatenate([x_own, x_par], 0).astype(F32)
    inverse_one = rms_inverse(x)
    normed_one = (x * inverse_one * gain_one).astype(BF16)

    places = positions.reshape(length).astype(F32)
    half = HEAD_DIM // 2
    places = jnp.where(side_index == 0, places, jnp.roll(places, length // 2))
    ladder = jnp.power(F32(ROPE_BASE), -2.0 * jnp.arange(half, dtype=F32) / HEAD_DIM)
    angles = ladder[:, None] * places[None, :]
    cos, sin = jnp.cos(angles), jnp.sin(angles)
    known = jnp.arange(DOCS, dtype=jnp.int32)[:, None] == segment_ids.reshape(1, length)
    doc_q = known.astype(BF16)
    doc_k = jnp.where(known, 0.0, -FAR).astype(BF16)

    qkv = mm(qkv_full, normed_one, 0, 1)
    att, q, k, v, lse = attend(side, qkv, cos, sin, doc_q, doc_k)

    sent = swap_halves(mm(att[:, own_rows:], out_full, 0, 1, BF16))
    middle = x_own.astype(F32) + (mm(att[:, :own_rows], out_full, 0, 1) + sent.astype(F32))
    inverse_two = rms_inverse(middle)
    b_own = (middle * inverse_two * gain_two).astype(BF16)
    b = jnp.concatenate([b_own, swap_halves(b_own)], 0)
    e = jnp.concatenate([e_own, e_par], 0)

    gate = mm(b, gate_full, 1, 0)
    up = mm(b, up_full, 1, 0)
    sig = jax.nn.sigmoid(gate)
    silu = gate * sig
    hidden = (silu * up).astype(BF16)
    dhid = mm(e, down_full, 1, 0)
    dgate = (dhid * up * (sig * (1.0 + gate * (1.0 - sig)))).astype(BF16)
    dup = (dhid * silu).astype(BF16)

    def db_of(rows):
        return mm(dgate[rows], gate_full, 1, 1) + mm(dup[rows], up_full, 1, 1)

    own, par = slice(0, own_rows), slice(own_rows, None)
    db_sent = swap_halves(db_of(par).astype(BF16))
    db = db_of(own) + db_sent.astype(F32)
    dh = e_own.astype(F32) + norm_back(db, middle, inverse_two, gain_two)
    gain_two_grad = jnp.sum(db * middle * inverse_two, 0)
    eh_own = dh.astype(BF16)
    eh = jnp.concatenate([eh_own, swap_halves(eh_own)], 0)

    down_sent = swap_halves(mm(hidden[par], down_full, 1, 1, BF16))
    output = (middle + (mm(hidden[own], down_full, 1, 1) + down_sent.astype(F32))).astype(BF16)

    grad_down = scatter_rows(mm(e, hidden, 0, 0, BF16), dp)
    grad_gate = scatter_rows(mm(b, dgate, 0, 0, BF16), dp)
    grad_up = scatter_rows(mm(b, dup, 0, 0, BF16), dp)

    datt = mm(out_full, eh, 0, 1, BF16)
    grad_out = mm(eh, att, 0, 1, BF16)
    dq, dk, dv = attend_back(side, q, k, v, att, datt, lse, cos, sin, doc_q, doc_k)
    dqkv = jnp.concatenate([dq, dk, dv], 0)
    grad_qkv = mm(normed_one, dqkv, 0, 1, BF16)
    da_par = mm(dqkv[:, own_rows:], qkv_full, 0, 1)
    da_own = mm(dqkv[:, :own_rows], qkv_full, 0, 1)
    scaled = x * inverse_one
    gain_one_grad = jnp.sum(da_own * scaled[own], 0) + jnp.sum(da_par * scaled[par], 0)
    gain_grads = jnp.pad(jnp.stack([gain_one_grad, gain_two_grad], 1), ((0, 0), (0, 126)))
    da = da_own + swap_halves(da_par.astype(BF16)).astype(F32)
    input_grad = (dh + norm_back(da, x[own], inverse_one[own], gain_one)).astype(BF16)

    last = scatter_rows(jnp.concatenate([grad_qkv, grad_out, gain_grads.astype(BF16)], 1), dp)
    gain_shard = last[:, qkv_width + heads :]
    gain_shard = gain_shard + swap_halves(gain_shard)
    kv = heads // 2
    return (
        output.reshape(seqs, own_rows, model),
        input_grad.reshape(seqs, own_rows, model),
        last[:, :heads],
        last[:, heads : heads + kv],
        last[:, heads + kv : qkv_width],
        last[:, qkv_width : qkv_width + heads].T,
        gain_shard[:, 0],
        grad_gate,
        grad_up,
        grad_down.T,
        gain_shard[:, 1],
    )


def solution(mesh):
    in_specs = (
        P("dp", "tensor", None),
        P("dp", None),
        P("dp", None),
        P("dp", "tensor"),
        P("dp", "tensor"),
        P("dp", "tensor"),
        P("tensor", "dp"),
        P("dp"),
        P("dp", "tensor"),
        P("dp", "tensor"),
        P("tensor", "dp"),
        P("dp"),
        P("dp", "tensor", None),
    )
    out_specs = (
        P("dp", "tensor", None),
        P("dp", "tensor", None),
        P("dp", "tensor"),
        P("dp", "tensor"),
        P("dp", "tensor"),
        P("tensor", "dp"),
        P("dp"),
        P("dp", "tensor"),
        P("dp", "tensor"),
        P("tensor", "dp"),
        P("dp"),
    )
    return jax.shard_map(
        functools.partial(layer, mesh.shape["dp"]),
        mesh=mesh,
        in_specs=in_specs,
        out_specs=out_specs,
        check_vma=False,
    )
```

```python
import functools
import math

import jax
import jax.numpy as jnp
from jax import lax
from jax.experimental import pallas as pl
from jax.experimental.pallas import tpu as pltpu
from jax.sharding import PartitionSpec as P

HEAD_DIM = 96
PAD_DIM = 128
BLOCK = 256
DOCS = 16
EPSILON = 1e-05
ROPE_BASE = 100000.0
FAR = float(2**30)
RING_LIMIT = 16
TILE = 512
SCALE = 1.0 / math.sqrt(HEAD_DIM)
LOG2E = math.log2(math.e)

F32 = jnp.float32
BF16 = jnp.bfloat16


def mm(left, right, left_dim, right_dim, dtype=F32):
    return lax.dot_general(
        left, right, (((left_dim,), (right_dim,)), ((), ())), preferred_element_type=F32
    ).astype(dtype)


def swap_halves(value):
    return lax.ppermute(value, "tensor", [(0, 1), (1, 0)])


def is_ring(dp):
    return 8 <= dp <= RING_LIMIT and dp & (dp - 1) == 0


def chip_of(spot, chips):
    return jnp.where(2 * spot < chips, 2 * spot, 2 * (chips - 1 - spot) + 1)


def ring_pairs(dp):
    chips = dp // 2
    order = list(range(0, chips, 2)) + list(range(chips - 1, 0, -2))
    ahead = []
    for spot in range(chips):
        here, following = order[spot], order[(spot + 1) % chips]
        ahead += [(2 * here, 2 * following), (2 * here + 1, 2 * following + 1)]
    return ahead, [(b, a) for a, b in ahead]


def ring_place(dp):
    chips = dp // 2
    me = lax.axis_index("dp").astype(jnp.int32)
    chip = me >> 1
    return me & 1, jnp.where(chip & 1 == 0, chip >> 1, chips - 1 - (chip >> 1))


def piece_steps(dp):
    reach = dp // 4
    return [0, *range(-1, -reach, -1), *range(1, reach), reach, reach]


def piece_blocks(dp):
    if not is_ring(dp):
        return jnp.zeros((1,), jnp.int32)
    chips = dp // 2
    core, spot = ring_place(dp)
    chip = chip_of((spot + jnp.asarray(piece_steps(dp), jnp.int32)) & (chips - 1), chips)
    return jnp.concatenate([2 * chip + core, 2 * chip + 1 - core])


def turn_blocks(dp):
    if not is_ring(dp):
        return jnp.zeros((1,), jnp.int32)
    chips = dp // 2
    core, spot = ring_place(dp)
    chip = chip_of((spot + jnp.arange(chips, dtype=jnp.int32)) & (chips - 1), chips)
    return jnp.concatenate([2 * chip + 1 - core, 2 * chip + core])


class Order:
    def __init__(self, flag):
        self.token = lax.create_token()
        self.flag = flag

    def tie(self, *values):
        tied = lax.optimization_barrier((self.token, *values))[1:]
        return tied if len(values) > 1 else tied[0]

    def done(self, *values):
        self.token, *values = lax.optimization_barrier((self.token, *values))
        return values if len(values) > 1 else values[0]


class Gather:
    def __init__(self, shard, dp, cut):
        self.dp, self.cut = dp, cut
        self.behind, self.ahead, self.other, self.shard = [], [], [], shard

    def share(self, order):
        if not is_ring(self.dp):
            return
        found = (self.behind[-1], self.ahead[-1]) if self.other else (self.shard,)
        swap = [(i, i ^ 1) for i in range(self.dp)]

        def both(*pieces):
            return tuple(lax.ppermute(piece, "dp", swap) for piece in pieces)

        def neither(*pieces):
            return tuple(jnp.zeros_like(piece) for piece in pieces)

        found = order.tie(*found) if len(found) > 1 else (order.tie(*found),)
        got = lax.cond(order.flag, both, neither, *found)
        self.other.append(order.done(*got) if len(got) > 1 else [order.done(*got)])

    def round(self, order):
        if not is_ring(self.dp):
            return
        forth, back = ring_pairs(self.dp)
        left = self.behind[-1] if self.behind else self.shard
        right = self.ahead[-1] if self.ahead else self.shard
        if len(self.behind) == self.dp // 4 - 1:
            left, right = left[:, : self.cut], right[:, self.cut :]
        left, right = order.done(*order.tie(left, right))
        self.behind.append(lax.ppermute(left, "dp", forth))
        self.ahead.append(lax.ppermute(right, "dp", back))

    def arrive(self, order):
        if is_ring(self.dp):
            self.behind[-1], self.ahead[-1] = order.done(self.behind[-1], self.ahead[-1])

    def next(self, order):
        if not is_ring(self.dp):
            return
        self.arrive(order)
        arrived = self.behind[-1], self.ahead[-1]
        self.round(order)
        sent = self.behind.pop(), self.ahead.pop()
        self.behind[-1], self.ahead[-1] = arrived
        self.share(order)
        self.behind.append(sent[0])
        self.ahead.append(sent[1])

    def pieces(self, order):
        if not is_ring(self.dp):
            return [(lax.all_gather(self.shard, "dp", axis=0, tiled=True), 0)]
        self.arrive(order)
        self.share(order)
        held = [self.shard, *self.behind[:-1], *self.ahead[:-1], self.behind[-1], self.ahead[-1]]
        other = [self.other[0][0], *(pair[0] for pair in self.other[1:-1])]
        other += [*(pair[1] for pair in self.other[1:-1]), *self.other[-1]]
        columns = [0] * (len(held) - 1) + [self.cut]
        return list(zip([*held, *other], columns * 2))


class Scatter:
    def __init__(self, dp, order, *columns):
        self.dp, self.order = dp, order
        lefts, rights, dims = zip(*columns)
        rights = order.tie(*rights) if len(rights) > 1 else (order.tie(*rights),)
        if not is_ring(dp):
            full = order.done(products(0, 1, lefts, rights, dims))
            self.total = lax.psum_scatter(full, "dp", scatter_dimension=0, tiled=True).astype(F32)
            return
        self.chips = dp // 2
        self.reach = self.chips // 2
        self.rows = lefts[0].shape[0] // dp

        def both(lefts, rights):
            token = lax.create_token()
            theirs = products(0, 2, lefts, rights, dims)
            token, theirs = lax.optimization_barrier((token, theirs))
            got = lax.ppermute(theirs, "dp", [(i, i ^ 1) for i in range(dp)])
            rights = lax.optimization_barrier((token, *rights))[1:]
            return got, products(1, 2, lefts, rights, dims)

        def neither(lefts, rights):
            width = sum(right.shape[1 - dim] for right, dim in zip(rights, dims))
            return (jnp.zeros((lefts[0].shape[0] // 2, width), BF16),) * 2

        self.got, self.mine = order.done(*lax.cond(order.flag, both, neither, lefts, tuple(rights)))
        self.width = self.mine.shape[1]
        self.ahead = self.behind = None

    def local(self, steps, mine, first, low_edge, high_edge):
        block = steps % self.chips
        return [(part, block, first, low_edge, high_edge) for part in (mine, self.got)]

    def round(self):
        if not is_ring(self.dp):
            return
        forth, back = ring_pairs(self.dp)
        half = self.width // 2
        tile = half if half <= 1536 else half // 2
        count = half // tile
        mine = self.order.tie(self.mine)
        reach = self.reach
        if self.ahead is None:
            right = self.local(reach, mine, 0, 0, count)
            left = self.local(reach, mine, count, 0, count)
        else:
            cut = count if self.ahead.shape[1] == half else 2 * count
            right = [*self.local(reach, mine, 0, 0, 2 * count), (self.ahead, 0, 0, 0, cut)]
            left = [*self.local(-reach, mine, 0, 0, 2 * count)]
            left.append((self.behind, 0, 0, 2 * count - cut, 2 * count))
        right, left = self.order.done(*combine(self.rows, tile, [right, left]))
        self.ahead = lax.ppermute(right, "dp", forth)
        self.behind = lax.ppermute(left, "dp", back)
        self.reach -= 1

    def result(self):
        if not is_ring(self.dp):
            return self.total
        mine = self.order.tie(self.mine)
        half = self.width // 2
        tile = half if half <= 1536 else half // 2
        count = self.width // tile
        terms = self.local(0, mine, 0, 0, count)
        terms += [(self.ahead, 0, 0, 0, count), (self.behind, 0, 0, 0, count)]
        return self.order.done(*combine(self.rows, tile, [terms], F32))


def rope_rows(top, bottom, cos, sin):
    return top * cos - bottom * sin, bottom * cos + top * sin


def project_kernel(columns, rows, heads, block_ref, turn_ref, own_ref, par_ref, cos_ref, sin_ref, *rest):
    count = len(columns)
    pieces = rest[:count]
    qkv_ref, gain_ref, at_ref, wide_ref, out_ref = rest[count : count + 5]
    w_scr, a_scr, at_scr, in_sem, out_sem, turn_sem = rest[count + 5 :]
    step = pl.program_id(0)
    tiles = pl.num_programs(0)
    own_rows, model = own_ref.shape
    tile = qkv_ref.shape[0]
    half = HEAD_DIM // 2
    qkv_width = 2 * heads

    def loads(i):
        base = pl.multiple_of(block_ref[i] * rows, rows)
        place = slice(columns[i], columns[i] + pieces[i].shape[1])
        return pltpu.make_async_copy(pieces[i], w_scr.at[pl.ds(base, rows), place], in_sem.at[i])

    def stores():
        return (
            pltpu.make_async_copy(w_scr.at[:, :qkv_width], wide_ref, out_sem.at[0]),
            pltpu.make_async_copy(
                w_scr.at[:, qkv_width : qkv_width + heads], out_ref, out_sem.at[1]
            ),
        )

    def turns(i):
        block = model // turn_ref.shape[0]
        base = pl.multiple_of(turn_ref[i] * block, block)
        return pltpu.make_async_copy(
            at_scr.at[pl.ds(base, block), :], at_ref.at[pl.ds(i * block, block), :], turn_sem.at[i]
        )

    @pl.when(step == 0)
    def _():
        for i in range(count):
            loads(i).start()
        for i in range(count):
            loads(i).wait()
        gains = w_scr[:, qkv_width + heads :].astype(F32).T
        gain_ref[...] = gains[:8, :]
        gain = gains[:1, :]
        for number, ref in enumerate((own_ref, par_ref)):

            @pl.loop(0, own_rows // BLOCK)
            def _(part, ref=ref, number=number):
                start = pl.multiple_of(part * BLOCK, BLOCK)
                x = ref[pl.ds(start, BLOCK), :].astype(F32)
                inverse = lax.rsqrt(jnp.mean(x * x, -1, keepdims=True) + EPSILON)
                normed = x * inverse * gain
                place = pl.multiple_of(start + number * own_rows, BLOCK)
                a_scr[pl.ds(place, BLOCK), :] = normed.astype(BF16)
                at_scr[:, pl.ds(place, BLOCK)] = normed.T.astype(BF16)

        for copy in stores():
            copy.start()
        for i in range(turn_ref.shape[0]):
            turns(i).start()

    start = pl.multiple_of(step * tile, 128)
    flat = mm(a_scr[...], w_scr[:, pl.ds(start, tile)], 1, 0).T

    @pl.when(step < tiles - tiles // 4)
    def _():
        cos, sin = cos_ref[...], sin_ref[...]
        for h in range(tile // HEAD_DIM):
            base = h * HEAD_DIM
            top, bottom = rope_rows(
                flat[base : base + half, :], flat[base + half : base + HEAD_DIM, :], cos, sin
            )
            qkv_ref[base : base + half, :] = top.astype(BF16)
            qkv_ref[base + half : base + HEAD_DIM, :] = bottom.astype(BF16)

    @pl.when(step >= tiles - tiles // 4)
    def _():
        qkv_ref[...] = flat.astype(BF16)

    @pl.when(step == tiles - 1)
    def _():
        for copy in stores():
            copy.wait()
        for i in range(turn_ref.shape[0]):
            turns(i).wait()


FREE = pl.CostEstimate(flops=0, bytes_accessed=0, transcendentals=0)
LONG = pl.CostEstimate(flops=0, bytes_accessed=40 * 2**20, transcendentals=0)


def product_kernel(dim, flip, left_ref, right_ref, *out_refs):
    out = mm(left_ref[...], right_ref[...], 1, dim)
    out = (out.T if flip else out).astype(out_refs[0].dtype)
    start = 0
    for ref in out_refs:
        ref[...] = out[start : start + ref.shape[0], :]
        start += ref.shape[0]


def product(left, right, dim, tile=TILE, dtype=BF16, flip=False, parts=None):
    rows, depth = left.shape
    width = right.shape[1 - dim]
    tile = next(t for t in (tile, 384, 256, width) if width % t == 0)
    spec = pl.BlockSpec
    block, where = ((tile, depth), lambda j: (j, 0)) if dim else ((depth, tile), lambda j: (0, j))
    if flip:
        out_specs = [spec((tile, rows), lambda j: (j, 0))]
        shapes = [jax.ShapeDtypeStruct((width, rows), dtype)]
    else:
        parts = parts or [rows]
        out_specs = [spec((part, tile), lambda j: (0, j)) for part in parts]
        shapes = [jax.ShapeDtypeStruct((part, width), dtype) for part in parts]
    out = pl.pallas_call(
        functools.partial(product_kernel, dim, flip),
        grid=(width // tile,),
        in_specs=[spec((rows, depth), lambda j: (0, 0)), spec(block, where)],
        out_specs=out_specs,
        out_shape=shapes,
        compiler_params=pltpu.CompilerParams(vmem_limit_bytes=56 * 2**20),
        cost_estimate=FREE,
        name="product",
    )(left, right)
    return out if len(out) > 1 else out[0]


def products_kernel(starts, dims, *refs):
    count = len(dims)
    out_ref = refs[-1]
    step = pl.program_id(0)
    for i, dim in enumerate(dims):

        @pl.when((step >= starts[i]) & (step < starts[i + 1]))
        def _(i=i, dim=dim):
            out_ref[...] = mm(refs[i][...], refs[count + i][...], 1, dim, out_ref.dtype)


def products(part, parts, lefts, rights, dims):
    rows, depth = lefts[0].shape
    rows = rows // parts
    widths = [right.shape[1 - dim] for right, dim in zip(rights, dims)]
    tile = next(t for t in (1024, 768, TILE, 384) if all(width % t == 0 for width in widths))
    starts = [0]
    for width in widths:
        starts.append(starts[-1] + width // tile)
    spec = pl.BlockSpec
    in_specs = [spec((rows, depth), lambda j: (part, 0)) for _ in lefts]
    for i, dim in enumerate(dims):

        def place(j, i=i):
            return jnp.clip(j - starts[i], 0, starts[i + 1] - starts[i] - 1)

        if dim:
            in_specs.append(spec((tile, depth), lambda j, place=place: (place(j), 0)))
        else:
            in_specs.append(spec((depth, tile), lambda j, place=place: (0, place(j))))
    return pl.pallas_call(
        functools.partial(products_kernel, starts, dims),
        grid=(starts[-1],),
        in_specs=in_specs,
        out_specs=spec((rows, tile), lambda j: (0, j)),
        out_shape=jax.ShapeDtypeStruct((rows, sum(widths)), BF16),
        compiler_params=pltpu.CompilerParams(vmem_limit_bytes=56 * 2**20),
        cost_estimate=FREE,
        name="products",
    )(*lefts, *rights)


def combine_kernel(outs, *refs):
    step = pl.program_id(0)
    inputs = list(refs[: -len(outs)])
    for out_ref, terms in zip(refs[-len(outs) :], outs):
        total = None
        for low_edge, high_edge in terms:
            value = inputs.pop(0)[...].astype(F32)
            if high_edge - low_edge < pl.num_programs(0):
                value = jnp.where((step >= low_edge) & (step < high_edge), value, 0.0)
            total = value if total is None else total + value
        out_ref[...] = total.astype(out_ref.dtype)


def combine(rows, tile, outs, dtype=BF16):
    tiles = max(high for terms in outs for *_, high in terms)
    in_specs, arrays, edges = [], [], []
    for terms in outs:
        edges.append([(low_edge, high_edge) for *_, low_edge, high_edge in terms])
        for array, block, first, low_edge, high_edge in terms:

            def place(j, block=block, first=first, low_edge=low_edge, high_edge=high_edge):
                return block, jnp.clip(j, low_edge, high_edge - 1) - low_edge + first

            in_specs.append(pl.BlockSpec((rows, tile), place))
            arrays.append(array)
    return pl.pallas_call(
        functools.partial(combine_kernel, edges),
        grid=(tiles,),
        in_specs=in_specs,
        out_specs=[pl.BlockSpec((rows, tile), lambda j: (0, j)) for _ in outs],
        out_shape=[jax.ShapeDtypeStruct((rows, tiles * tile), dtype) for _ in outs],
        compiler_params=pltpu.CompilerParams(vmem_limit_bytes=40 * 2**20),
        cost_estimate=FREE,
        name="combine",
    )(*arrays)


def turn_kernel(turn_ref, own_ref, par_ref, out_ref, scr):
    own_rows, model = own_ref.shape
    step = BLOCK // 2
    for number, ref in enumerate((own_ref, par_ref)):

        @pl.loop(0, own_rows // step)
        def _(part, ref=ref, number=number):
            start = pl.multiple_of(part * step, step)
            place = pl.multiple_of(start + number * own_rows, step)
            scr[:, pl.ds(place, step)] = ref[pl.ds(start, step), :].astype(F32).T.astype(BF16)

    count = turn_ref.shape[0]
    block = model // count

    @pl.loop(0, count)
    def _(i):
        base = pl.multiple_of(turn_ref[i] * block, block)
        place = pl.multiple_of(i * block, block)
        out_ref[pl.ds(place, block), :] = scr[pl.ds(base, block), :]


def turn(turned, own, par):
    own_rows, model = own.shape
    length = 2 * own_rows
    whole = lambda i, t: (0, 0)
    spec = pl.BlockSpec
    return pl.pallas_call(
        turn_kernel,
        grid_spec=pltpu.PrefetchScalarGridSpec(
            num_scalar_prefetch=1,
            grid=(1,),
            in_specs=[spec((own_rows, model), whole)] * 2,
            out_specs=spec((model, length), whole),
            scratch_shapes=[pltpu.VMEM((model, length), BF16)],
        ),
        out_shape=jax.ShapeDtypeStruct((model, length), BF16),
        compiler_params=pltpu.CompilerParams(vmem_limit_bytes=48 * 2**20),
        cost_estimate=LONG,
        name="turn",
    )(turned, own, par)


def project(blocks, turned, x_own, x_par, cos, sin, pieces, heads):
    own_rows, model = x_own.shape
    length = 2 * own_rows
    count = len(pieces)
    columns = [column for _, column in pieces]
    pieces = [piece for piece, _ in pieces]
    rows, width = pieces[0].shape
    qkv_width = 2 * heads
    tile = heads // 2
    spec = pl.BlockSpec
    whole = lambda j, s, t: (0, 0)
    anywhere = spec(memory_space=pl.ANY)
    return pl.pallas_call(
        functools.partial(project_kernel, columns, rows, heads),
        grid_spec=pltpu.PrefetchScalarGridSpec(
            num_scalar_prefetch=2,
            grid=(qkv_width // tile,),
            in_specs=[
                spec((own_rows, model), whole),
                spec((own_rows, model), whole),
                spec((HEAD_DIM // 2, length), whole),
                spec((HEAD_DIM // 2, length), whole),
            ]
            + [anywhere] * count,
            out_specs=[
                spec((tile, length), lambda j, s, t: (j, 0)),
                spec((8, model), whole),
                anywhere,
                anywhere,
                anywhere,
            ],
            scratch_shapes=[
                pltpu.VMEM((model, width), BF16),
                pltpu.VMEM((length, model), BF16),
                pltpu.VMEM((model, length), BF16),
                pltpu.SemaphoreType.DMA((count,)),
                pltpu.SemaphoreType.DMA((2,)),
                pltpu.SemaphoreType.DMA(turned.shape),
            ],
        ),
        out_shape=[
            jax.ShapeDtypeStruct((qkv_width, length), BF16),
            jax.ShapeDtypeStruct((8, model), F32),
            jax.ShapeDtypeStruct((model, length), BF16),
            jax.ShapeDtypeStruct((model, qkv_width), BF16),
            jax.ShapeDtypeStruct((model, heads), BF16),
        ],
        compiler_params=pltpu.CompilerParams(vmem_limit_bytes=52 * 2**20),
        cost_estimate=FREE,
        name="project",
    )(blocks, turned, x_own, x_par, cos, sin, *pieces)


def ffn_kernel(columns, rows, ff, block_ref, b_own, b_par, e_own, e_par, *rest):
    count = len(columns)
    pieces = rest[:count]
    hidden_ref, pair_ref, own_ref, par_ref, down_ref = rest[count : count + 5]
    b_scr, e_scr, w_scr, total, sem, save_sem = rest[count + 5 :]
    step = pl.program_id(0)
    tiles = pl.num_programs(0)
    slot = lax.rem(step, 2)
    width = hidden_ref.shape[1]
    half = b_own.shape[0]

    def fetch(number, into):
        for kind in range(3):
            for i in range(count):
                base = pl.multiple_of(block_ref[i] * rows, rows)
                column = pl.multiple_of(kind * ff + number * width, 128)
                low_edge, high_edge = columns[i], columns[i] + pieces[i].shape[1]

                def start(i=i, base=base, column=column, kind=kind):
                    pltpu.make_async_copy(
                        pieces[i].at[:, pl.ds(pl.multiple_of(column - columns[i], 128), width)],
                        w_scr.at[into, kind, pl.ds(base, rows), :],
                        sem.at[into, kind],
                    ).start()

                if low_edge <= kind * ff and (kind + 1) * ff <= high_edge:
                    start()
                elif low_edge < (kind + 1) * ff and kind * ff < high_edge:
                    pl.when((column >= low_edge) & (column < high_edge))(start)

    def saved(number, source):
        column = pl.multiple_of(number * width, 128)
        return pltpu.make_async_copy(
            w_scr.at[source, 2], down_ref.at[:, pl.ds(column, width)], save_sem.at[source]
        )

    @pl.when(step == 0)
    def _():
        fetch(0, 0)
        for target, own, par in ((b_scr, b_own, b_par), (e_scr, e_own, e_par)):
            target[:half, :] = own[...]
            target[half:, :] = par[...]

    @pl.when(step > 0)
    def _():
        saved(step - 1, 1 - slot).wait()

    @pl.when(step + 1 < tiles)
    def _():
        fetch(step + 1, 1 - slot)

    for kind in range(3):
        pltpu.make_async_copy(w_scr.at[slot, kind], w_scr.at[slot, kind], sem.at[slot, kind]).wait()
    saved(step, slot).start()
    gate = mm(b_scr[...], w_scr[slot, 0], 1, 0)
    up = mm(b_scr[...], w_scr[slot, 1], 1, 0)
    dhid = mm(e_scr[...], w_scr[slot, 2], 1, 0)
    sig = 1.0 / (1.0 + jnp.exp(-gate))
    silu = gate * sig
    hidden_ref[...] = (silu * up).astype(BF16)
    dgate = (dhid * up * (sig * (1.0 + gate * (1.0 - sig)))).astype(BF16)
    dup = (dhid * silu).astype(BF16)
    pair_ref[:, :width] = dgate
    pair_ref[:, width:] = dup
    part = mm(dgate, w_scr[slot, 0], 1, 1) + mm(dup, w_scr[slot, 1], 1, 1)

    @pl.when(step == 0)
    def _():
        total[...] = part

    @pl.when((step > 0) & (step < tiles - 1))
    def _():
        total[...] += part

    @pl.when(step == tiles - 1)
    def _():
        own_ref[...] = total[:half, :] + part[:half, :]
        par_ref[...] = (total[half:, :] + part[half:, :]).astype(BF16)
        saved(step, slot).wait()


def ffn(blocks, b_own, b_par, e_own, e_par, pieces):
    half, model = b_own.shape
    count = len(pieces)
    columns = [column for _, column in pieces]
    pieces = [piece for piece, _ in pieces]
    rows = pieces[0].shape[0]
    ff = max(piece.shape[1] + column for piece, column in zip(pieces, columns)) // 3
    spec = pl.BlockSpec
    whole = lambda j, s: (0, 0)
    anywhere = spec(memory_space=pl.ANY)
    once = spec((half, model), whole, pipeline_mode=pl.Buffered(1))
    return pl.pallas_call(
        functools.partial(ffn_kernel, columns, rows, ff),
        grid_spec=pltpu.PrefetchScalarGridSpec(
            num_scalar_prefetch=1,
            grid=(ff // TILE,),
            in_specs=[once] * 4 + [anywhere] * count,
            out_specs=[
                spec((2 * half, TILE), lambda j, s: (0, j)),
                spec((2 * half, 2 * TILE), lambda j, s: (0, j)),
                once,
                once,
                anywhere,
            ],
            scratch_shapes=[
                pltpu.VMEM((2 * half, model), BF16),
                pltpu.VMEM((2 * half, model), BF16),
                pltpu.VMEM((2, 3, model, TILE), BF16),
                pltpu.VMEM((2 * half, model), F32),
                pltpu.SemaphoreType.DMA((2, 3)),
                pltpu.SemaphoreType.DMA((2,)),
            ],
        ),
        out_shape=[
            jax.ShapeDtypeStruct((2 * half, ff), BF16),
            jax.ShapeDtypeStruct((2 * half, 2 * ff), BF16),
            jax.ShapeDtypeStruct((half, model), F32),
            jax.ShapeDtypeStruct((half, model), BF16),
            jax.ShapeDtypeStruct((model, ff), BF16),
        ],
        compiler_params=pltpu.CompilerParams(vmem_limit_bytes=60 * 2**20),
        cost_estimate=FREE,
        name="ffn",
    )(blocks, b_own, b_par, e_own, e_par, *pieces)


def place_of(natural, side, length):
    return pl.multiple_of((natural + side * (length // 2)) & (length - 1), BLOCK)


def diagonal():
    keys = lax.broadcasted_iota(jnp.int32, (BLOCK, BLOCK), 0)
    queries = lax.broadcasted_iota(jnp.int32, (BLOCK, BLOCK), 1)
    return keys <= queries


def fill(scratch, rows, side, docs):
    length = rows.shape[1]
    half = length // 2
    scratch[HEAD_DIM:, :] = jnp.zeros((PAD_DIM - HEAD_DIM, length), BF16)
    if docs is not None:
        scratch[HEAD_DIM : HEAD_DIM + DOCS, :] = docs[...]
    for part in range(2):
        there = pl.ds(place_of(part * half, side, length), half)
        scratch[:HEAD_DIM, part * half : (part + 1) * half] = rows[:, there]


def forward_kernel(
    side_ref, q_in, k_in, v_in, oq_ref, ok_ref, *rest
):
    att_ref, lse_ref, q_scr, kt_scr, k_scr, v_scr = rest[-6:]
    length = q_in.shape[1]
    side = side_ref[0]
    blocks = length // BLOCK
    fill(kt_scr, k_in, side, ok_ref)
    fill(v_scr, v_in, side, None)
    k_scr[...] = kt_scr[...].T
    causal = diagonal()
    for h in range(2):
        rows = slice(h * HEAD_DIM, (h + 1) * HEAD_DIM)
        fill(q_scr, q_in.at[rows, :], side, oq_ref)
        for b in range(blocks):
            here = pl.ds(b * BLOCK, BLOCK)
            keys = (b + 1) * BLOCK
            query = q_scr[:, here]
            last = mm(k_scr[b * BLOCK : keys, :], query, 1, 0)
            last = jnp.where(causal, last, -FAR)
            top = jnp.max(last, 0, keepdims=True)
            if b:
                early = mm(k_scr[: b * BLOCK, :], query, 1, 0)
                top = jnp.maximum(top, jnp.max(early, 0, keepdims=True))
            top = top * (SCALE * LOG2E)
            weight = jnp.exp2(last * (SCALE * LOG2E) - top)
            total = jnp.sum(weight, 0, keepdims=True)
            out = mm(v_scr[:HEAD_DIM, b * BLOCK : keys], weight.astype(BF16), 1, 0)
            if b:
                weight = jnp.exp2(early * (SCALE * LOG2E) - top)
                total = total + jnp.sum(weight, 0, keepdims=True)
                out = out + mm(v_scr[:HEAD_DIM, : b * BLOCK], weight.astype(BF16), 1, 0)
            out = out / total
            there = pl.ds(place_of(b * BLOCK, side, length), BLOCK)
            att_ref[rows, there] = out.astype(BF16)
            lse_ref[0, h : h + 1, here] = top + jnp.log2(total)


def group_specs(groups, length, first=0):
    spec = pl.BlockSpec
    return [
        spec((2 * HEAD_DIM, length), lambda g, s: (first + g, 0)),
        spec((HEAD_DIM, length), lambda g, s: (2 * groups + first + g, 0)),
        spec((HEAD_DIM, length), lambda g, s: (3 * groups + first + g, 0)),
    ]


def attend(side, qkv, doc_q, doc_k, first, count, earlier=()):
    hidden, length = qkv.shape
    groups = hidden // (4 * HEAD_DIM)
    whole = lambda g, s: (0, 0)
    spec = pl.BlockSpec
    return pl.pallas_call(
        forward_kernel,
        grid_spec=pltpu.PrefetchScalarGridSpec(
            num_scalar_prefetch=1,
            grid=(count,),
            in_specs=group_specs(groups, length, first)
            + [spec((DOCS, length), whole)] * 2
            + [spec(memory_space=pl.ANY)] * len(earlier),
            out_specs=[
                spec((2 * HEAD_DIM, length), lambda g, s: (first + g, 0)),
                spec((1, 2, length), lambda g, s: (first + g, 0, 0)),
            ],
            scratch_shapes=[
                pltpu.VMEM((PAD_DIM, length), BF16),
                pltpu.VMEM((PAD_DIM, length), BF16),
                pltpu.VMEM((length, PAD_DIM), BF16),
                pltpu.VMEM((PAD_DIM, length), BF16),
            ],
        ),
        out_shape=[
            jax.ShapeDtypeStruct((2 * groups * HEAD_DIM, length), BF16),
            jax.ShapeDtypeStruct((groups, 2, length), F32),
        ],
        compiler_params=pltpu.CompilerParams(vmem_limit_bytes=48 * 2**20),
        cost_estimate=FREE,
        input_output_aliases={6 + i: i for i in range(len(earlier))},
        name="attend",
    )(side, qkv, qkv, qkv, doc_q, doc_k, *earlier)


def backward_kernel(
    first, side_ref, q_ref, k_ref, v_ref, att_ref, datt_own, datt_par, lse_ref, cos_ref, sin_ref,
    oq_ref, ok_ref, *rest,
):
    out_ref, *rest = rest[1:] if first else rest
    q_scr, kt_scr, k_scr, vt_scr, v_scr, do_scr, dk_scr, dv_scr, datt_ref, dq_ref, sem = rest
    length = q_ref.shape[1]
    group = pl.program_id(0)
    groups = out_ref.shape[0] // (4 * HEAD_DIM)
    datt_ref[:, : length // 2] = datt_own[...]
    datt_ref[:, length // 2 :] = datt_par[...]
    slot = lax.rem(group, 2)
    dk_ref = dq_ref.at[slot, 2 * HEAD_DIM : 3 * HEAD_DIM, :]
    dv_ref = dq_ref.at[slot, 3 * HEAD_DIM :, :]
    dq_ref = dq_ref.at[slot]

    def stores(number, source):
        number = first + number
        for i, (start, size) in enumerate(((0, 2), (2, 1), (3, 1))):
            base = (start * groups + number * size) * HEAD_DIM
            yield pltpu.make_async_copy(
                rest[-2].at[source, start * HEAD_DIM : (start + size) * HEAD_DIM, :],
                out_ref.at[pl.ds(pl.multiple_of(base, HEAD_DIM), size * HEAD_DIM), :],
                sem.at[source, i],
            )

    half = HEAD_DIM // 2
    side = side_ref[0]
    blocks = length // BLOCK
    fill(kt_scr, k_ref, side, ok_ref)
    fill(vt_scr, v_ref, side, None)
    k_scr[...] = kt_scr[...].T
    v_scr[...] = vt_scr[...].T
    causal = diagonal()
    for h in range(2):
        rows = slice(h * HEAD_DIM, (h + 1) * HEAD_DIM)
        fill(q_scr, q_ref.at[rows, :], side, oq_ref)
        fill(do_scr, datt_ref.at[rows, :], side, None)
        for b in range(blocks):
            here = pl.ds(b * BLOCK, BLOCK)
            there = pl.ds(place_of(b * BLOCK, side, length), BLOCK)
            base = jnp.sum(
                datt_ref[rows, there].astype(F32) * att_ref[rows, there].astype(F32), 0, keepdims=True
            )
            keys = (b + 1) * BLOCK
            query, upstream = q_scr[:, here], do_scr[:, here]
            level = lse_ref[0, h : h + 1, here]
            dq = None
            for start, stop in ((b * BLOCK, keys), (0, b * BLOCK)):
                if start == stop:
                    continue
                span = slice(start, stop)
                score = mm(k_scr[span, :], query, 1, 0)
                prob = jnp.exp2(score * (SCALE * LOG2E) - level)
                if stop == keys:
                    prob = jnp.where(causal, prob, 0.0)
                slope = mm(v_scr[span, :], upstream, 1, 0)
                ds = (prob * (slope - base)).astype(BF16)
                part = mm(kt_scr[:HEAD_DIM, span], ds, 1, 0)
                dq = part if dq is None else dq + part
                dk = mm(query[:HEAD_DIM, :], ds, 1, 1)
                dv = mm(upstream[:HEAD_DIM, :], prob.astype(BF16), 1, 1)
                if h == 0 and stop == keys:
                    dk_scr[:, span] = dk
                    dv_scr[:, span] = dv
                else:
                    dk_scr[:, span] += dk
                    dv_scr[:, span] += dv
            cos, sin = cos_ref[:, there], sin_ref[:, there]
            dq = dq * SCALE
            top, bottom = rope_rows(dq[:half, :], dq[half:, :], cos, -sin)
            dq_ref[h * HEAD_DIM : h * HEAD_DIM + half, there] = top.astype(BF16)
            dq_ref[h * HEAD_DIM + half : (h + 1) * HEAD_DIM, there] = bottom.astype(BF16)
    for b in range(blocks):
        here = pl.ds(b * BLOCK, BLOCK)
        there = pl.ds(place_of(b * BLOCK, side, length), BLOCK)
        cos, sin = cos_ref[:, there], sin_ref[:, there]
        dk = dk_scr[:, here] * SCALE
        top, bottom = rope_rows(dk[:half, :], dk[half:, :], cos, -sin)
        dk_ref[:half, there] = top.astype(BF16)
        dk_ref[half:, there] = bottom.astype(BF16)
        dv_ref[:, there] = dv_scr[:, here].astype(BF16)
    for copy in stores(group, slot):
        copy.start()

    @pl.when(group > 0)
    def _():
        for copy in stores(group - 1, 1 - slot):
            copy.wait()

    @pl.when(group == pl.num_programs(0) - 1)
    def _():
        for copy in stores(group, slot):
            copy.wait()


def attend_back(side, qkv, att, datt, lse, cos, sin, doc_q, doc_k, first, count, earlier=()):
    hidden, length = qkv.shape
    groups = hidden // (4 * HEAD_DIM)
    whole = lambda g, s: (0, 0)
    spec = pl.BlockSpec
    narrow = spec((2 * HEAD_DIM, length // 2), lambda g, s: (first + g, 0))
    source = spec((2 * HEAD_DIM, length), lambda g, s: (first + g, 0))
    level = spec((1, 2, length), lambda g, s: (first + g, 0, 0))
    anywhere = spec(memory_space=pl.ANY)
    table = spec((HEAD_DIM // 2, length), whole)
    docs = spec((DOCS, length), whole)
    tall = pltpu.VMEM((length, PAD_DIM), BF16)
    flat = pltpu.VMEM((PAD_DIM, length), BF16)
    return pl.pallas_call(
        functools.partial(backward_kernel, first),
        grid_spec=pltpu.PrefetchScalarGridSpec(
            num_scalar_prefetch=1,
            grid=(count,),
            in_specs=group_specs(groups, length, first)
            + [source, narrow, narrow, level, table, table, docs, docs]
            + [anywhere] * len(earlier),
            out_specs=anywhere,
            scratch_shapes=[flat, flat, tall, flat, tall, flat]
            + [pltpu.VMEM((HEAD_DIM, length), F32)] * 2
            + [
                pltpu.VMEM((2 * HEAD_DIM, length), BF16),
                pltpu.VMEM((2, 4 * HEAD_DIM, length), BF16),
                pltpu.SemaphoreType.DMA((2, 3)),
            ],
        ),
        out_shape=jax.ShapeDtypeStruct((hidden, length), BF16),
        input_output_aliases={12: 0} if earlier else {},
        compiler_params=pltpu.CompilerParams(vmem_limit_bytes=48 * 2**20),
        cost_estimate=FREE,
        name="attend_back",
    )(side, qkv, qkv, qkv, att, *datt, lse, cos, sin, doc_q, doc_k, *earlier)


def rms_inverse(value):
    return lax.rsqrt(jnp.mean(value * value, -1, keepdims=True) + EPSILON)


def norm_back(upstream, value, inverse, gain):
    scaled = upstream * gain
    inner = jnp.mean(scaled * value, -1, keepdims=True)
    return inverse * (scaled - value * inverse * inverse * inner)


def gain_of(pairs, gain):
    rows = sum(jnp.sum(low(weight).astype(F32) * grad, 1) for weight, grad in pairs)
    return rows / low(gain).astype(F32)


def low(weight):
    return weight.astype(BF16)


def layer(
    dp, tokens, segment_ids, positions, query_weight, key_weight, value_weight, out_weight,
    attn_gain, gate_weight, up_weight, down_weight, mlp_gain, cotangent,
):
    seqs, own_rows, model = tokens.shape
    length = segment_ids.shape[1]
    heads = query_weight.shape[1]
    ff = gate_weight.shape[1]
    side_index = lax.axis_index("tensor").astype(jnp.int32)
    side = side_index[None]
    blocks, turned = piece_blocks(dp), turn_blocks(dp)

    x_own = tokens.reshape(own_rows, model)
    e_own = cotangent.reshape(own_rows, model)
    gains = jnp.pad(jnp.stack([low(attn_gain), low(mlp_gain)], 1), ((0, 0), (0, 126)))
    order = Order(positions[0, 0] >= 0)
    first = Gather(
        jnp.concatenate(
            [low(query_weight), low(key_weight), low(value_weight), low(out_weight).T, gains], 1
        ),
        dp,
        1280,
    )
    x_par = swap_halves(x_own)
    first.round(order)
    first.share(order)
    second = order.done(
        jnp.concatenate([low(gate_weight), low(up_weight), low(down_weight).T], 1)
    )
    second = Gather(second, dp, 3 * ff // 2)
    for _ in range(dp // 4 - 1):
        first.next(order)
    second.share(order)
    first = first.pieces(order)
    x_first, x_par = order.done(*order.tie(x_own, x_par))
    e_par = swap_halves(order.tie(e_own))
    second.round(order)

    places = positions.reshape(length).astype(F32)
    half = HEAD_DIM // 2
    places = jnp.where(side_index == 0, places, jnp.roll(places, length // 2))
    ladder = jnp.power(F32(ROPE_BASE), -2.0 * jnp.arange(half, dtype=F32) / HEAD_DIM)
    angles = ladder[:, None] * places[None, :]
    cos, sin = jnp.cos(angles), jnp.sin(angles)
    known = jnp.arange(DOCS, dtype=jnp.int32)[:, None] == segment_ids.reshape(1, length)
    doc_q = known.astype(BF16)
    doc_k = jnp.where(known, 0.0, -FAR).astype(BF16)

    qkv, gain_rows, a_turned, qkv_full, out_full = project(
        blocks, turned, x_first, x_par, cos, sin, first, heads
    )
    gain_one, gain_two = gain_rows[0], gain_rows[1]
    qkv = order.done(qkv)
    groups = heads // (2 * HEAD_DIM)
    early = groups // 2
    att, lse = attend(side, order.tie(qkv), doc_q, doc_k, 0, groups)
    e_par, att = order.done(e_par, att)

    own, par = slice(0, own_rows), slice(own_rows, None)
    partial = order.done(mm(att[:, par], out_full, 0, 1, BF16))
    sent = swap_halves(partial)
    second.next(order)
    e_turned = order.done(turn(turned, order.tie(e_own), e_par))
    partial = order.done(mm(att[:, own], order.tie(out_full), 0, 1))
    second.next(order)
    sent = order.tie(sent)
    middle = x_own.astype(F32) + (partial + sent.astype(F32))
    inverse_two = rms_inverse(middle)
    b_own = order.done((middle * inverse_two * gain_two).astype(BF16))
    b_par = swap_halves(b_own)
    second.next(order)
    second = second.pieces(order)

    b_par = order.tie(b_par)
    hidden, pair, db_own, db_par, down_full = ffn(blocks, b_own, b_par, e_own, e_par, second)
    db_par = order.done(db_par)
    db_sent = swap_halves(db_par)
    b_turned = order.done(turn(turned, order.tie(b_own), b_par))
    grad_ffn = Scatter(dp, order, (e_turned, hidden, 0), (b_turned, pair, 0))
    db = db_own + order.tie(db_sent).astype(F32)
    dh = e_own.astype(F32) + norm_back(db, middle, inverse_two, gain_two)
    eh_own, dh = order.done(dh.astype(BF16), dh)
    eh_par = swap_halves(eh_own)
    grad_ffn.round()
    grad_ffn.round()
    down_own, down_par = order.done(*product(order.tie(hidden), down_full, 1, parts=[own_rows] * 2))
    eh_par = order.tie(eh_par)
    datt = order.done(*(product(part, out_full, 0, 384, flip=True) for part in (eh_own, eh_par)))
    down_sent = swap_halves(order.tie(down_par))
    grad_ffn.round()
    tables = (cos, sin, doc_q, doc_k)
    dqkv = attend_back(side, qkv, att, order.tie(*datt), lse, *tables, 0, early)
    dqkv = order.done(dqkv)
    dqkv = attend_back(
        side, qkv, att, order.tie(*datt), lse, *tables, early, groups - early, (dqkv,)
    )
    dqkv = order.done(dqkv)
    down_sent = order.done(down_sent)
    da_par = order.done(mm(order.tie(dqkv[:, par]), qkv_full, 0, 1, BF16))
    da_sent = swap_halves(da_par)
    grad_ffn.round()
    eh_turned = order.done(turn(turned, order.tie(eh_own), eh_par))
    grad_att = Scatter(dp, order, (a_turned, dqkv, 1), (eh_turned, att, 1))
    grad_att.round()
    grad_ffn = grad_ffn.result()
    output = (middle + (down_own.astype(F32) + order.tie(down_sent).astype(F32))).astype(BF16)
    output = order.done(output)
    grad_att.round()
    da_own = order.done(mm(order.tie(dqkv[:, own]), qkv_full, 0, 1))
    grad_down, grad_pair = grad_ffn[:, :ff], grad_ffn[:, ff:]
    grad_pair = grad_pair.reshape(-1, ff // TILE, 2, TILE)
    grad_gate, grad_up = (grad_pair[:, :, i].reshape(-1, ff) for i in range(2))
    gain_two_grad = order.done(gain_of(((gate_weight, grad_gate), (up_weight, grad_up)), mlp_gain))
    grad_att.round()
    da = da_own + order.tie(da_sent).astype(F32)
    x = x_own.astype(F32)
    input_grad = order.done((dh + norm_back(da, x, rms_inverse(x), gain_one)).astype(BF16))
    grad_att.round()
    grad_att = grad_att.result()
    grad_qkv, grad_out = grad_att[:, : 2 * heads], grad_att[:, 2 * heads :]

    grad_query, grad_key, grad_value = (
        grad_qkv[:, :heads],
        grad_qkv[:, heads : heads + heads // 2],
        grad_qkv[:, heads + heads // 2 :],
    )
    gain_one_grad = gain_of(
        ((query_weight, grad_query), (key_weight, grad_key), (value_weight, grad_value)), attn_gain
    )
    gain_grads = jnp.stack([gain_one_grad, gain_two_grad])
    gain_grads = gain_grads + swap_halves(gain_grads)
    return (
        output.reshape(seqs, own_rows, model),
        input_grad.reshape(seqs, own_rows, model),
        grad_query,
        grad_key,
        grad_value,
        grad_out.T,
        gain_grads[0],
        grad_gate,
        grad_up,
        grad_down.T,
        gain_grads[1],
    )


def solution(mesh):
    in_specs = (
        P("dp", "tensor", None),
        P("dp", None),
        P("dp", None),
        P("dp", "tensor"),
        P("dp", "tensor"),
        P("dp", "tensor"),
        P("tensor", "dp"),
        P("dp"),
        P("dp", "tensor"),
        P("dp", "tensor"),
        P("tensor", "dp"),
        P("dp"),
        P("dp", "tensor", None),
    )
    out_specs = (
        P("dp", "tensor", None),
        P("dp", "tensor", None),
        P("dp", "tensor"),
        P("dp", "tensor"),
        P("dp", "tensor"),
        P("tensor", "dp"),
        P("dp"),
        P("dp", "tensor"),
        P("dp", "tensor"),
        P("tensor", "dp"),
        P("dp"),
    )
    return jax.shard_map(
        functools.partial(layer, mesh.shape["dp"]),
        mesh=mesh,
        in_specs=in_specs,
        out_specs=out_specs,
        check_vma=False,
    )
```

```python
import functools
import math

import jax
import jax.numpy as jnp
from jax import lax
from jax.experimental import pallas as pl
from jax.experimental.pallas import tpu as pltpu
from jax.sharding import PartitionSpec as P

HEAD_DIM = 96
PAD_DIM = 128
BLOCK = 256
DOCS = 16
EPSILON = 1e-05
ROPE_BASE = 100000.0
FAR = float(2**30)
RING_LIMIT = 16
TILE = 512
VMEM = 66_000_000
SCALE = 1.0 / math.sqrt(HEAD_DIM)
LOG2E = math.log2(math.e)

F32 = jnp.float32
BF16 = jnp.bfloat16


def mm(left, right, left_dim, right_dim, dtype=F32):
    return lax.dot_general(
        left, right, (((left_dim,), (right_dim,)), ((), ())), preferred_element_type=F32
    ).astype(dtype)


def swap_halves(value):
    return lax.ppermute(value, "tensor", [(0, 1), (1, 0)])


def is_ring(dp):
    return 8 <= dp <= RING_LIMIT and dp & (dp - 1) == 0


def chip_of(spot, chips):
    return jnp.where(2 * spot < chips, 2 * spot, 2 * (chips - 1 - spot) + 1)


def ring_pairs(dp):
    chips = dp // 2
    order = list(range(0, chips, 2)) + list(range(chips - 1, 0, -2))
    ahead = []
    for spot in range(chips):
        here, following = order[spot], order[(spot + 1) % chips]
        ahead += [(2 * here, 2 * following), (2 * here + 1, 2 * following + 1)]
    return ahead, [(b, a) for a, b in ahead]


def ring_place(dp):
    chips = dp // 2
    me = lax.axis_index("dp").astype(jnp.int32)
    chip = me >> 1
    return me & 1, jnp.where(chip & 1 == 0, chip >> 1, chips - 1 - (chip >> 1))


def piece_steps(dp):
    reach = dp // 4
    return [0, *range(-1, -reach, -1), *range(1, reach), reach, reach]


def piece_blocks(dp):
    if not is_ring(dp):
        return jnp.zeros((1,), jnp.int32)
    chips = dp // 2
    core, spot = ring_place(dp)
    chip = chip_of((spot + jnp.asarray(piece_steps(dp), jnp.int32)) & (chips - 1), chips)
    return jnp.concatenate([2 * chip + core, 2 * chip + 1 - core])


def turn_blocks(dp):
    if not is_ring(dp):
        return jnp.zeros((1,), jnp.int32)
    chips = dp // 2
    core, spot = ring_place(dp)
    chip = chip_of((spot + jnp.arange(chips, dtype=jnp.int32)) & (chips - 1), chips)
    return jnp.concatenate([2 * chip + 1 - core, 2 * chip + core])


class Order:
    def __init__(self, flag):
        self.token = lax.create_token()
        self.flag = flag

    def tie(self, *values):
        tied = lax.optimization_barrier((self.token, *values))[1:]
        return tied if len(values) > 1 else tied[0]

    def done(self, *values):
        self.token, *values = lax.optimization_barrier((self.token, *values))
        return values if len(values) > 1 else values[0]


class Gather:
    def __init__(self, shard, dp, cut):
        self.dp, self.cut = dp, cut
        self.behind, self.ahead, self.other, self.shard = [], [], [], shard

    def share(self, order):
        if not is_ring(self.dp):
            return
        found = (self.behind[-1], self.ahead[-1]) if self.other else (self.shard,)
        swap = [(i, i ^ 1) for i in range(self.dp)]

        def both(*pieces):
            return tuple(lax.ppermute(piece, "dp", swap) for piece in pieces)

        def neither(*pieces):
            return tuple(jnp.zeros_like(piece) for piece in pieces)

        found = order.tie(*found) if len(found) > 1 else (order.tie(*found),)
        got = lax.cond(order.flag, both, neither, *found)
        self.other.append(order.done(*got) if len(got) > 1 else [order.done(*got)])

    def round(self, order):
        if not is_ring(self.dp):
            return
        forth, back = ring_pairs(self.dp)
        left = self.behind[-1] if self.behind else self.shard
        right = self.ahead[-1] if self.ahead else self.shard
        left, right = order.tie(left, right)
        if len(self.behind) == self.dp // 4 - 1:
            left, right = halves(left, right, self.cut)
        left, right = order.done(left, right)
        self.behind.append(lax.ppermute(left, "dp", forth))
        self.ahead.append(lax.ppermute(right, "dp", back))

    def arrive(self, order):
        if is_ring(self.dp):
            self.behind[-1], self.ahead[-1] = order.done(self.behind[-1], self.ahead[-1])

    def next(self, order):
        if not is_ring(self.dp):
            return
        self.arrive(order)
        arrived = self.behind[-1], self.ahead[-1]
        self.round(order)
        sent = self.behind.pop(), self.ahead.pop()
        self.behind[-1], self.ahead[-1] = arrived
        self.share(order)
        self.behind.append(sent[0])
        self.ahead.append(sent[1])

    def pieces(self, order):
        if not is_ring(self.dp):
            return [(lax.all_gather(self.shard, "dp", axis=0, tiled=True), 0)]
        self.arrive(order)
        self.share(order)
        held = [self.shard, *self.behind[:-1], *self.ahead[:-1], self.behind[-1], self.ahead[-1]]
        other = [self.other[0][0], *(pair[0] for pair in self.other[1:-1])]
        other += [*(pair[1] for pair in self.other[1:-1]), *self.other[-1]]
        columns = [0] * (len(held) - 1) + [self.cut]
        return list(zip([*held, *other], columns * 2))


class Scatter:
    def __init__(self, dp, order, *columns):
        self.dp, self.order = dp, order
        lefts, rights, dims = zip(*columns)
        rights = order.tie(*rights) if len(rights) > 1 else (order.tie(*rights),)
        if not is_ring(dp):
            full = order.done(products(0, 1, lefts, rights, dims))
            self.total = lax.psum_scatter(full, "dp", scatter_dimension=0, tiled=True).astype(F32)
            return
        self.chips = dp // 2
        self.reach = self.chips // 2
        self.rows = lefts[0].shape[0] // dp

        def both(lefts, rights):
            token = lax.create_token()
            theirs = products(0, 2, lefts, rights, dims)
            token, theirs = lax.optimization_barrier((token, theirs))
            got = lax.ppermute(theirs, "dp", [(i, i ^ 1) for i in range(dp)])
            rights = lax.optimization_barrier((token, *rights))[1:]
            return got, products(1, 2, lefts, rights, dims)

        def neither(lefts, rights):
            width = sum(right.shape[1 - dim] for right, dim in zip(rights, dims))
            return (jnp.zeros((lefts[0].shape[0] // 2, width), BF16),) * 2

        self.got, self.mine = order.done(*lax.cond(order.flag, both, neither, lefts, tuple(rights)))
        self.width = self.mine.shape[1]
        self.ahead = self.behind = None

    def local(self, steps, mine, first, low_edge, high_edge):
        block = steps % self.chips
        return [(part, block, first, low_edge, high_edge) for part in (mine, self.got)]

    def round(self):
        if not is_ring(self.dp):
            return
        forth, back = ring_pairs(self.dp)
        half = self.width // 2
        tile = half if half <= 1536 else half // 2
        count = half // tile
        mine = self.order.tie(self.mine)
        reach = self.reach
        if self.ahead is None:
            right = self.local(reach, mine, 0, 0, count)
            left = self.local(reach, mine, count, 0, count)
        else:
            cut = count if self.ahead.shape[1] == half else 2 * count
            right = [*self.local(reach, mine, 0, 0, 2 * count), (self.ahead, 0, 0, 0, cut)]
            left = [*self.local(-reach, mine, 0, 0, 2 * count)]
            left.append((self.behind, 0, 0, 2 * count - cut, 2 * count))
        right, left = self.order.done(*combine(self.rows, tile, [right, left]))
        self.ahead = lax.ppermute(right, "dp", forth)
        self.behind = lax.ppermute(left, "dp", back)
        self.reach -= 1

    def result(self, pieces, weights):
        if not is_ring(self.dp):
            parts = [self.total] + [jnp.zeros_like(self.total)] * 3
        else:
            parts = [self.order.tie(self.mine), self.got, self.ahead, self.behind]
        return self.order.done(*finish(parts, [0] * 4, pieces, weights))


def rope_rows(top, bottom, cos, sin):
    return top * cos - bottom * sin, bottom * cos + top * sin


def project_kernel(columns, rows, heads, block_ref, turn_ref, own_ref, par_ref, cos_ref, sin_ref, *rest):
    count = len(columns)
    pieces = rest[:count]
    qkv_ref, gain_ref, at_ref, wide_ref, out_ref = rest[count : count + 5]
    w_scr, a_scr, at_scr, in_sem, out_sem, turn_sem = rest[count + 5 :]
    step = pl.program_id(0)
    tiles = pl.num_programs(0)
    own_rows, model = own_ref.shape
    tile = qkv_ref.shape[0]
    half = HEAD_DIM // 2
    qkv_width = 2 * heads

    def loads(i):
        base = pl.multiple_of(block_ref[i] * rows, rows)
        place = slice(columns[i], columns[i] + pieces[i].shape[1])
        return pltpu.make_async_copy(pieces[i], w_scr.at[pl.ds(base, rows), place], in_sem.at[i])

    def stores():
        return (
            pltpu.make_async_copy(w_scr.at[:, :qkv_width], wide_ref, out_sem.at[0]),
            pltpu.make_async_copy(
                w_scr.at[:, qkv_width : qkv_width + heads], out_ref, out_sem.at[1]
            ),
        )

    def turns(i):
        block = model // turn_ref.shape[0]
        base = pl.multiple_of(turn_ref[i] * block, block)
        return pltpu.make_async_copy(
            at_scr.at[pl.ds(base, block), :], at_ref.at[pl.ds(i * block, block), :], turn_sem.at[i]
        )

    @pl.when(step == 0)
    def _():
        for i in range(count):
            loads(i).start()
        for i in range(count):
            loads(i).wait()
        gains = w_scr[:, qkv_width + heads :].astype(F32).T
        gain_ref[...] = gains[:8, :]
        gain = gains[:1, :]
        for number, ref in enumerate((own_ref, par_ref)):

            @pl.loop(0, own_rows // BLOCK)
            def _(part, ref=ref, number=number):
                start = pl.multiple_of(part * BLOCK, BLOCK)
                x = ref[pl.ds(start, BLOCK), :].astype(F32)
                inverse = lax.rsqrt(jnp.mean(x * x, -1, keepdims=True) + EPSILON)
                normed = x * inverse * gain
                place = pl.multiple_of(start + number * own_rows, BLOCK)
                a_scr[pl.ds(place, BLOCK), :] = normed.astype(BF16)
                at_scr[:, pl.ds(place, BLOCK)] = normed.T.astype(BF16)

        for copy in stores():
            copy.start()
        for i in range(turn_ref.shape[0]):
            turns(i).start()

    start = pl.multiple_of(step * tile, 128)
    flat = mm(a_scr[...], w_scr[:, pl.ds(start, tile)], 1, 0).T

    @pl.when(step < tiles - tiles // 4)
    def _():
        cos, sin = cos_ref[...], sin_ref[...]
        for h in range(tile // HEAD_DIM):
            base = h * HEAD_DIM
            top, bottom = rope_rows(
                flat[base : base + half, :], flat[base + half : base + HEAD_DIM, :], cos, sin
            )
            qkv_ref[base : base + half, :] = top.astype(BF16)
            qkv_ref[base + half : base + HEAD_DIM, :] = bottom.astype(BF16)

    @pl.when(step >= tiles - tiles // 4)
    def _():
        qkv_ref[...] = flat.astype(BF16)

    @pl.when(step == tiles - 1)
    def _():
        for copy in stores():
            copy.wait()
        for i in range(turn_ref.shape[0]):
            turns(i).wait()


FREE = pl.CostEstimate(flops=0, bytes_accessed=0, transcendentals=0)
LONG = pl.CostEstimate(flops=0, bytes_accessed=40 * 2**20, transcendentals=0)


def product_kernel(left_ref, right_ref, *out_refs):
    half = left_ref.shape[0] // 2

    @pl.loop(0, 2)
    def _(part):
        start = pl.multiple_of(part * half, half)
        out = mm(left_ref[pl.ds(start, half), :], right_ref[...], 1, 1, BF16)
        for number, ref in enumerate(out_refs):

            @pl.when(part == number)
            def _(ref=ref):
                ref[...] = out


def product(left, right):
    rows, depth = left.shape
    width = right.shape[0]
    tile = next(t for t in (TILE, 384, 256, width) if width % t == 0)
    spec = pl.BlockSpec
    return pl.pallas_call(
        product_kernel,
        grid=(width // tile,),
        in_specs=[spec((rows, depth), lambda j: (0, 0)), spec((tile, depth), lambda j: (j, 0))],
        out_specs=[spec((rows // 2, tile), lambda j: (0, j))] * 2,
        out_shape=[jax.ShapeDtypeStruct((rows // 2, width), BF16)] * 2,
        compiler_params=pltpu.CompilerParams(vmem_limit_bytes=VMEM),
        cost_estimate=FREE,
        name="product",
    )(left, right)


def products_kernel(starts, dims, *refs):
    count = len(dims)
    out_ref = refs[-1]
    step = pl.program_id(0)
    for i, dim in enumerate(dims):

        @pl.when((step >= starts[i]) & (step < starts[i + 1]))
        def _(i=i, dim=dim):
            width = out_ref.shape[1]
            size = TILE if width % TILE == 0 else width

            @pl.loop(0, width // size)
            def _(j):
                place = pl.ds(pl.multiple_of(j * size, 128), size)
                right = refs[count + i][place, :] if dim else refs[count + i][:, place]
                out_ref[:, place] = mm(refs[i][...], right, 1, dim, out_ref.dtype)


def products(part, parts, lefts, rights, dims):
    rows, depth = lefts[0].shape
    rows = rows // parts
    widths = [right.shape[1 - dim] for right, dim in zip(rights, dims)]
    tile = next(t for t in (1024, 768, TILE, 384) if all(width % t == 0 for width in widths))
    starts = [0]
    for width in widths:
        starts.append(starts[-1] + width // tile)
    spec = pl.BlockSpec
    in_specs = [spec((rows, depth), lambda j: (part, 0)) for _ in lefts]
    for i, dim in enumerate(dims):

        def place(j, i=i):
            return jnp.clip(j - starts[i], 0, starts[i + 1] - starts[i] - 1)

        if dim:
            in_specs.append(spec((tile, depth), lambda j, place=place: (place(j), 0)))
        else:
            in_specs.append(spec((depth, tile), lambda j, place=place: (0, place(j))))
    return pl.pallas_call(
        functools.partial(products_kernel, starts, dims),
        grid=(starts[-1],),
        in_specs=in_specs,
        out_specs=spec((rows, tile), lambda j: (0, j)),
        out_shape=jax.ShapeDtypeStruct((rows, sum(widths)), BF16),
        compiler_params=pltpu.CompilerParams(vmem_limit_bytes=VMEM),
        cost_estimate=FREE,
        name="products",
    )(*lefts, *rights)


def turned_kernel(left_ref, right_ref, out_ref):
    out_ref[...] = mm(left_ref[...], right_ref[...], 1, 0).T.astype(BF16)


def turned_product(left, right, tile, start=0, count=None):
    rows, depth = left.shape
    count = count or right.shape[1] // tile
    spec = pl.BlockSpec
    return pl.pallas_call(
        turned_kernel,
        grid=(count,),
        in_specs=[
            spec((rows, depth), lambda j: (0, 0)),
            spec((depth, tile), lambda j: (0, start + j)),
        ],
        out_specs=spec((tile, rows), lambda j: (j, 0)),
        out_shape=jax.ShapeDtypeStruct((count * tile, rows), BF16),
        compiler_params=pltpu.CompilerParams(vmem_limit_bytes=VMEM),
        cost_estimate=FREE,
        name="turned_product",
    )(left, right)


def join_kernel(*refs):
    start = 0
    for ref in refs[:-1]:
        refs[-1][:, start : start + ref.shape[1]] = ref[...].astype(BF16)
        start += ref.shape[1]


def join(*parts):
    rows = parts[0].shape[0]
    return pl.pallas_call(
        join_kernel,
        out_shape=jax.ShapeDtypeStruct((rows, sum(part.shape[1] for part in parts)), BF16),
        compiler_params=pltpu.CompilerParams(vmem_limit_bytes=VMEM),
        cost_estimate=FREE,
        name="join",
    )(*parts)


def halves_kernel(cut, left_ref, right_ref, low_ref, high_ref):
    low_ref[...] = left_ref[:, :cut]
    high_ref[...] = right_ref[:, cut:]


def halves(left, right, cut):
    rows, width = left.shape
    return pl.pallas_call(
        functools.partial(halves_kernel, cut),
        out_shape=[
            jax.ShapeDtypeStruct((rows, cut), left.dtype),
            jax.ShapeDtypeStruct((rows, width - cut), left.dtype),
        ],
        compiler_params=pltpu.CompilerParams(vmem_limit_bytes=VMEM),
        cost_estimate=FREE,
        name="halves",
    )(left, right)


def residual_kernel(part_ref, sent_ref, x_ref, gain_ref, middle_ref, b_ref):
    middle = x_ref[...].astype(F32) + (part_ref[...] + sent_ref[...].astype(F32))
    inverse = lax.rsqrt(jnp.mean(middle * middle, -1, keepdims=True) + EPSILON)
    middle_ref[...] = middle
    b_ref[...] = (middle * inverse * gain_ref[1:2, :]).astype(BF16)


def back_kernel(row, own_ref, sent_ref, value_ref, base_ref, gain_ref, *out_refs):
    upstream = own_ref[...].astype(F32) + sent_ref[...].astype(F32)
    value = value_ref[...].astype(F32)
    inverse = lax.rsqrt(jnp.mean(value * value, -1, keepdims=True) + EPSILON)
    scaled = upstream * gain_ref[row : row + 1, :]
    inner = jnp.mean(scaled * value, -1, keepdims=True)
    out = inverse * (scaled - value * (inverse * inverse * inner))
    out = base_ref[...].astype(F32) + out
    for ref in out_refs:
        ref[...] = out.astype(ref.dtype)


def by_rows(kernel, arrays, gain, dtypes, name):
    rows, width = arrays[0].shape
    step = 128
    block = pl.BlockSpec((step, width), lambda i: (i, 0))
    return pl.pallas_call(
        kernel,
        grid=(rows // step,),
        in_specs=[block] * len(arrays) + [pl.BlockSpec(gain.shape, lambda i: (0, 0))],
        out_specs=[block] * len(dtypes),
        out_shape=[jax.ShapeDtypeStruct((rows, width), dtype) for dtype in dtypes],
        compiler_params=pltpu.CompilerParams(vmem_limit_bytes=VMEM),
        cost_estimate=FREE,
        name=name,
    )(*arrays, gain)


def finish_kernel(pieces, weighted, *refs):
    parts, refs = refs[:4], refs[4:]
    weights, refs = refs[:weighted], refs[weighted:]
    outs, gain_ref, total_ref = refs[: len(pieces)], refs[-2], refs[-1]
    total_ref[...] = jnp.zeros_like(total_ref)
    for number, (out_ref, (start, size, stride, steps)) in enumerate(zip(outs, pieces)):

        @pl.loop(0, steps)
        def _(j, number=number, out_ref=out_ref, start=start, size=size, stride=stride):
            source = pl.ds(pl.multiple_of(start + j * stride, 128), size)
            target = pl.ds(pl.multiple_of(j * size, 128), size)
            total = sum(part[:, source].astype(F32) for part in parts)
            out_ref[:, target] = total
            if number < weighted:
                total = total * weights[number][:, target].astype(BF16).astype(F32)
                for k in range(0, size, 128):
                    total_ref[...] += total[:, k : k + 128]

    rows = jnp.broadcast_to(jnp.sum(total_ref[...], 1, keepdims=True), total_ref.shape)
    gain_ref[...] = rows.T[:8, :]


def finish(parts, blocks, pieces, weights):
    rows = weights[0].shape[0]
    width = parts[0].shape[1]
    spec = pl.BlockSpec
    whole = lambda i: (0, 0)
    widths = [size * steps for _, size, _, steps in pieces]
    return pl.pallas_call(
        functools.partial(finish_kernel, pieces, len(weights)),
        grid=(1,),
        in_specs=[spec((rows, width), lambda i, block=block: (block, 0)) for block in blocks]
        + [spec(weight.shape, whole) for weight in weights],
        out_specs=[spec((rows, size), whole) for size in widths] + [spec((8, rows), whole)],
        out_shape=[jax.ShapeDtypeStruct((rows, size), F32) for size in widths]
        + [jax.ShapeDtypeStruct((8, rows), F32)],
        scratch_shapes=[pltpu.VMEM((rows, 128), F32)],
        compiler_params=pltpu.CompilerParams(vmem_limit_bytes=VMEM),
        cost_estimate=FREE,
        name="finish",
    )(*parts, *weights)


def combine_kernel(outs, *refs):
    step = pl.program_id(0)
    inputs = list(refs[: -len(outs)])
    for out_ref, terms in zip(refs[-len(outs) :], outs):
        total = None
        for low_edge, high_edge in terms:
            value = inputs.pop(0)[...].astype(F32)
            if high_edge - low_edge < pl.num_programs(0):
                value = jnp.where((step >= low_edge) & (step < high_edge), value, 0.0)
            total = value if total is None else total + value
        out_ref[...] = total.astype(out_ref.dtype)


def combine(rows, tile, outs, dtype=BF16):
    tiles = max(high for terms in outs for *_, high in terms)
    in_specs, arrays, edges = [], [], []
    for terms in outs:
        edges.append([(low_edge, high_edge) for *_, low_edge, high_edge in terms])
        for array, block, first, low_edge, high_edge in terms:

            def place(j, block=block, first=first, low_edge=low_edge, high_edge=high_edge):
                return block, jnp.clip(j, low_edge, high_edge - 1) - low_edge + first

            in_specs.append(pl.BlockSpec((rows, tile), place))
            arrays.append(array)
    return pl.pallas_call(
        functools.partial(combine_kernel, edges),
        grid=(tiles,),
        in_specs=in_specs,
        out_specs=[pl.BlockSpec((rows, tile), lambda j: (0, j)) for _ in outs],
        out_shape=[jax.ShapeDtypeStruct((rows, tiles * tile), dtype) for _ in outs],
        compiler_params=pltpu.CompilerParams(vmem_limit_bytes=VMEM),
        cost_estimate=FREE,
        name="combine",
    )(*arrays)


def turn_kernel(turn_ref, own_ref, par_ref, out_ref, scr):
    own_rows, model = own_ref.shape
    step = BLOCK // 2
    for number, ref in enumerate((own_ref, par_ref)):

        @pl.loop(0, own_rows // step)
        def _(part, ref=ref, number=number):
            start = pl.multiple_of(part * step, step)
            place = pl.multiple_of(start + number * own_rows, step)
            scr[:, pl.ds(place, step)] = ref[pl.ds(start, step), :].astype(F32).T.astype(BF16)

    count = turn_ref.shape[0]
    block = model // count

    @pl.loop(0, count)
    def _(i):
        base = pl.multiple_of(turn_ref[i] * block, block)
        place = pl.multiple_of(i * block, block)
        out_ref[pl.ds(place, block), :] = scr[pl.ds(base, block), :]


def turn(turned, own, par):
    own_rows, model = own.shape
    length = 2 * own_rows
    whole = lambda i, t: (0, 0)
    spec = pl.BlockSpec
    return pl.pallas_call(
        turn_kernel,
        grid_spec=pltpu.PrefetchScalarGridSpec(
            num_scalar_prefetch=1,
            grid=(1,),
            in_specs=[spec((own_rows, model), whole)] * 2,
            out_specs=spec((model, length), whole),
            scratch_shapes=[pltpu.VMEM((model, length), BF16)],
        ),
        out_shape=jax.ShapeDtypeStruct((model, length), BF16),
        compiler_params=pltpu.CompilerParams(vmem_limit_bytes=VMEM),
        cost_estimate=LONG,
        name="turn",
    )(turned, own, par)


def project(blocks, turned, x_own, x_par, cos, sin, pieces, heads):
    own_rows, model = x_own.shape
    length = 2 * own_rows
    count = len(pieces)
    columns = [column for _, column in pieces]
    pieces = [piece for piece, _ in pieces]
    rows, width = pieces[0].shape
    qkv_width = 2 * heads
    tile = heads // 2
    spec = pl.BlockSpec
    whole = lambda j, s, t: (0, 0)
    anywhere = spec(memory_space=pl.ANY)
    return pl.pallas_call(
        functools.partial(project_kernel, columns, rows, heads),
        grid_spec=pltpu.PrefetchScalarGridSpec(
            num_scalar_prefetch=2,
            grid=(qkv_width // tile,),
            in_specs=[
                spec((own_rows, model), whole),
                spec((own_rows, model), whole),
                spec((HEAD_DIM // 2, length), whole),
                spec((HEAD_DIM // 2, length), whole),
            ]
            + [anywhere] * count,
            out_specs=[
                spec((tile, length), lambda j, s, t: (j, 0)),
                spec((8, model), whole),
                anywhere,
                anywhere,
                anywhere,
            ],
            scratch_shapes=[
                pltpu.VMEM((model, width), BF16),
                pltpu.VMEM((length, model), BF16),
                pltpu.VMEM((model, length), BF16),
                pltpu.SemaphoreType.DMA((count,)),
                pltpu.SemaphoreType.DMA((2,)),
                pltpu.SemaphoreType.DMA(turned.shape),
            ],
        ),
        out_shape=[
            jax.ShapeDtypeStruct((qkv_width, length), BF16),
            jax.ShapeDtypeStruct((8, model), F32),
            jax.ShapeDtypeStruct((model, length), BF16),
            jax.ShapeDtypeStruct((model, qkv_width), BF16),
            jax.ShapeDtypeStruct((model, heads), BF16),
        ],
        compiler_params=pltpu.CompilerParams(vmem_limit_bytes=VMEM),
        cost_estimate=FREE,
        name="project",
    )(blocks, turned, x_own, x_par, cos, sin, *pieces)


def ffn_kernel(columns, rows, ff, block_ref, b_own, b_par, e_own, e_par, *rest):
    count = len(columns)
    pieces = rest[:count]
    hidden_ref, pair_ref, own_ref, par_ref, down_ref = rest[count : count + 5]
    b_scr, e_scr, w_scr, total, sem, save_sem = rest[count + 5 :]
    step = pl.program_id(0)
    tiles = pl.num_programs(0)
    slot = lax.rem(step, 2)
    width = hidden_ref.shape[1]
    half = b_own.shape[0]

    def fetch(number, into):
        for kind in range(3):
            for i in range(count):
                base = pl.multiple_of(block_ref[i] * rows, rows)
                column = pl.multiple_of(kind * ff + number * width, 128)
                low_edge, high_edge = columns[i], columns[i] + pieces[i].shape[1]

                def start(i=i, base=base, column=column, kind=kind):
                    pltpu.make_async_copy(
                        pieces[i].at[:, pl.ds(pl.multiple_of(column - columns[i], 128), width)],
                        w_scr.at[into, pl.ds(base, rows), kind * width : (kind + 1) * width],
                        sem.at[into],
                    ).start()

                if low_edge <= kind * ff and (kind + 1) * ff <= high_edge:
                    start()
                elif low_edge < (kind + 1) * ff and kind * ff < high_edge:
                    pl.when((column >= low_edge) & (column < high_edge))(start)

    def saved(number, source):
        column = pl.multiple_of(number * width, 128)
        return pltpu.make_async_copy(
            w_scr.at[source, :, 2 * width :], down_ref.at[:, pl.ds(column, width)], save_sem.at[source]
        )

    @pl.when(step == 0)
    def _():
        fetch(0, 0)
        for target, own, par in ((b_scr, b_own, b_par), (e_scr, e_own, e_par)):
            target[:half, :] = own[...]
            target[half:, :] = par[...]

    @pl.when(step > 0)
    def _():
        saved(step - 1, 1 - slot).wait()

    @pl.when(step + 1 < tiles)
    def _():
        fetch(step + 1, 1 - slot)

    pltpu.make_async_copy(w_scr.at[slot], w_scr.at[slot], sem.at[slot]).wait()
    saved(step, slot).start()
    first = mm(b_scr[...], w_scr[slot, :, : 2 * width], 1, 0)
    gate, up = first[:, :width], first[:, width:]
    dhid = mm(e_scr[...], w_scr[slot, :, 2 * width :], 1, 0)
    sig = 1.0 / (1.0 + jnp.exp(-gate))
    silu = gate * sig
    hidden_ref[...] = (silu * up).astype(BF16)
    dgate = (dhid * up * (sig * (1.0 + gate * (1.0 - sig)))).astype(BF16)
    dup = (dhid * silu).astype(BF16)
    pair_ref[:, :width] = dgate
    pair_ref[:, width:] = dup
    part = mm(pair_ref[...], w_scr[slot, :, : 2 * width], 1, 1)

    @pl.when(step == 0)
    def _():
        total[...] = part

    @pl.when((step > 0) & (step < tiles - 1))
    def _():
        total[...] += part

    @pl.when(step == tiles - 1)
    def _():
        own_ref[...] = total[:half, :] + part[:half, :]
        par_ref[...] = (total[half:, :] + part[half:, :]).astype(BF16)
        saved(step, slot).wait()


def ffn(blocks, b_own, b_par, e_own, e_par, pieces):
    half, model = b_own.shape
    count = len(pieces)
    columns = [column for _, column in pieces]
    pieces = [piece for piece, _ in pieces]
    rows = pieces[0].shape[0]
    ff = max(piece.shape[1] + column for piece, column in zip(pieces, columns)) // 3
    spec = pl.BlockSpec
    whole = lambda j, s: (0, 0)
    anywhere = spec(memory_space=pl.ANY)
    once = spec((half, model), whole, pipeline_mode=pl.Buffered(1))
    return pl.pallas_call(
        functools.partial(ffn_kernel, columns, rows, ff),
        grid_spec=pltpu.PrefetchScalarGridSpec(
            num_scalar_prefetch=1,
            grid=(ff // TILE,),
            in_specs=[once] * 4 + [anywhere] * count,
            out_specs=[
                spec((2 * half, TILE), lambda j, s: (0, j)),
                spec((2 * half, 2 * TILE), lambda j, s: (0, j)),
                once,
                once,
                anywhere,
            ],
            scratch_shapes=[
                pltpu.VMEM((2 * half, model), BF16),
                pltpu.VMEM((2 * half, model), BF16),
                pltpu.VMEM((2, model, 3 * TILE), BF16),
                pltpu.VMEM((2 * half, model), F32),
                pltpu.SemaphoreType.DMA((2,)),
                pltpu.SemaphoreType.DMA((2,)),
            ],
        ),
        out_shape=[
            jax.ShapeDtypeStruct((2 * half, ff), BF16),
            jax.ShapeDtypeStruct((2 * half, 2 * ff), BF16),
            jax.ShapeDtypeStruct((half, model), F32),
            jax.ShapeDtypeStruct((half, model), BF16),
            jax.ShapeDtypeStruct((model, ff), BF16),
        ],
        compiler_params=pltpu.CompilerParams(vmem_limit_bytes=VMEM),
        cost_estimate=FREE,
        name="ffn",
    )(blocks, b_own, b_par, e_own, e_par, *pieces)


def place_of(natural, side, length):
    return pl.multiple_of((natural + side * (length // 2)) & (length - 1), BLOCK)


def diagonal():
    keys = lax.broadcasted_iota(jnp.int32, (BLOCK, BLOCK), 0)
    queries = lax.broadcasted_iota(jnp.int32, (BLOCK, BLOCK), 1)
    return keys <= queries


def fill(scratch, rows, side, docs):
    length = rows.shape[1]
    half = length // 2
    scratch[HEAD_DIM:, :] = jnp.zeros((PAD_DIM - HEAD_DIM, length), BF16)
    if docs is not None:
        scratch[HEAD_DIM : HEAD_DIM + DOCS, :] = docs[...]
    for part in range(2):
        there = pl.ds(place_of(part * half, side, length), half)
        scratch[:HEAD_DIM, part * half : (part + 1) * half] = rows[:, there]


def forward_kernel(
    side_ref, q_in, k_in, v_in, oq_ref, ok_ref, *rest
):
    att_ref, lse_ref, q_scr, kt_scr, k_scr, v_scr = rest[-6:]
    length = q_in.shape[1]
    side = side_ref[0]
    blocks = length // BLOCK
    fill(kt_scr, k_in, side, ok_ref)
    fill(v_scr, v_in, side, None)
    k_scr[...] = kt_scr[...].T
    causal = diagonal()
    for h in range(2):
        rows = slice(h * HEAD_DIM, (h + 1) * HEAD_DIM)
        fill(q_scr, q_in.at[rows, :], side, oq_ref)
        for b in range(blocks):
            here = pl.ds(b * BLOCK, BLOCK)
            keys = (b + 1) * BLOCK
            query = q_scr[:, here]
            last = mm(k_scr[b * BLOCK : keys, :], query, 1, 0)
            last = jnp.where(causal, last, -FAR)
            top = jnp.max(last, 0, keepdims=True)
            if b:
                early = mm(k_scr[: b * BLOCK, :], query, 1, 0)
                top = jnp.maximum(top, jnp.max(early, 0, keepdims=True))
            top = top * (SCALE * LOG2E)
            weight = jnp.exp2(last * (SCALE * LOG2E) - top)
            total = jnp.sum(weight, 0, keepdims=True)
            out = mm(v_scr[:HEAD_DIM, b * BLOCK : keys], weight.astype(BF16), 1, 0)
            if b:
                weight = jnp.exp2(early * (SCALE * LOG2E) - top)
                total = total + jnp.sum(weight, 0, keepdims=True)
                out = out + mm(v_scr[:HEAD_DIM, : b * BLOCK], weight.astype(BF16), 1, 0)
            out = out / total
            there = pl.ds(place_of(b * BLOCK, side, length), BLOCK)
            att_ref[rows, there] = out.astype(BF16)
            lse_ref[0, h : h + 1, here] = top + jnp.log2(total)


def group_specs(groups, length):
    spec = pl.BlockSpec
    return [
        spec((2 * HEAD_DIM, length), lambda g, s: (g, 0)),
        spec((HEAD_DIM, length), lambda g, s: (2 * groups + g, 0)),
        spec((HEAD_DIM, length), lambda g, s: (3 * groups + g, 0)),
    ]


def attend(side, qkv, doc_q, doc_k):
    hidden, length = qkv.shape
    groups = hidden // (4 * HEAD_DIM)
    whole = lambda g, s: (0, 0)
    spec = pl.BlockSpec
    return pl.pallas_call(
        forward_kernel,
        grid_spec=pltpu.PrefetchScalarGridSpec(
            num_scalar_prefetch=1,
            grid=(groups,),
            in_specs=group_specs(groups, length) + [spec((DOCS, length), whole)] * 2,
            out_specs=[
                spec((2 * HEAD_DIM, length), lambda g, s: (g, 0)),
                spec((1, 2, length), lambda g, s: (g, 0, 0)),
            ],
            scratch_shapes=[
                pltpu.VMEM((PAD_DIM, length), BF16),
                pltpu.VMEM((PAD_DIM, length), BF16),
                pltpu.VMEM((length, PAD_DIM), BF16),
                pltpu.VMEM((PAD_DIM, length), BF16),
            ],
        ),
        out_shape=[
            jax.ShapeDtypeStruct((2 * groups * HEAD_DIM, length), BF16),
            jax.ShapeDtypeStruct((groups, 2, length), F32),
        ],
        compiler_params=pltpu.CompilerParams(vmem_limit_bytes=VMEM),
        cost_estimate=FREE,
        name="attend",
    )(side, qkv, qkv, qkv, doc_q, doc_k)


def backward_kernel(
    side_ref, q_ref, k_ref, v_ref, att_ref, datt_own, datt_par, lse_ref, cos_ref, sin_ref,
    oq_ref, ok_ref, *rest,
):
    out_ref, *rest = rest
    q_scr, kt_scr, k_scr, vt_scr, v_scr, do_scr, dk_scr, dv_scr, datt_ref, dq_ref, sem = rest
    length = q_ref.shape[1]
    group = pl.program_id(0)
    groups = out_ref.shape[0] // (4 * HEAD_DIM)
    datt_ref[:, : length // 2] = datt_own[...]
    datt_ref[:, length // 2 :] = datt_par[...]
    slot = lax.rem(group, 2)
    dk_ref = dq_ref.at[slot, 2 * HEAD_DIM : 3 * HEAD_DIM, :]
    dv_ref = dq_ref.at[slot, 3 * HEAD_DIM :, :]
    dq_ref = dq_ref.at[slot]

    def stores(number, source):
        for i, (start, size) in enumerate(((0, 2), (2, 1), (3, 1))):
            base = (start * groups + number * size) * HEAD_DIM
            yield pltpu.make_async_copy(
                rest[-2].at[source, start * HEAD_DIM : (start + size) * HEAD_DIM, :],
                out_ref.at[pl.ds(pl.multiple_of(base, HEAD_DIM), size * HEAD_DIM), :],
                sem.at[source, i],
            )

    half = HEAD_DIM // 2
    side = side_ref[0]
    blocks = length // BLOCK
    fill(kt_scr, k_ref, side, ok_ref)
    fill(vt_scr, v_ref, side, None)
    k_scr[...] = kt_scr[...].T
    v_scr[...] = vt_scr[...].T
    causal = diagonal()
    for h in range(2):
        rows = slice(h * HEAD_DIM, (h + 1) * HEAD_DIM)
        fill(q_scr, q_ref.at[rows, :], side, oq_ref)
        fill(do_scr, datt_ref.at[rows, :], side, None)
        for b in range(blocks):
            here = pl.ds(b * BLOCK, BLOCK)
            there = pl.ds(place_of(b * BLOCK, side, length), BLOCK)
            base = jnp.sum(
                datt_ref[rows, there].astype(F32) * att_ref[rows, there].astype(F32), 0, keepdims=True
            )
            keys = (b + 1) * BLOCK
            query, upstream = q_scr[:, here], do_scr[:, here]
            level = lse_ref[0, h : h + 1, here]
            dq = None
            for start, stop in ((b * BLOCK, keys), (0, b * BLOCK)):
                if start == stop:
                    continue
                span = slice(start, stop)
                score = mm(k_scr[span, :], query, 1, 0)
                prob = jnp.exp2(score * (SCALE * LOG2E) - level)
                if stop == keys:
                    prob = jnp.where(causal, prob, 0.0)
                slope = mm(v_scr[span, :], upstream, 1, 0)
                ds = (prob * (slope - base)).astype(BF16)
                part = mm(kt_scr[:HEAD_DIM, span], ds, 1, 0)
                dq = part if dq is None else dq + part
                dk = mm(query[:HEAD_DIM, :], ds, 1, 1)
                dv = mm(upstream[:HEAD_DIM, :], prob.astype(BF16), 1, 1)
                if h == 0 and stop == keys:
                    dk_scr[:, span] = dk
                    dv_scr[:, span] = dv
                else:
                    dk_scr[:, span] += dk
                    dv_scr[:, span] += dv
            cos, sin = cos_ref[:, there], sin_ref[:, there]
            dq = dq * SCALE
            top, bottom = rope_rows(dq[:half, :], dq[half:, :], cos, -sin)
            dq_ref[h * HEAD_DIM : h * HEAD_DIM + half, there] = top.astype(BF16)
            dq_ref[h * HEAD_DIM + half : (h + 1) * HEAD_DIM, there] = bottom.astype(BF16)
    for b in range(blocks):
        here = pl.ds(b * BLOCK, BLOCK)
        there = pl.ds(place_of(b * BLOCK, side, length), BLOCK)
        cos, sin = cos_ref[:, there], sin_ref[:, there]
        dk = dk_scr[:, here] * SCALE
        top, bottom = rope_rows(dk[:half, :], dk[half:, :], cos, -sin)
        dk_ref[:half, there] = top.astype(BF16)
        dk_ref[half:, there] = bottom.astype(BF16)
        dv_ref[:, there] = dv_scr[:, here].astype(BF16)
    for copy in stores(group, slot):
        copy.start()

    @pl.when(group > 0)
    def _():
        for copy in stores(group - 1, 1 - slot):
            copy.wait()

    @pl.when(group == pl.num_programs(0) - 1)
    def _():
        for copy in stores(group, slot):
            copy.wait()


def attend_back(side, qkv, att, datt, lse, cos, sin, doc_q, doc_k):
    hidden, length = qkv.shape
    groups = hidden // (4 * HEAD_DIM)
    whole = lambda g, s: (0, 0)
    spec = pl.BlockSpec
    narrow = spec((2 * HEAD_DIM, length // 2), lambda g, s: (g, 0))
    source = spec((2 * HEAD_DIM, length), lambda g, s: (g, 0))
    level = spec((1, 2, length), lambda g, s: (g, 0, 0))
    anywhere = spec(memory_space=pl.ANY)
    table = spec((HEAD_DIM // 2, length), whole)
    docs = spec((DOCS, length), whole)
    tall = pltpu.VMEM((length, PAD_DIM), BF16)
    flat = pltpu.VMEM((PAD_DIM, length), BF16)
    return pl.pallas_call(
        backward_kernel,
        grid_spec=pltpu.PrefetchScalarGridSpec(
            num_scalar_prefetch=1,
            grid=(groups,),
            in_specs=group_specs(groups, length)
            + [source, narrow, narrow, level, table, table, docs, docs],
            out_specs=anywhere,
            scratch_shapes=[flat, flat, tall, flat, tall, flat]
            + [pltpu.VMEM((HEAD_DIM, length), F32)] * 2
            + [
                pltpu.VMEM((2 * HEAD_DIM, length), BF16),
                pltpu.VMEM((2, 4 * HEAD_DIM, length), BF16),
                pltpu.SemaphoreType.DMA((2, 3)),
            ],
        ),
        out_shape=jax.ShapeDtypeStruct((hidden, length), BF16),
        compiler_params=pltpu.CompilerParams(vmem_limit_bytes=VMEM),
        cost_estimate=FREE,
        name="attend_back",
    )(side, qkv, qkv, qkv, att, *datt, lse, cos, sin, doc_q, doc_k)


def low(weight):
    return weight.astype(BF16)


def layer(
    dp, tokens, segment_ids, positions, query_weight, key_weight, value_weight, out_weight,
    attn_gain, gate_weight, up_weight, down_weight, mlp_gain, cotangent,
):
    seqs, own_rows, model = tokens.shape
    length = segment_ids.shape[1]
    heads = query_weight.shape[1]
    ff = gate_weight.shape[1]
    side_index = lax.axis_index("tensor").astype(jnp.int32)
    side = side_index[None]
    blocks, turned = piece_blocks(dp), turn_blocks(dp)

    x_own = tokens.reshape(own_rows, model)
    e_own = cotangent.reshape(own_rows, model)
    gains = jnp.pad(jnp.stack([low(attn_gain), low(mlp_gain)], 1), ((0, 0), (0, 126)))
    order = Order(positions[0, 0] >= 0)
    first = order.done(join(query_weight, key_weight, value_weight, out_weight.T, gains))
    first = Gather(first, dp, 1280)
    x_par = swap_halves(x_own)
    first.round(order)
    first.share(order)
    second = order.done(join(gate_weight, up_weight, down_weight.T))
    second = Gather(second, dp, 3 * ff // 2)
    for _ in range(dp // 4 - 1):
        first.next(order)
    second.share(order)
    first = first.pieces(order)
    x_first, x_par = order.done(*order.tie(x_own, x_par))
    e_par = swap_halves(order.tie(e_own))
    second.round(order)

    places = positions.reshape(length).astype(F32)
    half = HEAD_DIM // 2
    places = jnp.where(side_index == 0, places, jnp.roll(places, length // 2))
    ladder = jnp.power(F32(ROPE_BASE), -2.0 * jnp.arange(half, dtype=F32) / HEAD_DIM)
    angles = ladder[:, None] * places[None, :]
    cos, sin = jnp.cos(angles), jnp.sin(angles)
    known = jnp.arange(DOCS, dtype=jnp.int32)[:, None] == segment_ids.reshape(1, length)
    doc_q = known.astype(BF16)
    doc_k = jnp.where(known, 0.0, -FAR).astype(BF16)

    qkv, gain_rows, a_turned, qkv_full, out_full = project(
        blocks, turned, x_first, x_par, cos, sin, first, heads
    )
    qkv = order.done(qkv)
    att, lse = attend(side, order.tie(qkv), doc_q, doc_k)
    e_par, att = order.done(e_par, att)

    own, par = slice(0, own_rows), slice(own_rows, None)
    partial = order.done(mm(att[:, par], out_full, 0, 1, BF16))
    sent = swap_halves(partial)
    second.next(order)
    e_turned = order.done(turn(turned, order.tie(e_own), e_par))
    partial = order.done(mm(att[:, own], order.tie(out_full), 0, 1))
    second.next(order)
    sent = order.tie(sent)
    middle, b_own = order.done(
        *by_rows(residual_kernel, (partial, sent, x_own), gain_rows, (F32, BF16), "residual")
    )
    b_par = swap_halves(b_own)
    second.next(order)
    second = second.pieces(order)

    b_par = order.tie(b_par)
    hidden, pair, db_own, db_par, down_full = ffn(blocks, b_own, b_par, e_own, e_par, second)
    db_par = order.done(db_par)
    db_sent = swap_halves(db_par)
    b_turned = order.done(turn(turned, order.tie(b_own), b_par))
    grad_ffn = Scatter(dp, order, (e_turned, hidden, 0), (b_turned, pair, 0))
    dh, eh_own = order.done(
        *by_rows(
            functools.partial(back_kernel, 1),
            (db_own, order.tie(db_sent), middle, e_own),
            gain_rows,
            (F32, BF16),
            "norm_back",
        )
    )
    eh_par = swap_halves(eh_own)
    grad_ffn.round()
    down_own, down_par = order.done(*product(order.tie(hidden), down_full))
    grad_ffn.round()
    datt_own = order.done(turned_product(order.tie(eh_own), out_full, 384))
    eh_par = order.tie(eh_par)
    datt_par = order.done(turned_product(eh_par, out_full, 384))
    down_sent = swap_halves(order.tie(down_par))
    eh_turned = order.done(turn(turned, order.tie(eh_own), eh_par))
    grad_ffn.round()
    datt = order.tie(datt_own, datt_par)
    dqkv = order.done(attend_back(side, qkv, att, datt, lse, cos, sin, doc_q, doc_k))
    down_sent = order.done(down_sent)
    da = order.done(turned_product(qkv_full, order.tie(dqkv), own_rows))
    da_sent = swap_halves(da[par])
    grad_ffn.round()
    grad_att = Scatter(dp, order, (a_turned, dqkv, 1), (eh_turned, att, 1))
    grad_att.round()
    output = (middle + (down_own.astype(F32) + order.tie(down_sent).astype(F32))).astype(BF16)
    output = order.done(output)
    grad_gate, grad_up, grad_down, gain_two = grad_ffn.result(
        (
            (ff, TILE, 2 * TILE, ff // TILE),
            (ff + TILE, TILE, 2 * TILE, ff // TILE),
            (0, TILE, TILE, ff // TILE),
        ),
        (gate_weight, up_weight),
    )
    grad_att.round()
    da_sent = order.done(da_sent)
    grad_att.round()
    (input_grad,) = by_rows(
        functools.partial(back_kernel, 0),
        (order.tie(da[own]), da_sent, x_own, dh),
        gain_rows,
        (BF16,),
        "norm_back",
    )
    input_grad = order.done(input_grad)
    grad_att.round()
    kv = heads // 2
    size = kv // 3 if kv % 384 else 384
    grad_query, grad_key, grad_value, grad_out, gain_one = grad_att.result(
        (
            (0, size, size, heads // size),
            (heads, size, size, kv // size),
            (heads + kv, size, size, kv // size),
            (2 * heads, size, size, heads // size),
        ),
        (query_weight, key_weight, value_weight),
    )
    gain_grads = jnp.stack(
        [gain_one[0] / low(attn_gain).astype(F32), gain_two[0] / low(mlp_gain).astype(F32)]
    )
    gain_grads = gain_grads + swap_halves(gain_grads)
    return (
        output.reshape(seqs, own_rows, model),
        input_grad.reshape(seqs, own_rows, model),
        grad_query,
        grad_key,
        grad_value,
        grad_out.T,
        gain_grads[0],
        grad_gate,
        grad_up,
        grad_down.T,
        gain_grads[1],
    )


def solution(mesh):
    in_specs = (
        P("dp", "tensor", None),
        P("dp", None),
        P("dp", None),
        P("dp", "tensor"),
        P("dp", "tensor"),
        P("dp", "tensor"),
        P("tensor", "dp"),
        P("dp"),
        P("dp", "tensor"),
        P("dp", "tensor"),
        P("tensor", "dp"),
        P("dp"),
        P("dp", "tensor", None),
    )
    out_specs = (
        P("dp", "tensor", None),
        P("dp", "tensor", None),
        P("dp", "tensor"),
        P("dp", "tensor"),
        P("dp", "tensor"),
        P("tensor", "dp"),
        P("dp"),
        P("dp", "tensor"),
        P("dp", "tensor"),
        P("tensor", "dp"),
        P("dp"),
    )
    return jax.shard_map(
        functools.partial(layer, mesh.shape["dp"]),
        mesh=mesh,
        in_specs=in_specs,
        out_specs=out_specs,
        check_vma=False,
    )
```

```python
import functools
import math

import jax
import jax.numpy as jnp
from jax import lax
from jax.experimental import pallas as pl
from jax.experimental.pallas import tpu as pltpu
from jax.sharding import PartitionSpec as P

HEAD_DIM = 96
PAD_DIM = 128
BLOCK = 256
DOCS = 16
EPSILON = 1e-05
ROPE_BASE = 100000.0
FAR = float(2**30)
RING_LIMIT = 16
TILE = 512
MIB = 2**20
SCALE = 1.0 / math.sqrt(HEAD_DIM)
LOG2E = math.log2(math.e)

F32 = jnp.float32
BF16 = jnp.bfloat16


def mm(left, right, left_dim, right_dim, dtype=F32):
    return lax.dot_general(
        left, right, (((left_dim,), (right_dim,)), ((), ())), preferred_element_type=F32
    ).astype(dtype)


def swap_halves(value):
    return lax.ppermute(value, "tensor", [(0, 1), (1, 0)])


def is_ring(dp):
    return 8 <= dp <= RING_LIMIT and dp & (dp - 1) == 0


def chip_of(spot, chips):
    return jnp.where(2 * spot < chips, 2 * spot, 2 * (chips - 1 - spot) + 1)


def ring_pairs(dp):
    chips = dp // 2
    order = list(range(0, chips, 2)) + list(range(chips - 1, 0, -2))
    ahead = []
    for spot in range(chips):
        here, following = order[spot], order[(spot + 1) % chips]
        ahead += [(2 * here, 2 * following), (2 * here + 1, 2 * following + 1)]
    return ahead, [(b, a) for a, b in ahead]


def ring_place(dp):
    chips = dp // 2
    me = lax.axis_index("dp").astype(jnp.int32)
    chip = me >> 1
    return me & 1, jnp.where(chip & 1 == 0, chip >> 1, chips - 1 - (chip >> 1))


def piece_steps(dp):
    reach = dp // 4
    return [0, *range(-1, -reach, -1), *range(1, reach), reach, reach]


def piece_blocks(dp):
    if not is_ring(dp):
        return jnp.zeros((1,), jnp.int32)
    chips = dp // 2
    core, spot = ring_place(dp)
    chip = chip_of((spot + jnp.asarray(piece_steps(dp), jnp.int32)) & (chips - 1), chips)
    return jnp.concatenate([2 * chip + core, 2 * chip + 1 - core])


def turn_blocks(dp):
    if not is_ring(dp):
        return jnp.zeros((1,), jnp.int32)
    chips = dp // 2
    core, spot = ring_place(dp)
    chip = chip_of((spot + jnp.arange(chips, dtype=jnp.int32)) & (chips - 1), chips)
    return jnp.concatenate([2 * chip + 1 - core, 2 * chip + core])


class Order:
    def __init__(self, flag):
        self.token = lax.create_token()
        self.flag = flag

    def tie(self, *values):
        tied = lax.optimization_barrier((self.token, *values))[1:]
        return tied if len(values) > 1 else tied[0]

    def done(self, *values):
        self.token, *values = lax.optimization_barrier((self.token, *values))
        return values if len(values) > 1 else values[0]


class Gather:
    def __init__(self, shard, dp, cut):
        self.dp, self.cut = dp, cut
        self.behind, self.ahead, self.other, self.shard = [], [], [], shard

    def share(self, order):
        if not is_ring(self.dp):
            return
        found = (self.behind[-1], self.ahead[-1]) if self.other else (self.shard,)
        swap = [(i, i ^ 1) for i in range(self.dp)]

        def both(*pieces):
            return tuple(lax.ppermute(piece, "dp", swap) for piece in pieces)

        def neither(*pieces):
            return tuple(jnp.zeros_like(piece) for piece in pieces)

        found = order.tie(*found) if len(found) > 1 else (order.tie(*found),)
        got = lax.cond(order.flag, both, neither, *found)
        self.other.append(order.done(*got) if len(got) > 1 else [order.done(*got)])

    def round(self, order):
        if not is_ring(self.dp):
            return
        forth, back = ring_pairs(self.dp)
        left = self.behind[-1] if self.behind else self.shard
        right = self.ahead[-1] if self.ahead else self.shard
        left, right = order.tie(left, right)
        if len(self.behind) == self.dp // 4 - 1:
            left, right = halves(left, right, self.cut)
        left, right = order.done(left, right)
        self.behind.append(lax.ppermute(left, "dp", forth))
        self.ahead.append(lax.ppermute(right, "dp", back))

    def arrive(self, order):
        if is_ring(self.dp):
            self.behind[-1], self.ahead[-1] = order.done(self.behind[-1], self.ahead[-1])

    def next(self, order):
        if not is_ring(self.dp):
            return
        self.arrive(order)
        arrived = self.behind[-1], self.ahead[-1]
        self.round(order)
        sent = self.behind.pop(), self.ahead.pop()
        self.behind[-1], self.ahead[-1] = arrived
        self.share(order)
        self.behind.append(sent[0])
        self.ahead.append(sent[1])

    def pieces(self, order):
        if not is_ring(self.dp):
            return [(lax.all_gather(self.shard, "dp", axis=0, tiled=True), 0)]
        self.arrive(order)
        self.share(order)
        held = [self.shard, *self.behind[:-1], *self.ahead[:-1], self.behind[-1], self.ahead[-1]]
        other = [self.other[0][0], *(pair[0] for pair in self.other[1:-1])]
        other += [*(pair[1] for pair in self.other[1:-1]), *self.other[-1]]
        columns = [0] * (len(held) - 1) + [self.cut]
        return list(zip([*held, *other], columns * 2))


class Scatter:
    def __init__(self, dp, order, *columns):
        self.dp, self.order = dp, order
        lefts, rights, dims = zip(*columns)
        rights = order.tie(*rights) if len(rights) > 1 else (order.tie(*rights),)
        if not is_ring(dp):
            full = order.done(products(0, 1, lefts, rights, dims))
            self.total = lax.psum_scatter(full, "dp", scatter_dimension=0, tiled=True).astype(F32)
            return
        self.chips = dp // 2
        self.reach = self.chips // 2
        self.rows = lefts[0].shape[0] // dp

        def both(lefts, rights):
            token = lax.create_token()
            theirs = products(0, 2, lefts, rights, dims)
            token, theirs = lax.optimization_barrier((token, theirs))
            got = lax.ppermute(theirs, "dp", [(i, i ^ 1) for i in range(dp)])
            rights = lax.optimization_barrier((token, *rights))[1:]
            return got, products(1, 2, lefts, rights, dims)

        def neither(lefts, rights):
            width = sum(right.shape[1 - dim] for right, dim in zip(rights, dims))
            return (jnp.zeros((lefts[0].shape[0] // 2, width), BF16),) * 2

        self.got, self.mine = order.done(*lax.cond(order.flag, both, neither, lefts, tuple(rights)))
        self.width = self.mine.shape[1]
        self.ahead = self.behind = None

    def local(self, steps, mine, first, low_edge, high_edge):
        block = steps % self.chips
        return [(part, block, first, low_edge, high_edge) for part in (mine, self.got)]

    def round(self):
        if not is_ring(self.dp):
            return
        forth, back = ring_pairs(self.dp)
        half = self.width // 2
        tile = half if half <= 1536 else half // 2
        count = half // tile
        mine = self.order.tie(self.mine)
        reach = self.reach
        if self.ahead is None:
            right = self.local(reach, mine, 0, 0, count)
            left = self.local(reach, mine, count, 0, count)
        else:
            cut = count if self.ahead.shape[1] == half else 2 * count
            right = [*self.local(reach, mine, 0, 0, 2 * count), (self.ahead, 0, 0, 0, cut)]
            left = [*self.local(-reach, mine, 0, 0, 2 * count)]
            left.append((self.behind, 0, 0, 2 * count - cut, 2 * count))
        right, left = self.order.done(*combine(self.rows, tile, [right, left]))
        self.ahead = lax.ppermute(right, "dp", forth)
        self.behind = lax.ppermute(left, "dp", back)
        self.reach -= 1

    def result(self, pieces, weights):
        if not is_ring(self.dp):
            parts = [self.total] + [jnp.zeros_like(self.total)] * 3
        else:
            parts = [self.order.tie(self.mine), self.got, self.ahead, self.behind]
        return self.order.done(*finish(parts, [0] * 4, pieces, weights))


def rope_rows(top, bottom, cos, sin):
    return top * cos - bottom * sin, bottom * cos + top * sin


def project_kernel(columns, rows, heads, block_ref, turn_ref, own_ref, par_ref, cos_ref, sin_ref, *rest):
    count = len(columns)
    pieces = rest[:count]
    qkv_ref, gain_ref, at_ref, wide_ref, out_ref = rest[count : count + 5]
    w_scr, a_scr, at_scr, in_sem, out_sem, turn_sem = rest[count + 5 :]
    step = pl.program_id(0)
    tiles = pl.num_programs(0)
    own_rows, model = own_ref.shape
    tile = qkv_ref.shape[0]
    half = HEAD_DIM // 2
    qkv_width = 2 * heads

    def loads(i):
        base = pl.multiple_of(block_ref[i] * rows, rows)
        place = slice(columns[i], columns[i] + pieces[i].shape[1])
        return pltpu.make_async_copy(pieces[i], w_scr.at[pl.ds(base, rows), place], in_sem.at[i])

    def stores():
        return (
            pltpu.make_async_copy(w_scr.at[:, :qkv_width], wide_ref, out_sem.at[0]),
            pltpu.make_async_copy(
                w_scr.at[:, qkv_width : qkv_width + heads], out_ref, out_sem.at[1]
            ),
        )

    def turns(i):
        block = model // turn_ref.shape[0]
        base = pl.multiple_of(turn_ref[i] * block, block)
        return pltpu.make_async_copy(
            at_scr.at[pl.ds(base, block), :], at_ref.at[pl.ds(i * block, block), :], turn_sem.at[i]
        )

    @pl.when(step == 0)
    def _():
        for i in range(count):
            loads(i).start()
        for i in range(count):
            loads(i).wait()
        gains = w_scr[:, qkv_width + heads :].astype(F32).T
        gain_ref[...] = gains[:8, :]
        gain = gains[:1, :]
        for number, ref in enumerate((own_ref, par_ref)):

            @pl.loop(0, own_rows // BLOCK)
            def _(part, ref=ref, number=number):
                start = pl.multiple_of(part * BLOCK, BLOCK)
                x = ref[pl.ds(start, BLOCK), :].astype(F32)
                inverse = lax.rsqrt(jnp.mean(x * x, -1, keepdims=True) + EPSILON)
                normed = x * inverse * gain
                place = pl.multiple_of(start + number * own_rows, BLOCK)
                a_scr[pl.ds(place, BLOCK), :] = normed.astype(BF16)
                at_scr[:, pl.ds(place, BLOCK)] = normed.T.astype(BF16)

        for copy in stores():
            copy.start()
        for i in range(turn_ref.shape[0]):
            turns(i).start()

    start = pl.multiple_of(step * tile, 128)
    flat = mm(a_scr[...], w_scr[:, pl.ds(start, tile)], 1, 0).T

    @pl.when(step < tiles - tiles // 4)
    def _():
        cos, sin = cos_ref[...], sin_ref[...]
        for h in range(tile // HEAD_DIM):
            base = h * HEAD_DIM
            top, bottom = rope_rows(
                flat[base : base + half, :], flat[base + half : base + HEAD_DIM, :], cos, sin
            )
            qkv_ref[base : base + half, :] = top.astype(BF16)
            qkv_ref[base + half : base + HEAD_DIM, :] = bottom.astype(BF16)

    @pl.when(step >= tiles - tiles // 4)
    def _():
        qkv_ref[...] = flat.astype(BF16)

    @pl.when(step == tiles - 1)
    def _():
        for copy in stores():
            copy.wait()
        for i in range(turn_ref.shape[0]):
            turns(i).wait()


FREE = pl.CostEstimate(flops=0, bytes_accessed=0, transcendentals=0)
LONG = pl.CostEstimate(flops=0, bytes_accessed=40 * 2**20, transcendentals=0)


def product_kernel(left_ref, right_ref, *out_refs):
    half = left_ref.shape[0] // 2

    @pl.loop(0, 2)
    def _(part):
        start = pl.multiple_of(part * half, half)
        out = mm(left_ref[pl.ds(start, half), :], right_ref[...], 1, 1, BF16)
        for number, ref in enumerate(out_refs):

            @pl.when(part == number)
            def _(ref=ref):
                ref[...] = out


def product(left, right):
    rows, depth = left.shape
    width = right.shape[0]
    tile = next(t for t in (TILE, 384, 256, width) if width % t == 0)
    spec = pl.BlockSpec
    return pl.pallas_call(
        product_kernel,
        grid=(width // tile,),
        in_specs=[spec((rows, depth), lambda j: (0, 0)), spec((tile, depth), lambda j: (j, 0))],
        out_specs=[spec((rows // 2, tile), lambda j: (0, j))] * 2,
        out_shape=[jax.ShapeDtypeStruct((rows // 2, width), BF16)] * 2,
        compiler_params=pltpu.CompilerParams(vmem_limit_bytes=28 * MIB),
        cost_estimate=FREE,
        name="product",
    )(left, right)


def products_kernel(starts, dims, *refs):
    count = len(dims)
    out_ref = refs[-1]
    step = pl.program_id(0)
    for i, dim in enumerate(dims):

        @pl.when((step >= starts[i]) & (step < starts[i + 1]))
        def _(i=i, dim=dim):
            width = out_ref.shape[1]
            size = TILE if width % TILE == 0 else width

            @pl.loop(0, width // size)
            def _(j):
                place = pl.ds(pl.multiple_of(j * size, 128), size)
                right = refs[count + i][place, :] if dim else refs[count + i][:, place]
                out_ref[:, place] = mm(refs[i][...], right, 1, dim, out_ref.dtype)


def products(part, parts, lefts, rights, dims):
    rows, depth = lefts[0].shape
    rows = rows // parts
    widths = [right.shape[1 - dim] for right, dim in zip(rights, dims)]
    tile = next(t for t in (1024, 768, TILE, 384) if all(width % t == 0 for width in widths))
    starts = [0]
    for width in widths:
        starts.append(starts[-1] + width // tile)
    spec = pl.BlockSpec
    in_specs = [spec((rows, depth), lambda j: (part, 0)) for _ in lefts]
    for i, dim in enumerate(dims):

        def place(j, i=i):
            return jnp.clip(j - starts[i], 0, starts[i + 1] - starts[i] - 1)

        if dim:
            in_specs.append(spec((tile, depth), lambda j, place=place: (place(j), 0)))
        else:
            in_specs.append(spec((depth, tile), lambda j, place=place: (0, place(j))))
    return pl.pallas_call(
        functools.partial(products_kernel, starts, dims),
        grid=(starts[-1],),
        in_specs=in_specs,
        out_specs=spec((rows, tile), lambda j: (0, j)),
        out_shape=jax.ShapeDtypeStruct((rows, sum(widths)), BF16),
        compiler_params=pltpu.CompilerParams(vmem_limit_bytes=32 * MIB),
        cost_estimate=FREE,
        name="products",
    )(*lefts, *rights)


def turned_kernel(left_ref, right_ref, out_ref):
    out_ref[...] = mm(left_ref[...], right_ref[...], 1, 0).T.astype(BF16)


def turned_product(left, right, tile, start=0, count=None):
    rows, depth = left.shape
    count = count or right.shape[1] // tile
    spec = pl.BlockSpec
    return pl.pallas_call(
        turned_kernel,
        grid=(count,),
        in_specs=[
            spec((rows, depth), lambda j: (0, 0)),
            spec((depth, tile), lambda j: (0, start + j)),
        ],
        out_specs=spec((tile, rows), lambda j: (j, 0)),
        out_shape=jax.ShapeDtypeStruct((count * tile, rows), BF16),
        compiler_params=pltpu.CompilerParams(vmem_limit_bytes=28 * MIB),
        cost_estimate=FREE,
        name="turned_product",
    )(left, right)


def join_kernel(*refs):
    start = 0
    for ref in refs[:-1]:
        refs[-1][:, start : start + ref.shape[1]] = ref[...].astype(BF16)
        start += ref.shape[1]


def join(*parts):
    rows = parts[0].shape[0]
    return pl.pallas_call(
        join_kernel,
        out_shape=jax.ShapeDtypeStruct((rows, sum(part.shape[1] for part in parts)), BF16),
        compiler_params=pltpu.CompilerParams(vmem_limit_bytes=63 * MIB),
        cost_estimate=FREE,
        name="join",
    )(*parts)


def halves_kernel(cut, left_ref, right_ref, low_ref, high_ref):
    low_ref[...] = left_ref[:, :cut]
    high_ref[...] = right_ref[:, cut:]


def halves(left, right, cut):
    rows, width = left.shape
    return pl.pallas_call(
        functools.partial(halves_kernel, cut),
        out_shape=[
            jax.ShapeDtypeStruct((rows, cut), left.dtype),
            jax.ShapeDtypeStruct((rows, width - cut), left.dtype),
        ],
        compiler_params=pltpu.CompilerParams(vmem_limit_bytes=63 * MIB),
        cost_estimate=FREE,
        name="halves",
    )(left, right)


def residual_kernel(part_ref, sent_ref, x_ref, gain_ref, middle_ref, b_ref):
    middle = x_ref[...].astype(F32) + (part_ref[...] + sent_ref[...].astype(F32))
    inverse = lax.rsqrt(jnp.mean(middle * middle, -1, keepdims=True) + EPSILON)
    middle_ref[...] = middle
    b_ref[...] = (middle * inverse * gain_ref[1:2, :]).astype(BF16)


def back_kernel(row, own_ref, sent_ref, value_ref, base_ref, gain_ref, *out_refs):
    upstream = own_ref[...].astype(F32) + sent_ref[...].astype(F32)
    value = value_ref[...].astype(F32)
    inverse = lax.rsqrt(jnp.mean(value * value, -1, keepdims=True) + EPSILON)
    scaled = upstream * gain_ref[row : row + 1, :]
    inner = jnp.mean(scaled * value, -1, keepdims=True)
    out = inverse * (scaled - value * (inverse * inverse * inner))
    out = base_ref[...].astype(F32) + out
    for ref in out_refs:
        ref[...] = out.astype(ref.dtype)


def by_rows(kernel, arrays, gain, dtypes, name):
    rows, width = arrays[0].shape
    step = 128
    block = pl.BlockSpec((step, width), lambda i: (i, 0))
    return pl.pallas_call(
        kernel,
        grid=(rows // step,),
        in_specs=[block] * len(arrays) + [pl.BlockSpec(gain.shape, lambda i: (0, 0))],
        out_specs=[block] * len(dtypes),
        out_shape=[jax.ShapeDtypeStruct((rows, width), dtype) for dtype in dtypes],
        compiler_params=pltpu.CompilerParams(vmem_limit_bytes=63 * MIB),
        cost_estimate=FREE,
        name=name,
    )(*arrays, gain)


def finish_kernel(pieces, weighted, *refs):
    parts, refs = refs[:4], refs[4:]
    weights, refs = refs[:weighted], refs[weighted:]
    outs, gain_ref, total_ref = refs[: len(pieces)], refs[-2], refs[-1]
    total_ref[...] = jnp.zeros_like(total_ref)
    for number, (out_ref, (start, size, stride, steps)) in enumerate(zip(outs, pieces)):

        @pl.loop(0, steps)
        def _(j, number=number, out_ref=out_ref, start=start, size=size, stride=stride):
            source = pl.ds(pl.multiple_of(start + j * stride, 128), size)
            target = pl.ds(pl.multiple_of(j * size, 128), size)
            total = sum(part[:, source].astype(F32) for part in parts)
            out_ref[:, target] = total
            if number < weighted:
                total = total * weights[number][:, target].astype(BF16).astype(F32)
                for k in range(0, size, 128):
                    total_ref[...] += total[:, k : k + 128]

    rows = jnp.broadcast_to(jnp.sum(total_ref[...], 1, keepdims=True), total_ref.shape)
    gain_ref[...] = rows.T[:8, :]


def finish(parts, blocks, pieces, weights):
    rows = weights[0].shape[0]
    width = parts[0].shape[1]
    spec = pl.BlockSpec
    whole = lambda i: (0, 0)
    widths = [size * steps for _, size, _, steps in pieces]
    return pl.pallas_call(
        functools.partial(finish_kernel, pieces, len(weights)),
        grid=(1,),
        in_specs=[spec((rows, width), lambda i, block=block: (block, 0)) for block in blocks]
        + [spec(weight.shape, whole) for weight in weights],
        out_specs=[spec((rows, size), whole) for size in widths] + [spec((8, rows), whole)],
        out_shape=[jax.ShapeDtypeStruct((rows, size), F32) for size in widths]
        + [jax.ShapeDtypeStruct((8, rows), F32)],
        scratch_shapes=[pltpu.VMEM((rows, 128), F32)],
        compiler_params=pltpu.CompilerParams(vmem_limit_bytes=28 * MIB),
        cost_estimate=FREE,
        name="finish",
    )(*parts, *weights)


def combine_kernel(outs, *refs):
    step = pl.program_id(0)
    inputs = list(refs[: -len(outs)])
    for out_ref, terms in zip(refs[-len(outs) :], outs):
        total = None
        for low_edge, high_edge in terms:
            value = inputs.pop(0)[...].astype(F32)
            if high_edge - low_edge < pl.num_programs(0):
                value = jnp.where((step >= low_edge) & (step < high_edge), value, 0.0)
            total = value if total is None else total + value
        out_ref[...] = total.astype(out_ref.dtype)


def combine(rows, tile, outs, dtype=BF16):
    tiles = max(high for terms in outs for *_, high in terms)
    in_specs, arrays, edges = [], [], []
    for terms in outs:
        edges.append([(low_edge, high_edge) for *_, low_edge, high_edge in terms])
        for array, block, first, low_edge, high_edge in terms:

            def place(j, block=block, first=first, low_edge=low_edge, high_edge=high_edge):
                return block, jnp.clip(j, low_edge, high_edge - 1) - low_edge + first

            in_specs.append(pl.BlockSpec((rows, tile), place))
            arrays.append(array)
    return pl.pallas_call(
        functools.partial(combine_kernel, edges),
        grid=(tiles,),
        in_specs=in_specs,
        out_specs=[pl.BlockSpec((rows, tile), lambda j: (0, j)) for _ in outs],
        out_shape=[jax.ShapeDtypeStruct((rows, tiles * tile), dtype) for _ in outs],
        compiler_params=pltpu.CompilerParams(vmem_limit_bytes=16 * MIB),
        cost_estimate=FREE,
        name="combine",
    )(*arrays)


def turn_kernel(turn_ref, own_ref, par_ref, out_ref, scr):
    own_rows, model = own_ref.shape
    step = BLOCK // 2
    for number, ref in enumerate((own_ref, par_ref)):

        @pl.loop(0, own_rows // step)
        def _(part, ref=ref, number=number):
            start = pl.multiple_of(part * step, step)
            place = pl.multiple_of(start + number * own_rows, step)
            scr[:, pl.ds(place, step)] = ref[pl.ds(start, step), :].astype(F32).T.astype(BF16)

    count = turn_ref.shape[0]
    block = model // count

    @pl.loop(0, count)
    def _(i):
        base = pl.multiple_of(turn_ref[i] * block, block)
        place = pl.multiple_of(i * block, block)
        out_ref[pl.ds(place, block), :] = scr[pl.ds(base, block), :]


def turn(turned, own, par):
    own_rows, model = own.shape
    length = 2 * own_rows
    whole = lambda i, t: (0, 0)
    spec = pl.BlockSpec
    return pl.pallas_call(
        turn_kernel,
        grid_spec=pltpu.PrefetchScalarGridSpec(
            num_scalar_prefetch=1,
            grid=(1,),
            in_specs=[spec((own_rows, model), whole)] * 2,
            out_specs=spec((model, length), whole),
            scratch_shapes=[pltpu.VMEM((model, length), BF16)],
        ),
        out_shape=jax.ShapeDtypeStruct((model, length), BF16),
        compiler_params=pltpu.CompilerParams(vmem_limit_bytes=24 * MIB),
        cost_estimate=LONG,
        name="turn",
    )(turned, own, par)


def project(blocks, turned, x_own, x_par, cos, sin, pieces, heads):
    own_rows, model = x_own.shape
    length = 2 * own_rows
    count = len(pieces)
    columns = [column for _, column in pieces]
    pieces = [piece for piece, _ in pieces]
    rows, width = pieces[0].shape
    qkv_width = 2 * heads
    tile = heads // 2
    spec = pl.BlockSpec
    whole = lambda j, s, t: (0, 0)
    anywhere = spec(memory_space=pl.ANY)
    return pl.pallas_call(
        functools.partial(project_kernel, columns, rows, heads),
        grid_spec=pltpu.PrefetchScalarGridSpec(
            num_scalar_prefetch=2,
            grid=(qkv_width // tile,),
            in_specs=[
                spec((own_rows, model), whole),
                spec((own_rows, model), whole),
                spec((HEAD_DIM // 2, length), whole),
                spec((HEAD_DIM // 2, length), whole),
            ]
            + [anywhere] * count,
            out_specs=[
                spec((tile, length), lambda j, s, t: (j, 0)),
                spec((8, model), whole),
                anywhere,
                anywhere,
                anywhere,
            ],
            scratch_shapes=[
                pltpu.VMEM((model, width), BF16),
                pltpu.VMEM((length, model), BF16),
                pltpu.VMEM((model, length), BF16),
                pltpu.SemaphoreType.DMA((count,)),
                pltpu.SemaphoreType.DMA((2,)),
                pltpu.SemaphoreType.DMA(turned.shape),
            ],
        ),
        out_shape=[
            jax.ShapeDtypeStruct((qkv_width, length), BF16),
            jax.ShapeDtypeStruct((8, model), F32),
            jax.ShapeDtypeStruct((model, length), BF16),
            jax.ShapeDtypeStruct((model, qkv_width), BF16),
            jax.ShapeDtypeStruct((model, heads), BF16),
        ],
        compiler_params=pltpu.CompilerParams(vmem_limit_bytes=40 * MIB),
        cost_estimate=FREE,
        name="project",
    )(blocks, turned, x_own, x_par, cos, sin, *pieces)


def ffn_kernel(columns, rows, ff, block_ref, b_own, b_par, e_own, e_par, *rest):
    count = len(columns)
    pieces = rest[:count]
    hidden_ref, pair_ref, own_ref, par_ref, down_ref = rest[count : count + 5]
    b_scr, e_scr, w_scr, total, sem, save_sem = rest[count + 5 :]
    step = pl.program_id(0)
    tiles = pl.num_programs(0)
    slot = lax.rem(step, 2)
    width = hidden_ref.shape[1]
    half = b_own.shape[0]

    def fetch(number, into):
        for kind in range(3):
            for i in range(count):
                base = pl.multiple_of(block_ref[i] * rows, rows)
                column = pl.multiple_of(kind * ff + number * width, 128)
                low_edge, high_edge = columns[i], columns[i] + pieces[i].shape[1]

                def start(i=i, base=base, column=column, kind=kind):
                    pltpu.make_async_copy(
                        pieces[i].at[:, pl.ds(pl.multiple_of(column - columns[i], 128), width)],
                        w_scr.at[into, pl.ds(base, rows), kind * width : (kind + 1) * width],
                        sem.at[into],
                    ).start()

                if low_edge <= kind * ff and (kind + 1) * ff <= high_edge:
                    start()
                elif low_edge < (kind + 1) * ff and kind * ff < high_edge:
                    pl.when((column >= low_edge) & (column < high_edge))(start)

    def saved(number, source):
        column = pl.multiple_of(number * width, 128)
        return pltpu.make_async_copy(
            w_scr.at[source, :, 2 * width :], down_ref.at[:, pl.ds(column, width)], save_sem.at[source]
        )

    @pl.when(step == 0)
    def _():
        fetch(0, 0)
        for target, own, par in ((b_scr, b_own, b_par), (e_scr, e_own, e_par)):
            target[:half, :] = own[...]
            target[half:, :] = par[...]

    @pl.when(step > 0)
    def _():
        saved(step - 1, 1 - slot).wait()

    @pl.when(step + 1 < tiles)
    def _():
        fetch(step + 1, 1 - slot)

    pltpu.make_async_copy(w_scr.at[slot], w_scr.at[slot], sem.at[slot]).wait()
    saved(step, slot).start()
    first = mm(b_scr[...], w_scr[slot, :, : 2 * width], 1, 0)
    gate, up = first[:, :width], first[:, width:]
    dhid = mm(e_scr[...], w_scr[slot, :, 2 * width :], 1, 0)
    sig = 1.0 / (1.0 + jnp.exp(-gate))
    silu = gate * sig
    hidden_ref[...] = (silu * up).astype(BF16)
    dgate = (dhid * up * (sig * (1.0 + gate * (1.0 - sig)))).astype(BF16)
    dup = (dhid * silu).astype(BF16)
    pair_ref[:, :width] = dgate
    pair_ref[:, width:] = dup
    part = mm(pair_ref[...], w_scr[slot, :, : 2 * width], 1, 1)

    @pl.when(step == 0)
    def _():
        total[...] = part

    @pl.when((step > 0) & (step < tiles - 1))
    def _():
        total[...] += part

    @pl.when(step == tiles - 1)
    def _():
        own_ref[...] = total[:half, :] + part[:half, :]
        par_ref[...] = (total[half:, :] + part[half:, :]).astype(BF16)
        saved(step, slot).wait()


def ffn(blocks, b_own, b_par, e_own, e_par, pieces):
    half, model = b_own.shape
    count = len(pieces)
    columns = [column for _, column in pieces]
    pieces = [piece for piece, _ in pieces]
    rows = pieces[0].shape[0]
    ff = max(piece.shape[1] + column for piece, column in zip(pieces, columns)) // 3
    spec = pl.BlockSpec
    whole = lambda j, s: (0, 0)
    anywhere = spec(memory_space=pl.ANY)
    once = spec((half, model), whole, pipeline_mode=pl.Buffered(1))
    return pl.pallas_call(
        functools.partial(ffn_kernel, columns, rows, ff),
        grid_spec=pltpu.PrefetchScalarGridSpec(
            num_scalar_prefetch=1,
            grid=(ff // TILE,),
            in_specs=[once] * 4 + [anywhere] * count,
            out_specs=[
                spec((2 * half, TILE), lambda j, s: (0, j)),
                spec((2 * half, 2 * TILE), lambda j, s: (0, j)),
                once,
                once,
                anywhere,
            ],
            scratch_shapes=[
                pltpu.VMEM((2 * half, model), BF16),
                pltpu.VMEM((2 * half, model), BF16),
                pltpu.VMEM((2, model, 3 * TILE), BF16),
                pltpu.VMEM((2 * half, model), F32),
                pltpu.SemaphoreType.DMA((2,)),
                pltpu.SemaphoreType.DMA((2,)),
            ],
        ),
        out_shape=[
            jax.ShapeDtypeStruct((2 * half, ff), BF16),
            jax.ShapeDtypeStruct((2 * half, 2 * ff), BF16),
            jax.ShapeDtypeStruct((half, model), F32),
            jax.ShapeDtypeStruct((half, model), BF16),
            jax.ShapeDtypeStruct((model, ff), BF16),
        ],
        compiler_params=pltpu.CompilerParams(vmem_limit_bytes=60 * MIB),
        cost_estimate=FREE,
        name="ffn",
    )(blocks, b_own, b_par, e_own, e_par, *pieces)


def place_of(natural, side, length):
    return pl.multiple_of((natural + side * (length // 2)) & (length - 1), BLOCK)


def diagonal():
    keys = lax.broadcasted_iota(jnp.int32, (BLOCK, BLOCK), 0)
    queries = lax.broadcasted_iota(jnp.int32, (BLOCK, BLOCK), 1)
    return keys <= queries


def fill(scratch, rows, side, docs):
    length = rows.shape[1]
    half = length // 2
    scratch[HEAD_DIM:, :] = jnp.zeros((PAD_DIM - HEAD_DIM, length), BF16)
    if docs is not None:
        scratch[HEAD_DIM : HEAD_DIM + DOCS, :] = docs[...]
    for part in range(2):
        there = pl.ds(place_of(part * half, side, length), half)
        scratch[:HEAD_DIM, part * half : (part + 1) * half] = rows[:, there]


def forward_kernel(
    side_ref, q_in, k_in, v_in, oq_ref, ok_ref, *rest
):
    att_ref, lse_ref, q_scr, kt_scr, k_scr, v_scr = rest[-6:]
    length = q_in.shape[1]
    side = side_ref[0]
    blocks = length // BLOCK
    fill(kt_scr, k_in, side, ok_ref)
    fill(v_scr, v_in, side, None)
    k_scr[...] = kt_scr[...].T
    causal = diagonal()
    for h in range(2):
        rows = slice(h * HEAD_DIM, (h + 1) * HEAD_DIM)
        fill(q_scr, q_in.at[rows, :], side, oq_ref)
        for b in range(blocks):
            here = pl.ds(b * BLOCK, BLOCK)
            keys = (b + 1) * BLOCK
            query = q_scr[:, here]
            last = mm(k_scr[b * BLOCK : keys, :], query, 1, 0)
            last = jnp.where(causal, last, -FAR)
            top = jnp.max(last, 0, keepdims=True)
            if b:
                early = mm(k_scr[: b * BLOCK, :], query, 1, 0)
                top = jnp.maximum(top, jnp.max(early, 0, keepdims=True))
            top = top * (SCALE * LOG2E)
            weight = jnp.exp2(last * (SCALE * LOG2E) - top)
            total = jnp.sum(weight, 0, keepdims=True)
            out = mm(v_scr[:HEAD_DIM, b * BLOCK : keys], weight.astype(BF16), 1, 0)
            if b:
                weight = jnp.exp2(early * (SCALE * LOG2E) - top)
                total = total + jnp.sum(weight, 0, keepdims=True)
                out = out + mm(v_scr[:HEAD_DIM, : b * BLOCK], weight.astype(BF16), 1, 0)
            out = out / total
            there = pl.ds(place_of(b * BLOCK, side, length), BLOCK)
            att_ref[rows, there] = out.astype(BF16)
            lse_ref[0, h : h + 1, here] = top + jnp.log2(total)


def group_specs(groups, length):
    spec = pl.BlockSpec
    return [
        spec((2 * HEAD_DIM, length), lambda g, s: (g, 0)),
        spec((HEAD_DIM, length), lambda g, s: (2 * groups + g, 0)),
        spec((HEAD_DIM, length), lambda g, s: (3 * groups + g, 0)),
    ]


def attend(side, qkv, doc_q, doc_k):
    hidden, length = qkv.shape
    groups = hidden // (4 * HEAD_DIM)
    whole = lambda g, s: (0, 0)
    spec = pl.BlockSpec
    return pl.pallas_call(
        forward_kernel,
        grid_spec=pltpu.PrefetchScalarGridSpec(
            num_scalar_prefetch=1,
            grid=(groups,),
            in_specs=group_specs(groups, length) + [spec((DOCS, length), whole)] * 2,
            out_specs=[
                spec((2 * HEAD_DIM, length), lambda g, s: (g, 0)),
                spec((1, 2, length), lambda g, s: (g, 0, 0)),
            ],
            scratch_shapes=[
                pltpu.VMEM((PAD_DIM, length), BF16),
                pltpu.VMEM((PAD_DIM, length), BF16),
                pltpu.VMEM((length, PAD_DIM), BF16),
                pltpu.VMEM((PAD_DIM, length), BF16),
            ],
        ),
        out_shape=[
            jax.ShapeDtypeStruct((2 * groups * HEAD_DIM, length), BF16),
            jax.ShapeDtypeStruct((groups, 2, length), F32),
        ],
        compiler_params=pltpu.CompilerParams(vmem_limit_bytes=24 * MIB),
        cost_estimate=FREE,
        name="attend",
    )(side, qkv, qkv, qkv, doc_q, doc_k)


def backward_kernel(
    side_ref, q_ref, k_ref, v_ref, att_ref, datt_own, datt_par, lse_ref, cos_ref, sin_ref,
    oq_ref, ok_ref, *rest,
):
    out_ref, *rest = rest
    q_scr, kt_scr, k_scr, vt_scr, v_scr, do_scr, dk_scr, dv_scr, datt_ref, dq_ref, sem = rest
    length = q_ref.shape[1]
    group = pl.program_id(0)
    groups = out_ref.shape[0] // (4 * HEAD_DIM)
    datt_ref[:, : length // 2] = datt_own[...]
    datt_ref[:, length // 2 :] = datt_par[...]
    slot = lax.rem(group, 2)
    dk_ref = dq_ref.at[slot, 2 * HEAD_DIM : 3 * HEAD_DIM, :]
    dv_ref = dq_ref.at[slot, 3 * HEAD_DIM :, :]
    dq_ref = dq_ref.at[slot]

    def stores(number, source):
        for i, (start, size) in enumerate(((0, 2), (2, 1), (3, 1))):
            base = (start * groups + number * size) * HEAD_DIM
            yield pltpu.make_async_copy(
                rest[-2].at[source, start * HEAD_DIM : (start + size) * HEAD_DIM, :],
                out_ref.at[pl.ds(pl.multiple_of(base, HEAD_DIM), size * HEAD_DIM), :],
                sem.at[source, i],
            )

    half = HEAD_DIM // 2
    side = side_ref[0]
    blocks = length // BLOCK
    fill(kt_scr, k_ref, side, ok_ref)
    fill(vt_scr, v_ref, side, None)
    k_scr[...] = kt_scr[...].T
    v_scr[...] = vt_scr[...].T
    causal = diagonal()
    for h in range(2):
        rows = slice(h * HEAD_DIM, (h + 1) * HEAD_DIM)
        fill(q_scr, q_ref.at[rows, :], side, oq_ref)
        fill(do_scr, datt_ref.at[rows, :], side, None)
        for b in range(blocks):
            here = pl.ds(b * BLOCK, BLOCK)
            there = pl.ds(place_of(b * BLOCK, side, length), BLOCK)
            base = jnp.sum(
                datt_ref[rows, there].astype(F32) * att_ref[rows, there].astype(F32), 0, keepdims=True
            )
            keys = (b + 1) * BLOCK
            query, upstream = q_scr[:, here], do_scr[:, here]
            level = lse_ref[0, h : h + 1, here]
            dq = None
            for start, stop in ((b * BLOCK, keys), (0, b * BLOCK)):
                if start == stop:
                    continue
                span = slice(start, stop)
                score = mm(k_scr[span, :], query, 1, 0)
                prob = jnp.exp2(score * (SCALE * LOG2E) - level)
                if stop == keys:
                    prob = jnp.where(causal, prob, 0.0)
                slope = mm(v_scr[span, :], upstream, 1, 0)
                ds = (prob * (slope - base)).astype(BF16)
                part = mm(kt_scr[:HEAD_DIM, span], ds, 1, 0)
                dq = part if dq is None else dq + part
                dk = mm(query[:HEAD_DIM, :], ds, 1, 1)
                dv = mm(upstream[:HEAD_DIM, :], prob.astype(BF16), 1, 1)
                if h == 0 and stop == keys:
                    dk_scr[:, span] = dk
                    dv_scr[:, span] = dv
                else:
                    dk_scr[:, span] += dk
                    dv_scr[:, span] += dv
            cos, sin = cos_ref[:, there], sin_ref[:, there]
            dq = dq * SCALE
            top, bottom = rope_rows(dq[:half, :], dq[half:, :], cos, -sin)
            dq_ref[h * HEAD_DIM : h * HEAD_DIM + half, there] = top.astype(BF16)
            dq_ref[h * HEAD_DIM + half : (h + 1) * HEAD_DIM, there] = bottom.astype(BF16)
    for b in range(blocks):
        here = pl.ds(b * BLOCK, BLOCK)
        there = pl.ds(place_of(b * BLOCK, side, length), BLOCK)
        cos, sin = cos_ref[:, there], sin_ref[:, there]
        dk = dk_scr[:, here] * SCALE
        top, bottom = rope_rows(dk[:half, :], dk[half:, :], cos, -sin)
        dk_ref[:half, there] = top.astype(BF16)
        dk_ref[half:, there] = bottom.astype(BF16)
        dv_ref[:, there] = dv_scr[:, here].astype(BF16)
    for copy in stores(group, slot):
        copy.start()

    @pl.when(group > 0)
    def _():
        for copy in stores(group - 1, 1 - slot):
            copy.wait()

    @pl.when(group == pl.num_programs(0) - 1)
    def _():
        for copy in stores(group, slot):
            copy.wait()


def attend_back(side, qkv, att, datt, lse, cos, sin, doc_q, doc_k):
    hidden, length = qkv.shape
    groups = hidden // (4 * HEAD_DIM)
    whole = lambda g, s: (0, 0)
    spec = pl.BlockSpec
    narrow = spec((2 * HEAD_DIM, length // 2), lambda g, s: (g, 0))
    source = spec((2 * HEAD_DIM, length), lambda g, s: (g, 0))
    level = spec((1, 2, length), lambda g, s: (g, 0, 0))
    anywhere = spec(memory_space=pl.ANY)
    table = spec((HEAD_DIM // 2, length), whole)
    docs = spec((DOCS, length), whole)
    tall = pltpu.VMEM((length, PAD_DIM), BF16)
    flat = pltpu.VMEM((PAD_DIM, length), BF16)
    return pl.pallas_call(
        backward_kernel,
        grid_spec=pltpu.PrefetchScalarGridSpec(
            num_scalar_prefetch=1,
            grid=(groups,),
            in_specs=group_specs(groups, length)
            + [source, narrow, narrow, level, table, table, docs, docs],
            out_specs=anywhere,
            scratch_shapes=[flat, flat, tall, flat, tall, flat]
            + [pltpu.VMEM((HEAD_DIM, length), F32)] * 2
            + [
                pltpu.VMEM((2 * HEAD_DIM, length), BF16),
                pltpu.VMEM((2, 4 * HEAD_DIM, length), BF16),
                pltpu.SemaphoreType.DMA((2, 3)),
            ],
        ),
        out_shape=jax.ShapeDtypeStruct((hidden, length), BF16),
        compiler_params=pltpu.CompilerParams(vmem_limit_bytes=32 * MIB),
        cost_estimate=FREE,
        name="attend_back",
    )(side, qkv, qkv, qkv, att, *datt, lse, cos, sin, doc_q, doc_k)


def low(weight):
    return weight.astype(BF16)


def layer(
    dp, tokens, segment_ids, positions, query_weight, key_weight, value_weight, out_weight,
    attn_gain, gate_weight, up_weight, down_weight, mlp_gain, cotangent,
):
    seqs, own_rows, model = tokens.shape
    length = segment_ids.shape[1]
    heads = query_weight.shape[1]
    ff = gate_weight.shape[1]
    side_index = lax.axis_index("tensor").astype(jnp.int32)
    side = side_index[None]
    blocks, turned = piece_blocks(dp), turn_blocks(dp)

    x_own = tokens.reshape(own_rows, model)
    e_own = cotangent.reshape(own_rows, model)
    gains = jnp.pad(jnp.stack([low(attn_gain), low(mlp_gain)], 1), ((0, 0), (0, 126)))
    order = Order(positions[0, 0] >= 0)
    first = order.done(join(query_weight, key_weight, value_weight, out_weight.T, gains))
    first = Gather(first, dp, 1280)
    x_par = swap_halves(x_own)
    first.round(order)
    first.share(order)
    second = order.done(join(gate_weight, up_weight, down_weight.T))
    second = Gather(second, dp, 3 * ff // 2)
    for _ in range(dp // 4 - 1):
        first.next(order)
    second.share(order)
    first = first.pieces(order)
    x_first, x_par = order.done(*order.tie(x_own, x_par))
    e_par = swap_halves(order.tie(e_own))
    second.round(order)

    places = positions.reshape(length).astype(F32)
    half = HEAD_DIM // 2
    places = jnp.where(side_index == 0, places, jnp.roll(places, length // 2))
    ladder = jnp.power(F32(ROPE_BASE), -2.0 * jnp.arange(half, dtype=F32) / HEAD_DIM)
    angles = ladder[:, None] * places[None, :]
    cos, sin = jnp.cos(angles), jnp.sin(angles)
    known = jnp.arange(DOCS, dtype=jnp.int32)[:, None] == segment_ids.reshape(1, length)
    doc_q = known.astype(BF16)
    doc_k = jnp.where(known, 0.0, -FAR).astype(BF16)

    qkv, gain_rows, a_turned, qkv_full, out_full = project(
        blocks, turned, x_first, x_par, cos, sin, first, heads
    )
    qkv = order.done(qkv)
    att, lse = attend(side, order.tie(qkv), doc_q, doc_k)
    e_par, att = order.done(e_par, att)

    own, par = slice(0, own_rows), slice(own_rows, None)
    partial = order.done(mm(att[:, par], out_full, 0, 1, BF16))
    sent = swap_halves(partial)
    second.next(order)
    e_turned = order.done(turn(turned, order.tie(e_own), e_par))
    partial = order.done(mm(att[:, own], order.tie(out_full), 0, 1))
    second.next(order)
    sent = order.tie(sent)
    middle, b_own = order.done(
        *by_rows(residual_kernel, (partial, sent, x_own), gain_rows, (F32, BF16), "residual")
    )
    b_par = swap_halves(b_own)
    second.next(order)
    second = second.pieces(order)

    b_par = order.tie(b_par)
    hidden, pair, db_own, db_par, down_full = ffn(blocks, b_own, b_par, e_own, e_par, second)
    db_par = order.done(db_par)
    db_sent = swap_halves(db_par)
    b_turned = order.done(turn(turned, order.tie(b_own), b_par))
    grad_ffn = Scatter(dp, order, (e_turned, hidden, 0), (b_turned, pair, 0))
    dh, eh_own = order.done(
        *by_rows(
            functools.partial(back_kernel, 1),
            (db_own, order.tie(db_sent), middle, e_own),
            gain_rows,
            (F32, BF16),
            "norm_back",
        )
    )
    eh_par = swap_halves(eh_own)
    grad_ffn.round()
    down_own, down_par = order.done(*product(order.tie(hidden), down_full))
    grad_ffn.round()
    datt_own = order.done(turned_product(order.tie(eh_own), out_full, 384))
    eh_par = order.tie(eh_par)
    datt_par = order.done(turned_product(eh_par, out_full, 384))
    down_sent = swap_halves(order.tie(down_par))
    eh_turned = order.done(turn(turned, order.tie(eh_own), eh_par))
    grad_ffn.round()
    datt = order.tie(datt_own, datt_par)
    dqkv = order.done(attend_back(side, qkv, att, datt, lse, cos, sin, doc_q, doc_k))
    down_sent = order.done(down_sent)
    da = order.done(turned_product(qkv_full, order.tie(dqkv), own_rows))
    da_sent = swap_halves(da[par])
    grad_ffn.round()
    grad_att = Scatter(dp, order, (a_turned, dqkv, 1), (eh_turned, att, 1))
    grad_att.round()
    output = (middle + (down_own.astype(F32) + order.tie(down_sent).astype(F32))).astype(BF16)
    output = order.done(output)
    grad_gate, grad_up, grad_down, gain_two = grad_ffn.result(
        (
            (ff, TILE, 2 * TILE, ff // TILE),
            (ff + TILE, TILE, 2 * TILE, ff // TILE),
            (0, TILE, TILE, ff // TILE),
        ),
        (gate_weight, up_weight),
    )
    grad_att.round()
    da_sent = order.done(da_sent)
    grad_att.round()
    (input_grad,) = by_rows(
        functools.partial(back_kernel, 0),
        (order.tie(da[own]), da_sent, x_own, dh),
        gain_rows,
        (BF16,),
        "norm_back",
    )
    input_grad = order.done(input_grad)
    grad_att.round()
    kv = heads // 2
    size = kv // 3 if kv % 384 else 384
    grad_query, grad_key, grad_value, grad_out, gain_one = grad_att.result(
        (
            (0, size, size, heads // size),
            (heads, size, size, kv // size),
            (heads + kv, size, size, kv // size),
            (2 * heads, size, size, heads // size),
        ),
        (query_weight, key_weight, value_weight),
    )
    gain_grads = jnp.stack(
        [gain_one[0] / low(attn_gain).astype(F32), gain_two[0] / low(mlp_gain).astype(F32)]
    )
    gain_grads = gain_grads + swap_halves(gain_grads)
    return (
        output.reshape(seqs, own_rows, model),
        input_grad.reshape(seqs, own_rows, model),
        grad_query,
        grad_key,
        grad_value,
        grad_out.T,
        gain_grads[0],
        grad_gate,
        grad_up,
        grad_down.T,
        gain_grads[1],
    )


def solution(mesh):
    in_specs = (
        P("dp", "tensor", None),
        P("dp", None),
        P("dp", None),
        P("dp", "tensor"),
        P("dp", "tensor"),
        P("dp", "tensor"),
        P("tensor", "dp"),
        P("dp"),
        P("dp", "tensor"),
        P("dp", "tensor"),
        P("tensor", "dp"),
        P("dp"),
        P("dp", "tensor", None),
    )
    out_specs = (
        P("dp", "tensor", None),
        P("dp", "tensor", None),
        P("dp", "tensor"),
        P("dp", "tensor"),
        P("dp", "tensor"),
        P("tensor", "dp"),
        P("dp"),
        P("dp", "tensor"),
        P("dp", "tensor"),
        P("tensor", "dp"),
        P("dp"),
    )
    return jax.shard_map(
        functools.partial(layer, mesh.shape["dp"]),
        mesh=mesh,
        in_specs=in_specs,
        out_specs=out_specs,
        check_vma=False,
    )
```

```python
import functools
import math

import jax
import jax.numpy as jnp
from jax import lax
from jax.experimental import pallas as pl
from jax.experimental.pallas import tpu as pltpu
from jax.sharding import PartitionSpec as P

HEAD_DIM = 96
PAD_DIM = 128
BLOCK = 256
DOCS = 16
EPSILON = 1e-05
ROPE_BASE = 100000.0
FAR = float(2**30)
RING_LIMIT = 16
TILE = 512
MIB = 2**20
SCALE = 1.0 / math.sqrt(HEAD_DIM)
LOG2E = math.log2(math.e)

F32 = jnp.float32
BF16 = jnp.bfloat16


def mm(left, right, left_dim, right_dim, dtype=F32):
    return lax.dot_general(
        left, right, (((left_dim,), (right_dim,)), ((), ())), preferred_element_type=F32
    ).astype(dtype)


def swap_halves(value):
    return lax.ppermute(value, "tensor", [(0, 1), (1, 0)])


def is_ring(dp):
    return 8 <= dp <= RING_LIMIT and dp & (dp - 1) == 0


def chip_of(spot, chips):
    return jnp.where(2 * spot < chips, 2 * spot, 2 * (chips - 1 - spot) + 1)


def ring_pairs(dp):
    chips = dp // 2
    order = list(range(0, chips, 2)) + list(range(chips - 1, 0, -2))
    ahead = []
    for spot in range(chips):
        here, following = order[spot], order[(spot + 1) % chips]
        ahead += [(2 * here, 2 * following), (2 * here + 1, 2 * following + 1)]
    return ahead, [(b, a) for a, b in ahead]


def ring_place(dp):
    chips = dp // 2
    me = lax.axis_index("dp").astype(jnp.int32)
    chip = me >> 1
    return me & 1, jnp.where(chip & 1 == 0, chip >> 1, chips - 1 - (chip >> 1))


def piece_steps(dp):
    reach = dp // 4
    return [0, *range(-1, -reach, -1), *range(1, reach), reach, reach]


def piece_blocks(dp):
    if not is_ring(dp):
        return jnp.zeros((1,), jnp.int32)
    chips = dp // 2
    core, spot = ring_place(dp)
    chip = chip_of((spot + jnp.asarray(piece_steps(dp), jnp.int32)) & (chips - 1), chips)
    return jnp.concatenate([2 * chip + core, 2 * chip + 1 - core])


def turn_blocks(dp):
    if not is_ring(dp):
        return jnp.zeros((1,), jnp.int32)
    chips = dp // 2
    core, spot = ring_place(dp)
    chip = chip_of((spot + jnp.arange(chips, dtype=jnp.int32)) & (chips - 1), chips)
    return jnp.concatenate([2 * chip + 1 - core, 2 * chip + core])


class Order:
    def __init__(self, flag):
        self.token = lax.create_token()
        self.flag = flag

    def tie(self, *values):
        tied = lax.optimization_barrier((self.token, *values))[1:]
        return tied if len(values) > 1 else tied[0]

    def done(self, *values):
        self.token, *values = lax.optimization_barrier((self.token, *values))
        return values if len(values) > 1 else values[0]


class Gather:
    def __init__(self, shard, dp, cut):
        self.dp, self.cut = dp, cut
        self.behind, self.ahead, self.other, self.shard = [], [], [], shard

    def share(self, order):
        if not is_ring(self.dp):
            return
        found = (self.behind[-1], self.ahead[-1]) if self.other else (self.shard,)
        swap = [(i, i ^ 1) for i in range(self.dp)]

        def both(*pieces):
            return tuple(lax.ppermute(piece, "dp", swap) for piece in pieces)

        def neither(*pieces):
            return tuple(jnp.zeros_like(piece) for piece in pieces)

        found = order.tie(*found) if len(found) > 1 else (order.tie(*found),)
        got = lax.cond(order.flag, both, neither, *found)
        self.other.append(order.done(*got) if len(got) > 1 else [order.done(*got)])

    def round(self, order):
        if not is_ring(self.dp):
            return
        forth, back = ring_pairs(self.dp)
        left = self.behind[-1] if self.behind else self.shard
        right = self.ahead[-1] if self.ahead else self.shard
        left, right = order.tie(left, right)
        if len(self.behind) == self.dp // 4 - 1:
            left, right = halves(left, right, self.cut)
        left, right = order.done(left, right)
        self.behind.append(lax.ppermute(left, "dp", forth))
        self.ahead.append(lax.ppermute(right, "dp", back))

    def arrive(self, order):
        if is_ring(self.dp):
            self.behind[-1], self.ahead[-1] = order.done(self.behind[-1], self.ahead[-1])

    def next(self, order):
        if not is_ring(self.dp):
            return
        self.arrive(order)
        arrived = self.behind[-1], self.ahead[-1]
        self.round(order)
        sent = self.behind.pop(), self.ahead.pop()
        self.behind[-1], self.ahead[-1] = arrived
        self.share(order)
        self.behind.append(sent[0])
        self.ahead.append(sent[1])

    def pieces(self, order):
        if not is_ring(self.dp):
            return [(lax.all_gather(self.shard, "dp", axis=0, tiled=True), 0)]
        self.arrive(order)
        self.share(order)
        held = [self.shard, *self.behind[:-1], *self.ahead[:-1], self.behind[-1], self.ahead[-1]]
        other = [self.other[0][0], *(pair[0] for pair in self.other[1:-1])]
        other += [*(pair[1] for pair in self.other[1:-1]), *self.other[-1]]
        columns = [0] * (len(held) - 1) + [self.cut]
        return list(zip([*held, *other], columns * 2))


class Scatter:
    def __init__(self, dp, order, *columns):
        self.dp, self.order = dp, order
        lefts, rights, dims = zip(*columns)
        rights = order.tie(*rights) if len(rights) > 1 else (order.tie(*rights),)
        if not is_ring(dp):
            full = order.done(products(0, 1, lefts, rights, dims))
            self.total = lax.psum_scatter(full, "dp", scatter_dimension=0, tiled=True).astype(F32)
            return
        self.chips = dp // 2
        self.reach = self.chips // 2
        self.rows = lefts[0].shape[0] // dp

        def both(lefts, rights):
            token = lax.create_token()
            theirs = products(0, 2, lefts, rights, dims)
            token, theirs = lax.optimization_barrier((token, theirs))
            got = lax.ppermute(theirs, "dp", [(i, i ^ 1) for i in range(dp)])
            rights = lax.optimization_barrier((token, *rights))[1:]
            return got, products(1, 2, lefts, rights, dims)

        def neither(lefts, rights):
            width = sum(right.shape[1 - dim] for right, dim in zip(rights, dims))
            return (jnp.zeros((lefts[0].shape[0] // 2, width), BF16),) * 2

        self.got, self.mine = order.done(*lax.cond(order.flag, both, neither, lefts, tuple(rights)))
        self.width = self.mine.shape[1]
        self.ahead = self.behind = None

    def local(self, steps, mine, first, low_edge, high_edge):
        block = steps % self.chips
        return [(part, block, first, low_edge, high_edge) for part in (mine, self.got)]

    def round(self):
        if not is_ring(self.dp):
            return
        forth, back = ring_pairs(self.dp)
        half = self.width // 2
        tile = half if half <= 1536 else half // 2
        count = half // tile
        mine = self.order.tie(self.mine)
        reach = self.reach
        if self.ahead is None:
            right = self.local(reach, mine, 0, 0, count)
            left = self.local(reach, mine, count, 0, count)
        else:
            cut = count if self.ahead.shape[1] == half else 2 * count
            right = [*self.local(reach, mine, 0, 0, 2 * count), (self.ahead, 0, 0, 0, cut)]
            left = [*self.local(-reach, mine, 0, 0, 2 * count)]
            left.append((self.behind, 0, 0, 2 * count - cut, 2 * count))
        right, left = self.order.done(*combine(self.rows, tile, [right, left]))
        self.ahead = lax.ppermute(right, "dp", forth)
        self.behind = lax.ppermute(left, "dp", back)
        self.reach -= 1

    def arrive(self):
        if is_ring(self.dp):
            self.ahead, self.behind = self.order.done(self.ahead, self.behind)

    def result(self, pieces, weights):
        if not is_ring(self.dp):
            parts = [self.total] + [jnp.zeros_like(self.total)] * 3
        else:
            parts = [self.order.tie(self.mine), self.got, self.ahead, self.behind]
        return self.order.done(*finish(parts, [0] * 4, pieces, weights))


def rope_rows(top, bottom, cos, sin):
    return top * cos - bottom * sin, bottom * cos + top * sin


def project_kernel(columns, rows, heads, block_ref, turn_ref, own_ref, par_ref, cos_ref, sin_ref, *rest):
    count = len(columns)
    pieces = rest[:count]
    qkv_ref, gain_ref, at_ref, wide_ref, out_ref = rest[count : count + 5]
    w_scr, a_scr, at_scr, in_sem, out_sem, turn_sem = rest[count + 5 :]
    step = pl.program_id(0)
    tiles = pl.num_programs(0)
    own_rows, model = own_ref.shape
    tile = qkv_ref.shape[0]
    half = HEAD_DIM // 2
    qkv_width = 2 * heads

    def loads(i):
        base = pl.multiple_of(block_ref[i] * rows, rows)
        place = slice(columns[i], columns[i] + pieces[i].shape[1])
        return pltpu.make_async_copy(pieces[i], w_scr.at[pl.ds(base, rows), place], in_sem.at[i])

    def stores():
        return (
            pltpu.make_async_copy(w_scr.at[:, :qkv_width], wide_ref, out_sem.at[0]),
            pltpu.make_async_copy(
                w_scr.at[:, qkv_width : qkv_width + heads], out_ref, out_sem.at[1]
            ),
        )

    def turns(i):
        block = model // turn_ref.shape[0]
        base = pl.multiple_of(turn_ref[i] * block, block)
        return pltpu.make_async_copy(
            at_scr.at[pl.ds(base, block), :], at_ref.at[pl.ds(i * block, block), :], turn_sem.at[i]
        )

    @pl.when(step == 0)
    def _():
        for i in range(count):
            loads(i).start()
        for i in range(count):
            loads(i).wait()
        gains = w_scr[:, qkv_width + heads :].astype(F32).T
        gain_ref[...] = gains[:8, :]
        gain = gains[:1, :]
        for number, ref in enumerate((own_ref, par_ref)):

            @pl.loop(0, own_rows // BLOCK)
            def _(part, ref=ref, number=number):
                start = pl.multiple_of(part * BLOCK, BLOCK)
                x = ref[pl.ds(start, BLOCK), :].astype(F32)
                inverse = lax.rsqrt(jnp.mean(x * x, -1, keepdims=True) + EPSILON)
                normed = x * inverse * gain
                place = pl.multiple_of(start + number * own_rows, BLOCK)
                a_scr[pl.ds(place, BLOCK), :] = normed.astype(BF16)
                at_scr[:, pl.ds(place, BLOCK)] = normed.T.astype(BF16)

        for copy in stores():
            copy.start()
        for i in range(turn_ref.shape[0]):
            turns(i).start()

    start = pl.multiple_of(step * tile, 128)
    flat = mm(a_scr[...], w_scr[:, pl.ds(start, tile)], 1, 0).T

    @pl.when(step < tiles - tiles // 4)
    def _():
        cos, sin = cos_ref[...], sin_ref[...]
        for h in range(tile // HEAD_DIM):
            base = h * HEAD_DIM
            top, bottom = rope_rows(
                flat[base : base + half, :], flat[base + half : base + HEAD_DIM, :], cos, sin
            )
            qkv_ref[base : base + half, :] = top.astype(BF16)
            qkv_ref[base + half : base + HEAD_DIM, :] = bottom.astype(BF16)

    @pl.when(step >= tiles - tiles // 4)
    def _():
        qkv_ref[...] = flat.astype(BF16)

    @pl.when(step == tiles - 1)
    def _():
        for copy in stores():
            copy.wait()
        for i in range(turn_ref.shape[0]):
            turns(i).wait()


FREE = pl.CostEstimate(flops=0, bytes_accessed=0, transcendentals=0)
LONG = pl.CostEstimate(flops=0, bytes_accessed=40 * 2**20, transcendentals=0)


def product_kernel(left_ref, right_ref, *out_refs):
    half = left_ref.shape[0] // 2

    @pl.loop(0, 2)
    def _(part):
        start = pl.multiple_of(part * half, half)
        out = mm(left_ref[pl.ds(start, half), :], right_ref[...], 1, 1, BF16)
        for number, ref in enumerate(out_refs):

            @pl.when(part == number)
            def _(ref=ref):
                ref[...] = out


def product(left, right):
    rows, depth = left.shape
    width = right.shape[0]
    tile = next(t for t in (TILE, 384, 256, width) if width % t == 0)
    spec = pl.BlockSpec
    return pl.pallas_call(
        product_kernel,
        grid=(width // tile,),
        in_specs=[spec((rows, depth), lambda j: (0, 0)), spec((tile, depth), lambda j: (j, 0))],
        out_specs=[spec((rows // 2, tile), lambda j: (0, j))] * 2,
        out_shape=[jax.ShapeDtypeStruct((rows // 2, width), BF16)] * 2,
        compiler_params=pltpu.CompilerParams(vmem_limit_bytes=28 * MIB),
        cost_estimate=FREE,
        name="product",
    )(left, right)


def products_kernel(starts, dims, *refs):
    count = len(dims)
    out_ref = refs[-1]
    step = pl.program_id(0)
    for i, dim in enumerate(dims):

        @pl.when((step >= starts[i]) & (step < starts[i + 1]))
        def _(i=i, dim=dim):
            width = out_ref.shape[1]
            size = TILE if width % TILE == 0 else width

            @pl.loop(0, width // size)
            def _(j):
                place = pl.ds(pl.multiple_of(j * size, 128), size)
                right = refs[count + i][place, :] if dim else refs[count + i][:, place]
                out_ref[:, place] = mm(refs[i][...], right, 1, dim, out_ref.dtype)


def products(part, parts, lefts, rights, dims):
    rows, depth = lefts[0].shape
    rows = rows // parts
    widths = [right.shape[1 - dim] for right, dim in zip(rights, dims)]
    tile = next(t for t in (1024, 768, TILE, 384) if all(width % t == 0 for width in widths))
    starts = [0]
    for width in widths:
        starts.append(starts[-1] + width // tile)
    spec = pl.BlockSpec
    in_specs = [spec((rows, depth), lambda j: (part, 0)) for _ in lefts]
    for i, dim in enumerate(dims):

        def place(j, i=i):
            return jnp.clip(j - starts[i], 0, starts[i + 1] - starts[i] - 1)

        if dim:
            in_specs.append(spec((tile, depth), lambda j, place=place: (place(j), 0)))
        else:
            in_specs.append(spec((depth, tile), lambda j, place=place: (0, place(j))))
    return pl.pallas_call(
        functools.partial(products_kernel, starts, dims),
        grid=(starts[-1],),
        in_specs=in_specs,
        out_specs=spec((rows, tile), lambda j: (0, j)),
        out_shape=jax.ShapeDtypeStruct((rows, sum(widths)), BF16),
        compiler_params=pltpu.CompilerParams(vmem_limit_bytes=32 * MIB),
        cost_estimate=FREE,
        name="products",
    )(*lefts, *rights)


def turned_kernel(left_ref, right_ref, out_ref):
    out_ref[...] = mm(left_ref[...], right_ref[...], 1, 0).T.astype(BF16)


def turned_product(left, right, tile, start=0, count=None):
    rows, depth = left.shape
    count = count or right.shape[1] // tile
    spec = pl.BlockSpec
    return pl.pallas_call(
        turned_kernel,
        grid=(count,),
        in_specs=[
            spec((rows, depth), lambda j: (0, 0)),
            spec((depth, tile), lambda j: (0, start + j)),
        ],
        out_specs=spec((tile, rows), lambda j: (j, 0)),
        out_shape=jax.ShapeDtypeStruct((count * tile, rows), BF16),
        compiler_params=pltpu.CompilerParams(vmem_limit_bytes=28 * MIB),
        cost_estimate=FREE,
        name="turned_product",
    )(left, right)


def join_kernel(*refs):
    start = 0
    for ref in refs[:-1]:
        refs[-1][:, start : start + ref.shape[1]] = ref[...].astype(BF16)
        start += ref.shape[1]


def join(*parts):
    rows = parts[0].shape[0]
    return pl.pallas_call(
        join_kernel,
        out_shape=jax.ShapeDtypeStruct((rows, sum(part.shape[1] for part in parts)), BF16),
        compiler_params=pltpu.CompilerParams(vmem_limit_bytes=63 * MIB),
        cost_estimate=FREE,
        name="join",
    )(*parts)


def halves_kernel(cut, left_ref, right_ref, low_ref, high_ref):
    low_ref[...] = left_ref[:, :cut]
    high_ref[...] = right_ref[:, cut:]


def halves(left, right, cut):
    rows, width = left.shape
    return pl.pallas_call(
        functools.partial(halves_kernel, cut),
        out_shape=[
            jax.ShapeDtypeStruct((rows, cut), left.dtype),
            jax.ShapeDtypeStruct((rows, width - cut), left.dtype),
        ],
        compiler_params=pltpu.CompilerParams(vmem_limit_bytes=63 * MIB),
        cost_estimate=FREE,
        name="halves",
    )(left, right)


def residual_kernel(part_ref, sent_ref, x_ref, gain_ref, middle_ref, b_ref):
    middle = part_ref[...].astype(F32) + sent_ref[...].astype(F32)
    middle = x_ref[...].astype(F32) + middle
    inverse = lax.rsqrt(jnp.mean(middle * middle, -1, keepdims=True) + EPSILON)
    middle_ref[...] = middle.astype(middle_ref.dtype)
    b_ref[...] = (middle * inverse * gain_ref[1:2, :]).astype(BF16)


def back_kernel(row, own_ref, sent_ref, value_ref, base_ref, gain_ref, *out_refs):
    upstream = own_ref[...].astype(F32) + sent_ref[...].astype(F32)
    value = value_ref[...].astype(F32)
    inverse = lax.rsqrt(jnp.mean(value * value, -1, keepdims=True) + EPSILON)
    scaled = upstream * gain_ref[row : row + 1, :]
    inner = jnp.mean(scaled * value, -1, keepdims=True)
    out = inverse * (scaled - value * (inverse * inverse * inner))
    out = base_ref[...].astype(F32) + out
    for ref in out_refs:
        ref[...] = out.astype(ref.dtype)


def by_rows(kernel, arrays, gain, dtypes, name):
    rows, width = arrays[0].shape
    step = 256
    block = pl.BlockSpec((step, width), lambda i: (i, 0))
    return pl.pallas_call(
        kernel,
        grid=(rows // step,),
        in_specs=[block] * len(arrays) + [pl.BlockSpec(gain.shape, lambda i: (0, 0))],
        out_specs=[block] * len(dtypes),
        out_shape=[jax.ShapeDtypeStruct((rows, width), dtype) for dtype in dtypes],
        compiler_params=pltpu.CompilerParams(vmem_limit_bytes=63 * MIB),
        cost_estimate=FREE,
        name=name,
    )(*arrays, gain)


def finish_kernel(pieces, weighted, *refs):
    parts, refs = refs[:4], refs[4:]
    weights, refs = refs[:weighted], refs[weighted:]
    outs, gain_ref, total_ref = refs[: len(pieces)], refs[-2], refs[-1]
    total_ref[...] = jnp.zeros_like(total_ref)
    for number, (out_ref, (start, size, stride, steps)) in enumerate(zip(outs, pieces)):

        @pl.loop(0, steps)
        def _(j, number=number, out_ref=out_ref, start=start, size=size, stride=stride):
            source = pl.ds(pl.multiple_of(start + j * stride, 128), size)
            target = pl.ds(pl.multiple_of(j * size, 128), size)
            total = sum(part[:, source].astype(F32) for part in parts)
            out_ref[:, target] = total
            if number < weighted:
                total = total * weights[number][:, target].astype(BF16).astype(F32)
                for k in range(0, size, 128):
                    total_ref[...] += total[:, k : k + 128]

    rows = jnp.broadcast_to(jnp.sum(total_ref[...], 1, keepdims=True), total_ref.shape)
    gain_ref[...] = rows.T[:8, :]


def finish(parts, blocks, pieces, weights):
    rows = weights[0].shape[0]
    width = parts[0].shape[1]
    spec = pl.BlockSpec
    whole = lambda i: (0, 0)
    widths = [size * steps for _, size, _, steps in pieces]
    return pl.pallas_call(
        functools.partial(finish_kernel, pieces, len(weights)),
        grid=(1,),
        in_specs=[spec((rows, width), lambda i, block=block: (block, 0)) for block in blocks]
        + [spec(weight.shape, whole) for weight in weights],
        out_specs=[spec((rows, size), whole) for size in widths] + [spec((8, rows), whole)],
        out_shape=[jax.ShapeDtypeStruct((rows, size), F32) for size in widths]
        + [jax.ShapeDtypeStruct((8, rows), F32)],
        scratch_shapes=[pltpu.VMEM((rows, 128), F32)],
        compiler_params=pltpu.CompilerParams(vmem_limit_bytes=28 * MIB),
        cost_estimate=FREE,
        name="finish",
    )(*parts, *weights)


def combine_kernel(outs, *refs):
    step = pl.program_id(0)
    inputs = list(refs[: -len(outs)])
    for out_ref, terms in zip(refs[-len(outs) :], outs):
        total = None
        for low_edge, high_edge in terms:
            value = inputs.pop(0)[...].astype(F32)
            if high_edge - low_edge < pl.num_programs(0):
                value = jnp.where((step >= low_edge) & (step < high_edge), value, 0.0)
            total = value if total is None else total + value
        out_ref[...] = total.astype(out_ref.dtype)


def combine(rows, tile, outs, dtype=BF16):
    tiles = max(high for terms in outs for *_, high in terms)
    in_specs, arrays, edges = [], [], []
    for terms in outs:
        edges.append([(low_edge, high_edge) for *_, low_edge, high_edge in terms])
        for array, block, first, low_edge, high_edge in terms:

            def place(j, block=block, first=first, low_edge=low_edge, high_edge=high_edge):
                return block, jnp.clip(j, low_edge, high_edge - 1) - low_edge + first

            in_specs.append(pl.BlockSpec((rows, tile), place))
            arrays.append(array)
    return pl.pallas_call(
        functools.partial(combine_kernel, edges),
        grid=(tiles,),
        in_specs=in_specs,
        out_specs=[pl.BlockSpec((rows, tile), lambda j: (0, j)) for _ in outs],
        out_shape=[jax.ShapeDtypeStruct((rows, tiles * tile), dtype) for _ in outs],
        compiler_params=pltpu.CompilerParams(vmem_limit_bytes=16 * MIB),
        cost_estimate=FREE,
        name="combine",
    )(*arrays)


def turn_kernel(turn_ref, own_ref, par_ref, out_ref, scr):
    own_rows, model = own_ref.shape
    step = BLOCK // 2
    for number, ref in enumerate((own_ref, par_ref)):

        @pl.loop(0, own_rows // step)
        def _(part, ref=ref, number=number):
            start = pl.multiple_of(part * step, step)
            place = pl.multiple_of(start + number * own_rows, step)
            scr[:, pl.ds(place, step)] = ref[pl.ds(start, step), :].astype(F32).T.astype(BF16)

    count = turn_ref.shape[0]
    block = model // count

    @pl.loop(0, count)
    def _(i):
        base = pl.multiple_of(turn_ref[i] * block, block)
        place = pl.multiple_of(i * block, block)
        out_ref[pl.ds(place, block), :] = scr[pl.ds(base, block), :]


def turn(turned, own, par):
    own_rows, model = own.shape
    length = 2 * own_rows
    whole = lambda i, t: (0, 0)
    spec = pl.BlockSpec
    return pl.pallas_call(
        turn_kernel,
        grid_spec=pltpu.PrefetchScalarGridSpec(
            num_scalar_prefetch=1,
            grid=(1,),
            in_specs=[spec((own_rows, model), whole)] * 2,
            out_specs=spec((model, length), whole),
            scratch_shapes=[pltpu.VMEM((model, length), BF16)],
        ),
        out_shape=jax.ShapeDtypeStruct((model, length), BF16),
        compiler_params=pltpu.CompilerParams(vmem_limit_bytes=24 * MIB),
        cost_estimate=LONG,
        name="turn",
    )(turned, own, par)


def project(blocks, turned, x_own, x_par, cos, sin, pieces, heads):
    own_rows, model = x_own.shape
    length = 2 * own_rows
    count = len(pieces)
    columns = [column for _, column in pieces]
    pieces = [piece for piece, _ in pieces]
    rows, width = pieces[0].shape
    qkv_width = 2 * heads
    tile = heads // 2
    spec = pl.BlockSpec
    whole = lambda j, s, t: (0, 0)
    anywhere = spec(memory_space=pl.ANY)
    return pl.pallas_call(
        functools.partial(project_kernel, columns, rows, heads),
        grid_spec=pltpu.PrefetchScalarGridSpec(
            num_scalar_prefetch=2,
            grid=(qkv_width // tile,),
            in_specs=[
                spec((own_rows, model), whole),
                spec((own_rows, model), whole),
                spec((HEAD_DIM // 2, length), whole),
                spec((HEAD_DIM // 2, length), whole),
            ]
            + [anywhere] * count,
            out_specs=[
                spec((tile, length), lambda j, s, t: (j, 0)),
                spec((8, model), whole),
                spec(memory_space=pltpu.MemorySpace.HBM),
                spec(memory_space=pltpu.MemorySpace.HBM),
                spec(memory_space=pltpu.MemorySpace.HBM),
            ],
            scratch_shapes=[
                pltpu.VMEM((model, width), BF16),
                pltpu.VMEM((length, model), BF16),
                pltpu.VMEM((model, length), BF16),
                pltpu.SemaphoreType.DMA((count,)),
                pltpu.SemaphoreType.DMA((2,)),
                pltpu.SemaphoreType.DMA(turned.shape),
            ],
        ),
        out_shape=[
            jax.ShapeDtypeStruct((qkv_width, length), BF16),
            jax.ShapeDtypeStruct((8, model), F32),
            jax.ShapeDtypeStruct((model, length), BF16),
            jax.ShapeDtypeStruct((model, qkv_width), BF16),
            jax.ShapeDtypeStruct((model, heads), BF16),
        ],
        compiler_params=pltpu.CompilerParams(vmem_limit_bytes=40 * MIB),
        cost_estimate=FREE,
        name="project",
    )(blocks, turned, x_own, x_par, cos, sin, *pieces)


def ffn_kernel(columns, rows, ff, block_ref, b_own, b_par, e_own, e_par, *rest):
    count = len(columns)
    pieces = rest[:count]
    hidden_ref, pair_ref, own_ref, par_ref, down_ref = rest[count : count + 5]
    b_scr, e_scr, w_scr, total, sem, save_sem = rest[count + 5 :]
    step = pl.program_id(0)
    tiles = pl.num_programs(0)
    slot = lax.rem(step, 2)
    width = hidden_ref.shape[1]
    half = b_own.shape[0]

    def fetch(number, into):
        for kind in range(3):
            for i in range(count):
                base = pl.multiple_of(block_ref[i] * rows, rows)
                column = pl.multiple_of(kind * ff + number * width, 128)
                low_edge, high_edge = columns[i], columns[i] + pieces[i].shape[1]

                def start(i=i, base=base, column=column, kind=kind):
                    pltpu.make_async_copy(
                        pieces[i].at[:, pl.ds(pl.multiple_of(column - columns[i], 128), width)],
                        w_scr.at[into, pl.ds(base, rows), kind * width : (kind + 1) * width],
                        sem.at[into],
                    ).start()

                if low_edge <= kind * ff and (kind + 1) * ff <= high_edge:
                    start()
                elif low_edge < (kind + 1) * ff and kind * ff < high_edge:
                    pl.when((column >= low_edge) & (column < high_edge))(start)

    def saved(number, source):
        column = pl.multiple_of(number * width, 128)
        return pltpu.make_async_copy(
            w_scr.at[source, :, 2 * width :], down_ref.at[:, pl.ds(column, width)], save_sem.at[source]
        )

    @pl.when(step == 0)
    def _():
        fetch(0, 0)
        for target, own, par in ((b_scr, b_own, b_par), (e_scr, e_own, e_par)):
            target[:half, :] = own[...]
            target[half:, :] = par[...]

    @pl.when(step > 0)
    def _():
        saved(step - 1, 1 - slot).wait()

    @pl.when(step + 1 < tiles)
    def _():
        fetch(step + 1, 1 - slot)

    pltpu.make_async_copy(w_scr.at[slot], w_scr.at[slot], sem.at[slot]).wait()
    saved(step, slot).start()
    first = mm(b_scr[...], w_scr[slot, :, : 2 * width], 1, 0)
    gate, up = first[:, :width], first[:, width:]
    dhid = mm(e_scr[...], w_scr[slot, :, 2 * width :], 1, 0)
    sig = 1.0 / (1.0 + jnp.exp(-gate))
    silu = gate * sig
    hidden_ref[...] = (silu * up).astype(BF16)
    dgate = (dhid * up * (sig * (1.0 + gate * (1.0 - sig)))).astype(BF16)
    dup = (dhid * silu).astype(BF16)
    pair_ref[:, :width] = dgate
    pair_ref[:, width:] = dup
    part = mm(pair_ref[...], w_scr[slot, :, : 2 * width], 1, 1)

    @pl.when(step == 0)
    def _():
        total[...] = part

    @pl.when((step > 0) & (step < tiles - 1))
    def _():
        total[...] += part

    @pl.when(step == tiles - 1)
    def _():
        own_ref[...] = (total[:half, :] + part[:half, :]).astype(BF16)
        par_ref[...] = (total[half:, :] + part[half:, :]).astype(BF16)
        saved(step, slot).wait()


def ffn(blocks, b_own, b_par, e_own, e_par, pieces):
    half, model = b_own.shape
    count = len(pieces)
    columns = [column for _, column in pieces]
    pieces = [piece for piece, _ in pieces]
    rows = pieces[0].shape[0]
    ff = max(piece.shape[1] + column for piece, column in zip(pieces, columns)) // 3
    spec = pl.BlockSpec
    whole = lambda j, s: (0, 0)
    anywhere = spec(memory_space=pl.ANY)
    once = spec((half, model), whole, pipeline_mode=pl.Buffered(1))
    return pl.pallas_call(
        functools.partial(ffn_kernel, columns, rows, ff),
        grid_spec=pltpu.PrefetchScalarGridSpec(
            num_scalar_prefetch=1,
            grid=(ff // TILE,),
            in_specs=[once] * 4 + [anywhere] * count,
            out_specs=[
                spec((2 * half, TILE), lambda j, s: (0, j)),
                spec((2 * half, 2 * TILE), lambda j, s: (0, j)),
                once,
                once,
                anywhere,
            ],
            scratch_shapes=[
                pltpu.VMEM((2 * half, model), BF16),
                pltpu.VMEM((2 * half, model), BF16),
                pltpu.VMEM((2, model, 3 * TILE), BF16),
                pltpu.VMEM((2 * half, model), F32),
                pltpu.SemaphoreType.DMA((2,)),
                pltpu.SemaphoreType.DMA((2,)),
            ],
        ),
        out_shape=[
            jax.ShapeDtypeStruct((2 * half, ff), BF16),
            jax.ShapeDtypeStruct((2 * half, 2 * ff), BF16),
            jax.ShapeDtypeStruct((half, model), BF16),
            jax.ShapeDtypeStruct((half, model), BF16),
            jax.ShapeDtypeStruct((model, ff), BF16),
        ],
        compiler_params=pltpu.CompilerParams(vmem_limit_bytes=60 * MIB),
        cost_estimate=FREE,
        name="ffn",
    )(blocks, b_own, b_par, e_own, e_par, *pieces)


def place_of(natural, side, length):
    return pl.multiple_of((natural + side * (length // 2)) & (length - 1), BLOCK)


def diagonal():
    keys = lax.broadcasted_iota(jnp.int32, (BLOCK, BLOCK), 0)
    queries = lax.broadcasted_iota(jnp.int32, (BLOCK, BLOCK), 1)
    return keys <= queries


def fill(scratch, rows, side, docs):
    length = rows.shape[1]
    half = length // 2
    scratch[HEAD_DIM:, :] = jnp.zeros((PAD_DIM - HEAD_DIM, length), BF16)
    if docs is not None:
        scratch[HEAD_DIM : HEAD_DIM + DOCS, :] = docs[...]
    for part in range(2):
        there = pl.ds(place_of(part * half, side, length), half)
        scratch[:HEAD_DIM, part * half : (part + 1) * half] = rows[:, there]


def forward_kernel(
    side_ref, q_in, k_in, v_in, oq_ref, ok_ref, *rest
):
    att_ref, lse_ref, q_scr, kt_scr, k_scr, v_scr = rest[-6:]
    length = q_in.shape[1]
    side = side_ref[0]
    blocks = length // BLOCK
    fill(kt_scr, k_in, side, ok_ref)
    fill(v_scr, v_in, side, None)
    k_scr[...] = kt_scr[...].T
    causal = diagonal()
    for h in range(2):
        rows = slice(h * HEAD_DIM, (h + 1) * HEAD_DIM)
        fill(q_scr, q_in.at[rows, :], side, oq_ref)
        for b in range(blocks):
            here = pl.ds(b * BLOCK, BLOCK)
            keys = (b + 1) * BLOCK
            query = q_scr[:, here]
            last = mm(k_scr[b * BLOCK : keys, :], query, 1, 0)
            last = jnp.where(causal, last, -FAR)
            top = jnp.max(last, 0, keepdims=True)
            if b:
                early = mm(k_scr[: b * BLOCK, :], query, 1, 0)
                top = jnp.maximum(top, jnp.max(early, 0, keepdims=True))
            top = top * (SCALE * LOG2E)
            weight = jnp.exp2(last * (SCALE * LOG2E) - top)
            total = jnp.sum(weight, 0, keepdims=True)
            out = mm(v_scr[:HEAD_DIM, b * BLOCK : keys], weight.astype(BF16), 1, 0)
            if b:
                weight = jnp.exp2(early * (SCALE * LOG2E) - top)
                total = total + jnp.sum(weight, 0, keepdims=True)
                out = out + mm(v_scr[:HEAD_DIM, : b * BLOCK], weight.astype(BF16), 1, 0)
            out = out / total
            there = pl.ds(place_of(b * BLOCK, side, length), BLOCK)
            att_ref[rows, there] = out.astype(BF16)
            lse_ref[0, h : h + 1, here] = top + jnp.log2(total)


def group_specs(groups, length):
    spec = pl.BlockSpec
    return [
        spec((2 * HEAD_DIM, length), lambda g, s: (g, 0)),
        spec((HEAD_DIM, length), lambda g, s: (2 * groups + g, 0)),
        spec((HEAD_DIM, length), lambda g, s: (3 * groups + g, 0)),
    ]


def attend(side, qkv, doc_q, doc_k):
    hidden, length = qkv.shape
    groups = hidden // (4 * HEAD_DIM)
    whole = lambda g, s: (0, 0)
    spec = pl.BlockSpec
    return pl.pallas_call(
        forward_kernel,
        grid_spec=pltpu.PrefetchScalarGridSpec(
            num_scalar_prefetch=1,
            grid=(groups,),
            in_specs=group_specs(groups, length) + [spec((DOCS, length), whole)] * 2,
            out_specs=[
                spec((2 * HEAD_DIM, length), lambda g, s: (g, 0)),
                spec((1, 2, length), lambda g, s: (g, 0, 0)),
            ],
            scratch_shapes=[
                pltpu.VMEM((PAD_DIM, length), BF16),
                pltpu.VMEM((PAD_DIM, length), BF16),
                pltpu.VMEM((length, PAD_DIM), BF16),
                pltpu.VMEM((PAD_DIM, length), BF16),
            ],
        ),
        out_shape=[
            jax.ShapeDtypeStruct((2 * groups * HEAD_DIM, length), BF16),
            jax.ShapeDtypeStruct((groups, 2, length), F32),
        ],
        compiler_params=pltpu.CompilerParams(vmem_limit_bytes=24 * MIB),
        cost_estimate=FREE,
        name="attend",
    )(side, qkv, qkv, qkv, doc_q, doc_k)


def backward_kernel(
    side_ref, q_ref, k_ref, v_ref, att_ref, datt_own, datt_par, lse_ref, cos_ref, sin_ref,
    oq_ref, ok_ref, *rest,
):
    out_ref, *rest = rest
    q_scr, kt_scr, k_scr, vt_scr, v_scr, do_scr, dk_scr, dv_scr, datt_ref, dq_ref, sem = rest
    length = q_ref.shape[1]
    group = pl.program_id(0)
    groups = out_ref.shape[0] // (4 * HEAD_DIM)
    datt_ref[:, : length // 2] = datt_own[...]
    datt_ref[:, length // 2 :] = datt_par[...]
    slot = lax.rem(group, 2)
    dk_ref = dq_ref.at[slot, 2 * HEAD_DIM : 3 * HEAD_DIM, :]
    dv_ref = dq_ref.at[slot, 3 * HEAD_DIM :, :]
    dq_ref = dq_ref.at[slot]

    def stores(number, source):
        for i, (start, size) in enumerate(((0, 2), (2, 1), (3, 1))):
            base = (start * groups + number * size) * HEAD_DIM
            yield pltpu.make_async_copy(
                rest[-2].at[source, start * HEAD_DIM : (start + size) * HEAD_DIM, :],
                out_ref.at[pl.ds(pl.multiple_of(base, HEAD_DIM), size * HEAD_DIM), :],
                sem.at[source, i],
            )

    half = HEAD_DIM // 2
    side = side_ref[0]
    blocks = length // BLOCK
    fill(kt_scr, k_ref, side, ok_ref)
    fill(vt_scr, v_ref, side, None)
    k_scr[...] = kt_scr[...].T
    v_scr[...] = vt_scr[...].T
    causal = diagonal()
    for h in range(2):
        rows = slice(h * HEAD_DIM, (h + 1) * HEAD_DIM)
        fill(q_scr, q_ref.at[rows, :], side, oq_ref)
        fill(do_scr, datt_ref.at[rows, :], side, None)
        for b in range(blocks):
            here = pl.ds(b * BLOCK, BLOCK)
            there = pl.ds(place_of(b * BLOCK, side, length), BLOCK)
            base = jnp.sum(
                datt_ref[rows, there].astype(F32) * att_ref[rows, there].astype(F32), 0, keepdims=True
            )
            keys = (b + 1) * BLOCK
            query, upstream = q_scr[:, here], do_scr[:, here]
            level = lse_ref[0, h : h + 1, here]
            dq = None
            for start, stop in ((b * BLOCK, keys), (0, b * BLOCK)):
                if start == stop:
                    continue
                span = slice(start, stop)
                score = mm(k_scr[span, :], query, 1, 0)
                prob = jnp.exp2(score * (SCALE * LOG2E) - level)
                if stop == keys:
                    prob = jnp.where(causal, prob, 0.0)
                slope = mm(v_scr[span, :], upstream, 1, 0)
                ds = (prob * (slope - base)).astype(BF16)
                part = mm(kt_scr[:HEAD_DIM, span], ds, 1, 0)
                dq = part if dq is None else dq + part
                dk = mm(query[:HEAD_DIM, :], ds, 1, 1)
                dv = mm(upstream[:HEAD_DIM, :], prob.astype(BF16), 1, 1)
                if h == 0 and stop == keys:
                    dk_scr[:, span] = dk
                    dv_scr[:, span] = dv
                else:
                    dk_scr[:, span] += dk
                    dv_scr[:, span] += dv
            cos, sin = cos_ref[:, there], sin_ref[:, there]
            dq = dq * SCALE
            top, bottom = rope_rows(dq[:half, :], dq[half:, :], cos, -sin)
            dq_ref[h * HEAD_DIM : h * HEAD_DIM + half, there] = top.astype(BF16)
            dq_ref[h * HEAD_DIM + half : (h + 1) * HEAD_DIM, there] = bottom.astype(BF16)
    for b in range(blocks):
        here = pl.ds(b * BLOCK, BLOCK)
        there = pl.ds(place_of(b * BLOCK, side, length), BLOCK)
        cos, sin = cos_ref[:, there], sin_ref[:, there]
        dk = dk_scr[:, here] * SCALE
        top, bottom = rope_rows(dk[:half, :], dk[half:, :], cos, -sin)
        dk_ref[:half, there] = top.astype(BF16)
        dk_ref[half:, there] = bottom.astype(BF16)
        dv_ref[:, there] = dv_scr[:, here].astype(BF16)
    for copy in stores(group, slot):
        copy.start()

    @pl.when(group > 0)
    def _():
        for copy in stores(group - 1, 1 - slot):
            copy.wait()

    @pl.when(group == pl.num_programs(0) - 1)
    def _():
        for copy in stores(group, slot):
            copy.wait()


def attend_back(side, qkv, att, datt, lse, cos, sin, doc_q, doc_k):
    hidden, length = qkv.shape
    groups = hidden // (4 * HEAD_DIM)
    whole = lambda g, s: (0, 0)
    spec = pl.BlockSpec
    narrow = spec((2 * HEAD_DIM, length // 2), lambda g, s: (g, 0))
    source = spec((2 * HEAD_DIM, length), lambda g, s: (g, 0))
    level = spec((1, 2, length), lambda g, s: (g, 0, 0))
    anywhere = spec(memory_space=pl.ANY)
    table = spec((HEAD_DIM // 2, length), whole)
    docs = spec((DOCS, length), whole)
    tall = pltpu.VMEM((length, PAD_DIM), BF16)
    flat = pltpu.VMEM((PAD_DIM, length), BF16)
    return pl.pallas_call(
        backward_kernel,
        grid_spec=pltpu.PrefetchScalarGridSpec(
            num_scalar_prefetch=1,
            grid=(groups,),
            in_specs=group_specs(groups, length)
            + [source, narrow, narrow, level, table, table, docs, docs],
            out_specs=anywhere,
            scratch_shapes=[flat, flat, tall, flat, tall, flat]
            + [pltpu.VMEM((HEAD_DIM, length), F32)] * 2
            + [
                pltpu.VMEM((2 * HEAD_DIM, length), BF16),
                pltpu.VMEM((2, 4 * HEAD_DIM, length), BF16),
                pltpu.SemaphoreType.DMA((2, 3)),
            ],
        ),
        out_shape=jax.ShapeDtypeStruct((hidden, length), BF16),
        compiler_params=pltpu.CompilerParams(vmem_limit_bytes=32 * MIB),
        cost_estimate=FREE,
        name="attend_back",
    )(side, qkv, qkv, qkv, att, *datt, lse, cos, sin, doc_q, doc_k)


def low(weight):
    return weight.astype(BF16)


def layer(
    dp, tokens, segment_ids, positions, query_weight, key_weight, value_weight, out_weight,
    attn_gain, gate_weight, up_weight, down_weight, mlp_gain, cotangent,
):
    seqs, own_rows, model = tokens.shape
    length = segment_ids.shape[1]
    heads = query_weight.shape[1]
    ff = gate_weight.shape[1]
    side_index = lax.axis_index("tensor").astype(jnp.int32)
    side = side_index[None]
    blocks, turned = piece_blocks(dp), turn_blocks(dp)

    x_own = tokens.reshape(own_rows, model)
    e_own = cotangent.reshape(own_rows, model)
    gains = jnp.pad(jnp.stack([low(attn_gain), low(mlp_gain)], 1), ((0, 0), (0, 126)))
    order = Order(positions[0, 0] >= 0)
    first = order.done(join(query_weight, key_weight, value_weight, out_weight.T, gains))
    first = Gather(first, dp, 1280)
    x_par = swap_halves(x_own)
    first.round(order)
    first.share(order)
    second = order.done(join(gate_weight, up_weight, down_weight.T))
    second = Gather(second, dp, 3 * ff // 2)
    for _ in range(dp // 4 - 1):
        first.next(order)
    second.share(order)
    first = first.pieces(order)
    x_first, x_par = order.done(*order.tie(x_own, x_par))
    e_par = swap_halves(order.tie(e_own))
    second.round(order)

    places = positions.reshape(length).astype(F32)
    half = HEAD_DIM // 2
    places = jnp.where(side_index == 0, places, jnp.roll(places, length // 2))
    ladder = jnp.power(F32(ROPE_BASE), -2.0 * jnp.arange(half, dtype=F32) / HEAD_DIM)
    angles = ladder[:, None] * places[None, :]
    cos, sin = jnp.cos(angles), jnp.sin(angles)
    known = jnp.arange(DOCS, dtype=jnp.int32)[:, None] == segment_ids.reshape(1, length)
    doc_q = known.astype(BF16)
    doc_k = jnp.where(known, 0.0, -FAR).astype(BF16)

    qkv, gain_rows, a_turned, qkv_full, out_full = project(
        blocks, turned, x_first, x_par, cos, sin, first, heads
    )
    qkv = order.done(qkv)
    att, lse = attend(side, order.tie(qkv), doc_q, doc_k)
    e_par, att = order.done(e_par, att)

    own, par = slice(0, own_rows), slice(own_rows, None)
    partial = order.done(mm(att[:, par], out_full, 0, 1, BF16))
    sent = swap_halves(partial)
    second.next(order)
    e_turned = order.done(turn(turned, order.tie(e_own), e_par))
    partial = order.done(mm(att[:, own], order.tie(out_full), 0, 1, BF16))
    second.next(order)
    sent = order.tie(sent)
    middle, b_own = order.done(
        *by_rows(residual_kernel, (partial, sent, x_own), gain_rows, (BF16, BF16), "residual")
    )
    b_par = swap_halves(b_own)
    second.next(order)
    second = second.pieces(order)

    b_par = order.tie(b_par)
    hidden, pair, db_own, db_par, down_full = ffn(blocks, b_own, b_par, e_own, e_par, second)
    db_par = order.done(db_par)
    db_sent = swap_halves(db_par)
    b_turned = order.done(turn(turned, order.tie(b_own), b_par))
    grad_ffn = Scatter(dp, order, (e_turned, hidden, 0), (b_turned, pair, 0))
    eh_own = order.done(
        *by_rows(
            functools.partial(back_kernel, 1),
            (db_own, order.tie(db_sent), middle, e_own),
            gain_rows,
            (BF16,),
            "norm_back",
        )
    )
    eh_par = swap_halves(eh_own)
    grad_ffn.round()
    down_own, down_par = order.done(*product(order.tie(hidden), down_full))
    grad_ffn.round()
    datt_own = order.done(turned_product(order.tie(eh_own), out_full, 384))
    eh_par = order.tie(eh_par)
    datt_par = order.done(turned_product(eh_par, out_full, 384))
    down_sent = swap_halves(order.tie(down_par))
    eh_turned = order.done(turn(turned, order.tie(eh_own), eh_par))
    grad_ffn.round()
    datt = order.tie(datt_own, datt_par)
    dqkv = order.done(attend_back(side, qkv, att, datt, lse, cos, sin, doc_q, doc_k))
    down_sent = order.done(down_sent)
    da = order.done(turned_product(qkv_full, order.tie(dqkv), own_rows))
    da_sent = swap_halves(da[par])
    grad_ffn.round()
    grad_att = Scatter(dp, order, (a_turned, dqkv, 1), (eh_turned, att, 1))
    grad_att.round()
    output = (middle.astype(F32) + (down_own.astype(F32) + order.tie(down_sent).astype(F32))).astype(BF16)
    output = order.done(output)
    grad_ffn.arrive()
    grad_att.round()
    grad_gate, grad_up, grad_down, gain_two = grad_ffn.result(
        (
            (ff, TILE, 2 * TILE, ff // TILE),
            (ff + TILE, TILE, 2 * TILE, ff // TILE),
            (0, TILE, TILE, ff // TILE),
        ),
        (gate_weight, up_weight),
    )
    da_sent = order.done(da_sent)
    grad_att.round()
    (input_grad,) = by_rows(
        functools.partial(back_kernel, 0),
        (order.tie(da[own]), da_sent, x_own, eh_own),
        gain_rows,
        (BF16,),
        "norm_back",
    )
    input_grad = order.done(input_grad)
    grad_att.round()
    kv = heads // 2
    size = kv // 3 if kv % 384 else 384
    grad_query, grad_key, grad_value, grad_out, gain_one = grad_att.result(
        (
            (0, size, size, heads // size),
            (heads, size, size, kv // size),
            (heads + kv, size, size, kv // size),
            (2 * heads, size, size, heads // size),
        ),
        (query_weight, key_weight, value_weight),
    )
    gain_grads = jnp.stack(
        [gain_one[0] / low(attn_gain).astype(F32), gain_two[0] / low(mlp_gain).astype(F32)]
    )
    gain_grads = gain_grads + swap_halves(gain_grads)
    return (
        output.reshape(seqs, own_rows, model),
        input_grad.reshape(seqs, own_rows, model),
        grad_query,
        grad_key,
        grad_value,
        grad_out.T,
        gain_grads[0],
        grad_gate,
        grad_up,
        grad_down.T,
        gain_grads[1],
    )


def solution(mesh):
    in_specs = (
        P("dp", "tensor", None),
        P("dp", None),
        P("dp", None),
        P("dp", "tensor"),
        P("dp", "tensor"),
        P("dp", "tensor"),
        P("tensor", "dp"),
        P("dp"),
        P("dp", "tensor"),
        P("dp", "tensor"),
        P("tensor", "dp"),
        P("dp"),
        P("dp", "tensor", None),
    )
    out_specs = (
        P("dp", "tensor", None),
        P("dp", "tensor", None),
        P("dp", "tensor"),
        P("dp", "tensor"),
        P("dp", "tensor"),
        P("tensor", "dp"),
        P("dp"),
        P("dp", "tensor"),
        P("dp", "tensor"),
        P("tensor", "dp"),
        P("dp"),
    )
    return jax.shard_map(
        functools.partial(layer, mesh.shape["dp"]),
        mesh=mesh,
        in_specs=in_specs,
        out_specs=out_specs,
        check_vma=False,
    )
```

```python
import functools
import math

import jax
import jax.numpy as jnp
from jax import lax
from jax.experimental import pallas as pl
from jax.experimental.pallas import tpu as pltpu
from jax.sharding import PartitionSpec as P

HEAD_DIM = 96
PAD_DIM = 128
BLOCK = 256
DOCS = 16
EPSILON = 1e-05
ROPE_BASE = 100000.0
FAR = float(2**30)
RING_LIMIT = 16
TILE = 512
MIB = 2**20
SCALE = 1.0 / math.sqrt(HEAD_DIM)
LOG2E = math.log2(math.e)

F32 = jnp.float32
BF16 = jnp.bfloat16


def mm(left, right, left_dim, right_dim, dtype=F32):
    return lax.dot_general(
        left, right, (((left_dim,), (right_dim,)), ((), ())), preferred_element_type=F32
    ).astype(dtype)


def swap_halves(value):
    return lax.ppermute(value, "tensor", [(0, 1), (1, 0)])


def is_ring(dp):
    return 8 <= dp <= RING_LIMIT and dp & (dp - 1) == 0


def chip_of(spot, chips):
    return jnp.where(2 * spot < chips, 2 * spot, 2 * (chips - 1 - spot) + 1)


def ring_pairs(dp):
    chips = dp // 2
    order = list(range(0, chips, 2)) + list(range(chips - 1, 0, -2))
    ahead = []
    for spot in range(chips):
        here, following = order[spot], order[(spot + 1) % chips]
        ahead += [(2 * here, 2 * following), (2 * here + 1, 2 * following + 1)]
    return ahead, [(b, a) for a, b in ahead]


def ring_place(dp):
    chips = dp // 2
    me = lax.axis_index("dp").astype(jnp.int32)
    chip = me >> 1
    return me & 1, jnp.where(chip & 1 == 0, chip >> 1, chips - 1 - (chip >> 1))


def piece_steps(dp):
    reach = dp // 4
    return [0, *range(-1, -reach, -1), *range(1, reach), reach, reach]


def piece_blocks(dp):
    if not is_ring(dp):
        return jnp.zeros((1,), jnp.int32)
    chips = dp // 2
    core, spot = ring_place(dp)
    chip = chip_of((spot + jnp.asarray(piece_steps(dp), jnp.int32)) & (chips - 1), chips)
    return jnp.concatenate([2 * chip + core, 2 * chip + 1 - core])


def turn_blocks(dp):
    if not is_ring(dp):
        return jnp.zeros((1,), jnp.int32)
    chips = dp // 2
    core, spot = ring_place(dp)
    chip = chip_of((spot + jnp.arange(chips, dtype=jnp.int32)) & (chips - 1), chips)
    return jnp.concatenate([2 * chip + 1 - core, 2 * chip + core])


class Order:
    def __init__(self, flag):
        self.token = lax.create_token()
        self.flag = flag

    def tie(self, *values):
        tied = lax.optimization_barrier((self.token, *values))[1:]
        return tied if len(values) > 1 else tied[0]

    def done(self, *values):
        self.token, *values = lax.optimization_barrier((self.token, *values))
        return values if len(values) > 1 else values[0]


class Gather:
    def __init__(self, shard, dp, cut):
        self.dp, self.cut = dp, cut
        self.behind, self.ahead, self.other, self.shard = [], [], [], shard

    def share(self, order):
        if not is_ring(self.dp):
            return
        found = (self.behind[-1], self.ahead[-1]) if self.other else (self.shard,)
        swap = [(i, i ^ 1) for i in range(self.dp)]

        def both(*pieces):
            return tuple(lax.ppermute(piece, "dp", swap) for piece in pieces)

        def neither(*pieces):
            return tuple(jnp.zeros_like(piece) for piece in pieces)

        found = order.tie(*found) if len(found) > 1 else (order.tie(*found),)
        got = lax.cond(order.flag, both, neither, *found)
        self.other.append(order.done(*got) if len(got) > 1 else [order.done(*got)])

    def round(self, order):
        if not is_ring(self.dp):
            return
        forth, back = ring_pairs(self.dp)
        left = self.behind[-1] if self.behind else self.shard
        right = self.ahead[-1] if self.ahead else self.shard
        left, right = order.tie(left, right)
        if len(self.behind) == self.dp // 4 - 1:
            left, right = halves(left, right, self.cut)
        left, right = order.done(left, right)
        self.behind.append(lax.ppermute(left, "dp", forth))
        self.ahead.append(lax.ppermute(right, "dp", back))

    def arrive(self, order):
        if is_ring(self.dp):
            self.behind[-1], self.ahead[-1] = order.done(self.behind[-1], self.ahead[-1])

    def next(self, order):
        if not is_ring(self.dp):
            return
        self.arrive(order)
        arrived = self.behind[-1], self.ahead[-1]
        self.round(order)
        sent = self.behind.pop(), self.ahead.pop()
        self.behind[-1], self.ahead[-1] = arrived
        self.share(order)
        self.behind.append(sent[0])
        self.ahead.append(sent[1])

    def pieces(self, order):
        if not is_ring(self.dp):
            return [(lax.all_gather(self.shard, "dp", axis=0, tiled=True), 0)]
        self.arrive(order)
        self.share(order)
        held = [self.shard, *self.behind[:-1], *self.ahead[:-1], self.behind[-1], self.ahead[-1]]
        other = [self.other[0][0], *(pair[0] for pair in self.other[1:-1])]
        other += [*(pair[1] for pair in self.other[1:-1]), *self.other[-1]]
        columns = [0] * (len(held) - 1) + [self.cut]
        return list(zip([*held, *other], columns * 2))


class Scatter:
    def __init__(self, dp, order, *columns):
        self.dp, self.order = dp, order
        lefts, rights, dims = zip(*columns)
        rights = order.tie(*rights) if len(rights) > 1 else (order.tie(*rights),)
        if not is_ring(dp):
            full = order.done(products(0, 1, lefts, rights, dims))
            self.total = lax.psum_scatter(full, "dp", scatter_dimension=0, tiled=True).astype(F32)
            return
        self.chips = dp // 2
        self.reach = self.chips // 2
        self.rows = lefts[0].shape[0] // dp

        def both(lefts, rights):
            token = lax.create_token()
            theirs = products(0, 2, lefts, rights, dims)
            token, theirs = lax.optimization_barrier((token, theirs))
            got = lax.ppermute(theirs, "dp", [(i, i ^ 1) for i in range(dp)])
            rights = lax.optimization_barrier((token, *rights))[1:]
            return got, products(1, 2, lefts, rights, dims)

        def neither(lefts, rights):
            width = sum(right.shape[1 - dim] for right, dim in zip(rights, dims))
            return (jnp.zeros((lefts[0].shape[0] // 2, width), BF16),) * 2

        self.got, self.mine = order.done(*lax.cond(order.flag, both, neither, lefts, tuple(rights)))
        self.width = self.mine.shape[1]
        self.ahead = self.behind = None

    def local(self, steps, mine, first, low_edge, high_edge):
        block = steps % self.chips
        return [(part, block, first, low_edge, high_edge) for part in (mine, self.got)]

    def round(self):
        if not is_ring(self.dp):
            return
        forth, back = ring_pairs(self.dp)
        half = self.width // 2
        tile = half if half <= 1536 else half // 2
        count = half // tile
        mine = self.order.tie(self.mine)
        reach = self.reach
        if self.ahead is None:
            right = self.local(reach, mine, 0, 0, count)
            left = self.local(reach, mine, count, 0, count)
        else:
            cut = count if self.ahead.shape[1] == half else 2 * count
            right = [*self.local(reach, mine, 0, 0, 2 * count), (self.ahead, 0, 0, 0, cut)]
            left = [*self.local(-reach, mine, 0, 0, 2 * count)]
            left.append((self.behind, 0, 0, 2 * count - cut, 2 * count))
        right, left = self.order.done(*combine(self.rows, tile, [right, left]))
        self.ahead = lax.ppermute(right, "dp", forth)
        self.behind = lax.ppermute(left, "dp", back)
        self.reach -= 1

    def arrive(self):
        if is_ring(self.dp):
            self.ahead, self.behind = self.order.done(self.ahead, self.behind)

    def result(self, pieces, weights):
        if not is_ring(self.dp):
            parts = [self.total] + [jnp.zeros_like(self.total)] * 3
        else:
            parts = [self.order.tie(self.mine), self.got, self.ahead, self.behind]
        return self.order.done(*finish(parts, [0] * 4, pieces, weights))


def rope_rows(top, bottom, cos, sin):
    return top * cos - bottom * sin, bottom * cos + top * sin


def project_kernel(columns, rows, heads, block_ref, turn_ref, own_ref, par_ref, cos_ref, sin_ref, *rest):
    count = len(columns)
    pieces = rest[:count]
    qkv_ref, gain_ref, at_ref, wide_ref, out_ref = rest[count : count + 5]
    w_scr, a_scr, at_scr, in_sem, out_sem, turn_sem = rest[count + 5 :]
    step = pl.program_id(0)
    tiles = pl.num_programs(0)
    own_rows, model = own_ref.shape
    tile = qkv_ref.shape[0]
    half = HEAD_DIM // 2
    qkv_width = 2 * heads

    def loads(i):
        base = pl.multiple_of(block_ref[i] * rows, rows)
        place = slice(columns[i], columns[i] + pieces[i].shape[1])
        return pltpu.make_async_copy(pieces[i], w_scr.at[pl.ds(base, rows), place], in_sem.at[i])

    def stores():
        return (
            pltpu.make_async_copy(w_scr.at[:, :qkv_width], wide_ref, out_sem.at[0]),
            pltpu.make_async_copy(
                w_scr.at[:, qkv_width : qkv_width + heads], out_ref, out_sem.at[1]
            ),
        )

    def turns(i):
        block = model // turn_ref.shape[0]
        base = pl.multiple_of(turn_ref[i] * block, block)
        return pltpu.make_async_copy(
            at_scr.at[pl.ds(base, block), :], at_ref.at[pl.ds(i * block, block), :], turn_sem.at[i]
        )

    @pl.when(step == 0)
    def _():
        for i in range(count):
            loads(i).start()
        for i in range(count):
            loads(i).wait()
        gains = w_scr[:, qkv_width + heads :].astype(F32).T
        gain_ref[...] = gains[:8, :]
        gain = gains[:1, :]
        for number, ref in enumerate((own_ref, par_ref)):

            @pl.loop(0, own_rows // BLOCK)
            def _(part, ref=ref, number=number):
                start = pl.multiple_of(part * BLOCK, BLOCK)
                x = ref[pl.ds(start, BLOCK), :].astype(F32)
                inverse = lax.rsqrt(jnp.mean(x * x, -1, keepdims=True) + EPSILON)
                normed = x * inverse * gain
                place = pl.multiple_of(start + number * own_rows, BLOCK)
                a_scr[pl.ds(place, BLOCK), :] = normed.astype(BF16)
                at_scr[:, pl.ds(place, BLOCK)] = normed.T.astype(BF16)

        for copy in stores():
            copy.start()
        for i in range(turn_ref.shape[0]):
            turns(i).start()

    start = pl.multiple_of(step * tile, 128)
    flat = mm(a_scr[...], w_scr[:, pl.ds(start, tile)], 1, 0).T

    @pl.when(step < tiles - tiles // 4)
    def _():
        cos, sin = cos_ref[...], sin_ref[...]
        for h in range(tile // HEAD_DIM):
            base = h * HEAD_DIM
            top, bottom = rope_rows(
                flat[base : base + half, :], flat[base + half : base + HEAD_DIM, :], cos, sin
            )
            qkv_ref[base : base + half, :] = top.astype(BF16)
            qkv_ref[base + half : base + HEAD_DIM, :] = bottom.astype(BF16)

    @pl.when(step >= tiles - tiles // 4)
    def _():
        qkv_ref[...] = flat.astype(BF16)

    @pl.when(step == tiles - 1)
    def _():
        for copy in stores():
            copy.wait()
        for i in range(turn_ref.shape[0]):
            turns(i).wait()


FREE = pl.CostEstimate(flops=0, bytes_accessed=0, transcendentals=0)
LONG = pl.CostEstimate(flops=0, bytes_accessed=40 * 2**20, transcendentals=0)


def product_kernel(left_ref, right_ref, *out_refs):
    half = left_ref.shape[0] // 2

    @pl.loop(0, 2)
    def _(part):
        start = pl.multiple_of(part * half, half)
        out = mm(left_ref[pl.ds(start, half), :], right_ref[...], 1, 1, BF16)
        for number, ref in enumerate(out_refs):

            @pl.when(part == number)
            def _(ref=ref):
                ref[...] = out


def product(left, right):
    rows, depth = left.shape
    width = right.shape[0]
    tile = next(t for t in (TILE, 384, 256, width) if width % t == 0)
    spec = pl.BlockSpec
    return pl.pallas_call(
        product_kernel,
        grid=(width // tile,),
        in_specs=[spec((rows, depth), lambda j: (0, 0)), spec((tile, depth), lambda j: (j, 0))],
        out_specs=[spec((rows // 2, tile), lambda j: (0, j))] * 2,
        out_shape=[jax.ShapeDtypeStruct((rows // 2, width), BF16)] * 2,
        compiler_params=pltpu.CompilerParams(vmem_limit_bytes=28 * MIB),
        cost_estimate=FREE,
        name="product",
    )(left, right)


def products_kernel(starts, dims, *refs):
    count = len(dims)
    out_ref = refs[-1]
    step = pl.program_id(0)
    for i, dim in enumerate(dims):

        @pl.when((step >= starts[i]) & (step < starts[i + 1]))
        def _(i=i, dim=dim):
            width = out_ref.shape[1]
            size = TILE if width % TILE == 0 else width

            @pl.loop(0, width // size)
            def _(j):
                place = pl.ds(pl.multiple_of(j * size, 128), size)
                right = refs[count + i][place, :] if dim else refs[count + i][:, place]
                out_ref[:, place] = mm(refs[i][...], right, 1, dim, out_ref.dtype)


def products(part, parts, lefts, rights, dims):
    rows, depth = lefts[0].shape
    rows = rows // parts
    widths = [right.shape[1 - dim] for right, dim in zip(rights, dims)]
    tile = next(t for t in (1024, 768, TILE, 384) if all(width % t == 0 for width in widths))
    starts = [0]
    for width in widths:
        starts.append(starts[-1] + width // tile)
    spec = pl.BlockSpec
    in_specs = [spec((rows, depth), lambda j: (part, 0)) for _ in lefts]
    for i, dim in enumerate(dims):

        def place(j, i=i):
            return jnp.clip(j - starts[i], 0, starts[i + 1] - starts[i] - 1)

        if dim:
            in_specs.append(spec((tile, depth), lambda j, place=place: (place(j), 0)))
        else:
            in_specs.append(spec((depth, tile), lambda j, place=place: (0, place(j))))
    return pl.pallas_call(
        functools.partial(products_kernel, starts, dims),
        grid=(starts[-1],),
        in_specs=in_specs,
        out_specs=spec((rows, tile), lambda j: (0, j)),
        out_shape=jax.ShapeDtypeStruct((rows, sum(widths)), BF16),
        compiler_params=pltpu.CompilerParams(vmem_limit_bytes=32 * MIB),
        cost_estimate=FREE,
        name="products",
    )(*lefts, *rights)


def turned_kernel(left_ref, right_ref, out_ref):
    out_ref[...] = mm(left_ref[...], right_ref[...], 1, 0).T.astype(BF16)


def turned_product(left, right, tile, start=0, count=None):
    rows, depth = left.shape
    count = count or right.shape[1] // tile
    spec = pl.BlockSpec
    return pl.pallas_call(
        turned_kernel,
        grid=(count,),
        in_specs=[
            spec((rows, depth), lambda j: (0, 0)),
            spec((depth, tile), lambda j: (0, start + j)),
        ],
        out_specs=spec((tile, rows), lambda j: (j, 0)),
        out_shape=jax.ShapeDtypeStruct((count * tile, rows), BF16),
        compiler_params=pltpu.CompilerParams(vmem_limit_bytes=28 * MIB),
        cost_estimate=FREE,
        name="turned_product",
    )(left, right)


def join_kernel(*refs):
    start = 0
    for ref in refs[:-1]:
        refs[-1][:, start : start + ref.shape[1]] = ref[...].astype(BF16)
        start += ref.shape[1]


def join(*parts):
    rows = parts[0].shape[0]
    return pl.pallas_call(
        join_kernel,
        out_shape=jax.ShapeDtypeStruct((rows, sum(part.shape[1] for part in parts)), BF16),
        compiler_params=pltpu.CompilerParams(vmem_limit_bytes=63 * MIB),
        cost_estimate=FREE,
        name="join",
    )(*parts)


def halves_kernel(cut, left_ref, right_ref, low_ref, high_ref):
    low_ref[...] = left_ref[:, :cut]
    high_ref[...] = right_ref[:, cut:]


def halves(left, right, cut):
    rows, width = left.shape
    return pl.pallas_call(
        functools.partial(halves_kernel, cut),
        out_shape=[
            jax.ShapeDtypeStruct((rows, cut), left.dtype),
            jax.ShapeDtypeStruct((rows, width - cut), left.dtype),
        ],
        compiler_params=pltpu.CompilerParams(vmem_limit_bytes=63 * MIB),
        cost_estimate=FREE,
        name="halves",
    )(left, right)


def residual_kernel(part_ref, sent_ref, x_ref, gain_ref, middle_ref, b_ref):
    middle = part_ref[...].astype(F32) + sent_ref[...].astype(F32)
    middle = x_ref[...].astype(F32) + middle
    inverse = lax.rsqrt(jnp.mean(middle * middle, -1, keepdims=True) + EPSILON)
    middle_ref[...] = middle.astype(middle_ref.dtype)
    b_ref[...] = (middle * inverse * gain_ref[1:2, :]).astype(BF16)


def back_kernel(row, own_ref, sent_ref, value_ref, base_ref, gain_ref, *out_refs):
    upstream = own_ref[...].astype(F32) + sent_ref[...].astype(F32)
    value = value_ref[...].astype(F32)
    inverse = lax.rsqrt(jnp.mean(value * value, -1, keepdims=True) + EPSILON)
    scaled = upstream * gain_ref[row : row + 1, :]
    inner = jnp.mean(scaled * value, -1, keepdims=True)
    out = inverse * (scaled - value * (inverse * inverse * inner))
    out = base_ref[...].astype(F32) + out
    for ref in out_refs:
        ref[...] = out.astype(ref.dtype)


def by_rows(kernel, arrays, gain, dtypes, name):
    rows, width = arrays[0].shape
    step = 256
    block = pl.BlockSpec((step, width), lambda i: (i, 0))
    return pl.pallas_call(
        kernel,
        grid=(rows // step,),
        in_specs=[block] * len(arrays) + [pl.BlockSpec(gain.shape, lambda i: (0, 0))],
        out_specs=[block] * len(dtypes),
        out_shape=[jax.ShapeDtypeStruct((rows, width), dtype) for dtype in dtypes],
        compiler_params=pltpu.CompilerParams(vmem_limit_bytes=63 * MIB),
        cost_estimate=FREE,
        name=name,
    )(*arrays, gain)


def finish_kernel(pieces, weighted, *refs):
    parts, refs = refs[:4], refs[4:]
    weights, refs = refs[:weighted], refs[weighted:]
    outs, gain_ref, total_ref = refs[: len(pieces)], refs[-2], refs[-1]
    total_ref[...] = jnp.zeros_like(total_ref)
    for number, (out_ref, (start, size, stride, steps)) in enumerate(zip(outs, pieces)):

        @pl.loop(0, steps)
        def _(j, number=number, out_ref=out_ref, start=start, size=size, stride=stride):
            source = pl.ds(pl.multiple_of(start + j * stride, 128), size)
            target = pl.ds(pl.multiple_of(j * size, 128), size)
            total = sum(part[:, source].astype(F32) for part in parts)
            out_ref[:, target] = total
            if number < weighted:
                total = total * weights[number][:, target].astype(BF16).astype(F32)
                for k in range(0, size, 128):
                    total_ref[...] += total[:, k : k + 128]

    rows = jnp.broadcast_to(jnp.sum(total_ref[...], 1, keepdims=True), total_ref.shape)
    gain_ref[...] = rows.T[:8, :]


def finish(parts, blocks, pieces, weights):
    rows = weights[0].shape[0]
    width = parts[0].shape[1]
    spec = pl.BlockSpec
    whole = lambda i: (0, 0)
    widths = [size * steps for _, size, _, steps in pieces]
    return pl.pallas_call(
        functools.partial(finish_kernel, pieces, len(weights)),
        grid=(1,),
        in_specs=[spec((rows, width), lambda i, block=block: (block, 0)) for block in blocks]
        + [spec(weight.shape, whole) for weight in weights],
        out_specs=[spec((rows, size), whole) for size in widths] + [spec((8, rows), whole)],
        out_shape=[jax.ShapeDtypeStruct((rows, size), F32) for size in widths]
        + [jax.ShapeDtypeStruct((8, rows), F32)],
        scratch_shapes=[pltpu.VMEM((rows, 128), F32)],
        compiler_params=pltpu.CompilerParams(vmem_limit_bytes=28 * MIB),
        cost_estimate=FREE,
        name="finish",
    )(*parts, *weights)


def combine_kernel(outs, *refs):
    step = pl.program_id(0)
    inputs = list(refs[: -len(outs)])
    for out_ref, terms in zip(refs[-len(outs) :], outs):
        total = None
        for low_edge, high_edge in terms:
            value = inputs.pop(0)[...].astype(F32)
            if high_edge - low_edge < pl.num_programs(0):
                value = jnp.where((step >= low_edge) & (step < high_edge), value, 0.0)
            total = value if total is None else total + value
        out_ref[...] = total.astype(out_ref.dtype)


def combine(rows, tile, outs, dtype=BF16):
    tiles = max(high for terms in outs for *_, high in terms)
    in_specs, arrays, edges = [], [], []
    for terms in outs:
        edges.append([(low_edge, high_edge) for *_, low_edge, high_edge in terms])
        for array, block, first, low_edge, high_edge in terms:

            def place(j, block=block, first=first, low_edge=low_edge, high_edge=high_edge):
                return block, jnp.clip(j, low_edge, high_edge - 1) - low_edge + first

            in_specs.append(pl.BlockSpec((rows, tile), place))
            arrays.append(array)
    return pl.pallas_call(
        functools.partial(combine_kernel, edges),
        grid=(tiles,),
        in_specs=in_specs,
        out_specs=[pl.BlockSpec((rows, tile), lambda j: (0, j)) for _ in outs],
        out_shape=[jax.ShapeDtypeStruct((rows, tiles * tile), dtype) for _ in outs],
        compiler_params=pltpu.CompilerParams(vmem_limit_bytes=16 * MIB),
        cost_estimate=FREE,
        name="combine",
    )(*arrays)


def turn_kernel(turn_ref, own_ref, par_ref, out_ref, scr):
    own_rows, model = own_ref.shape
    step = BLOCK // 2
    for number, ref in enumerate((own_ref, par_ref)):

        @pl.loop(0, own_rows // step)
        def _(part, ref=ref, number=number):
            start = pl.multiple_of(part * step, step)
            place = pl.multiple_of(start + number * own_rows, step)
            scr[:, pl.ds(place, step)] = ref[pl.ds(start, step), :].astype(F32).T.astype(BF16)

    count = turn_ref.shape[0]
    block = model // count

    @pl.loop(0, count)
    def _(i):
        base = pl.multiple_of(turn_ref[i] * block, block)
        place = pl.multiple_of(i * block, block)
        out_ref[pl.ds(place, block), :] = scr[pl.ds(base, block), :]


def turn(turned, own, par):
    own_rows, model = own.shape
    length = 2 * own_rows
    whole = lambda i, t: (0, 0)
    spec = pl.BlockSpec
    return pl.pallas_call(
        turn_kernel,
        grid_spec=pltpu.PrefetchScalarGridSpec(
            num_scalar_prefetch=1,
            grid=(1,),
            in_specs=[spec((own_rows, model), whole)] * 2,
            out_specs=spec((model, length), whole),
            scratch_shapes=[pltpu.VMEM((model, length), BF16)],
        ),
        out_shape=jax.ShapeDtypeStruct((model, length), BF16),
        compiler_params=pltpu.CompilerParams(vmem_limit_bytes=24 * MIB),
        cost_estimate=LONG,
        name="turn",
    )(turned, own, par)


def project(blocks, turned, x_own, x_par, cos, sin, pieces, heads):
    own_rows, model = x_own.shape
    length = 2 * own_rows
    count = len(pieces)
    columns = [column for _, column in pieces]
    pieces = [piece for piece, _ in pieces]
    rows, width = pieces[0].shape
    qkv_width = 2 * heads
    tile = heads // 2
    spec = pl.BlockSpec
    whole = lambda j, s, t: (0, 0)
    anywhere = spec(memory_space=pl.ANY)
    return pl.pallas_call(
        functools.partial(project_kernel, columns, rows, heads),
        grid_spec=pltpu.PrefetchScalarGridSpec(
            num_scalar_prefetch=2,
            grid=(qkv_width // tile,),
            in_specs=[
                spec((own_rows, model), whole),
                spec((own_rows, model), whole),
                spec((HEAD_DIM // 2, length), whole),
                spec((HEAD_DIM // 2, length), whole),
            ]
            + [anywhere] * count,
            out_specs=[
                spec((tile, length), lambda j, s, t: (j, 0)),
                spec((8, model), whole),
                spec(memory_space=pltpu.MemorySpace.HBM),
                spec(memory_space=pltpu.MemorySpace.HBM),
                spec(memory_space=pltpu.MemorySpace.HBM),
            ],
            scratch_shapes=[
                pltpu.VMEM((model, width), BF16),
                pltpu.VMEM((length, model), BF16),
                pltpu.VMEM((model, length), BF16),
                pltpu.SemaphoreType.DMA((count,)),
                pltpu.SemaphoreType.DMA((2,)),
                pltpu.SemaphoreType.DMA(turned.shape),
            ],
        ),
        out_shape=[
            jax.ShapeDtypeStruct((qkv_width, length), BF16),
            jax.ShapeDtypeStruct((8, model), F32),
            jax.ShapeDtypeStruct((model, length), BF16),
            jax.ShapeDtypeStruct((model, qkv_width), BF16),
            jax.ShapeDtypeStruct((model, heads), BF16),
        ],
        compiler_params=pltpu.CompilerParams(vmem_limit_bytes=40 * MIB),
        cost_estimate=FREE,
        name="project",
    )(blocks, turned, x_own, x_par, cos, sin, *pieces)


def ffn_kernel(columns, rows, ff, block_ref, b_own, b_par, e_own, e_par, *rest):
    count = len(columns)
    pieces = rest[:count]
    hidden_ref, pair_ref, own_ref, par_ref, down_ref = rest[count : count + 5]
    b_scr, e_scr, w_scr, total, sem, save_sem = rest[count + 5 :]
    step = pl.program_id(0)
    tiles = pl.num_programs(0)
    slot = lax.rem(step, 2)
    width = hidden_ref.shape[1]
    half = b_own.shape[0]

    def fetch(number, into):
        for kind in range(3):
            for i in range(count):
                base = pl.multiple_of(block_ref[i] * rows, rows)
                column = pl.multiple_of(kind * ff + number * width, 128)
                low_edge, high_edge = columns[i], columns[i] + pieces[i].shape[1]

                def start(i=i, base=base, column=column, kind=kind):
                    pltpu.make_async_copy(
                        pieces[i].at[:, pl.ds(pl.multiple_of(column - columns[i], 128), width)],
                        w_scr.at[into, pl.ds(base, rows), kind * width : (kind + 1) * width],
                        sem.at[into],
                    ).start()

                if low_edge <= kind * ff and (kind + 1) * ff <= high_edge:
                    start()
                elif low_edge < (kind + 1) * ff and kind * ff < high_edge:
                    pl.when((column >= low_edge) & (column < high_edge))(start)

    def saved(number, source):
        column = pl.multiple_of(number * width, 128)
        return pltpu.make_async_copy(
            w_scr.at[source, :, 2 * width :], down_ref.at[:, pl.ds(column, width)], save_sem.at[source]
        )

    @pl.when(step == 0)
    def _():
        fetch(0, 0)
        for target, own, par in ((b_scr, b_own, b_par), (e_scr, e_own, e_par)):
            target[:half, :] = own[...]
            target[half:, :] = par[...]

    @pl.when(step > 0)
    def _():
        saved(step - 1, 1 - slot).wait()

    @pl.when(step + 1 < tiles)
    def _():
        fetch(step + 1, 1 - slot)

    pltpu.make_async_copy(w_scr.at[slot], w_scr.at[slot], sem.at[slot]).wait()
    saved(step, slot).start()
    first = mm(b_scr[...], w_scr[slot, :, : 2 * width], 1, 0)
    gate, up = first[:, :width], first[:, width:]
    dhid = mm(e_scr[...], w_scr[slot, :, 2 * width :], 1, 0)
    sig = 1.0 / (1.0 + jnp.exp(-gate))
    silu = gate * sig
    hidden_ref[...] = (silu * up).astype(BF16)
    dgate = (dhid * up * (sig * (1.0 + gate * (1.0 - sig)))).astype(BF16)
    dup = (dhid * silu).astype(BF16)
    pair_ref[:, :width] = dgate
    pair_ref[:, width:] = dup
    part = mm(pair_ref[...], w_scr[slot, :, : 2 * width], 1, 1)

    @pl.when(step == 0)
    def _():
        total[...] = part

    @pl.when((step > 0) & (step < tiles - 1))
    def _():
        total[...] += part

    @pl.when(step == tiles - 1)
    def _():
        own_ref[...] = (total[:half, :] + part[:half, :]).astype(BF16)
        par_ref[...] = (total[half:, :] + part[half:, :]).astype(BF16)
        saved(step, slot).wait()


def ffn(blocks, b_own, b_par, e_own, e_par, pieces):
    half, model = b_own.shape
    count = len(pieces)
    columns = [column for _, column in pieces]
    pieces = [piece for piece, _ in pieces]
    rows = pieces[0].shape[0]
    ff = max(piece.shape[1] + column for piece, column in zip(pieces, columns)) // 3
    spec = pl.BlockSpec
    whole = lambda j, s: (0, 0)
    anywhere = spec(memory_space=pl.ANY)
    once = spec((half, model), whole, pipeline_mode=pl.Buffered(1))
    return pl.pallas_call(
        functools.partial(ffn_kernel, columns, rows, ff),
        grid_spec=pltpu.PrefetchScalarGridSpec(
            num_scalar_prefetch=1,
            grid=(ff // TILE,),
            in_specs=[once] * 4 + [anywhere] * count,
            out_specs=[
                spec((2 * half, TILE), lambda j, s: (0, j)),
                spec((2 * half, 2 * TILE), lambda j, s: (0, j)),
                once,
                once,
                anywhere,
            ],
            scratch_shapes=[
                pltpu.VMEM((2 * half, model), BF16),
                pltpu.VMEM((2 * half, model), BF16),
                pltpu.VMEM((2, model, 3 * TILE), BF16),
                pltpu.VMEM((2 * half, model), F32),
                pltpu.SemaphoreType.DMA((2,)),
                pltpu.SemaphoreType.DMA((2,)),
            ],
        ),
        out_shape=[
            jax.ShapeDtypeStruct((2 * half, ff), BF16),
            jax.ShapeDtypeStruct((2 * half, 2 * ff), BF16),
            jax.ShapeDtypeStruct((half, model), BF16),
            jax.ShapeDtypeStruct((half, model), BF16),
            jax.ShapeDtypeStruct((model, ff), BF16),
        ],
        compiler_params=pltpu.CompilerParams(vmem_limit_bytes=60 * MIB),
        cost_estimate=FREE,
        name="ffn",
    )(blocks, b_own, b_par, e_own, e_par, *pieces)


def place_of(natural, side, length):
    return pl.multiple_of((natural + side * (length // 2)) & (length - 1), BLOCK)


def diagonal():
    keys = lax.broadcasted_iota(jnp.int32, (BLOCK, BLOCK), 0)
    queries = lax.broadcasted_iota(jnp.int32, (BLOCK, BLOCK), 1)
    return keys <= queries


def fill(scratch, rows, side, docs):
    length = rows.shape[1]
    half = length // 2
    scratch[HEAD_DIM:, :] = jnp.zeros((PAD_DIM - HEAD_DIM, length), BF16)
    if docs is not None:
        scratch[HEAD_DIM : HEAD_DIM + DOCS, :] = docs[...]
    for part in range(2):
        there = pl.ds(place_of(part * half, side, length), half)
        scratch[:HEAD_DIM, part * half : (part + 1) * half] = rows[:, there]


def forward_kernel(
    side_ref, q_in, k_in, v_in, oq_ref, ok_ref, *rest
):
    att_ref, lse_ref, q_scr, kt_scr, k_scr, v_scr = rest[-6:]
    length = q_in.shape[1]
    side = side_ref[0]
    blocks = length // BLOCK
    fill(kt_scr, k_in, side, ok_ref)
    fill(v_scr, v_in, side, None)
    k_scr[...] = kt_scr[...].T
    causal = diagonal()
    for h in range(2):
        rows = slice(h * HEAD_DIM, (h + 1) * HEAD_DIM)
        fill(q_scr, q_in.at[rows, :], side, oq_ref)
        for b in range(blocks):
            here = pl.ds(b * BLOCK, BLOCK)
            keys = (b + 1) * BLOCK
            query = q_scr[:, here]
            last = mm(k_scr[b * BLOCK : keys, :], query, 1, 0)
            last = jnp.where(causal, last, -FAR)
            top = jnp.max(last, 0, keepdims=True)
            if b:
                early = mm(k_scr[: b * BLOCK, :], query, 1, 0)
                top = jnp.maximum(top, jnp.max(early, 0, keepdims=True))
            top = top * (SCALE * LOG2E)
            weight = jnp.exp2(last * (SCALE * LOG2E) - top)
            total = jnp.sum(weight, 0, keepdims=True)
            out = mm(v_scr[:HEAD_DIM, b * BLOCK : keys], weight.astype(BF16), 1, 0)
            if b:
                weight = jnp.exp2(early * (SCALE * LOG2E) - top)
                total = total + jnp.sum(weight, 0, keepdims=True)
                out = out + mm(v_scr[:HEAD_DIM, : b * BLOCK], weight.astype(BF16), 1, 0)
            out = out / total
            there = pl.ds(place_of(b * BLOCK, side, length), BLOCK)
            att_ref[rows, there] = out.astype(BF16)
            lse_ref[0, h : h + 1, here] = top + jnp.log2(total)


def group_specs(groups, length):
    spec = pl.BlockSpec
    return [
        spec((2 * HEAD_DIM, length), lambda g, s: (g, 0)),
        spec((HEAD_DIM, length), lambda g, s: (2 * groups + g, 0)),
        spec((HEAD_DIM, length), lambda g, s: (3 * groups + g, 0)),
    ]


def attend(side, qkv, doc_q, doc_k):
    hidden, length = qkv.shape
    groups = hidden // (4 * HEAD_DIM)
    whole = lambda g, s: (0, 0)
    spec = pl.BlockSpec
    return pl.pallas_call(
        forward_kernel,
        grid_spec=pltpu.PrefetchScalarGridSpec(
            num_scalar_prefetch=1,
            grid=(groups,),
            in_specs=group_specs(groups, length) + [spec((DOCS, length), whole)] * 2,
            out_specs=[
                spec((2 * HEAD_DIM, length), lambda g, s: (g, 0)),
                spec((1, 2, length), lambda g, s: (g, 0, 0)),
            ],
            scratch_shapes=[
                pltpu.VMEM((PAD_DIM, length), BF16),
                pltpu.VMEM((PAD_DIM, length), BF16),
                pltpu.VMEM((length, PAD_DIM), BF16),
                pltpu.VMEM((PAD_DIM, length), BF16),
            ],
        ),
        out_shape=[
            jax.ShapeDtypeStruct((2 * groups * HEAD_DIM, length), BF16),
            jax.ShapeDtypeStruct((groups, 2, length), F32),
        ],
        compiler_params=pltpu.CompilerParams(vmem_limit_bytes=24 * MIB),
        cost_estimate=FREE,
        name="attend",
    )(side, qkv, qkv, qkv, doc_q, doc_k)


def backward_kernel(
    side_ref, q_ref, k_ref, v_ref, att_ref, datt_own, datt_par, lse_ref, cos_ref, sin_ref,
    oq_ref, ok_ref, *rest,
):
    out_ref, *rest = rest
    q_scr, kt_scr, k_scr, vt_scr, v_scr, do_scr, dk_scr, dv_scr, datt_ref, dq_ref, sem = rest
    length = q_ref.shape[1]
    group = pl.program_id(0)
    groups = out_ref.shape[0] // (4 * HEAD_DIM)
    datt_ref[:, : length // 2] = datt_own[...]
    datt_ref[:, length // 2 :] = datt_par[...]
    slot = lax.rem(group, 2)
    dk_ref = dq_ref.at[slot, 2 * HEAD_DIM : 3 * HEAD_DIM, :]
    dv_ref = dq_ref.at[slot, 3 * HEAD_DIM :, :]
    dq_ref = dq_ref.at[slot]

    def stores(number, source):
        for i, (start, size) in enumerate(((0, 2), (2, 1), (3, 1))):
            base = (start * groups + number * size) * HEAD_DIM
            yield pltpu.make_async_copy(
                rest[-2].at[source, start * HEAD_DIM : (start + size) * HEAD_DIM, :],
                out_ref.at[pl.ds(pl.multiple_of(base, HEAD_DIM), size * HEAD_DIM), :],
                sem.at[source, i],
            )

    half = HEAD_DIM // 2
    side = side_ref[0]
    blocks = length // BLOCK
    fill(kt_scr, k_ref, side, ok_ref)
    fill(vt_scr, v_ref, side, None)
    k_scr[...] = kt_scr[...].T
    v_scr[...] = vt_scr[...].T
    causal = diagonal()
    for h in range(2):
        rows = slice(h * HEAD_DIM, (h + 1) * HEAD_DIM)
        fill(q_scr, q_ref.at[rows, :], side, oq_ref)
        fill(do_scr, datt_ref.at[rows, :], side, None)
        for b in range(blocks):
            here = pl.ds(b * BLOCK, BLOCK)
            there = pl.ds(place_of(b * BLOCK, side, length), BLOCK)
            base = jnp.sum(
                datt_ref[rows, there].astype(F32) * att_ref[rows, there].astype(F32), 0, keepdims=True
            )
            keys = (b + 1) * BLOCK
            query, upstream = q_scr[:, here], do_scr[:, here]
            level = lse_ref[0, h : h + 1, here]
            dq = None
            for start, stop in ((b * BLOCK, keys), (0, b * BLOCK)):
                if start == stop:
                    continue
                span = slice(start, stop)
                score = mm(k_scr[span, :], query, 1, 0)
                prob = jnp.exp2(score * (SCALE * LOG2E) - level)
                if stop == keys:
                    prob = jnp.where(causal, prob, 0.0)
                slope = mm(v_scr[span, :], upstream, 1, 0)
                ds = (prob * (slope - base)).astype(BF16)
                part = mm(kt_scr[:HEAD_DIM, span], ds, 1, 0)
                dq = part if dq is None else dq + part
                dk = mm(query[:HEAD_DIM, :], ds, 1, 1)
                dv = mm(upstream[:HEAD_DIM, :], prob.astype(BF16), 1, 1)
                if h == 0 and stop == keys:
                    dk_scr[:, span] = dk
                    dv_scr[:, span] = dv
                else:
                    dk_scr[:, span] += dk
                    dv_scr[:, span] += dv
            cos, sin = cos_ref[:, there], sin_ref[:, there]
            dq = dq * SCALE
            top, bottom = rope_rows(dq[:half, :], dq[half:, :], cos, -sin)
            dq_ref[h * HEAD_DIM : h * HEAD_DIM + half, there] = top.astype(BF16)
            dq_ref[h * HEAD_DIM + half : (h + 1) * HEAD_DIM, there] = bottom.astype(BF16)
    for b in range(blocks):
        here = pl.ds(b * BLOCK, BLOCK)
        there = pl.ds(place_of(b * BLOCK, side, length), BLOCK)
        cos, sin = cos_ref[:, there], sin_ref[:, there]
        dk = dk_scr[:, here] * SCALE
        top, bottom = rope_rows(dk[:half, :], dk[half:, :], cos, -sin)
        dk_ref[:half, there] = top.astype(BF16)
        dk_ref[half:, there] = bottom.astype(BF16)
        dv_ref[:, there] = dv_scr[:, here].astype(BF16)
    for copy in stores(group, slot):
        copy.start()

    @pl.when(group > 0)
    def _():
        for copy in stores(group - 1, 1 - slot):
            copy.wait()

    @pl.when(group == pl.num_programs(0) - 1)
    def _():
        for copy in stores(group, slot):
            copy.wait()


def attend_back(side, qkv, att, datt, lse, cos, sin, doc_q, doc_k):
    hidden, length = qkv.shape
    groups = hidden // (4 * HEAD_DIM)
    whole = lambda g, s: (0, 0)
    spec = pl.BlockSpec
    narrow = spec((2 * HEAD_DIM, length // 2), lambda g, s: (g, 0))
    source = spec((2 * HEAD_DIM, length), lambda g, s: (g, 0))
    level = spec((1, 2, length), lambda g, s: (g, 0, 0))
    anywhere = spec(memory_space=pl.ANY)
    table = spec((HEAD_DIM // 2, length), whole)
    docs = spec((DOCS, length), whole)
    tall = pltpu.VMEM((length, PAD_DIM), BF16)
    flat = pltpu.VMEM((PAD_DIM, length), BF16)
    return pl.pallas_call(
        backward_kernel,
        grid_spec=pltpu.PrefetchScalarGridSpec(
            num_scalar_prefetch=1,
            grid=(groups,),
            in_specs=group_specs(groups, length)
            + [source, narrow, narrow, level, table, table, docs, docs],
            out_specs=anywhere,
            scratch_shapes=[flat, flat, tall, flat, tall, flat]
            + [pltpu.VMEM((HEAD_DIM, length), F32)] * 2
            + [
                pltpu.VMEM((2 * HEAD_DIM, length), BF16),
                pltpu.VMEM((2, 4 * HEAD_DIM, length), BF16),
                pltpu.SemaphoreType.DMA((2, 3)),
            ],
        ),
        out_shape=jax.ShapeDtypeStruct((hidden, length), BF16),
        compiler_params=pltpu.CompilerParams(vmem_limit_bytes=32 * MIB),
        cost_estimate=FREE,
        name="attend_back",
    )(side, qkv, qkv, qkv, att, *datt, lse, cos, sin, doc_q, doc_k)


def low(weight):
    return weight.astype(BF16)


def layer(
    dp, tokens, segment_ids, positions, query_weight, key_weight, value_weight, out_weight,
    attn_gain, gate_weight, up_weight, down_weight, mlp_gain, cotangent,
):
    seqs, own_rows, model = tokens.shape
    length = segment_ids.shape[1]
    heads = query_weight.shape[1]
    ff = gate_weight.shape[1]
    side_index = lax.axis_index("tensor").astype(jnp.int32)
    side = side_index[None]
    blocks, turned = piece_blocks(dp), turn_blocks(dp)

    x_own = tokens.reshape(own_rows, model)
    e_own = cotangent.reshape(own_rows, model)
    gains = jnp.pad(jnp.stack([low(attn_gain), low(mlp_gain)], 1), ((0, 0), (0, 126)))
    order = Order(positions[0, 0] >= 0)
    first = order.done(join(query_weight, key_weight, value_weight, out_weight.T, gains))
    first = Gather(first, dp, 1280)
    x_par = swap_halves(x_own)
    first.round(order)
    first.share(order)
    places = positions.reshape(length).astype(F32)
    half = HEAD_DIM // 2
    places = jnp.where(side_index == 0, places, jnp.roll(places, length // 2))
    ladder = jnp.power(F32(ROPE_BASE), -2.0 * jnp.arange(half, dtype=F32) / HEAD_DIM)
    angles = ladder[:, None] * places[None, :]
    cos, sin = jnp.cos(angles), jnp.sin(angles)
    cos, sin = order.done(cos, sin)
    second = order.done(join(gate_weight, up_weight, down_weight.T))
    second = Gather(second, dp, 3 * ff // 2)
    for _ in range(dp // 4 - 1):
        first.next(order)
    second.share(order)
    first = first.pieces(order)
    x_first, x_par = order.done(*order.tie(x_own, x_par))
    e_par = swap_halves(order.tie(e_own))
    second.round(order)

    known = jnp.arange(DOCS, dtype=jnp.int32)[:, None] == segment_ids.reshape(1, length)
    doc_q = known.astype(BF16)
    doc_k = jnp.where(known, 0.0, -FAR).astype(BF16)

    qkv, gain_rows, a_turned, qkv_full, out_full = project(
        blocks, turned, x_first, x_par, cos, sin, first, heads
    )
    qkv = order.done(qkv)
    att, lse = attend(side, order.tie(qkv), doc_q, doc_k)
    e_par, att = order.done(e_par, att)

    own, par = slice(0, own_rows), slice(own_rows, None)
    partial = order.done(mm(att[:, par], out_full, 0, 1, BF16))
    sent = swap_halves(partial)
    second.next(order)
    e_turned = order.done(turn(turned, order.tie(e_own), e_par))
    partial = order.done(mm(att[:, own], order.tie(out_full), 0, 1, BF16))
    second.next(order)
    sent = order.tie(sent)
    middle, b_own = order.done(
        *by_rows(residual_kernel, (partial, sent, x_own), gain_rows, (BF16, BF16), "residual")
    )
    b_par = swap_halves(b_own)
    second.next(order)
    second = second.pieces(order)

    b_par = order.tie(b_par)
    hidden, pair, db_own, db_par, down_full = ffn(blocks, b_own, b_par, e_own, e_par, second)
    db_par = order.done(db_par)
    db_sent = swap_halves(db_par)
    b_turned = order.done(turn(turned, order.tie(b_own), b_par))
    grad_ffn = Scatter(dp, order, (e_turned, hidden, 0), (b_turned, pair, 0))
    eh_own = order.done(
        *by_rows(
            functools.partial(back_kernel, 1),
            (db_own, order.tie(db_sent), middle, e_own),
            gain_rows,
            (BF16,),
            "norm_back",
        )
    )
    eh_par = swap_halves(eh_own)
    grad_ffn.round()
    down_own, down_par = order.done(*product(order.tie(hidden), down_full))
    grad_ffn.round()
    datt_own = order.done(turned_product(order.tie(eh_own), out_full, 384))
    eh_par = order.tie(eh_par)
    datt_par = order.done(turned_product(eh_par, out_full, 384))
    down_sent = swap_halves(order.tie(down_par))
    eh_turned = order.done(turn(turned, order.tie(eh_own), eh_par))
    grad_ffn.round()
    datt = order.tie(datt_own, datt_par)
    dqkv = order.done(attend_back(side, qkv, att, datt, lse, cos, sin, doc_q, doc_k))
    down_sent = order.done(down_sent)
    da_par = order.done(turned_product(qkv_full, order.tie(dqkv), own_rows, 1, 1))
    da_sent = swap_halves(da_par)
    grad_ffn.round()
    grad_att = Scatter(dp, order, (a_turned, dqkv, 1), (eh_turned, att, 1))
    grad_att.round()
    output = (middle.astype(F32) + (down_own.astype(F32) + order.tie(down_sent).astype(F32))).astype(BF16)
    output = order.done(output)
    da_own = order.done(turned_product(qkv_full, order.tie(dqkv), own_rows, 0, 1))
    grad_ffn.arrive()
    grad_att.round()
    grad_gate, grad_up, grad_down, gain_two = grad_ffn.result(
        (
            (ff, TILE, 2 * TILE, ff // TILE),
            (ff + TILE, TILE, 2 * TILE, ff // TILE),
            (0, TILE, TILE, ff // TILE),
        ),
        (gate_weight, up_weight),
    )
    da_sent = order.done(da_sent)
    grad_att.round()
    (input_grad,) = by_rows(
        functools.partial(back_kernel, 0),
        (order.tie(da_own), da_sent, x_own, eh_own),
        gain_rows,
        (BF16,),
        "norm_back",
    )
    input_grad = order.done(input_grad)
    grad_att.round()
    kv = heads // 2
    size = kv // 3 if kv % 384 else 384
    grad_query, grad_key, grad_value, grad_out, gain_one = grad_att.result(
        (
            (0, size, size, heads // size),
            (heads, size, size, kv // size),
            (heads + kv, size, size, kv // size),
            (2 * heads, size, size, heads // size),
        ),
        (query_weight, key_weight, value_weight),
    )
    gain_grads = jnp.stack(
        [gain_one[0] / low(attn_gain).astype(F32), gain_two[0] / low(mlp_gain).astype(F32)]
    )
    gain_grads = gain_grads + swap_halves(gain_grads)
    return (
        output.reshape(seqs, own_rows, model),
        input_grad.reshape(seqs, own_rows, model),
        grad_query,
        grad_key,
        grad_value,
        grad_out.T,
        gain_grads[0],
        grad_gate,
        grad_up,
        grad_down.T,
        gain_grads[1],
    )


def solution(mesh):
    in_specs = (
        P("dp", "tensor", None),
        P("dp", None),
        P("dp", None),
        P("dp", "tensor"),
        P("dp", "tensor"),
        P("dp", "tensor"),
        P("tensor", "dp"),
        P("dp"),
        P("dp", "tensor"),
        P("dp", "tensor"),
        P("tensor", "dp"),
        P("dp"),
        P("dp", "tensor", None),
    )
    out_specs = (
        P("dp", "tensor", None),
        P("dp", "tensor", None),
        P("dp", "tensor"),
        P("dp", "tensor"),
        P("dp", "tensor"),
        P("tensor", "dp"),
        P("dp"),
        P("dp", "tensor"),
        P("dp", "tensor"),
        P("tensor", "dp"),
        P("dp"),
    )
    return jax.shard_map(
        functools.partial(layer, mesh.shape["dp"]),
        mesh=mesh,
        in_specs=in_specs,
        out_specs=out_specs,
        check_vma=False,
    )
```

```python
import functools
import math

import jax
import jax.numpy as jnp
from jax import lax
from jax.experimental import pallas as pl
from jax.experimental.pallas import tpu as pltpu
from jax.sharding import PartitionSpec as P

HEAD_DIM = 96
PAD_DIM = 128
BLOCK = 256
DOCS = 16
EPSILON = 1e-05
ROPE_BASE = 100000.0
FAR = float(2**30)
RING_LIMIT = 16
TILE = 512
MIB = 2**20
SCALE = 1.0 / math.sqrt(HEAD_DIM)
LOG2E = math.log2(math.e)

F32 = jnp.float32
BF16 = jnp.bfloat16


def mm(left, right, left_dim, right_dim, dtype=F32):
    return lax.dot_general(
        left, right, (((left_dim,), (right_dim,)), ((), ())), preferred_element_type=F32
    ).astype(dtype)


def swap_halves(value):
    return lax.ppermute(value, "tensor", [(0, 1), (1, 0)])


def is_ring(dp):
    return 8 <= dp <= RING_LIMIT and dp & (dp - 1) == 0


def chip_of(spot, chips):
    return jnp.where(2 * spot < chips, 2 * spot, 2 * (chips - 1 - spot) + 1)


def ring_pairs(dp):
    chips = dp // 2
    order = list(range(0, chips, 2)) + list(range(chips - 1, 0, -2))
    ahead = []
    for spot in range(chips):
        here, following = order[spot], order[(spot + 1) % chips]
        ahead += [(2 * here, 2 * following), (2 * here + 1, 2 * following + 1)]
    return ahead, [(b, a) for a, b in ahead]


def ring_place(dp):
    chips = dp // 2
    me = lax.axis_index("dp").astype(jnp.int32)
    chip = me >> 1
    return me & 1, jnp.where(chip & 1 == 0, chip >> 1, chips - 1 - (chip >> 1))


def piece_steps(dp):
    reach = dp // 4
    return [0, *range(-1, -reach, -1), *range(1, reach), reach, reach]


def piece_blocks(dp):
    if not is_ring(dp):
        return jnp.zeros((1,), jnp.int32)
    chips = dp // 2
    core, spot = ring_place(dp)
    chip = chip_of((spot + jnp.asarray(piece_steps(dp), jnp.int32)) & (chips - 1), chips)
    return jnp.concatenate([2 * chip + core, 2 * chip + 1 - core])


def turn_blocks(dp):
    if not is_ring(dp):
        return jnp.zeros((1,), jnp.int32)
    chips = dp // 2
    core, spot = ring_place(dp)
    chip = chip_of((spot + jnp.arange(chips, dtype=jnp.int32)) & (chips - 1), chips)
    return jnp.concatenate([2 * chip + 1 - core, 2 * chip + core])


class Order:
    def __init__(self, flag):
        self.token = lax.create_token()
        self.flag = flag

    def tie(self, *values):
        tied = lax.optimization_barrier((self.token, *values))[1:]
        return tied if len(values) > 1 else tied[0]

    def done(self, *values):
        self.token, *values = lax.optimization_barrier((self.token, *values))
        return values if len(values) > 1 else values[0]


class Gather:
    def __init__(self, shard, dp, cut):
        self.dp, self.cut = dp, cut
        self.behind, self.ahead, self.other, self.shard = [], [], [], shard

    def share(self, order):
        if not is_ring(self.dp):
            return
        found = (self.behind[-1], self.ahead[-1]) if self.other else (self.shard,)
        swap = [(i, i ^ 1) for i in range(self.dp)]

        def both(*pieces):
            return tuple(lax.ppermute(piece, "dp", swap) for piece in pieces)

        def neither(*pieces):
            return tuple(jnp.zeros_like(piece) for piece in pieces)

        found = order.tie(*found) if len(found) > 1 else (order.tie(*found),)
        got = lax.cond(order.flag, both, neither, *found)
        self.other.append(order.done(*got) if len(got) > 1 else [order.done(*got)])

    def round(self, order):
        if not is_ring(self.dp):
            return
        forth, back = ring_pairs(self.dp)
        left = self.behind[-1] if self.behind else self.shard
        right = self.ahead[-1] if self.ahead else self.shard
        left, right = order.tie(left, right)
        if len(self.behind) == self.dp // 4 - 1:
            left, right = halves(left, right, self.cut)
        left, right = order.done(left, right)
        self.behind.append(lax.ppermute(left, "dp", forth))
        self.ahead.append(lax.ppermute(right, "dp", back))

    def arrive(self, order):
        if is_ring(self.dp):
            self.behind[-1], self.ahead[-1] = order.done(self.behind[-1], self.ahead[-1])

    def next(self, order):
        if not is_ring(self.dp):
            return
        self.arrive(order)
        arrived = self.behind[-1], self.ahead[-1]
        self.round(order)
        sent = self.behind.pop(), self.ahead.pop()
        self.behind[-1], self.ahead[-1] = arrived
        self.share(order)
        self.behind.append(sent[0])
        self.ahead.append(sent[1])

    def pieces(self, order):
        if not is_ring(self.dp):
            return [(lax.all_gather(self.shard, "dp", axis=0, tiled=True), 0)]
        self.arrive(order)
        self.share(order)
        held = [self.shard, *self.behind[:-1], *self.ahead[:-1], self.behind[-1], self.ahead[-1]]
        other = [self.other[0][0], *(pair[0] for pair in self.other[1:-1])]
        other += [*(pair[1] for pair in self.other[1:-1]), *self.other[-1]]
        columns = [0] * (len(held) - 1) + [self.cut]
        return list(zip([*held, *other], columns * 2))


class Scatter:
    def __init__(self, dp, order, *columns):
        self.dp, self.order = dp, order
        lefts, rights, dims = zip(*columns)
        rights = order.tie(*rights) if len(rights) > 1 else (order.tie(*rights),)
        if not is_ring(dp):
            full = order.done(products(0, 1, lefts, rights, dims))
            self.total = lax.psum_scatter(full, "dp", scatter_dimension=0, tiled=True).astype(F32)
            return
        self.chips = dp // 2
        self.reach = self.chips // 2
        self.rows = lefts[0].shape[0] // dp

        def both(lefts, rights):
            token = lax.create_token()
            theirs = products(0, 2, lefts, rights, dims)
            token, theirs = lax.optimization_barrier((token, theirs))
            got = lax.ppermute(theirs, "dp", [(i, i ^ 1) for i in range(dp)])
            rights = lax.optimization_barrier((token, *rights))[1:]
            return got, products(1, 2, lefts, rights, dims)

        def neither(lefts, rights):
            width = sum(right.shape[1 - dim] for right, dim in zip(rights, dims))
            return (jnp.zeros((lefts[0].shape[0] // 2, width), BF16),) * 2

        self.got, self.mine = order.done(*lax.cond(order.flag, both, neither, lefts, tuple(rights)))
        self.width = self.mine.shape[1]
        self.ahead = self.behind = None

    def local(self, steps, mine, first, low_edge, high_edge):
        block = steps % self.chips
        return [(part, block, first, low_edge, high_edge) for part in (mine, self.got)]

    def round(self):
        if not is_ring(self.dp):
            return
        forth, back = ring_pairs(self.dp)
        half = self.width // 2
        tile = half if half <= 1536 else half // 2
        count = half // tile
        mine = self.order.tie(self.mine)
        reach = self.reach
        if self.ahead is None:
            right = self.local(reach, mine, 0, 0, count)
            left = self.local(reach, mine, count, 0, count)
        else:
            cut = count if self.ahead.shape[1] == half else 2 * count
            right = [*self.local(reach, mine, 0, 0, 2 * count), (self.ahead, 0, 0, 0, cut)]
            left = [*self.local(-reach, mine, 0, 0, 2 * count)]
            left.append((self.behind, 0, 0, 2 * count - cut, 2 * count))
        right, left = self.order.done(*combine(self.rows, tile, [right, left]))
        self.ahead = lax.ppermute(right, "dp", forth)
        self.behind = lax.ppermute(left, "dp", back)
        self.reach -= 1

    def arrive(self):
        if is_ring(self.dp):
            self.ahead, self.behind = self.order.done(self.ahead, self.behind)

    def result(self, pieces, weights):
        if not is_ring(self.dp):
            parts = [self.total] + [jnp.zeros_like(self.total)] * 3
        else:
            parts = [self.order.tie(self.mine), self.got, self.ahead, self.behind]
        return self.order.done(*finish(parts, [0] * 4, pieces, weights))


def rope_rows(top, bottom, cos, sin):
    return top * cos - bottom * sin, bottom * cos + top * sin


def project_kernel(columns, rows, heads, block_ref, turn_ref, own_ref, par_ref, cos_ref, sin_ref, *rest):
    count = len(columns)
    pieces = rest[:count]
    qkv_ref, gain_ref, at_ref, wide_ref, out_ref = rest[count : count + 5]
    w_scr, a_scr, at_scr, in_sem, out_sem, turn_sem = rest[count + 5 :]
    step = pl.program_id(0)
    tiles = pl.num_programs(0)
    own_rows, model = own_ref.shape
    tile = qkv_ref.shape[0]
    half = HEAD_DIM // 2
    qkv_width = 2 * heads

    def loads(i):
        base = pl.multiple_of(block_ref[i] * rows, rows)
        place = slice(columns[i], columns[i] + pieces[i].shape[1])
        return pltpu.make_async_copy(pieces[i], w_scr.at[pl.ds(base, rows), place], in_sem.at[i])

    def stores():
        return (
            pltpu.make_async_copy(w_scr.at[:, :qkv_width], wide_ref, out_sem.at[0]),
            pltpu.make_async_copy(
                w_scr.at[:, qkv_width : qkv_width + heads], out_ref, out_sem.at[1]
            ),
        )

    def turns(i):
        block = model // turn_ref.shape[0]
        base = pl.multiple_of(turn_ref[i] * block, block)
        return pltpu.make_async_copy(
            at_scr.at[pl.ds(base, block), :], at_ref.at[pl.ds(i * block, block), :], turn_sem.at[i]
        )

    @pl.when(step == 0)
    def _():
        for i in range(count):
            loads(i).start()
        for i in range(count):
            loads(i).wait()
        gains = w_scr[:, qkv_width + heads :].astype(F32).T
        gain_ref[...] = gains[:8, :]
        gain = gains[:1, :]
        for number, ref in enumerate((own_ref, par_ref)):

            @pl.loop(0, own_rows // BLOCK)
            def _(part, ref=ref, number=number):
                start = pl.multiple_of(part * BLOCK, BLOCK)
                x = ref[pl.ds(start, BLOCK), :].astype(F32)
                inverse = lax.rsqrt(jnp.mean(x * x, -1, keepdims=True) + EPSILON)
                normed = x * inverse * gain
                place = pl.multiple_of(start + number * own_rows, BLOCK)
                a_scr[pl.ds(place, BLOCK), :] = normed.astype(BF16)
                at_scr[:, pl.ds(place, BLOCK)] = normed.T.astype(BF16)

        for copy in stores():
            copy.start()
        for i in range(turn_ref.shape[0]):
            turns(i).start()

    start = pl.multiple_of(step * tile, 128)
    flat = mm(a_scr[...], w_scr[:, pl.ds(start, tile)], 1, 0).T

    @pl.when(step < tiles - tiles // 4)
    def _():
        cos, sin = cos_ref[...], sin_ref[...]
        for h in range(tile // HEAD_DIM):
            base = h * HEAD_DIM
            top, bottom = rope_rows(
                flat[base : base + half, :], flat[base + half : base + HEAD_DIM, :], cos, sin
            )
            qkv_ref[base : base + half, :] = top.astype(BF16)
            qkv_ref[base + half : base + HEAD_DIM, :] = bottom.astype(BF16)

    @pl.when(step >= tiles - tiles // 4)
    def _():
        qkv_ref[...] = flat.astype(BF16)

    @pl.when(step == tiles - 1)
    def _():
        for copy in stores():
            copy.wait()
        for i in range(turn_ref.shape[0]):
            turns(i).wait()


FREE = pl.CostEstimate(flops=0, bytes_accessed=0, transcendentals=0)
LONG = pl.CostEstimate(flops=0, bytes_accessed=40 * 2**20, transcendentals=0)


def product_kernel(left_ref, right_ref, *out_refs):
    half = left_ref.shape[0] // 2

    @pl.loop(0, 2)
    def _(part):
        start = pl.multiple_of(part * half, half)
        out = mm(left_ref[pl.ds(start, half), :], right_ref[...], 1, 1, BF16)
        for number, ref in enumerate(out_refs):

            @pl.when(part == number)
            def _(ref=ref):
                ref[...] = out


def product(left, right):
    rows, depth = left.shape
    width = right.shape[0]
    tile = next(t for t in (TILE, 384, 256, width) if width % t == 0)
    spec = pl.BlockSpec
    return pl.pallas_call(
        product_kernel,
        grid=(width // tile,),
        in_specs=[spec((rows, depth), lambda j: (0, 0)), spec((tile, depth), lambda j: (j, 0))],
        out_specs=[spec((rows // 2, tile), lambda j: (0, j))] * 2,
        out_shape=[jax.ShapeDtypeStruct((rows // 2, width), BF16)] * 2,
        compiler_params=pltpu.CompilerParams(vmem_limit_bytes=28 * MIB),
        cost_estimate=FREE,
        name="product",
    )(left, right)


def products_kernel(starts, dims, *refs):
    count = len(dims)
    out_ref = refs[-1]
    step = pl.program_id(0)
    for i, dim in enumerate(dims):

        @pl.when((step >= starts[i]) & (step < starts[i + 1]))
        def _(i=i, dim=dim):
            width = out_ref.shape[1]
            size = TILE if width % TILE == 0 else width

            @pl.loop(0, width // size)
            def _(j):
                place = pl.ds(pl.multiple_of(j * size, 128), size)
                right = refs[count + i][place, :] if dim else refs[count + i][:, place]
                out_ref[:, place] = mm(refs[i][...], right, 1, dim, out_ref.dtype)


def products(part, parts, lefts, rights, dims):
    rows, depth = lefts[0].shape
    rows = rows // parts
    widths = [right.shape[1 - dim] for right, dim in zip(rights, dims)]
    tile = next(t for t in (1024, 768, TILE, 384) if all(width % t == 0 for width in widths))
    starts = [0]
    for width in widths:
        starts.append(starts[-1] + width // tile)
    spec = pl.BlockSpec
    in_specs = [spec((rows, depth), lambda j: (part, 0)) for _ in lefts]
    for i, dim in enumerate(dims):

        def place(j, i=i):
            return jnp.clip(j - starts[i], 0, starts[i + 1] - starts[i] - 1)

        if dim:
            in_specs.append(spec((tile, depth), lambda j, place=place: (place(j), 0)))
        else:
            in_specs.append(spec((depth, tile), lambda j, place=place: (0, place(j))))
    return pl.pallas_call(
        functools.partial(products_kernel, starts, dims),
        grid=(starts[-1],),
        in_specs=in_specs,
        out_specs=spec((rows, tile), lambda j: (0, j)),
        out_shape=jax.ShapeDtypeStruct((rows, sum(widths)), BF16),
        compiler_params=pltpu.CompilerParams(vmem_limit_bytes=32 * MIB),
        cost_estimate=FREE,
        name="products",
    )(*lefts, *rights)


def turned_kernel(left_ref, right_ref, out_ref):
    out_ref[...] = mm(left_ref[...], right_ref[...], 1, 0).T.astype(BF16)


def turned_product(left, right, tile, start=0, count=None):
    rows, depth = left.shape
    count = count or right.shape[1] // tile
    spec = pl.BlockSpec
    return pl.pallas_call(
        turned_kernel,
        grid=(count,),
        in_specs=[
            spec((rows, depth), lambda j: (0, 0)),
            spec((depth, tile), lambda j: (0, start + j)),
        ],
        out_specs=spec((tile, rows), lambda j: (j, 0)),
        out_shape=jax.ShapeDtypeStruct((count * tile, rows), BF16),
        compiler_params=pltpu.CompilerParams(vmem_limit_bytes=28 * MIB),
        cost_estimate=FREE,
        name="turned_product",
    )(left, right)


def join_kernel(*refs):
    start = 0
    for ref in refs[:-1]:
        refs[-1][:, start : start + ref.shape[1]] = ref[...].astype(BF16)
        start += ref.shape[1]


def join(*parts):
    rows = parts[0].shape[0]
    return pl.pallas_call(
        join_kernel,
        out_shape=jax.ShapeDtypeStruct((rows, sum(part.shape[1] for part in parts)), BF16),
        compiler_params=pltpu.CompilerParams(vmem_limit_bytes=63 * MIB),
        cost_estimate=FREE,
        name="join",
    )(*parts)


def halves_kernel(left_ref, right_ref, low_ref, high_ref):
    low_ref[...] = left_ref[...]
    high_ref[...] = right_ref[:, right_ref.shape[1] - high_ref.shape[1] :]


def halves(left, right, cut):
    rows, width = left.shape
    rest = width - cut
    spec = pl.BlockSpec
    if cut % rest:
        right_spec = spec((rows, width), lambda i: (0, 0))
    else:
        right_spec = spec((rows, rest), lambda i: (0, cut // rest))
    return pl.pallas_call(
        halves_kernel,
        grid=(1,),
        in_specs=[spec((rows, cut), lambda i: (0, 0)), right_spec],
        out_specs=[spec((rows, cut), lambda i: (0, 0)), spec((rows, rest), lambda i: (0, 0))],
        out_shape=[
            jax.ShapeDtypeStruct((rows, cut), left.dtype),
            jax.ShapeDtypeStruct((rows, rest), left.dtype),
        ],
        compiler_params=pltpu.CompilerParams(vmem_limit_bytes=63 * MIB),
        cost_estimate=FREE,
        name="halves",
    )(left, right)


def residual_kernel(part_ref, sent_ref, x_ref, gain_ref, middle_ref, b_ref):
    middle = part_ref[...].astype(F32) + sent_ref[...].astype(F32)
    middle = x_ref[...].astype(F32) + middle
    inverse = lax.rsqrt(jnp.mean(middle * middle, -1, keepdims=True) + EPSILON)
    middle_ref[...] = middle.astype(middle_ref.dtype)
    b_ref[...] = (middle * inverse * gain_ref[1:2, :]).astype(BF16)


def back_kernel(row, own_ref, sent_ref, value_ref, base_ref, gain_ref, *out_refs):
    upstream = own_ref[...].astype(F32) + sent_ref[...].astype(F32)
    value = value_ref[...].astype(F32)
    inverse = lax.rsqrt(jnp.mean(value * value, -1, keepdims=True) + EPSILON)
    scaled = upstream * gain_ref[row : row + 1, :]
    inner = jnp.mean(scaled * value, -1, keepdims=True)
    out = inverse * (scaled - value * (inverse * inverse * inner))
    out = base_ref[...].astype(F32) + out
    for ref in out_refs:
        ref[...] = out.astype(ref.dtype)


def by_rows(kernel, arrays, gain, dtypes, name):
    rows, width = arrays[0].shape
    step = 256
    block = pl.BlockSpec((step, width), lambda i: (i, 0))
    return pl.pallas_call(
        kernel,
        grid=(rows // step,),
        in_specs=[block] * len(arrays) + [pl.BlockSpec(gain.shape, lambda i: (0, 0))],
        out_specs=[block] * len(dtypes),
        out_shape=[jax.ShapeDtypeStruct((rows, width), dtype) for dtype in dtypes],
        compiler_params=pltpu.CompilerParams(vmem_limit_bytes=63 * MIB),
        cost_estimate=FREE,
        name=name,
    )(*arrays, gain)


def finish_kernel(pieces, weighted, *refs):
    parts, refs = refs[:4], refs[4:]
    weights, refs = refs[:weighted], refs[weighted:]
    outs, gain_ref, total_ref = refs[: len(pieces)], refs[-2], refs[-1]
    total_ref[...] = jnp.zeros_like(total_ref)
    for number, (out_ref, (start, size, stride, steps)) in enumerate(zip(outs, pieces)):

        @pl.loop(0, steps)
        def _(j, number=number, out_ref=out_ref, start=start, size=size, stride=stride):
            source = pl.ds(pl.multiple_of(start + j * stride, 128), size)
            target = pl.ds(pl.multiple_of(j * size, 128), size)
            total = sum(part[:, source].astype(F32) for part in parts)
            out_ref[:, target] = total
            if number < weighted:
                total = total * weights[number][:, target].astype(BF16).astype(F32)
                for k in range(0, size, 128):
                    total_ref[...] += total[:, k : k + 128]

    rows = jnp.broadcast_to(jnp.sum(total_ref[...], 1, keepdims=True), total_ref.shape)
    gain_ref[...] = rows.T[:8, :]


def finish(parts, blocks, pieces, weights):
    rows = weights[0].shape[0]
    width = parts[0].shape[1]
    spec = pl.BlockSpec
    whole = lambda i: (0, 0)
    widths = [size * steps for _, size, _, steps in pieces]
    return pl.pallas_call(
        functools.partial(finish_kernel, pieces, len(weights)),
        grid=(1,),
        in_specs=[spec((rows, width), lambda i, block=block: (block, 0)) for block in blocks]
        + [spec(weight.shape, whole) for weight in weights],
        out_specs=[spec((rows, size), whole) for size in widths] + [spec((8, rows), whole)],
        out_shape=[jax.ShapeDtypeStruct((rows, size), F32) for size in widths]
        + [jax.ShapeDtypeStruct((8, rows), F32)],
        scratch_shapes=[pltpu.VMEM((rows, 128), F32)],
        compiler_params=pltpu.CompilerParams(vmem_limit_bytes=28 * MIB),
        cost_estimate=FREE,
        name="finish",
    )(*parts, *weights)


def combine_kernel(outs, *refs):
    step = pl.program_id(0)
    inputs = list(refs[: -len(outs)])
    for out_ref, terms in zip(refs[-len(outs) :], outs):
        total = None
        for low_edge, high_edge in terms:
            value = inputs.pop(0)[...].astype(F32)
            if high_edge - low_edge < pl.num_programs(0):
                value = jnp.where((step >= low_edge) & (step < high_edge), value, 0.0)
            total = value if total is None else total + value
        out_ref[...] = total.astype(out_ref.dtype)


def combine(rows, tile, outs, dtype=BF16):
    tiles = max(high for terms in outs for *_, high in terms)
    in_specs, arrays, edges = [], [], []
    for terms in outs:
        edges.append([(low_edge, high_edge) for *_, low_edge, high_edge in terms])
        for array, block, first, low_edge, high_edge in terms:

            def place(j, block=block, first=first, low_edge=low_edge, high_edge=high_edge):
                return block, jnp.clip(j, low_edge, high_edge - 1) - low_edge + first

            in_specs.append(pl.BlockSpec((rows, tile), place))
            arrays.append(array)
    return pl.pallas_call(
        functools.partial(combine_kernel, edges),
        grid=(tiles,),
        in_specs=in_specs,
        out_specs=[pl.BlockSpec((rows, tile), lambda j: (0, j)) for _ in outs],
        out_shape=[jax.ShapeDtypeStruct((rows, tiles * tile), dtype) for _ in outs],
        compiler_params=pltpu.CompilerParams(vmem_limit_bytes=16 * MIB),
        cost_estimate=FREE,
        name="combine",
    )(*arrays)


def turn_kernel(turn_ref, own_ref, par_ref, out_ref, scr):
    own_rows, model = own_ref.shape
    step = BLOCK // 2
    for number, ref in enumerate((own_ref, par_ref)):

        @pl.loop(0, own_rows // step)
        def _(part, ref=ref, number=number):
            start = pl.multiple_of(part * step, step)
            place = pl.multiple_of(start + number * own_rows, step)
            scr[:, pl.ds(place, step)] = ref[pl.ds(start, step), :].astype(F32).T.astype(BF16)

    count = turn_ref.shape[0]
    block = model // count

    @pl.loop(0, count)
    def _(i):
        base = pl.multiple_of(turn_ref[i] * block, block)
        place = pl.multiple_of(i * block, block)
        out_ref[pl.ds(place, block), :] = scr[pl.ds(base, block), :]


def turn(turned, own, par):
    own_rows, model = own.shape
    length = 2 * own_rows
    whole = lambda i, t: (0, 0)
    spec = pl.BlockSpec
    return pl.pallas_call(
        turn_kernel,
        grid_spec=pltpu.PrefetchScalarGridSpec(
            num_scalar_prefetch=1,
            grid=(1,),
            in_specs=[spec((own_rows, model), whole)] * 2,
            out_specs=spec((model, length), whole),
            scratch_shapes=[pltpu.VMEM((model, length), BF16)],
        ),
        out_shape=jax.ShapeDtypeStruct((model, length), BF16),
        compiler_params=pltpu.CompilerParams(vmem_limit_bytes=24 * MIB),
        cost_estimate=LONG,
        name="turn",
    )(turned, own, par)


def project(blocks, turned, x_own, x_par, cos, sin, pieces, heads):
    own_rows, model = x_own.shape
    length = 2 * own_rows
    count = len(pieces)
    columns = [column for _, column in pieces]
    pieces = [piece for piece, _ in pieces]
    rows, width = pieces[0].shape
    qkv_width = 2 * heads
    tile = heads // 2
    spec = pl.BlockSpec
    whole = lambda j, s, t: (0, 0)
    anywhere = spec(memory_space=pl.ANY)
    return pl.pallas_call(
        functools.partial(project_kernel, columns, rows, heads),
        grid_spec=pltpu.PrefetchScalarGridSpec(
            num_scalar_prefetch=2,
            grid=(qkv_width // tile,),
            in_specs=[
                spec((own_rows, model), whole),
                spec((own_rows, model), whole),
                spec((HEAD_DIM // 2, length), whole),
                spec((HEAD_DIM // 2, length), whole),
            ]
            + [anywhere] * count,
            out_specs=[
                spec((tile, length), lambda j, s, t: (j, 0)),
                spec((8, model), whole),
                spec(memory_space=pltpu.MemorySpace.HBM),
                spec(memory_space=pltpu.MemorySpace.HBM),
                spec(memory_space=pltpu.MemorySpace.HBM),
            ],
            scratch_shapes=[
                pltpu.VMEM((model, width), BF16),
                pltpu.VMEM((length, model), BF16),
                pltpu.VMEM((model, length), BF16),
                pltpu.SemaphoreType.DMA((count,)),
                pltpu.SemaphoreType.DMA((2,)),
                pltpu.SemaphoreType.DMA(turned.shape),
            ],
        ),
        out_shape=[
            jax.ShapeDtypeStruct((qkv_width, length), BF16),
            jax.ShapeDtypeStruct((8, model), F32),
            jax.ShapeDtypeStruct((model, length), BF16),
            jax.ShapeDtypeStruct((model, qkv_width), BF16),
            jax.ShapeDtypeStruct((model, heads), BF16),
        ],
        compiler_params=pltpu.CompilerParams(vmem_limit_bytes=40 * MIB),
        cost_estimate=FREE,
        name="project",
    )(blocks, turned, x_own, x_par, cos, sin, *pieces)


def ffn_kernel(columns, rows, ff, block_ref, b_own, b_par, e_own, e_par, *rest):
    count = len(columns)
    pieces = rest[:count]
    hidden_ref, pair_ref, own_ref, par_ref, down_ref = rest[count : count + 5]
    b_scr, e_scr, w_scr, total, sem, save_sem = rest[count + 5 :]
    step = pl.program_id(0)
    tiles = pl.num_programs(0)
    slot = lax.rem(step, 2)
    width = hidden_ref.shape[1]
    half = b_own.shape[0]

    def fetch(number, into):
        for kind in range(3):
            for i in range(count):
                base = pl.multiple_of(block_ref[i] * rows, rows)
                column = pl.multiple_of(kind * ff + number * width, 128)
                low_edge, high_edge = columns[i], columns[i] + pieces[i].shape[1]

                def start(i=i, base=base, column=column, kind=kind):
                    pltpu.make_async_copy(
                        pieces[i].at[:, pl.ds(pl.multiple_of(column - columns[i], 128), width)],
                        w_scr.at[into, pl.ds(base, rows), kind * width : (kind + 1) * width],
                        sem.at[into],
                    ).start()

                if low_edge <= kind * ff and (kind + 1) * ff <= high_edge:
                    start()
                elif low_edge < (kind + 1) * ff and kind * ff < high_edge:
                    pl.when((column >= low_edge) & (column < high_edge))(start)

    def saved(number, source):
        column = pl.multiple_of(number * width, 128)
        return pltpu.make_async_copy(
            w_scr.at[source, :, 2 * width :], down_ref.at[:, pl.ds(column, width)], save_sem.at[source]
        )

    @pl.when(step == 0)
    def _():
        fetch(0, 0)
        for target, own, par in ((b_scr, b_own, b_par), (e_scr, e_own, e_par)):
            target[:half, :] = own[...]
            target[half:, :] = par[...]

    @pl.when(step > 0)
    def _():
        saved(step - 1, 1 - slot).wait()

    @pl.when(step + 1 < tiles)
    def _():
        fetch(step + 1, 1 - slot)

    pltpu.make_async_copy(w_scr.at[slot], w_scr.at[slot], sem.at[slot]).wait()
    saved(step, slot).start()
    first = mm(b_scr[...], w_scr[slot, :, : 2 * width], 1, 0)
    gate, up = first[:, :width], first[:, width:]
    dhid = mm(e_scr[...], w_scr[slot, :, 2 * width :], 1, 0)
    sig = 1.0 / (1.0 + jnp.exp(-gate))
    silu = gate * sig
    hidden_ref[...] = (silu * up).astype(BF16)
    dgate = (dhid * up * (sig * (1.0 + gate * (1.0 - sig)))).astype(BF16)
    dup = (dhid * silu).astype(BF16)
    pair_ref[:, :width] = dgate
    pair_ref[:, width:] = dup
    part = mm(pair_ref[...], w_scr[slot, :, : 2 * width], 1, 1)

    @pl.when(step == 0)
    def _():
        total[...] = part

    @pl.when((step > 0) & (step < tiles - 1))
    def _():
        total[...] += part

    @pl.when(step == tiles - 1)
    def _():
        own_ref[...] = (total[:half, :] + part[:half, :]).astype(BF16)
        par_ref[...] = (total[half:, :] + part[half:, :]).astype(BF16)
        saved(step, slot).wait()


def ffn(blocks, b_own, b_par, e_own, e_par, pieces):
    half, model = b_own.shape
    count = len(pieces)
    columns = [column for _, column in pieces]
    pieces = [piece for piece, _ in pieces]
    rows = pieces[0].shape[0]
    ff = max(piece.shape[1] + column for piece, column in zip(pieces, columns)) // 3
    spec = pl.BlockSpec
    whole = lambda j, s: (0, 0)
    anywhere = spec(memory_space=pl.ANY)
    once = spec((half, model), whole, pipeline_mode=pl.Buffered(1))
    return pl.pallas_call(
        functools.partial(ffn_kernel, columns, rows, ff),
        grid_spec=pltpu.PrefetchScalarGridSpec(
            num_scalar_prefetch=1,
            grid=(ff // TILE,),
            in_specs=[once] * 4 + [anywhere] * count,
            out_specs=[
                spec((2 * half, TILE), lambda j, s: (0, j)),
                spec((2 * half, 2 * TILE), lambda j, s: (0, j)),
                once,
                once,
                anywhere,
            ],
            scratch_shapes=[
                pltpu.VMEM((2 * half, model), BF16),
                pltpu.VMEM((2 * half, model), BF16),
                pltpu.VMEM((2, model, 3 * TILE), BF16),
                pltpu.VMEM((2 * half, model), F32),
                pltpu.SemaphoreType.DMA((2,)),
                pltpu.SemaphoreType.DMA((2,)),
            ],
        ),
        out_shape=[
            jax.ShapeDtypeStruct((2 * half, ff), BF16),
            jax.ShapeDtypeStruct((2 * half, 2 * ff), BF16),
            jax.ShapeDtypeStruct((half, model), BF16),
            jax.ShapeDtypeStruct((half, model), BF16),
            jax.ShapeDtypeStruct((model, ff), BF16),
        ],
        compiler_params=pltpu.CompilerParams(vmem_limit_bytes=60 * MIB),
        cost_estimate=FREE,
        name="ffn",
    )(blocks, b_own, b_par, e_own, e_par, *pieces)


def place_of(natural, side, length):
    return pl.multiple_of((natural + side * (length // 2)) & (length - 1), BLOCK)


def diagonal():
    keys = lax.broadcasted_iota(jnp.int32, (BLOCK, BLOCK), 0)
    queries = lax.broadcasted_iota(jnp.int32, (BLOCK, BLOCK), 1)
    return keys <= queries


def fill(scratch, rows, side, docs):
    length = rows.shape[1]
    half = length // 2
    scratch[HEAD_DIM:, :] = jnp.zeros((PAD_DIM - HEAD_DIM, length), BF16)
    if docs is not None:
        scratch[HEAD_DIM : HEAD_DIM + DOCS, :] = docs[...]
    for part in range(2):
        there = pl.ds(place_of(part * half, side, length), half)
        scratch[:HEAD_DIM, part * half : (part + 1) * half] = rows[:, there]


def forward_kernel(
    side_ref, q_in, k_in, v_in, oq_ref, ok_ref, *rest
):
    att_ref, lse_ref, q_scr, kt_scr, k_scr, v_scr = rest[-6:]
    length = q_in.shape[1]
    side = side_ref[0]
    blocks = length // BLOCK
    fill(kt_scr, k_in, side, ok_ref)
    fill(v_scr, v_in, side, None)
    k_scr[...] = kt_scr[...].T
    causal = diagonal()
    for h in range(2):
        rows = slice(h * HEAD_DIM, (h + 1) * HEAD_DIM)
        fill(q_scr, q_in.at[rows, :], side, oq_ref)
        for b in range(blocks):
            here = pl.ds(b * BLOCK, BLOCK)
            keys = (b + 1) * BLOCK
            query = q_scr[:, here]
            last = mm(k_scr[b * BLOCK : keys, :], query, 1, 0)
            last = jnp.where(causal, last, -FAR)
            top = jnp.max(last, 0, keepdims=True)
            if b:
                early = mm(k_scr[: b * BLOCK, :], query, 1, 0)
                top = jnp.maximum(top, jnp.max(early, 0, keepdims=True))
            top = top * (SCALE * LOG2E)
            weight = jnp.exp2(last * (SCALE * LOG2E) - top)
            total = jnp.sum(weight, 0, keepdims=True)
            out = mm(v_scr[:HEAD_DIM, b * BLOCK : keys], weight.astype(BF16), 1, 0)
            if b:
                weight = jnp.exp2(early * (SCALE * LOG2E) - top)
                total = total + jnp.sum(weight, 0, keepdims=True)
                out = out + mm(v_scr[:HEAD_DIM, : b * BLOCK], weight.astype(BF16), 1, 0)
            out = out / total
            there = pl.ds(place_of(b * BLOCK, side, length), BLOCK)
            att_ref[rows, there] = out.astype(BF16)
            lse_ref[0, h : h + 1, here] = top + jnp.log2(total)


def group_specs(groups, length):
    spec = pl.BlockSpec
    return [
        spec((2 * HEAD_DIM, length), lambda g, s: (g, 0)),
        spec((HEAD_DIM, length), lambda g, s: (2 * groups + g, 0)),
        spec((HEAD_DIM, length), lambda g, s: (3 * groups + g, 0)),
    ]


def attend(side, qkv, doc_q, doc_k):
    hidden, length = qkv.shape
    groups = hidden // (4 * HEAD_DIM)
    whole = lambda g, s: (0, 0)
    spec = pl.BlockSpec
    return pl.pallas_call(
        forward_kernel,
        grid_spec=pltpu.PrefetchScalarGridSpec(
            num_scalar_prefetch=1,
            grid=(groups,),
            in_specs=group_specs(groups, length) + [spec((DOCS, length), whole)] * 2,
            out_specs=[
                spec((2 * HEAD_DIM, length), lambda g, s: (g, 0)),
                spec((1, 2, length), lambda g, s: (g, 0, 0)),
            ],
            scratch_shapes=[
                pltpu.VMEM((PAD_DIM, length), BF16),
                pltpu.VMEM((PAD_DIM, length), BF16),
                pltpu.VMEM((length, PAD_DIM), BF16),
                pltpu.VMEM((PAD_DIM, length), BF16),
            ],
        ),
        out_shape=[
            jax.ShapeDtypeStruct((2 * groups * HEAD_DIM, length), BF16),
            jax.ShapeDtypeStruct((groups, 2, length), F32),
        ],
        compiler_params=pltpu.CompilerParams(vmem_limit_bytes=24 * MIB),
        cost_estimate=FREE,
        name="attend",
    )(side, qkv, qkv, qkv, doc_q, doc_k)


def backward_kernel(
    side_ref, q_ref, k_ref, v_ref, att_ref, datt_own, datt_par, lse_ref, cos_ref, sin_ref,
    oq_ref, ok_ref, *rest,
):
    out_ref, *rest = rest
    q_scr, kt_scr, k_scr, vt_scr, v_scr, do_scr, dk_scr, dv_scr, datt_ref, dq_ref, sem = rest
    length = q_ref.shape[1]
    group = pl.program_id(0)
    groups = out_ref.shape[0] // (4 * HEAD_DIM)
    datt_ref[:, : length // 2] = datt_own[...]
    datt_ref[:, length // 2 :] = datt_par[...]
    slot = lax.rem(group, 2)
    dk_ref = dq_ref.at[slot, 2 * HEAD_DIM : 3 * HEAD_DIM, :]
    dv_ref = dq_ref.at[slot, 3 * HEAD_DIM :, :]
    dq_ref = dq_ref.at[slot]

    def stores(number, source):
        for i, (start, size) in enumerate(((0, 2), (2, 1), (3, 1))):
            base = (start * groups + number * size) * HEAD_DIM
            yield pltpu.make_async_copy(
                rest[-2].at[source, start * HEAD_DIM : (start + size) * HEAD_DIM, :],
                out_ref.at[pl.ds(pl.multiple_of(base, HEAD_DIM), size * HEAD_DIM), :],
                sem.at[source, i],
            )

    half = HEAD_DIM // 2
    side = side_ref[0]
    blocks = length // BLOCK
    fill(kt_scr, k_ref, side, ok_ref)
    fill(vt_scr, v_ref, side, None)
    k_scr[...] = kt_scr[...].T
    v_scr[...] = vt_scr[...].T
    causal = diagonal()
    for h in range(2):
        rows = slice(h * HEAD_DIM, (h + 1) * HEAD_DIM)
        fill(q_scr, q_ref.at[rows, :], side, oq_ref)
        fill(do_scr, datt_ref.at[rows, :], side, None)
        for b in range(blocks):
            here = pl.ds(b * BLOCK, BLOCK)
            there = pl.ds(place_of(b * BLOCK, side, length), BLOCK)
            base = jnp.sum(
                datt_ref[rows, there].astype(F32) * att_ref[rows, there].astype(F32), 0, keepdims=True
            )
            keys = (b + 1) * BLOCK
            query, upstream = q_scr[:, here], do_scr[:, here]
            level = lse_ref[0, h : h + 1, here]
            dq = None
            for start, stop in ((b * BLOCK, keys), (0, b * BLOCK)):
                if start == stop:
                    continue
                span = slice(start, stop)
                score = mm(k_scr[span, :], query, 1, 0)
                prob = jnp.exp2(score * (SCALE * LOG2E) - level)
                if stop == keys:
                    prob = jnp.where(causal, prob, 0.0)
                slope = mm(v_scr[span, :], upstream, 1, 0)
                ds = (prob * (slope - base)).astype(BF16)
                part = mm(kt_scr[:HEAD_DIM, span], ds, 1, 0)
                dq = part if dq is None else dq + part
                dk = mm(query[:HEAD_DIM, :], ds, 1, 1)
                dv = mm(upstream[:HEAD_DIM, :], prob.astype(BF16), 1, 1)
                if h == 0 and stop == keys:
                    dk_scr[:, span] = dk
                    dv_scr[:, span] = dv
                else:
                    dk_scr[:, span] += dk
                    dv_scr[:, span] += dv
            cos, sin = cos_ref[:, there], sin_ref[:, there]
            dq = dq * SCALE
            top, bottom = rope_rows(dq[:half, :], dq[half:, :], cos, -sin)
            dq_ref[h * HEAD_DIM : h * HEAD_DIM + half, there] = top.astype(BF16)
            dq_ref[h * HEAD_DIM + half : (h + 1) * HEAD_DIM, there] = bottom.astype(BF16)
    for b in range(blocks):
        here = pl.ds(b * BLOCK, BLOCK)
        there = pl.ds(place_of(b * BLOCK, side, length), BLOCK)
        cos, sin = cos_ref[:, there], sin_ref[:, there]
        dk = dk_scr[:, here] * SCALE
        top, bottom = rope_rows(dk[:half, :], dk[half:, :], cos, -sin)
        dk_ref[:half, there] = top.astype(BF16)
        dk_ref[half:, there] = bottom.astype(BF16)
        dv_ref[:, there] = dv_scr[:, here].astype(BF16)
    for copy in stores(group, slot):
        copy.start()

    @pl.when(group > 0)
    def _():
        for copy in stores(group - 1, 1 - slot):
            copy.wait()

    @pl.when(group == pl.num_programs(0) - 1)
    def _():
        for copy in stores(group, slot):
            copy.wait()


def attend_back(side, qkv, att, datt, lse, cos, sin, doc_q, doc_k):
    hidden, length = qkv.shape
    groups = hidden // (4 * HEAD_DIM)
    whole = lambda g, s: (0, 0)
    spec = pl.BlockSpec
    narrow = spec((2 * HEAD_DIM, length // 2), lambda g, s: (g, 0))
    source = spec((2 * HEAD_DIM, length), lambda g, s: (g, 0))
    level = spec((1, 2, length), lambda g, s: (g, 0, 0))
    anywhere = spec(memory_space=pl.ANY)
    table = spec((HEAD_DIM // 2, length), whole)
    docs = spec((DOCS, length), whole)
    tall = pltpu.VMEM((length, PAD_DIM), BF16)
    flat = pltpu.VMEM((PAD_DIM, length), BF16)
    return pl.pallas_call(
        backward_kernel,
        grid_spec=pltpu.PrefetchScalarGridSpec(
            num_scalar_prefetch=1,
            grid=(groups,),
            in_specs=group_specs(groups, length)
            + [source, narrow, narrow, level, table, table, docs, docs],
            out_specs=anywhere,
            scratch_shapes=[flat, flat, tall, flat, tall, flat]
            + [pltpu.VMEM((HEAD_DIM, length), F32)] * 2
            + [
                pltpu.VMEM((2 * HEAD_DIM, length), BF16),
                pltpu.VMEM((2, 4 * HEAD_DIM, length), BF16),
                pltpu.SemaphoreType.DMA((2, 3)),
            ],
        ),
        out_shape=jax.ShapeDtypeStruct((hidden, length), BF16),
        compiler_params=pltpu.CompilerParams(vmem_limit_bytes=32 * MIB),
        cost_estimate=FREE,
        name="attend_back",
    )(side, qkv, qkv, qkv, att, *datt, lse, cos, sin, doc_q, doc_k)


def low(weight):
    return weight.astype(BF16)


def layer(
    dp, tokens, segment_ids, positions, query_weight, key_weight, value_weight, out_weight,
    attn_gain, gate_weight, up_weight, down_weight, mlp_gain, cotangent,
):
    seqs, own_rows, model = tokens.shape
    length = segment_ids.shape[1]
    heads = query_weight.shape[1]
    ff = gate_weight.shape[1]
    side_index = lax.axis_index("tensor").astype(jnp.int32)
    side = side_index[None]
    blocks, turned = piece_blocks(dp), turn_blocks(dp)

    x_own = tokens.reshape(own_rows, model)
    e_own = cotangent.reshape(own_rows, model)
    gains = jnp.pad(jnp.stack([low(attn_gain), low(mlp_gain)], 1), ((0, 0), (0, 126)))
    order = Order(positions[0, 0] >= 0)
    first = order.done(join(query_weight, key_weight, value_weight, out_weight.T, gains))
    first = Gather(first, dp, 1280)
    x_par = swap_halves(x_own)
    first.round(order)
    first.share(order)
    places = positions.reshape(length).astype(F32)
    half = HEAD_DIM // 2
    places = jnp.where(side_index == 0, places, jnp.roll(places, length // 2))
    ladder = jnp.power(F32(ROPE_BASE), -2.0 * jnp.arange(half, dtype=F32) / HEAD_DIM)
    angles = ladder[:, None] * places[None, :]
    cos, sin = jnp.cos(angles), jnp.sin(angles)
    cos, sin = order.done(cos, sin)
    second = order.done(join(gate_weight, up_weight, down_weight.T))
    second = Gather(second, dp, 3 * ff // 2)
    for _ in range(dp // 4 - 1):
        first.next(order)
    second.share(order)
    first = first.pieces(order)
    x_first, x_par = order.done(*order.tie(x_own, x_par))
    e_par = swap_halves(order.tie(e_own))
    second.round(order)

    known = jnp.arange(DOCS, dtype=jnp.int32)[:, None] == segment_ids.reshape(1, length)
    doc_q = known.astype(BF16)
    doc_k = jnp.where(known, 0.0, -FAR).astype(BF16)

    qkv, gain_rows, a_turned, qkv_full, out_full = project(
        blocks, turned, x_first, x_par, cos, sin, first, heads
    )
    qkv = order.done(qkv)
    att, lse = attend(side, order.tie(qkv), doc_q, doc_k)
    att = order.done(att)

    own, par = slice(0, own_rows), slice(own_rows, None)
    partial = order.done(mm(att[:, par], out_full, 0, 1, BF16))
    sent = swap_halves(partial)
    e_par = order.done(e_par)
    second.next(order)
    e_turned = order.done(turn(turned, order.tie(e_own), e_par))
    partial = order.done(mm(att[:, own], order.tie(out_full), 0, 1, BF16))
    second.next(order)
    sent = order.tie(sent)
    middle, b_own = order.done(
        *by_rows(residual_kernel, (partial, sent, x_own), gain_rows, (BF16, BF16), "residual")
    )
    b_par = swap_halves(b_own)
    second.next(order)
    second = second.pieces(order)

    b_par = order.tie(b_par)
    hidden, pair, db_own, db_par, down_full = ffn(blocks, b_own, b_par, e_own, e_par, second)
    db_par = order.done(db_par)
    db_sent = swap_halves(db_par)
    b_turned = order.done(turn(turned, order.tie(b_own), b_par))
    grad_ffn = Scatter(dp, order, (e_turned, hidden, 0), (b_turned, pair, 0))
    eh_own = order.done(
        *by_rows(
            functools.partial(back_kernel, 1),
            (db_own, order.tie(db_sent), middle, e_own),
            gain_rows,
            (BF16,),
            "norm_back",
        )
    )
    eh_par = swap_halves(eh_own)
    grad_ffn.round()
    down_own, down_par = order.done(*product(order.tie(hidden), down_full))
    grad_ffn.round()
    datt_own = order.done(turned_product(order.tie(eh_own), out_full, 384))
    eh_par = order.tie(eh_par)
    datt_par = order.done(turned_product(eh_par, out_full, 384))
    down_sent = swap_halves(order.tie(down_par))
    eh_turned = order.done(turn(turned, order.tie(eh_own), eh_par))
    grad_ffn.round()
    datt = order.tie(datt_own, datt_par)
    dqkv = order.done(attend_back(side, qkv, att, datt, lse, cos, sin, doc_q, doc_k))
    down_sent = order.done(down_sent)
    da_par = order.done(turned_product(qkv_full, order.tie(dqkv), own_rows, 1, 1))
    da_sent = swap_halves(da_par)
    grad_ffn.round()
    grad_att = Scatter(dp, order, (a_turned, dqkv, 1), (eh_turned, att, 1))
    grad_att.round()
    output = (middle.astype(F32) + (down_own.astype(F32) + order.tie(down_sent).astype(F32))).astype(BF16)
    output = order.done(output)
    da_own = order.done(turned_product(qkv_full, order.tie(dqkv), own_rows, 0, 1))
    grad_ffn.arrive()
    grad_att.round()
    grad_gate, grad_up, grad_down, gain_two = grad_ffn.result(
        (
            (ff, TILE, 2 * TILE, ff // TILE),
            (ff + TILE, TILE, 2 * TILE, ff // TILE),
            (0, TILE, TILE, ff // TILE),
        ),
        (gate_weight, up_weight),
    )
    da_sent = order.done(da_sent)
    grad_att.round()
    (input_grad,) = by_rows(
        functools.partial(back_kernel, 0),
        (order.tie(da_own), da_sent, x_own, eh_own),
        gain_rows,
        (BF16,),
        "norm_back",
    )
    input_grad = order.done(input_grad)
    grad_att.round()
    kv = heads // 2
    size = kv // 3 if kv % 384 else 384
    grad_query, grad_key, grad_value, grad_out, gain_one = grad_att.result(
        (
            (0, size, size, heads // size),
            (heads, size, size, kv // size),
            (heads + kv, size, size, kv // size),
            (2 * heads, size, size, heads // size),
        ),
        (query_weight, key_weight, value_weight),
    )
    gain_grads = jnp.stack(
        [gain_one[0] / low(attn_gain).astype(F32), gain_two[0] / low(mlp_gain).astype(F32)]
    )
    gain_grads = gain_grads + swap_halves(gain_grads)
    return (
        output.reshape(seqs, own_rows, model),
        input_grad.reshape(seqs, own_rows, model),
        grad_query,
        grad_key,
        grad_value,
        grad_out.T,
        gain_grads[0],
        grad_gate,
        grad_up,
        grad_down.T,
        gain_grads[1],
    )


def solution(mesh):
    in_specs = (
        P("dp", "tensor", None),
        P("dp", None),
        P("dp", None),
        P("dp", "tensor"),
        P("dp", "tensor"),
        P("dp", "tensor"),
        P("tensor", "dp"),
        P("dp"),
        P("dp", "tensor"),
        P("dp", "tensor"),
        P("tensor", "dp"),
        P("dp"),
        P("dp", "tensor", None),
    )
    out_specs = (
        P("dp", "tensor", None),
        P("dp", "tensor", None),
        P("dp", "tensor"),
        P("dp", "tensor"),
        P("dp", "tensor"),
        P("tensor", "dp"),
        P("dp"),
        P("dp", "tensor"),
        P("dp", "tensor"),
        P("tensor", "dp"),
        P("dp"),
    )
    return jax.shard_map(
        functools.partial(layer, mesh.shape["dp"]),
        mesh=mesh,
        in_specs=in_specs,
        out_specs=out_specs,
        check_vma=False,
    )
```

```python
import functools
import math

import jax
import jax.numpy as jnp
from jax import lax
from jax.experimental import pallas as pl
from jax.experimental.pallas import tpu as pltpu
from jax.sharding import PartitionSpec as P

HEAD_DIM = 96
PAD_DIM = 128
BLOCK = 256
DOCS = 16
EPSILON = 1e-05
ROPE_BASE = 100000.0
FAR = float(2**30)
RING_LIMIT = 16
TILE = 512
MIB = 2**20
SCALE = 1.0 / math.sqrt(HEAD_DIM)
LOG2E = math.log2(math.e)

F32 = jnp.float32
BF16 = jnp.bfloat16


def mm(left, right, left_dim, right_dim, dtype=F32):
    return lax.dot_general(
        left, right, (((left_dim,), (right_dim,)), ((), ())), preferred_element_type=F32
    ).astype(dtype)


def swap_halves(value):
    return lax.ppermute(value, "tensor", [(0, 1), (1, 0)])


def is_ring(dp):
    return 8 <= dp <= RING_LIMIT and dp & (dp - 1) == 0


def chip_of(spot, chips):
    return jnp.where(2 * spot < chips, 2 * spot, 2 * (chips - 1 - spot) + 1)


def ring_pairs(dp):
    chips = dp // 2
    order = list(range(0, chips, 2)) + list(range(chips - 1, 0, -2))
    ahead = []
    for spot in range(chips):
        here, following = order[spot], order[(spot + 1) % chips]
        ahead += [(2 * here, 2 * following), (2 * here + 1, 2 * following + 1)]
    return ahead, [(b, a) for a, b in ahead]


def ring_place(dp):
    chips = dp // 2
    me = lax.axis_index("dp").astype(jnp.int32)
    chip = me >> 1
    return me & 1, jnp.where(chip & 1 == 0, chip >> 1, chips - 1 - (chip >> 1))


def piece_steps(dp):
    reach = dp // 4
    return [0, *range(-1, -reach, -1), *range(1, reach), reach, reach]


def piece_blocks(dp):
    if not is_ring(dp):
        return jnp.zeros((1,), jnp.int32)
    chips = dp // 2
    core, spot = ring_place(dp)
    chip = chip_of((spot + jnp.asarray(piece_steps(dp), jnp.int32)) & (chips - 1), chips)
    return jnp.concatenate([2 * chip + core, 2 * chip + 1 - core])


def turn_blocks(dp):
    if not is_ring(dp):
        return jnp.zeros((1,), jnp.int32)
    chips = dp // 2
    core, spot = ring_place(dp)
    chip = chip_of((spot + jnp.arange(chips, dtype=jnp.int32)) & (chips - 1), chips)
    return jnp.concatenate([2 * chip + 1 - core, 2 * chip + core])


class Order:
    def __init__(self, flag):
        self.token = lax.create_token()
        self.flag = flag

    def tie(self, *values):
        tied = lax.optimization_barrier((self.token, *values))[1:]
        return tied if len(values) > 1 else tied[0]

    def done(self, *values):
        self.token, *values = lax.optimization_barrier((self.token, *values))
        return values if len(values) > 1 else values[0]


class Gather:
    def __init__(self, shard, dp, cut):
        self.dp, self.cut = dp, cut
        self.behind, self.ahead, self.other, self.shard = [], [], [], shard

    def share(self, order):
        if not is_ring(self.dp):
            return
        found = (self.behind[-1], self.ahead[-1]) if self.other else (self.shard,)
        swap = [(i, i ^ 1) for i in range(self.dp)]

        def both(*pieces):
            return tuple(lax.ppermute(piece, "dp", swap) for piece in pieces)

        def neither(*pieces):
            return tuple(jnp.zeros_like(piece) for piece in pieces)

        found = order.tie(*found) if len(found) > 1 else (order.tie(*found),)
        got = lax.cond(order.flag, both, neither, *found)
        self.other.append(order.done(*got) if len(got) > 1 else [order.done(*got)])

    def round(self, order):
        if not is_ring(self.dp):
            return
        forth, back = ring_pairs(self.dp)
        left = self.behind[-1] if self.behind else self.shard
        right = self.ahead[-1] if self.ahead else self.shard
        left, right = order.tie(left, right)
        if len(self.behind) == self.dp // 4 - 1:
            left, right = halves(left, right, self.cut)
        left, right = order.done(left, right)
        self.behind.append(lax.ppermute(left, "dp", forth))
        self.ahead.append(lax.ppermute(right, "dp", back))

    def arrive(self, order):
        if is_ring(self.dp):
            self.behind[-1], self.ahead[-1] = order.done(self.behind[-1], self.ahead[-1])

    def next(self, order):
        if not is_ring(self.dp):
            return
        self.arrive(order)
        arrived = self.behind[-1], self.ahead[-1]
        self.round(order)
        sent = self.behind.pop(), self.ahead.pop()
        self.behind[-1], self.ahead[-1] = arrived
        self.share(order)
        self.behind.append(sent[0])
        self.ahead.append(sent[1])

    def pieces(self, order):
        if not is_ring(self.dp):
            return [(lax.all_gather(self.shard, "dp", axis=0, tiled=True), 0)]
        self.arrive(order)
        self.share(order)
        held = [self.shard, *self.behind[:-1], *self.ahead[:-1], self.behind[-1], self.ahead[-1]]
        other = [self.other[0][0], *(pair[0] for pair in self.other[1:-1])]
        other += [*(pair[1] for pair in self.other[1:-1]), *self.other[-1]]
        columns = [0] * (len(held) - 1) + [self.cut]
        return list(zip([*held, *other], columns * 2))


class Scatter:
    def __init__(self, dp, order, *columns):
        self.dp, self.order = dp, order
        lefts, rights, dims = zip(*columns)
        rights = order.tie(*rights) if len(rights) > 1 else (order.tie(*rights),)
        if not is_ring(dp):
            full = order.done(products(0, 1, lefts, rights, dims))
            self.total = lax.psum_scatter(full, "dp", scatter_dimension=0, tiled=True).astype(F32)
            return
        self.chips = dp // 2
        self.reach = self.chips // 2
        self.rows = lefts[0].shape[0] // dp

        def both(lefts, rights):
            token = lax.create_token()
            theirs = products(0, 2, lefts, rights, dims)
            token, theirs = lax.optimization_barrier((token, theirs))
            got = lax.ppermute(theirs, "dp", [(i, i ^ 1) for i in range(dp)])
            rights = lax.optimization_barrier((token, *rights))[1:]
            return got, products(1, 2, lefts, rights, dims)

        def neither(lefts, rights):
            width = sum(right.shape[1 - dim] for right, dim in zip(rights, dims))
            return (jnp.zeros((lefts[0].shape[0] // 2, width), BF16),) * 2

        self.got, self.mine = order.done(*lax.cond(order.flag, both, neither, lefts, tuple(rights)))
        self.width = self.mine.shape[1]
        self.ahead = self.behind = None

    def local(self, steps, mine, first, low_edge, high_edge):
        block = steps % self.chips
        return [(part, block, first, low_edge, high_edge) for part in (mine, self.got)]

    def round(self):
        if not is_ring(self.dp):
            return
        forth, back = ring_pairs(self.dp)
        half = self.width // 2
        tile = half if half <= 3072 else half // 2
        count = half // tile
        mine = self.order.tie(self.mine)
        reach = self.reach
        if self.ahead is None:
            right = self.local(reach, mine, 0, 0, count)
            left = self.local(reach, mine, count, 0, count)
        else:
            cut = count if self.ahead.shape[1] == half else 2 * count
            right = [*self.local(reach, mine, 0, 0, 2 * count), (self.ahead, 0, 0, 0, cut)]
            left = [*self.local(-reach, mine, 0, 0, 2 * count)]
            left.append((self.behind, 0, 0, 2 * count - cut, 2 * count))
        right, left = self.order.done(*combine(self.rows, tile, [right, left]))
        self.ahead = lax.ppermute(right, "dp", forth)
        self.behind = lax.ppermute(left, "dp", back)
        self.reach -= 1

    def arrive(self):
        if is_ring(self.dp):
            self.ahead, self.behind = self.order.done(self.ahead, self.behind)

    def result(self, pieces, weights):
        if not is_ring(self.dp):
            parts = [self.total] + [jnp.zeros_like(self.total)] * 3
        else:
            parts = [self.order.tie(self.mine), self.got, self.ahead, self.behind]
        return self.order.done(*finish(parts, [0] * 4, pieces, weights))


def rope_rows(top, bottom, cos, sin):
    return top * cos - bottom * sin, bottom * cos + top * sin


def project_kernel(columns, rows, heads, block_ref, turn_ref, own_ref, par_ref, cos_ref, sin_ref, *rest):
    count = len(columns)
    pieces = rest[:count]
    qkv_ref, gain_ref, at_ref, wide_ref, out_ref = rest[count : count + 5]
    w_scr, a_scr, at_scr, in_sem, out_sem, turn_sem = rest[count + 5 :]
    step = pl.program_id(0)
    tiles = pl.num_programs(0)
    own_rows, model = own_ref.shape
    tile = qkv_ref.shape[0]
    half = HEAD_DIM // 2
    qkv_width = 2 * heads

    def loads(i):
        base = pl.multiple_of(block_ref[i] * rows, rows)
        place = slice(columns[i], columns[i] + pieces[i].shape[1])
        return pltpu.make_async_copy(pieces[i], w_scr.at[pl.ds(base, rows), place], in_sem.at[i])

    def stores():
        return (
            pltpu.make_async_copy(w_scr.at[:, :qkv_width], wide_ref, out_sem.at[0]),
            pltpu.make_async_copy(
                w_scr.at[:, qkv_width : qkv_width + heads], out_ref, out_sem.at[1]
            ),
        )

    def turns(i):
        block = model // turn_ref.shape[0]
        base = pl.multiple_of(turn_ref[i] * block, block)
        return pltpu.make_async_copy(
            at_scr.at[pl.ds(base, block), :], at_ref.at[pl.ds(i * block, block), :], turn_sem.at[i]
        )

    @pl.when(step == 0)
    def _():
        for i in range(count):
            loads(i).start()
        for i in range(count):
            loads(i).wait()
        gains = w_scr[:, qkv_width + heads :].astype(F32).T
        gain_ref[...] = gains[:8, :]
        gain = gains[:1, :]
        for number, ref in enumerate((own_ref, par_ref)):

            @pl.loop(0, own_rows // BLOCK)
            def _(part, ref=ref, number=number):
                start = pl.multiple_of(part * BLOCK, BLOCK)
                x = ref[pl.ds(start, BLOCK), :].astype(F32)
                inverse = lax.rsqrt(jnp.mean(x * x, -1, keepdims=True) + EPSILON)
                normed = x * inverse * gain
                place = pl.multiple_of(start + number * own_rows, BLOCK)
                a_scr[pl.ds(place, BLOCK), :] = normed.astype(BF16)
                at_scr[:, pl.ds(place, BLOCK)] = normed.T.astype(BF16)

        for copy in stores():
            copy.start()
        for i in range(turn_ref.shape[0]):
            turns(i).start()

    start = pl.multiple_of(step * tile, 128)
    flat = mm(a_scr[...], w_scr[:, pl.ds(start, tile)], 1, 0).T

    @pl.when(step < tiles - tiles // 4)
    def _():
        cos, sin = cos_ref[...], sin_ref[...]
        for h in range(tile // HEAD_DIM):
            base = h * HEAD_DIM
            top, bottom = rope_rows(
                flat[base : base + half, :], flat[base + half : base + HEAD_DIM, :], cos, sin
            )
            qkv_ref[base : base + half, :] = top.astype(BF16)
            qkv_ref[base + half : base + HEAD_DIM, :] = bottom.astype(BF16)

    @pl.when(step >= tiles - tiles // 4)
    def _():
        qkv_ref[...] = flat.astype(BF16)

    @pl.when(step == tiles - 1)
    def _():
        for copy in stores():
            copy.wait()
        for i in range(turn_ref.shape[0]):
            turns(i).wait()


FREE = pl.CostEstimate(flops=0, bytes_accessed=0, transcendentals=0)
LONG = pl.CostEstimate(flops=0, bytes_accessed=40 * 2**20, transcendentals=0)


def product_kernel(left_ref, right_ref, *out_refs):
    half = left_ref.shape[0] // 2

    @pl.loop(0, 2)
    def _(part):
        start = pl.multiple_of(part * half, half)
        out = mm(left_ref[pl.ds(start, half), :], right_ref[...], 1, 1, BF16)
        for number, ref in enumerate(out_refs):

            @pl.when(part == number)
            def _(ref=ref):
                ref[...] = out


def product(left, right):
    rows, depth = left.shape
    width = right.shape[0]
    tile = next(t for t in (TILE, 384, 256, width) if width % t == 0)
    spec = pl.BlockSpec
    return pl.pallas_call(
        product_kernel,
        grid=(width // tile,),
        in_specs=[spec((rows, depth), lambda j: (0, 0)), spec((tile, depth), lambda j: (j, 0))],
        out_specs=[spec((rows // 2, tile), lambda j: (0, j))] * 2,
        out_shape=[jax.ShapeDtypeStruct((rows // 2, width), BF16)] * 2,
        compiler_params=pltpu.CompilerParams(vmem_limit_bytes=28 * MIB),
        cost_estimate=FREE,
        name="product",
    )(left, right)


def products_kernel(starts, dims, *refs):
    count = len(dims)
    out_ref = refs[-1]
    step = pl.program_id(0)
    for i, dim in enumerate(dims):

        @pl.when((step >= starts[i]) & (step < starts[i + 1]))
        def _(i=i, dim=dim):
            width = out_ref.shape[1]
            size = TILE if width % TILE == 0 else width

            @pl.loop(0, width // size)
            def _(j):
                place = pl.ds(pl.multiple_of(j * size, 128), size)
                right = refs[count + i][place, :] if dim else refs[count + i][:, place]
                out_ref[:, place] = mm(refs[i][...], right, 1, dim, out_ref.dtype)


def products(part, parts, lefts, rights, dims):
    rows, depth = lefts[0].shape
    rows = rows // parts
    widths = [right.shape[1 - dim] for right, dim in zip(rights, dims)]
    tile = next(t for t in (1024, 768, TILE, 384) if all(width % t == 0 for width in widths))
    starts = [0]
    for width in widths:
        starts.append(starts[-1] + width // tile)
    spec = pl.BlockSpec
    in_specs = [spec((rows, depth), lambda j: (part, 0)) for _ in lefts]
    for i, dim in enumerate(dims):

        def place(j, i=i):
            return jnp.clip(j - starts[i], 0, starts[i + 1] - starts[i] - 1)

        if dim:
            in_specs.append(spec((tile, depth), lambda j, place=place: (place(j), 0)))
        else:
            in_specs.append(spec((depth, tile), lambda j, place=place: (0, place(j))))
    return pl.pallas_call(
        functools.partial(products_kernel, starts, dims),
        grid=(starts[-1],),
        in_specs=in_specs,
        out_specs=spec((rows, tile), lambda j: (0, j)),
        out_shape=jax.ShapeDtypeStruct((rows, sum(widths)), BF16),
        compiler_params=pltpu.CompilerParams(vmem_limit_bytes=32 * MIB),
        cost_estimate=FREE,
        name="products",
    )(*lefts, *rights)


def turned_kernel(left_ref, right_ref, out_ref):
    out_ref[...] = mm(left_ref[...], right_ref[...], 1, 0).T.astype(BF16)


def turned_product(left, right, tile, start=0, count=None):
    rows, depth = left.shape
    count = count or right.shape[1] // tile
    spec = pl.BlockSpec
    return pl.pallas_call(
        turned_kernel,
        grid=(count,),
        in_specs=[
            spec((rows, depth), lambda j: (0, 0)),
            spec((depth, tile), lambda j: (0, start + j)),
        ],
        out_specs=spec((tile, rows), lambda j: (j, 0)),
        out_shape=jax.ShapeDtypeStruct((count * tile, rows), BF16),
        compiler_params=pltpu.CompilerParams(vmem_limit_bytes=28 * MIB),
        cost_estimate=FREE,
        name="turned_product",
    )(left, right)


def join_kernel(*refs):
    start = 0
    for ref in refs[:-1]:
        refs[-1][:, start : start + ref.shape[1]] = ref[...].astype(BF16)
        start += ref.shape[1]


def join(*parts):
    rows = parts[0].shape[0]
    return pl.pallas_call(
        join_kernel,
        out_shape=jax.ShapeDtypeStruct((rows, sum(part.shape[1] for part in parts)), BF16),
        compiler_params=pltpu.CompilerParams(vmem_limit_bytes=63 * MIB),
        cost_estimate=FREE,
        name="join",
    )(*parts)


def halves_kernel(left_ref, right_ref, low_ref, high_ref):
    low_ref[...] = left_ref[...]
    high_ref[...] = right_ref[:, right_ref.shape[1] - high_ref.shape[1] :]


def halves(left, right, cut):
    rows, width = left.shape
    rest = width - cut
    spec = pl.BlockSpec
    if cut % rest:
        right_spec = spec((rows, width), lambda i: (0, 0))
    else:
        right_spec = spec((rows, rest), lambda i: (0, cut // rest))
    return pl.pallas_call(
        halves_kernel,
        grid=(1,),
        in_specs=[spec((rows, cut), lambda i: (0, 0)), right_spec],
        out_specs=[spec((rows, cut), lambda i: (0, 0)), spec((rows, rest), lambda i: (0, 0))],
        out_shape=[
            jax.ShapeDtypeStruct((rows, cut), left.dtype),
            jax.ShapeDtypeStruct((rows, rest), left.dtype),
        ],
        compiler_params=pltpu.CompilerParams(vmem_limit_bytes=63 * MIB),
        cost_estimate=FREE,
        name="halves",
    )(left, right)


def residual_kernel(part_ref, sent_ref, x_ref, gain_ref, middle_ref, b_ref):
    middle = part_ref[...].astype(F32) + sent_ref[...].astype(F32)
    middle = x_ref[...].astype(F32) + middle
    inverse = lax.rsqrt(jnp.mean(middle * middle, -1, keepdims=True) + EPSILON)
    middle_ref[...] = middle.astype(middle_ref.dtype)
    b_ref[...] = (middle * inverse * gain_ref[1:2, :]).astype(BF16)


def back_kernel(row, own_ref, sent_ref, value_ref, base_ref, gain_ref, *out_refs):
    upstream = own_ref[...].astype(F32) + sent_ref[...].astype(F32)
    value = value_ref[...].astype(F32)
    inverse = lax.rsqrt(jnp.mean(value * value, -1, keepdims=True) + EPSILON)
    scaled = upstream * gain_ref[row : row + 1, :]
    inner = jnp.mean(scaled * value, -1, keepdims=True)
    out = inverse * (scaled - value * (inverse * inverse * inner))
    out = base_ref[...].astype(F32) + out
    for ref in out_refs:
        ref[...] = out.astype(ref.dtype)


def by_rows(kernel, arrays, gain, dtypes, name):
    rows, width = arrays[0].shape
    step = 256
    block = pl.BlockSpec((step, width), lambda i: (i, 0))
    return pl.pallas_call(
        kernel,
        grid=(rows // step,),
        in_specs=[block] * len(arrays) + [pl.BlockSpec(gain.shape, lambda i: (0, 0))],
        out_specs=[block] * len(dtypes),
        out_shape=[jax.ShapeDtypeStruct((rows, width), dtype) for dtype in dtypes],
        compiler_params=pltpu.CompilerParams(vmem_limit_bytes=63 * MIB),
        cost_estimate=FREE,
        name=name,
    )(*arrays, gain)


def finish_kernel(pieces, weighted, *refs):
    parts, refs = refs[:4], refs[4:]
    weights, refs = refs[:weighted], refs[weighted:]
    outs, gain_ref, total_ref = refs[: len(pieces)], refs[-2], refs[-1]
    total_ref[...] = jnp.zeros_like(total_ref)
    for number, (out_ref, (start, size, stride, steps)) in enumerate(zip(outs, pieces)):

        @pl.loop(0, steps)
        def _(j, number=number, out_ref=out_ref, start=start, size=size, stride=stride):
            source = pl.ds(pl.multiple_of(start + j * stride, 128), size)
            target = pl.ds(pl.multiple_of(j * size, 128), size)
            total = sum(part[:, source].astype(F32) for part in parts)
            out_ref[:, target] = total
            if number < weighted:
                total = total * weights[number][:, target].astype(BF16).astype(F32)
                for k in range(0, size, 128):
                    total_ref[...] += total[:, k : k + 128]

    rows = jnp.broadcast_to(jnp.sum(total_ref[...], 1, keepdims=True), total_ref.shape)
    gain_ref[...] = rows.T[:8, :]


def finish(parts, blocks, pieces, weights):
    rows = weights[0].shape[0]
    width = parts[0].shape[1]
    spec = pl.BlockSpec
    whole = lambda i: (0, 0)
    widths = [size * steps for _, size, _, steps in pieces]
    return pl.pallas_call(
        functools.partial(finish_kernel, pieces, len(weights)),
        grid=(1,),
        in_specs=[spec((rows, width), lambda i, block=block: (block, 0)) for block in blocks]
        + [spec(weight.shape, whole) for weight in weights],
        out_specs=[spec((rows, size), whole) for size in widths] + [spec((8, rows), whole)],
        out_shape=[jax.ShapeDtypeStruct((rows, size), F32) for size in widths]
        + [jax.ShapeDtypeStruct((8, rows), F32)],
        scratch_shapes=[pltpu.VMEM((rows, 128), F32)],
        compiler_params=pltpu.CompilerParams(vmem_limit_bytes=28 * MIB),
        cost_estimate=FREE,
        name="finish",
    )(*parts, *weights)


def combine_kernel(outs, *refs):
    step = pl.program_id(0)
    inputs = list(refs[: -len(outs)])
    for out_ref, terms in zip(refs[-len(outs) :], outs):
        total = None
        for low_edge, high_edge in terms:
            value = inputs.pop(0)[...].astype(F32)
            if high_edge - low_edge < pl.num_programs(0):
                value = jnp.where((step >= low_edge) & (step < high_edge), value, 0.0)
            total = value if total is None else total + value
        out_ref[...] = total.astype(out_ref.dtype)


def combine(rows, tile, outs, dtype=BF16):
    tiles = max(high for terms in outs for *_, high in terms)
    in_specs, arrays, edges = [], [], []
    for terms in outs:
        edges.append([(low_edge, high_edge) for *_, low_edge, high_edge in terms])
        for array, block, first, low_edge, high_edge in terms:

            def place(j, block=block, first=first, low_edge=low_edge, high_edge=high_edge):
                return block, jnp.clip(j, low_edge, high_edge - 1) - low_edge + first

            in_specs.append(pl.BlockSpec((rows, tile), place))
            arrays.append(array)
    return pl.pallas_call(
        functools.partial(combine_kernel, edges),
        grid=(tiles,),
        in_specs=in_specs,
        out_specs=[pl.BlockSpec((rows, tile), lambda j: (0, j)) for _ in outs],
        out_shape=[jax.ShapeDtypeStruct((rows, tiles * tile), dtype) for _ in outs],
        compiler_params=pltpu.CompilerParams(vmem_limit_bytes=16 * MIB),
        cost_estimate=FREE,
        name="combine",
    )(*arrays)


def turn_kernel(turn_ref, own_ref, par_ref, out_ref, scr):
    own_rows, model = own_ref.shape
    step = BLOCK // 2
    for number, ref in enumerate((own_ref, par_ref)):

        @pl.loop(0, own_rows // step)
        def _(part, ref=ref, number=number):
            start = pl.multiple_of(part * step, step)
            place = pl.multiple_of(start + number * own_rows, step)
            scr[:, pl.ds(place, step)] = ref[pl.ds(start, step), :].astype(F32).T.astype(BF16)

    count = turn_ref.shape[0]
    block = model // count

    @pl.loop(0, count)
    def _(i):
        base = pl.multiple_of(turn_ref[i] * block, block)
        place = pl.multiple_of(i * block, block)
        out_ref[pl.ds(place, block), :] = scr[pl.ds(base, block), :]


def turn(turned, own, par):
    own_rows, model = own.shape
    length = 2 * own_rows
    whole = lambda i, t: (0, 0)
    spec = pl.BlockSpec
    return pl.pallas_call(
        turn_kernel,
        grid_spec=pltpu.PrefetchScalarGridSpec(
            num_scalar_prefetch=1,
            grid=(1,),
            in_specs=[spec((own_rows, model), whole)] * 2,
            out_specs=spec((model, length), whole),
            scratch_shapes=[pltpu.VMEM((model, length), BF16)],
        ),
        out_shape=jax.ShapeDtypeStruct((model, length), BF16),
        compiler_params=pltpu.CompilerParams(vmem_limit_bytes=24 * MIB),
        cost_estimate=LONG,
        name="turn",
    )(turned, own, par)


def project(blocks, turned, x_own, x_par, cos, sin, pieces, heads):
    own_rows, model = x_own.shape
    length = 2 * own_rows
    count = len(pieces)
    columns = [column for _, column in pieces]
    pieces = [piece for piece, _ in pieces]
    rows, width = pieces[0].shape
    qkv_width = 2 * heads
    tile = heads // 2
    spec = pl.BlockSpec
    whole = lambda j, s, t: (0, 0)
    anywhere = spec(memory_space=pl.ANY)
    return pl.pallas_call(
        functools.partial(project_kernel, columns, rows, heads),
        grid_spec=pltpu.PrefetchScalarGridSpec(
            num_scalar_prefetch=2,
            grid=(qkv_width // tile,),
            in_specs=[
                spec((own_rows, model), whole),
                spec((own_rows, model), whole),
                spec((HEAD_DIM // 2, length), whole),
                spec((HEAD_DIM // 2, length), whole),
            ]
            + [anywhere] * count,
            out_specs=[
                spec((tile, length), lambda j, s, t: (j, 0)),
                spec((8, model), whole),
                spec(memory_space=pltpu.MemorySpace.HBM),
                spec(memory_space=pltpu.MemorySpace.HBM),
                spec(memory_space=pltpu.MemorySpace.HBM),
            ],
            scratch_shapes=[
                pltpu.VMEM((model, width), BF16),
                pltpu.VMEM((length, model), BF16),
                pltpu.VMEM((model, length), BF16),
                pltpu.SemaphoreType.DMA((count,)),
                pltpu.SemaphoreType.DMA((2,)),
                pltpu.SemaphoreType.DMA(turned.shape),
            ],
        ),
        out_shape=[
            jax.ShapeDtypeStruct((qkv_width, length), BF16),
            jax.ShapeDtypeStruct((8, model), F32),
            jax.ShapeDtypeStruct((model, length), BF16),
            jax.ShapeDtypeStruct((model, qkv_width), BF16),
            jax.ShapeDtypeStruct((model, heads), BF16),
        ],
        compiler_params=pltpu.CompilerParams(vmem_limit_bytes=40 * MIB),
        cost_estimate=FREE,
        name="project",
    )(blocks, turned, x_own, x_par, cos, sin, *pieces)


def ffn_kernel(columns, rows, ff, block_ref, b_own, b_par, e_own, e_par, *rest):
    count = len(columns)
    pieces = rest[:count]
    hidden_ref, pair_ref, own_ref, par_ref, down_ref = rest[count : count + 5]
    b_scr, e_scr, w_scr, total, sem, save_sem = rest[count + 5 :]
    step = pl.program_id(0)
    tiles = pl.num_programs(0)
    slot = lax.rem(step, 2)
    width = hidden_ref.shape[1]
    half = b_own.shape[0]

    def fetch(number, into):
        for kind in range(3):
            for i in range(count):
                base = pl.multiple_of(block_ref[i] * rows, rows)
                column = pl.multiple_of(kind * ff + number * width, 128)
                low_edge, high_edge = columns[i], columns[i] + pieces[i].shape[1]

                def start(i=i, base=base, column=column, kind=kind):
                    pltpu.make_async_copy(
                        pieces[i].at[:, pl.ds(pl.multiple_of(column - columns[i], 128), width)],
                        w_scr.at[into, pl.ds(base, rows), kind * width : (kind + 1) * width],
                        sem.at[into],
                    ).start()

                if low_edge <= kind * ff and (kind + 1) * ff <= high_edge:
                    start()
                elif low_edge < (kind + 1) * ff and kind * ff < high_edge:
                    pl.when((column >= low_edge) & (column < high_edge))(start)

    def saved(number, source):
        column = pl.multiple_of(number * width, 128)
        return pltpu.make_async_copy(
            w_scr.at[source, :, 2 * width :], down_ref.at[:, pl.ds(column, width)], save_sem.at[source]
        )

    @pl.when(step == 0)
    def _():
        fetch(0, 0)
        for target, own, par in ((b_scr, b_own, b_par), (e_scr, e_own, e_par)):
            target[:half, :] = own[...]
            target[half:, :] = par[...]

    @pl.when(step > 0)
    def _():
        saved(step - 1, 1 - slot).wait()

    @pl.when(step + 1 < tiles)
    def _():
        fetch(step + 1, 1 - slot)

    pltpu.make_async_copy(w_scr.at[slot], w_scr.at[slot], sem.at[slot]).wait()
    saved(step, slot).start()
    first = mm(b_scr[...], w_scr[slot, :, : 2 * width], 1, 0)
    gate, up = first[:, :width], first[:, width:]
    dhid = mm(e_scr[...], w_scr[slot, :, 2 * width :], 1, 0)
    sig = 1.0 / (1.0 + jnp.exp(-gate))
    silu = gate * sig
    hidden_ref[...] = (silu * up).astype(BF16)
    dgate = (dhid * up * (sig * (1.0 + gate * (1.0 - sig)))).astype(BF16)
    dup = (dhid * silu).astype(BF16)
    pair_ref[:, :width] = dgate
    pair_ref[:, width:] = dup
    part = mm(pair_ref[...], w_scr[slot, :, : 2 * width], 1, 1)

    @pl.when(step == 0)
    def _():
        total[...] = part

    @pl.when((step > 0) & (step < tiles - 1))
    def _():
        total[...] += part

    @pl.when(step == tiles - 1)
    def _():
        own_ref[...] = (total[:half, :] + part[:half, :]).astype(BF16)
        par_ref[...] = (total[half:, :] + part[half:, :]).astype(BF16)
        saved(step, slot).wait()


def ffn(blocks, b_own, b_par, e_own, e_par, pieces):
    half, model = b_own.shape
    count = len(pieces)
    columns = [column for _, column in pieces]
    pieces = [piece for piece, _ in pieces]
    rows = pieces[0].shape[0]
    ff = max(piece.shape[1] + column for piece, column in zip(pieces, columns)) // 3
    spec = pl.BlockSpec
    whole = lambda j, s: (0, 0)
    anywhere = spec(memory_space=pl.ANY)
    once = spec((half, model), whole, pipeline_mode=pl.Buffered(1))
    return pl.pallas_call(
        functools.partial(ffn_kernel, columns, rows, ff),
        grid_spec=pltpu.PrefetchScalarGridSpec(
            num_scalar_prefetch=1,
            grid=(ff // TILE,),
            in_specs=[once] * 4 + [anywhere] * count,
            out_specs=[
                spec((2 * half, TILE), lambda j, s: (0, j)),
                spec((2 * half, 2 * TILE), lambda j, s: (0, j)),
                once,
                once,
                anywhere,
            ],
            scratch_shapes=[
                pltpu.VMEM((2 * half, model), BF16),
                pltpu.VMEM((2 * half, model), BF16),
                pltpu.VMEM((2, model, 3 * TILE), BF16),
                pltpu.VMEM((2 * half, model), F32),
                pltpu.SemaphoreType.DMA((2,)),
                pltpu.SemaphoreType.DMA((2,)),
            ],
        ),
        out_shape=[
            jax.ShapeDtypeStruct((2 * half, ff), BF16),
            jax.ShapeDtypeStruct((2 * half, 2 * ff), BF16),
            jax.ShapeDtypeStruct((half, model), BF16),
            jax.ShapeDtypeStruct((half, model), BF16),
            jax.ShapeDtypeStruct((model, ff), BF16),
        ],
        compiler_params=pltpu.CompilerParams(vmem_limit_bytes=60 * MIB),
        cost_estimate=FREE,
        name="ffn",
    )(blocks, b_own, b_par, e_own, e_par, *pieces)


def place_of(natural, side, length):
    return pl.multiple_of((natural + side * (length // 2)) & (length - 1), BLOCK)


def diagonal():
    keys = lax.broadcasted_iota(jnp.int32, (BLOCK, BLOCK), 0)
    queries = lax.broadcasted_iota(jnp.int32, (BLOCK, BLOCK), 1)
    return keys <= queries


def fill(scratch, rows, side, docs):
    length = rows.shape[1]
    half = length // 2
    scratch[HEAD_DIM:, :] = jnp.zeros((PAD_DIM - HEAD_DIM, length), BF16)
    if docs is not None:
        scratch[HEAD_DIM : HEAD_DIM + DOCS, :] = docs[...]
    for part in range(2):
        there = pl.ds(place_of(part * half, side, length), half)
        scratch[:HEAD_DIM, part * half : (part + 1) * half] = rows[:, there]


def forward_kernel(
    side_ref, q_in, k_in, v_in, oq_ref, ok_ref, *rest
):
    att_ref, lse_ref, q_scr, kt_scr, k_scr, v_scr = rest[-6:]
    length = q_in.shape[1]
    side = side_ref[0]
    blocks = length // BLOCK
    fill(kt_scr, k_in, side, ok_ref)
    fill(v_scr, v_in, side, None)
    k_scr[...] = kt_scr[...].T
    causal = diagonal()
    for h in range(2):
        rows = slice(h * HEAD_DIM, (h + 1) * HEAD_DIM)
        fill(q_scr, q_in.at[rows, :], side, oq_ref)
        for b in range(blocks):
            here = pl.ds(b * BLOCK, BLOCK)
            keys = (b + 1) * BLOCK
            query = q_scr[:, here]
            last = mm(k_scr[b * BLOCK : keys, :], query, 1, 0)
            last = jnp.where(causal, last, -FAR)
            top = jnp.max(last, 0, keepdims=True)
            if b:
                early = mm(k_scr[: b * BLOCK, :], query, 1, 0)
                top = jnp.maximum(top, jnp.max(early, 0, keepdims=True))
            top = top * (SCALE * LOG2E)
            weight = jnp.exp2(last * (SCALE * LOG2E) - top)
            total = jnp.sum(weight, 0, keepdims=True)
            out = mm(v_scr[:HEAD_DIM, b * BLOCK : keys], weight.astype(BF16), 1, 0)
            if b:
                weight = jnp.exp2(early * (SCALE * LOG2E) - top)
                total = total + jnp.sum(weight, 0, keepdims=True)
                out = out + mm(v_scr[:HEAD_DIM, : b * BLOCK], weight.astype(BF16), 1, 0)
            out = out / total
            there = pl.ds(place_of(b * BLOCK, side, length), BLOCK)
            att_ref[rows, there] = out.astype(BF16)
            lse_ref[0, h : h + 1, here] = top + jnp.log2(total)


def group_specs(groups, length):
    spec = pl.BlockSpec
    return [
        spec((2 * HEAD_DIM, length), lambda g, s: (g, 0)),
        spec((HEAD_DIM, length), lambda g, s: (2 * groups + g, 0)),
        spec((HEAD_DIM, length), lambda g, s: (3 * groups + g, 0)),
    ]


def attend(side, qkv, doc_q, doc_k):
    hidden, length = qkv.shape
    groups = hidden // (4 * HEAD_DIM)
    whole = lambda g, s: (0, 0)
    spec = pl.BlockSpec
    return pl.pallas_call(
        forward_kernel,
        grid_spec=pltpu.PrefetchScalarGridSpec(
            num_scalar_prefetch=1,
            grid=(groups,),
            in_specs=group_specs(groups, length) + [spec((DOCS, length), whole)] * 2,
            out_specs=[
                spec((2 * HEAD_DIM, length), lambda g, s: (g, 0)),
                spec((1, 2, length), lambda g, s: (g, 0, 0)),
            ],
            scratch_shapes=[
                pltpu.VMEM((PAD_DIM, length), BF16),
                pltpu.VMEM((PAD_DIM, length), BF16),
                pltpu.VMEM((length, PAD_DIM), BF16),
                pltpu.VMEM((PAD_DIM, length), BF16),
            ],
        ),
        out_shape=[
            jax.ShapeDtypeStruct((2 * groups * HEAD_DIM, length), BF16),
            jax.ShapeDtypeStruct((groups, 2, length), F32),
        ],
        compiler_params=pltpu.CompilerParams(vmem_limit_bytes=24 * MIB),
        cost_estimate=FREE,
        name="attend",
    )(side, qkv, qkv, qkv, doc_q, doc_k)


def backward_kernel(
    side_ref, q_ref, k_ref, v_ref, att_ref, datt_own, datt_par, lse_ref, cos_ref, sin_ref,
    oq_ref, ok_ref, *rest,
):
    out_ref, *rest = rest
    q_scr, kt_scr, k_scr, vt_scr, v_scr, do_scr, dk_scr, dv_scr, datt_ref, dq_ref, sem = rest
    length = q_ref.shape[1]
    group = pl.program_id(0)
    groups = out_ref.shape[0] // (4 * HEAD_DIM)
    datt_ref[:, : length // 2] = datt_own[...]
    datt_ref[:, length // 2 :] = datt_par[...]
    slot = lax.rem(group, 2)
    dk_ref = dq_ref.at[slot, 2 * HEAD_DIM : 3 * HEAD_DIM, :]
    dv_ref = dq_ref.at[slot, 3 * HEAD_DIM :, :]
    dq_ref = dq_ref.at[slot]

    def stores(number, source):
        for i, (start, size) in enumerate(((0, 2), (2, 1), (3, 1))):
            base = (start * groups + number * size) * HEAD_DIM
            yield pltpu.make_async_copy(
                rest[-2].at[source, start * HEAD_DIM : (start + size) * HEAD_DIM, :],
                out_ref.at[pl.ds(pl.multiple_of(base, HEAD_DIM), size * HEAD_DIM), :],
                sem.at[source, i],
            )

    half = HEAD_DIM // 2
    side = side_ref[0]
    blocks = length // BLOCK
    fill(kt_scr, k_ref, side, ok_ref)
    fill(vt_scr, v_ref, side, None)
    k_scr[...] = kt_scr[...].T
    v_scr[...] = vt_scr[...].T
    causal = diagonal()
    for h in range(2):
        rows = slice(h * HEAD_DIM, (h + 1) * HEAD_DIM)
        fill(q_scr, q_ref.at[rows, :], side, oq_ref)
        fill(do_scr, datt_ref.at[rows, :], side, None)
        for b in range(blocks):
            here = pl.ds(b * BLOCK, BLOCK)
            there = pl.ds(place_of(b * BLOCK, side, length), BLOCK)
            base = jnp.sum(
                datt_ref[rows, there].astype(F32) * att_ref[rows, there].astype(F32), 0, keepdims=True
            )
            keys = (b + 1) * BLOCK
            query, upstream = q_scr[:, here], do_scr[:, here]
            level = lse_ref[0, h : h + 1, here]
            dq = None
            for start, stop in ((b * BLOCK, keys), (0, b * BLOCK)):
                if start == stop:
                    continue
                span = slice(start, stop)
                score = mm(k_scr[span, :], query, 1, 0)
                prob = jnp.exp2(score * (SCALE * LOG2E) - level)
                if stop == keys:
                    prob = jnp.where(causal, prob, 0.0)
                slope = mm(v_scr[span, :], upstream, 1, 0)
                ds = (prob * (slope - base)).astype(BF16)
                part = mm(kt_scr[:HEAD_DIM, span], ds, 1, 0)
                dq = part if dq is None else dq + part
                dk = mm(query[:HEAD_DIM, :], ds, 1, 1)
                dv = mm(upstream[:HEAD_DIM, :], prob.astype(BF16), 1, 1)
                if h == 0 and stop == keys:
                    dk_scr[:, span] = dk
                    dv_scr[:, span] = dv
                else:
                    dk_scr[:, span] += dk
                    dv_scr[:, span] += dv
            cos, sin = cos_ref[:, there], sin_ref[:, there]
            dq = dq * SCALE
            top, bottom = rope_rows(dq[:half, :], dq[half:, :], cos, -sin)
            dq_ref[h * HEAD_DIM : h * HEAD_DIM + half, there] = top.astype(BF16)
            dq_ref[h * HEAD_DIM + half : (h + 1) * HEAD_DIM, there] = bottom.astype(BF16)
    for b in range(blocks):
        here = pl.ds(b * BLOCK, BLOCK)
        there = pl.ds(place_of(b * BLOCK, side, length), BLOCK)
        cos, sin = cos_ref[:, there], sin_ref[:, there]
        dk = dk_scr[:, here] * SCALE
        top, bottom = rope_rows(dk[:half, :], dk[half:, :], cos, -sin)
        dk_ref[:half, there] = top.astype(BF16)
        dk_ref[half:, there] = bottom.astype(BF16)
        dv_ref[:, there] = dv_scr[:, here].astype(BF16)
    for copy in stores(group, slot):
        copy.start()

    @pl.when(group > 0)
    def _():
        for copy in stores(group - 1, 1 - slot):
            copy.wait()

    @pl.when(group == pl.num_programs(0) - 1)
    def _():
        for copy in stores(group, slot):
            copy.wait()


def attend_back(side, qkv, att, datt, lse, cos, sin, doc_q, doc_k):
    hidden, length = qkv.shape
    groups = hidden // (4 * HEAD_DIM)
    whole = lambda g, s: (0, 0)
    spec = pl.BlockSpec
    narrow = spec((2 * HEAD_DIM, length // 2), lambda g, s: (g, 0))
    source = spec((2 * HEAD_DIM, length), lambda g, s: (g, 0))
    level = spec((1, 2, length), lambda g, s: (g, 0, 0))
    anywhere = spec(memory_space=pl.ANY)
    table = spec((HEAD_DIM // 2, length), whole)
    docs = spec((DOCS, length), whole)
    tall = pltpu.VMEM((length, PAD_DIM), BF16)
    flat = pltpu.VMEM((PAD_DIM, length), BF16)
    return pl.pallas_call(
        backward_kernel,
        grid_spec=pltpu.PrefetchScalarGridSpec(
            num_scalar_prefetch=1,
            grid=(groups,),
            in_specs=group_specs(groups, length)
            + [source, narrow, narrow, level, table, table, docs, docs],
            out_specs=anywhere,
            scratch_shapes=[flat, flat, tall, flat, tall, flat]
            + [pltpu.VMEM((HEAD_DIM, length), F32)] * 2
            + [
                pltpu.VMEM((2 * HEAD_DIM, length), BF16),
                pltpu.VMEM((2, 4 * HEAD_DIM, length), BF16),
                pltpu.SemaphoreType.DMA((2, 3)),
            ],
        ),
        out_shape=jax.ShapeDtypeStruct((hidden, length), BF16),
        compiler_params=pltpu.CompilerParams(vmem_limit_bytes=32 * MIB),
        cost_estimate=FREE,
        name="attend_back",
    )(side, qkv, qkv, qkv, att, *datt, lse, cos, sin, doc_q, doc_k)


def low(weight):
    return weight.astype(BF16)


def layer(
    dp, tokens, segment_ids, positions, query_weight, key_weight, value_weight, out_weight,
    attn_gain, gate_weight, up_weight, down_weight, mlp_gain, cotangent,
):
    seqs, own_rows, model = tokens.shape
    length = segment_ids.shape[1]
    heads = query_weight.shape[1]
    ff = gate_weight.shape[1]
    side_index = lax.axis_index("tensor").astype(jnp.int32)
    side = side_index[None]
    blocks, turned = piece_blocks(dp), turn_blocks(dp)

    x_own = tokens.reshape(own_rows, model)
    e_own = cotangent.reshape(own_rows, model)
    gains = jnp.pad(jnp.stack([low(attn_gain), low(mlp_gain)], 1), ((0, 0), (0, 126)))
    order = Order(positions[0, 0] >= 0)
    first = order.done(join(query_weight, key_weight, value_weight, out_weight.T, gains))
    first = Gather(first, dp, 1280)
    x_par = swap_halves(x_own)
    first.round(order)
    first.share(order)
    places = positions.reshape(length).astype(F32)
    half = HEAD_DIM // 2
    places = jnp.where(side_index == 0, places, jnp.roll(places, length // 2))
    ladder = jnp.power(F32(ROPE_BASE), -2.0 * jnp.arange(half, dtype=F32) / HEAD_DIM)
    angles = ladder[:, None] * places[None, :]
    cos, sin = jnp.cos(angles), jnp.sin(angles)
    cos, sin = order.done(cos, sin)
    second = order.done(join(gate_weight, up_weight, down_weight.T))
    second = Gather(second, dp, 3 * ff // 2)
    for _ in range(dp // 4 - 1):
        first.next(order)
    second.share(order)
    first = first.pieces(order)
    x_first, x_par = order.done(*order.tie(x_own, x_par))
    e_par = swap_halves(order.tie(e_own))
    second.round(order)

    known = jnp.arange(DOCS, dtype=jnp.int32)[:, None] == segment_ids.reshape(1, length)
    doc_q = known.astype(BF16)
    doc_k = jnp.where(known, 0.0, -FAR).astype(BF16)

    qkv, gain_rows, a_turned, qkv_full, out_full = project(
        blocks, turned, x_first, x_par, cos, sin, first, heads
    )
    qkv = order.done(qkv)
    att, lse = attend(side, order.tie(qkv), doc_q, doc_k)
    att = order.done(att)

    own, par = slice(0, own_rows), slice(own_rows, None)
    partial = order.done(mm(att[:, par], out_full, 0, 1, BF16))
    sent = swap_halves(partial)
    e_par = order.done(e_par)
    second.next(order)
    e_turned = order.done(turn(turned, order.tie(e_own), e_par))
    partial = order.done(mm(att[:, own], order.tie(out_full), 0, 1, BF16))
    second.next(order)
    sent = order.tie(sent)
    middle, b_own = order.done(
        *by_rows(residual_kernel, (partial, sent, x_own), gain_rows, (BF16, BF16), "residual")
    )
    b_par = swap_halves(b_own)
    second.next(order)
    second = second.pieces(order)

    b_par = order.tie(b_par)
    hidden, pair, db_own, db_par, down_full = ffn(blocks, b_own, b_par, e_own, e_par, second)
    db_par = order.done(db_par)
    db_sent = swap_halves(db_par)
    b_turned = order.done(turn(turned, order.tie(b_own), b_par))
    grad_ffn = Scatter(dp, order, (e_turned, hidden, 0), (b_turned, pair, 0))
    eh_own = order.done(
        *by_rows(
            functools.partial(back_kernel, 1),
            (db_own, order.tie(db_sent), middle, e_own),
            gain_rows,
            (BF16,),
            "norm_back",
        )
    )
    eh_par = swap_halves(eh_own)
    grad_ffn.round()
    down_own, down_par = order.done(*product(order.tie(hidden), down_full))
    grad_ffn.round()
    datt_own = order.done(turned_product(order.tie(eh_own), out_full, 384))
    eh_par = order.tie(eh_par)
    datt_par = order.done(turned_product(eh_par, out_full, 384))
    down_sent = swap_halves(order.tie(down_par))
    eh_turned = order.done(turn(turned, order.tie(eh_own), eh_par))
    grad_ffn.round()
    datt = order.tie(datt_own, datt_par)
    dqkv = order.done(attend_back(side, qkv, att, datt, lse, cos, sin, doc_q, doc_k))
    down_sent = order.done(down_sent)
    da_par = order.done(turned_product(qkv_full, order.tie(dqkv), own_rows, 1, 1))
    da_sent = swap_halves(da_par)
    grad_ffn.round()
    grad_att = Scatter(dp, order, (a_turned, dqkv, 1), (eh_turned, att, 1))
    grad_att.round()
    output = (middle.astype(F32) + (down_own.astype(F32) + order.tie(down_sent).astype(F32))).astype(BF16)
    output = order.done(output)
    da_own = order.done(turned_product(qkv_full, order.tie(dqkv), own_rows, 0, 1))
    grad_ffn.arrive()
    grad_att.round()
    grad_gate, grad_up, grad_down, gain_two = grad_ffn.result(
        (
            (ff, TILE, 2 * TILE, ff // TILE),
            (ff + TILE, TILE, 2 * TILE, ff // TILE),
            (0, TILE, TILE, ff // TILE),
        ),
        (gate_weight, up_weight),
    )
    da_sent = order.done(da_sent)
    grad_att.round()
    (input_grad,) = by_rows(
        functools.partial(back_kernel, 0),
        (order.tie(da_own), da_sent, x_own, eh_own),
        gain_rows,
        (BF16,),
        "norm_back",
    )
    input_grad = order.done(input_grad)
    grad_att.round()
    kv = heads // 2
    size = kv // 3 if kv % 384 else 384
    grad_query, grad_key, grad_value, grad_out, gain_one = grad_att.result(
        (
            (0, size, size, heads // size),
            (heads, size, size, kv // size),
            (heads + kv, size, size, kv // size),
            (2 * heads, size, size, heads // size),
        ),
        (query_weight, key_weight, value_weight),
    )
    gain_grads = jnp.stack(
        [gain_one[0] / low(attn_gain).astype(F32), gain_two[0] / low(mlp_gain).astype(F32)]
    )
    gain_grads = gain_grads + swap_halves(gain_grads)
    return (
        output.reshape(seqs, own_rows, model),
        input_grad.reshape(seqs, own_rows, model),
        grad_query,
        grad_key,
        grad_value,
        grad_out.T,
        gain_grads[0],
        grad_gate,
        grad_up,
        grad_down.T,
        gain_grads[1],
    )


def solution(mesh):
    in_specs = (
        P("dp", "tensor", None),
        P("dp", None),
        P("dp", None),
        P("dp", "tensor"),
        P("dp", "tensor"),
        P("dp", "tensor"),
        P("tensor", "dp"),
        P("dp"),
        P("dp", "tensor"),
        P("dp", "tensor"),
        P("tensor", "dp"),
        P("dp"),
        P("dp", "tensor", None),
    )
    out_specs = (
        P("dp", "tensor", None),
        P("dp", "tensor", None),
        P("dp", "tensor"),
        P("dp", "tensor"),
        P("dp", "tensor"),
        P("tensor", "dp"),
        P("dp"),
        P("dp", "tensor"),
        P("dp", "tensor"),
        P("tensor", "dp"),
        P("dp"),
    )
    return jax.shard_map(
        functools.partial(layer, mesh.shape["dp"]),
        mesh=mesh,
        in_specs=in_specs,
        out_specs=out_specs,
        check_vma=False,
    )
```

```python
import functools
import math

import jax
import jax.numpy as jnp
from jax import lax
from jax.experimental import pallas as pl
from jax.experimental.pallas import tpu as pltpu
from jax.sharding import PartitionSpec as P

HEAD_DIM = 96
PAD_DIM = 128
BLOCK = 256
DOCS = 16
EPSILON = 1e-05
ROPE_BASE = 100000.0
FAR = float(2**30)
RING_LIMIT = 16
TILE = 512
MIB = 2**20
SCALE = 1.0 / math.sqrt(HEAD_DIM)
LOG2E = math.log2(math.e)

F32 = jnp.float32
BF16 = jnp.bfloat16


def mm(left, right, left_dim, right_dim, dtype=F32):
    return lax.dot_general(
        left, right, (((left_dim,), (right_dim,)), ((), ())), preferred_element_type=F32
    ).astype(dtype)


def swap_halves(value):
    return lax.ppermute(value, "tensor", [(0, 1), (1, 0)])


def is_ring(dp):
    return 8 <= dp <= RING_LIMIT and dp & (dp - 1) == 0


def chip_of(spot, chips):
    return jnp.where(2 * spot < chips, 2 * spot, 2 * (chips - 1 - spot) + 1)


def ring_pairs(dp):
    chips = dp // 2
    order = list(range(0, chips, 2)) + list(range(chips - 1, 0, -2))
    ahead = []
    for spot in range(chips):
        here, following = order[spot], order[(spot + 1) % chips]
        ahead += [(2 * here, 2 * following), (2 * here + 1, 2 * following + 1)]
    return ahead, [(b, a) for a, b in ahead]


def ring_place(dp):
    chips = dp // 2
    me = lax.axis_index("dp").astype(jnp.int32)
    chip = me >> 1
    return me & 1, jnp.where(chip & 1 == 0, chip >> 1, chips - 1 - (chip >> 1))


def piece_steps(dp):
    reach = dp // 4
    return [0, *range(-1, -reach, -1), *range(1, reach), reach, reach]


def piece_blocks(dp):
    if not is_ring(dp):
        return jnp.zeros((1,), jnp.int32)
    chips = dp // 2
    core, spot = ring_place(dp)
    chip = chip_of((spot + jnp.asarray(piece_steps(dp), jnp.int32)) & (chips - 1), chips)
    return jnp.concatenate([2 * chip + core, 2 * chip + 1 - core])


def turn_blocks(dp):
    if not is_ring(dp):
        return jnp.zeros((1,), jnp.int32)
    chips = dp // 2
    core, spot = ring_place(dp)
    chip = chip_of((spot + jnp.arange(chips, dtype=jnp.int32)) & (chips - 1), chips)
    return jnp.concatenate([2 * chip + 1 - core, 2 * chip + core])


class Order:
    def __init__(self, flag):
        self.token = lax.create_token()
        self.flag = flag

    def tie(self, *values):
        tied = lax.optimization_barrier((self.token, *values))[1:]
        return tied if len(values) > 1 else tied[0]

    def done(self, *values):
        self.token, *values = lax.optimization_barrier((self.token, *values))
        return values if len(values) > 1 else values[0]


class Gather:
    def __init__(self, shard, dp, cut):
        self.dp, self.cut = dp, cut
        self.behind, self.ahead, self.other, self.shard = [], [], [], shard

    def share(self, order):
        if not is_ring(self.dp):
            return
        found = (self.behind[-1], self.ahead[-1]) if self.other else (self.shard,)
        swap = [(i, i ^ 1) for i in range(self.dp)]

        def both(*pieces):
            return tuple(lax.ppermute(piece, "dp", swap) for piece in pieces)

        def neither(*pieces):
            return tuple(jnp.zeros_like(piece) for piece in pieces)

        found = order.tie(*found) if len(found) > 1 else (order.tie(*found),)
        got = lax.cond(order.flag, both, neither, *found)
        self.other.append(order.done(*got) if len(got) > 1 else [order.done(*got)])

    def round(self, order):
        if not is_ring(self.dp):
            return
        forth, back = ring_pairs(self.dp)
        left = self.behind[-1] if self.behind else self.shard
        right = self.ahead[-1] if self.ahead else self.shard
        left, right = order.tie(left, right)
        if len(self.behind) == self.dp // 4 - 1:
            left, right = halves(left, right, self.cut)
        left, right = order.done(left, right)
        self.behind.append(lax.ppermute(left, "dp", forth))
        self.ahead.append(lax.ppermute(right, "dp", back))

    def arrive(self, order):
        if is_ring(self.dp):
            self.behind[-1], self.ahead[-1] = order.done(self.behind[-1], self.ahead[-1])

    def next(self, order):
        if not is_ring(self.dp):
            return
        self.arrive(order)
        arrived = self.behind[-1], self.ahead[-1]
        self.round(order)
        sent = self.behind.pop(), self.ahead.pop()
        self.behind[-1], self.ahead[-1] = arrived
        self.share(order)
        self.behind.append(sent[0])
        self.ahead.append(sent[1])

    def pieces(self, order):
        if not is_ring(self.dp):
            return [(lax.all_gather(self.shard, "dp", axis=0, tiled=True), 0)]
        self.arrive(order)
        self.share(order)
        held = [self.shard, *self.behind[:-1], *self.ahead[:-1], self.behind[-1], self.ahead[-1]]
        other = [self.other[0][0], *(pair[0] for pair in self.other[1:-1])]
        other += [*(pair[1] for pair in self.other[1:-1]), *self.other[-1]]
        columns = [0] * (len(held) - 1) + [self.cut]
        return list(zip([*held, *other], columns * 2))


class Scatter:
    def __init__(self, dp, order, *columns):
        self.dp, self.order = dp, order
        lefts, rights, dims = zip(*columns)
        rights = order.tie(*rights) if len(rights) > 1 else (order.tie(*rights),)
        if not is_ring(dp):
            full = order.done(products(0, 1, lefts, rights, dims))
            self.total = lax.psum_scatter(full, "dp", scatter_dimension=0, tiled=True).astype(F32)
            return
        self.chips = dp // 2
        self.reach = self.chips // 2
        self.rows = lefts[0].shape[0] // dp

        def both(lefts, rights):
            token = lax.create_token()
            theirs = products(0, 2, lefts, rights, dims)
            token, theirs = lax.optimization_barrier((token, theirs))
            got = lax.ppermute(theirs, "dp", [(i, i ^ 1) for i in range(dp)])
            rights = lax.optimization_barrier((token, *rights))[1:]
            return got, products(1, 2, lefts, rights, dims)

        def neither(lefts, rights):
            width = sum(right.shape[1 - dim] for right, dim in zip(rights, dims))
            return (jnp.zeros((lefts[0].shape[0] // 2, width), BF16),) * 2

        self.got, self.mine = order.done(*lax.cond(order.flag, both, neither, lefts, tuple(rights)))
        self.width = self.mine.shape[1]
        self.ahead = self.behind = None

    def local(self, steps, mine, first, low_edge, high_edge):
        block = steps % self.chips
        return [(part, block, first, low_edge, high_edge) for part in (mine, self.got)]

    def round(self):
        if not is_ring(self.dp):
            return
        forth, back = ring_pairs(self.dp)
        half = self.width // 2
        tile = half if half <= 3072 else half // 2
        count = half // tile
        mine = self.order.tie(self.mine)
        reach = self.reach
        if self.ahead is None:
            right = self.local(reach, mine, 0, 0, count)
            left = self.local(reach, mine, count, 0, count)
        else:
            if self.ahead.shape[1] > half and self.width <= 3072:
                tile, cut = self.width, 1
            else:
                cut = count if self.ahead.shape[1] == half else 2 * count
            steps = self.width // tile
            right = [*self.local(reach, mine, 0, 0, steps), (self.ahead, 0, 0, 0, cut)]
            left = [*self.local(-reach, mine, 0, 0, steps)]
            left.append((self.behind, 0, 0, steps - cut, steps))
        right, left = self.order.done(*combine(self.rows, tile, [right, left]))
        self.ahead = lax.ppermute(right, "dp", forth)
        self.behind = lax.ppermute(left, "dp", back)
        self.reach -= 1

    def arrive(self):
        if is_ring(self.dp):
            self.ahead, self.behind = self.order.done(self.ahead, self.behind)

    def result(self, pieces, weights):
        if not is_ring(self.dp):
            parts = [self.total] + [jnp.zeros_like(self.total)] * 3
        else:
            parts = [self.order.tie(self.mine), self.got, self.ahead, self.behind]
        return self.order.done(*finish(parts, [0] * 4, pieces, weights))


def rope_rows(top, bottom, cos, sin):
    return top * cos - bottom * sin, bottom * cos + top * sin


def project_kernel(columns, rows, heads, block_ref, turn_ref, own_ref, par_ref, cos_ref, sin_ref, *rest):
    count = len(columns)
    pieces = rest[:count]
    qkv_ref, gain_ref, at_ref, wide_ref, out_ref = rest[count : count + 5]
    w_scr, a_scr, at_scr, in_sem, out_sem, turn_sem = rest[count + 5 :]
    step = pl.program_id(0)
    tiles = pl.num_programs(0)
    own_rows, model = own_ref.shape
    tile = qkv_ref.shape[0]
    half = HEAD_DIM // 2
    qkv_width = 2 * heads

    def loads(i):
        base = pl.multiple_of(block_ref[i] * rows, rows)
        place = slice(columns[i], columns[i] + pieces[i].shape[1])
        return pltpu.make_async_copy(pieces[i], w_scr.at[pl.ds(base, rows), place], in_sem.at[i])

    def stores():
        return (
            pltpu.make_async_copy(w_scr.at[:, :qkv_width], wide_ref, out_sem.at[0]),
            pltpu.make_async_copy(
                w_scr.at[:, qkv_width : qkv_width + heads], out_ref, out_sem.at[1]
            ),
        )

    def turns(i):
        block = model // turn_ref.shape[0]
        base = pl.multiple_of(turn_ref[i] * block, block)
        return pltpu.make_async_copy(
            at_scr.at[pl.ds(base, block), :], at_ref.at[pl.ds(i * block, block), :], turn_sem.at[i]
        )

    @pl.when(step == 0)
    def _():
        for i in range(count):
            loads(i).start()
        for i in range(count):
            loads(i).wait()
        gains = w_scr[:, qkv_width + heads :].astype(F32).T
        gain_ref[...] = gains[:8, :]
        gain = gains[:1, :]
        for number, ref in enumerate((own_ref, par_ref)):

            @pl.loop(0, own_rows // BLOCK)
            def _(part, ref=ref, number=number):
                start = pl.multiple_of(part * BLOCK, BLOCK)
                x = ref[pl.ds(start, BLOCK), :].astype(F32)
                inverse = lax.rsqrt(jnp.mean(x * x, -1, keepdims=True) + EPSILON)
                normed = x * inverse * gain
                place = pl.multiple_of(start + number * own_rows, BLOCK)
                a_scr[pl.ds(place, BLOCK), :] = normed.astype(BF16)
                at_scr[:, pl.ds(place, BLOCK)] = normed.T.astype(BF16)

        for copy in stores():
            copy.start()
        for i in range(turn_ref.shape[0]):
            turns(i).start()

    start = pl.multiple_of(step * tile, 128)
    flat = mm(a_scr[...], w_scr[:, pl.ds(start, tile)], 1, 0).T

    @pl.when(step < tiles - tiles // 4)
    def _():
        cos, sin = cos_ref[...], sin_ref[...]
        for h in range(tile // HEAD_DIM):
            base = h * HEAD_DIM
            top, bottom = rope_rows(
                flat[base : base + half, :], flat[base + half : base + HEAD_DIM, :], cos, sin
            )
            qkv_ref[base : base + half, :] = top.astype(BF16)
            qkv_ref[base + half : base + HEAD_DIM, :] = bottom.astype(BF16)

    @pl.when(step >= tiles - tiles // 4)
    def _():
        qkv_ref[...] = flat.astype(BF16)

    @pl.when(step == tiles - 1)
    def _():
        for copy in stores():
            copy.wait()
        for i in range(turn_ref.shape[0]):
            turns(i).wait()


FREE = pl.CostEstimate(flops=0, bytes_accessed=0, transcendentals=0)
LONG = pl.CostEstimate(flops=0, bytes_accessed=40 * 2**20, transcendentals=0)


def product_kernel(left_ref, right_ref, *out_refs):
    half = left_ref.shape[0] // 2

    @pl.loop(0, 2)
    def _(part):
        start = pl.multiple_of(part * half, half)
        out = mm(left_ref[pl.ds(start, half), :], right_ref[...], 1, 1, BF16)
        for number, ref in enumerate(out_refs):

            @pl.when(part == number)
            def _(ref=ref):
                ref[...] = out


def product(left, right):
    rows, depth = left.shape
    width = right.shape[0]
    tile = next(t for t in (TILE, 384, 256, width) if width % t == 0)
    spec = pl.BlockSpec
    return pl.pallas_call(
        product_kernel,
        grid=(width // tile,),
        in_specs=[spec((rows, depth), lambda j: (0, 0)), spec((tile, depth), lambda j: (j, 0))],
        out_specs=[spec((rows // 2, tile), lambda j: (0, j))] * 2,
        out_shape=[jax.ShapeDtypeStruct((rows // 2, width), BF16)] * 2,
        compiler_params=pltpu.CompilerParams(vmem_limit_bytes=28 * MIB),
        cost_estimate=FREE,
        name="product",
    )(left, right)


def products_kernel(starts, dims, *refs):
    count = len(dims)
    out_ref = refs[-1]
    step = pl.program_id(0)
    for i, dim in enumerate(dims):

        @pl.when((step >= starts[i]) & (step < starts[i + 1]))
        def _(i=i, dim=dim):
            width = out_ref.shape[1]
            size = TILE if width % TILE == 0 else width

            @pl.loop(0, width // size)
            def _(j):
                place = pl.ds(pl.multiple_of(j * size, 128), size)
                right = refs[count + i][place, :] if dim else refs[count + i][:, place]
                out_ref[:, place] = mm(refs[i][...], right, 1, dim, out_ref.dtype)


def products(part, parts, lefts, rights, dims):
    rows, depth = lefts[0].shape
    rows = rows // parts
    widths = [right.shape[1 - dim] for right, dim in zip(rights, dims)]
    tile = next(t for t in (1024, 768, TILE, 384) if all(width % t == 0 for width in widths))
    starts = [0]
    for width in widths:
        starts.append(starts[-1] + width // tile)
    spec = pl.BlockSpec
    in_specs = [spec((rows, depth), lambda j: (part, 0)) for _ in lefts]
    for i, dim in enumerate(dims):

        def place(j, i=i):
            return jnp.clip(j - starts[i], 0, starts[i + 1] - starts[i] - 1)

        if dim:
            in_specs.append(spec((tile, depth), lambda j, place=place: (place(j), 0)))
        else:
            in_specs.append(spec((depth, tile), lambda j, place=place: (0, place(j))))
    return pl.pallas_call(
        functools.partial(products_kernel, starts, dims),
        grid=(starts[-1],),
        in_specs=in_specs,
        out_specs=spec((rows, tile), lambda j: (0, j)),
        out_shape=jax.ShapeDtypeStruct((rows, sum(widths)), BF16),
        compiler_params=pltpu.CompilerParams(vmem_limit_bytes=32 * MIB),
        cost_estimate=FREE,
        name="products",
    )(*lefts, *rights)


def turned_kernel(left_ref, right_ref, out_ref):
    out_ref[...] = mm(left_ref[...], right_ref[...], 1, 0).T.astype(BF16)


def turned_product(left, right, tile, start=0, count=None):
    rows, depth = left.shape
    count = count or right.shape[1] // tile
    spec = pl.BlockSpec
    return pl.pallas_call(
        turned_kernel,
        grid=(count,),
        in_specs=[
            spec((rows, depth), lambda j: (0, 0)),
            spec((depth, tile), lambda j: (0, start + j)),
        ],
        out_specs=spec((tile, rows), lambda j: (j, 0)),
        out_shape=jax.ShapeDtypeStruct((count * tile, rows), BF16),
        compiler_params=pltpu.CompilerParams(vmem_limit_bytes=28 * MIB),
        cost_estimate=FREE,
        name="turned_product",
    )(left, right)


def join_kernel(*refs):
    start = 0
    for ref in refs[:-1]:
        refs[-1][:, start : start + ref.shape[1]] = ref[...].astype(BF16)
        start += ref.shape[1]


def join(*parts):
    rows = parts[0].shape[0]
    return pl.pallas_call(
        join_kernel,
        out_shape=jax.ShapeDtypeStruct((rows, sum(part.shape[1] for part in parts)), BF16),
        compiler_params=pltpu.CompilerParams(vmem_limit_bytes=63 * MIB),
        cost_estimate=FREE,
        name="join",
    )(*parts)


def halves_kernel(left_ref, right_ref, low_ref, high_ref):
    low_ref[...] = left_ref[...]
    high_ref[...] = right_ref[:, right_ref.shape[1] - high_ref.shape[1] :]


def halves(left, right, cut):
    rows, width = left.shape
    rest = width - cut
    spec = pl.BlockSpec
    if cut % rest:
        right_spec = spec((rows, width), lambda i: (0, 0))
    else:
        right_spec = spec((rows, rest), lambda i: (0, cut // rest))
    return pl.pallas_call(
        halves_kernel,
        grid=(1,),
        in_specs=[spec((rows, cut), lambda i: (0, 0)), right_spec],
        out_specs=[spec((rows, cut), lambda i: (0, 0)), spec((rows, rest), lambda i: (0, 0))],
        out_shape=[
            jax.ShapeDtypeStruct((rows, cut), left.dtype),
            jax.ShapeDtypeStruct((rows, rest), left.dtype),
        ],
        compiler_params=pltpu.CompilerParams(vmem_limit_bytes=63 * MIB),
        cost_estimate=FREE,
        name="halves",
    )(left, right)


def residual_kernel(part_ref, sent_ref, x_ref, gain_ref, middle_ref, b_ref):
    middle = part_ref[...].astype(F32) + sent_ref[...].astype(F32)
    middle = x_ref[...].astype(F32) + middle
    inverse = lax.rsqrt(jnp.mean(middle * middle, -1, keepdims=True) + EPSILON)
    middle_ref[...] = middle.astype(middle_ref.dtype)
    b_ref[...] = (middle * inverse * gain_ref[1:2, :]).astype(BF16)


def back_kernel(row, own_ref, sent_ref, value_ref, base_ref, gain_ref, *out_refs):
    upstream = own_ref[...].astype(F32) + sent_ref[...].astype(F32)
    value = value_ref[...].astype(F32)
    inverse = lax.rsqrt(jnp.mean(value * value, -1, keepdims=True) + EPSILON)
    scaled = upstream * gain_ref[row : row + 1, :]
    inner = jnp.mean(scaled * value, -1, keepdims=True)
    out = inverse * (scaled - value * (inverse * inverse * inner))
    out = base_ref[...].astype(F32) + out
    for ref in out_refs:
        ref[...] = out.astype(ref.dtype)


def by_rows(kernel, arrays, gain, dtypes, name):
    rows, width = arrays[0].shape
    step = 256
    block = pl.BlockSpec((step, width), lambda i: (i, 0))
    return pl.pallas_call(
        kernel,
        grid=(rows // step,),
        in_specs=[block] * len(arrays) + [pl.BlockSpec(gain.shape, lambda i: (0, 0))],
        out_specs=[block] * len(dtypes),
        out_shape=[jax.ShapeDtypeStruct((rows, width), dtype) for dtype in dtypes],
        compiler_params=pltpu.CompilerParams(vmem_limit_bytes=63 * MIB),
        cost_estimate=FREE,
        name=name,
    )(*arrays, gain)


def finish_kernel(pieces, weighted, *refs):
    parts, refs = refs[:4], refs[4:]
    weights, refs = refs[:weighted], refs[weighted:]
    outs, gain_ref, total_ref = refs[: len(pieces)], refs[-2], refs[-1]
    total_ref[...] = jnp.zeros_like(total_ref)
    for number, (out_ref, (start, size, stride, steps)) in enumerate(zip(outs, pieces)):

        @pl.loop(0, steps)
        def _(j, number=number, out_ref=out_ref, start=start, size=size, stride=stride):
            source = pl.ds(pl.multiple_of(start + j * stride, 128), size)
            target = pl.ds(pl.multiple_of(j * size, 128), size)
            total = sum(part[:, source].astype(F32) for part in parts)
            out_ref[:, target] = total
            if number < weighted:
                total = total * weights[number][:, target].astype(BF16).astype(F32)
                for k in range(0, size, 128):
                    total_ref[...] += total[:, k : k + 128]

    rows = jnp.broadcast_to(jnp.sum(total_ref[...], 1, keepdims=True), total_ref.shape)
    gain_ref[...] = rows.T[:8, :]


def finish(parts, blocks, pieces, weights):
    rows = weights[0].shape[0]
    width = parts[0].shape[1]
    spec = pl.BlockSpec
    whole = lambda i: (0, 0)
    widths = [size * steps for _, size, _, steps in pieces]
    return pl.pallas_call(
        functools.partial(finish_kernel, pieces, len(weights)),
        grid=(1,),
        in_specs=[spec((rows, width), lambda i, block=block: (block, 0)) for block in blocks]
        + [spec(weight.shape, whole) for weight in weights],
        out_specs=[spec((rows, size), whole) for size in widths] + [spec((8, rows), whole)],
        out_shape=[jax.ShapeDtypeStruct((rows, size), F32) for size in widths]
        + [jax.ShapeDtypeStruct((8, rows), F32)],
        scratch_shapes=[pltpu.VMEM((rows, 128), F32)],
        compiler_params=pltpu.CompilerParams(vmem_limit_bytes=28 * MIB),
        cost_estimate=FREE,
        name="finish",
    )(*parts, *weights)


def combine_kernel(outs, *refs):
    step = pl.program_id(0)
    inputs = list(refs[: -len(outs)])
    for out_ref, terms in zip(refs[-len(outs) :], outs):
        total = None
        for low_edge, high_edge in terms:
            value = inputs.pop(0)[...].astype(F32)
            if high_edge - low_edge < pl.num_programs(0):
                value = jnp.where((step >= low_edge) & (step < high_edge), value, 0.0)
            total = value if total is None else total + value
        out_ref[...] = total.astype(out_ref.dtype)


def combine(rows, tile, outs, dtype=BF16):
    tiles = max(high for terms in outs for *_, high in terms)
    in_specs, arrays, edges = [], [], []
    for terms in outs:
        edges.append([(low_edge, high_edge) for *_, low_edge, high_edge in terms])
        for array, block, first, low_edge, high_edge in terms:

            def place(j, block=block, first=first, low_edge=low_edge, high_edge=high_edge):
                return block, jnp.clip(j, low_edge, high_edge - 1) - low_edge + first

            in_specs.append(pl.BlockSpec((rows, tile), place))
            arrays.append(array)
    return pl.pallas_call(
        functools.partial(combine_kernel, edges),
        grid=(tiles,),
        in_specs=in_specs,
        out_specs=[pl.BlockSpec((rows, tile), lambda j: (0, j)) for _ in outs],
        out_shape=[jax.ShapeDtypeStruct((rows, tiles * tile), dtype) for _ in outs],
        compiler_params=pltpu.CompilerParams(vmem_limit_bytes=16 * MIB),
        cost_estimate=FREE,
        name="combine",
    )(*arrays)


def turn_kernel(turn_ref, own_ref, par_ref, out_ref, scr):
    own_rows, model = own_ref.shape
    step = BLOCK // 2
    for number, ref in enumerate((own_ref, par_ref)):

        @pl.loop(0, own_rows // step)
        def _(part, ref=ref, number=number):
            start = pl.multiple_of(part * step, step)
            place = pl.multiple_of(start + number * own_rows, step)
            scr[:, pl.ds(place, step)] = ref[pl.ds(start, step), :].astype(F32).T.astype(BF16)

    count = turn_ref.shape[0]
    block = model // count

    @pl.loop(0, count)
    def _(i):
        base = pl.multiple_of(turn_ref[i] * block, block)
        place = pl.multiple_of(i * block, block)
        out_ref[pl.ds(place, block), :] = scr[pl.ds(base, block), :]


def turn(turned, own, par):
    own_rows, model = own.shape
    length = 2 * own_rows
    whole = lambda i, t: (0, 0)
    spec = pl.BlockSpec
    return pl.pallas_call(
        turn_kernel,
        grid_spec=pltpu.PrefetchScalarGridSpec(
            num_scalar_prefetch=1,
            grid=(1,),
            in_specs=[spec((own_rows, model), whole)] * 2,
            out_specs=spec((model, length), whole),
            scratch_shapes=[pltpu.VMEM((model, length), BF16)],
        ),
        out_shape=jax.ShapeDtypeStruct((model, length), BF16),
        compiler_params=pltpu.CompilerParams(vmem_limit_bytes=24 * MIB),
        cost_estimate=LONG,
        name="turn",
    )(turned, own, par)


def project(blocks, turned, x_own, x_par, cos, sin, pieces, heads):
    own_rows, model = x_own.shape
    length = 2 * own_rows
    count = len(pieces)
    columns = [column for _, column in pieces]
    pieces = [piece for piece, _ in pieces]
    rows, width = pieces[0].shape
    qkv_width = 2 * heads
    tile = heads // 2
    spec = pl.BlockSpec
    whole = lambda j, s, t: (0, 0)
    anywhere = spec(memory_space=pl.ANY)
    return pl.pallas_call(
        functools.partial(project_kernel, columns, rows, heads),
        grid_spec=pltpu.PrefetchScalarGridSpec(
            num_scalar_prefetch=2,
            grid=(qkv_width // tile,),
            in_specs=[
                spec((own_rows, model), whole),
                spec((own_rows, model), whole),
                spec((HEAD_DIM // 2, length), whole),
                spec((HEAD_DIM // 2, length), whole),
            ]
            + [anywhere] * count,
            out_specs=[
                spec((tile, length), lambda j, s, t: (j, 0)),
                spec((8, model), whole),
                spec(memory_space=pltpu.MemorySpace.HBM),
                spec(memory_space=pltpu.MemorySpace.HBM),
                spec(memory_space=pltpu.MemorySpace.HBM),
            ],
            scratch_shapes=[
                pltpu.VMEM((model, width), BF16),
                pltpu.VMEM((length, model), BF16),
                pltpu.VMEM((model, length), BF16),
                pltpu.SemaphoreType.DMA((count,)),
                pltpu.SemaphoreType.DMA((2,)),
                pltpu.SemaphoreType.DMA(turned.shape),
            ],
        ),
        out_shape=[
            jax.ShapeDtypeStruct((qkv_width, length), BF16),
            jax.ShapeDtypeStruct((8, model), F32),
            jax.ShapeDtypeStruct((model, length), BF16),
            jax.ShapeDtypeStruct((model, qkv_width), BF16),
            jax.ShapeDtypeStruct((model, heads), BF16),
        ],
        compiler_params=pltpu.CompilerParams(vmem_limit_bytes=40 * MIB),
        cost_estimate=FREE,
        name="project",
    )(blocks, turned, x_own, x_par, cos, sin, *pieces)


def ffn_kernel(columns, rows, ff, block_ref, b_own, b_par, e_own, e_par, *rest):
    count = len(columns)
    pieces = rest[:count]
    hidden_ref, pair_ref, own_ref, par_ref, down_ref = rest[count : count + 5]
    b_scr, e_scr, w_scr, total, sem, save_sem = rest[count + 5 :]
    step = pl.program_id(0)
    tiles = pl.num_programs(0)
    slot = lax.rem(step, 2)
    width = hidden_ref.shape[1]
    half = b_own.shape[0]

    def fetch(number, into):
        for kind in range(3):
            for i in range(count):
                base = pl.multiple_of(block_ref[i] * rows, rows)
                column = pl.multiple_of(kind * ff + number * width, 128)
                low_edge, high_edge = columns[i], columns[i] + pieces[i].shape[1]

                def start(i=i, base=base, column=column, kind=kind):
                    pltpu.make_async_copy(
                        pieces[i].at[:, pl.ds(pl.multiple_of(column - columns[i], 128), width)],
                        w_scr.at[into, pl.ds(base, rows), kind * width : (kind + 1) * width],
                        sem.at[into],
                    ).start()

                if low_edge <= kind * ff and (kind + 1) * ff <= high_edge:
                    start()
                elif low_edge < (kind + 1) * ff and kind * ff < high_edge:
                    pl.when((column >= low_edge) & (column < high_edge))(start)

    def saved(number, source):
        column = pl.multiple_of(number * width, 128)
        return pltpu.make_async_copy(
            w_scr.at[source, :, 2 * width :], down_ref.at[:, pl.ds(column, width)], save_sem.at[source]
        )

    @pl.when(step == 0)
    def _():
        fetch(0, 0)
        for target, own, par in ((b_scr, b_own, b_par), (e_scr, e_own, e_par)):
            target[:half, :] = own[...]
            target[half:, :] = par[...]

    @pl.when(step > 0)
    def _():
        saved(step - 1, 1 - slot).wait()

    @pl.when(step + 1 < tiles)
    def _():
        fetch(step + 1, 1 - slot)

    pltpu.make_async_copy(w_scr.at[slot], w_scr.at[slot], sem.at[slot]).wait()
    saved(step, slot).start()
    first = mm(b_scr[...], w_scr[slot, :, : 2 * width], 1, 0)
    gate, up = first[:, :width], first[:, width:]
    dhid = mm(e_scr[...], w_scr[slot, :, 2 * width :], 1, 0)
    sig = 1.0 / (1.0 + jnp.exp(-gate))
    silu = gate * sig
    hidden_ref[...] = (silu * up).astype(BF16)
    dgate = (dhid * up * (sig * (1.0 + gate * (1.0 - sig)))).astype(BF16)
    dup = (dhid * silu).astype(BF16)
    pair_ref[:, :width] = dgate
    pair_ref[:, width:] = dup
    part = mm(pair_ref[...], w_scr[slot, :, : 2 * width], 1, 1)

    @pl.when(step == 0)
    def _():
        total[...] = part

    @pl.when((step > 0) & (step < tiles - 1))
    def _():
        total[...] += part

    @pl.when(step == tiles - 1)
    def _():
        own_ref[...] = (total[:half, :] + part[:half, :]).astype(BF16)
        par_ref[...] = (total[half:, :] + part[half:, :]).astype(BF16)
        saved(step, slot).wait()


def ffn(blocks, b_own, b_par, e_own, e_par, pieces):
    half, model = b_own.shape
    count = len(pieces)
    columns = [column for _, column in pieces]
    pieces = [piece for piece, _ in pieces]
    rows = pieces[0].shape[0]
    ff = max(piece.shape[1] + column for piece, column in zip(pieces, columns)) // 3
    spec = pl.BlockSpec
    whole = lambda j, s: (0, 0)
    anywhere = spec(memory_space=pl.ANY)
    once = spec((half, model), whole, pipeline_mode=pl.Buffered(1))
    return pl.pallas_call(
        functools.partial(ffn_kernel, columns, rows, ff),
        grid_spec=pltpu.PrefetchScalarGridSpec(
            num_scalar_prefetch=1,
            grid=(ff // TILE,),
            in_specs=[once] * 4 + [anywhere] * count,
            out_specs=[
                spec((2 * half, TILE), lambda j, s: (0, j)),
                spec((2 * half, 2 * TILE), lambda j, s: (0, j)),
                once,
                once,
                anywhere,
            ],
            scratch_shapes=[
                pltpu.VMEM((2 * half, model), BF16),
                pltpu.VMEM((2 * half, model), BF16),
                pltpu.VMEM((2, model, 3 * TILE), BF16),
                pltpu.VMEM((2 * half, model), F32),
                pltpu.SemaphoreType.DMA((2,)),
                pltpu.SemaphoreType.DMA((2,)),
            ],
        ),
        out_shape=[
            jax.ShapeDtypeStruct((2 * half, ff), BF16),
            jax.ShapeDtypeStruct((2 * half, 2 * ff), BF16),
            jax.ShapeDtypeStruct((half, model), BF16),
            jax.ShapeDtypeStruct((half, model), BF16),
            jax.ShapeDtypeStruct((model, ff), BF16),
        ],
        compiler_params=pltpu.CompilerParams(vmem_limit_bytes=60 * MIB),
        cost_estimate=FREE,
        name="ffn",
    )(blocks, b_own, b_par, e_own, e_par, *pieces)


def place_of(natural, side, length):
    return pl.multiple_of((natural + side * (length // 2)) & (length - 1), BLOCK)


def diagonal():
    keys = lax.broadcasted_iota(jnp.int32, (BLOCK, BLOCK), 0)
    queries = lax.broadcasted_iota(jnp.int32, (BLOCK, BLOCK), 1)
    return keys <= queries


def fill(scratch, rows, side, docs):
    length = rows.shape[1]
    half = length // 2
    scratch[HEAD_DIM:, :] = jnp.zeros((PAD_DIM - HEAD_DIM, length), BF16)
    if docs is not None:
        scratch[HEAD_DIM : HEAD_DIM + DOCS, :] = docs[...]
    for part in range(2):
        there = pl.ds(place_of(part * half, side, length), half)
        scratch[:HEAD_DIM, part * half : (part + 1) * half] = rows[:, there]


def forward_kernel(
    side_ref, q_in, k_in, v_in, oq_ref, ok_ref, *rest
):
    att_ref, lse_ref, q_scr, kt_scr, k_scr, v_scr = rest[-6:]
    length = q_in.shape[1]
    side = side_ref[0]
    blocks = length // BLOCK
    fill(kt_scr, k_in, side, ok_ref)
    fill(v_scr, v_in, side, None)
    k_scr[...] = kt_scr[...].T
    causal = diagonal()
    for h in range(2):
        rows = slice(h * HEAD_DIM, (h + 1) * HEAD_DIM)
        fill(q_scr, q_in.at[rows, :], side, oq_ref)
        for b in range(blocks):
            here = pl.ds(b * BLOCK, BLOCK)
            keys = (b + 1) * BLOCK
            query = q_scr[:, here]
            last = mm(k_scr[b * BLOCK : keys, :], query, 1, 0)
            last = jnp.where(causal, last, -FAR)
            top = jnp.max(last, 0, keepdims=True)
            if b:
                early = mm(k_scr[: b * BLOCK, :], query, 1, 0)
                top = jnp.maximum(top, jnp.max(early, 0, keepdims=True))
            top = top * (SCALE * LOG2E)
            weight = jnp.exp2(last * (SCALE * LOG2E) - top)
            total = jnp.sum(weight, 0, keepdims=True)
            out = mm(v_scr[:HEAD_DIM, b * BLOCK : keys], weight.astype(BF16), 1, 0)
            if b:
                weight = jnp.exp2(early * (SCALE * LOG2E) - top)
                total = total + jnp.sum(weight, 0, keepdims=True)
                out = out + mm(v_scr[:HEAD_DIM, : b * BLOCK], weight.astype(BF16), 1, 0)
            out = out / total
            there = pl.ds(place_of(b * BLOCK, side, length), BLOCK)
            att_ref[rows, there] = out.astype(BF16)
            lse_ref[0, h : h + 1, here] = top + jnp.log2(total)


def group_specs(groups, length):
    spec = pl.BlockSpec
    return [
        spec((2 * HEAD_DIM, length), lambda g, s: (g, 0)),
        spec((HEAD_DIM, length), lambda g, s: (2 * groups + g, 0)),
        spec((HEAD_DIM, length), lambda g, s: (3 * groups + g, 0)),
    ]


def attend(side, qkv, doc_q, doc_k):
    hidden, length = qkv.shape
    groups = hidden // (4 * HEAD_DIM)
    whole = lambda g, s: (0, 0)
    spec = pl.BlockSpec
    return pl.pallas_call(
        forward_kernel,
        grid_spec=pltpu.PrefetchScalarGridSpec(
            num_scalar_prefetch=1,
            grid=(groups,),
            in_specs=group_specs(groups, length) + [spec((DOCS, length), whole)] * 2,
            out_specs=[
                spec((2 * HEAD_DIM, length), lambda g, s: (g, 0)),
                spec((1, 2, length), lambda g, s: (g, 0, 0)),
            ],
            scratch_shapes=[
                pltpu.VMEM((PAD_DIM, length), BF16),
                pltpu.VMEM((PAD_DIM, length), BF16),
                pltpu.VMEM((length, PAD_DIM), BF16),
                pltpu.VMEM((PAD_DIM, length), BF16),
            ],
        ),
        out_shape=[
            jax.ShapeDtypeStruct((2 * groups * HEAD_DIM, length), BF16),
            jax.ShapeDtypeStruct((groups, 2, length), F32),
        ],
        compiler_params=pltpu.CompilerParams(vmem_limit_bytes=24 * MIB),
        cost_estimate=FREE,
        name="attend",
    )(side, qkv, qkv, qkv, doc_q, doc_k)


def backward_kernel(
    side_ref, q_ref, k_ref, v_ref, att_ref, datt_own, datt_par, lse_ref, cos_ref, sin_ref,
    oq_ref, ok_ref, *rest,
):
    out_ref, *rest = rest
    q_scr, kt_scr, k_scr, vt_scr, v_scr, do_scr, dk_scr, dv_scr, datt_ref, dq_ref, sem = rest
    length = q_ref.shape[1]
    group = pl.program_id(0)
    groups = out_ref.shape[0] // (4 * HEAD_DIM)
    datt_ref[:, : length // 2] = datt_own[...]
    datt_ref[:, length // 2 :] = datt_par[...]
    slot = lax.rem(group, 2)
    dk_ref = dq_ref.at[slot, 2 * HEAD_DIM : 3 * HEAD_DIM, :]
    dv_ref = dq_ref.at[slot, 3 * HEAD_DIM :, :]
    dq_ref = dq_ref.at[slot]

    def stores(number, source):
        for i, (start, size) in enumerate(((0, 2), (2, 1), (3, 1))):
            base = (start * groups + number * size) * HEAD_DIM
            yield pltpu.make_async_copy(
                rest[-2].at[source, start * HEAD_DIM : (start + size) * HEAD_DIM, :],
                out_ref.at[pl.ds(pl.multiple_of(base, HEAD_DIM), size * HEAD_DIM), :],
                sem.at[source, i],
            )

    half = HEAD_DIM // 2
    side = side_ref[0]
    blocks = length // BLOCK
    fill(kt_scr, k_ref, side, ok_ref)
    fill(vt_scr, v_ref, side, None)
    k_scr[...] = kt_scr[...].T
    v_scr[...] = vt_scr[...].T
    causal = diagonal()
    for h in range(2):
        rows = slice(h * HEAD_DIM, (h + 1) * HEAD_DIM)
        fill(q_scr, q_ref.at[rows, :], side, oq_ref)
        fill(do_scr, datt_ref.at[rows, :], side, None)
        for b in range(blocks):
            here = pl.ds(b * BLOCK, BLOCK)
            there = pl.ds(place_of(b * BLOCK, side, length), BLOCK)
            base = jnp.sum(
                datt_ref[rows, there].astype(F32) * att_ref[rows, there].astype(F32), 0, keepdims=True
            )
            keys = (b + 1) * BLOCK
            query, upstream = q_scr[:, here], do_scr[:, here]
            level = lse_ref[0, h : h + 1, here]
            dq = None
            for start, stop in ((b * BLOCK, keys), (0, b * BLOCK)):
                if start == stop:
                    continue
                span = slice(start, stop)
                score = mm(k_scr[span, :], query, 1, 0)
                prob = jnp.exp2(score * (SCALE * LOG2E) - level)
                if stop == keys:
                    prob = jnp.where(causal, prob, 0.0)
                slope = mm(v_scr[span, :], upstream, 1, 0)
                ds = (prob * (slope - base)).astype(BF16)
                part = mm(kt_scr[:HEAD_DIM, span], ds, 1, 0)
                dq = part if dq is None else dq + part
                dk = mm(query[:HEAD_DIM, :], ds, 1, 1)
                dv = mm(upstream[:HEAD_DIM, :], prob.astype(BF16), 1, 1)
                if h == 0 and stop == keys:
                    dk_scr[:, span] = dk
                    dv_scr[:, span] = dv
                else:
                    dk_scr[:, span] += dk
                    dv_scr[:, span] += dv
            cos, sin = cos_ref[:, there], sin_ref[:, there]
            dq = dq * SCALE
            top, bottom = rope_rows(dq[:half, :], dq[half:, :], cos, -sin)
            dq_ref[h * HEAD_DIM : h * HEAD_DIM + half, there] = top.astype(BF16)
            dq_ref[h * HEAD_DIM + half : (h + 1) * HEAD_DIM, there] = bottom.astype(BF16)
    for b in range(blocks):
        here = pl.ds(b * BLOCK, BLOCK)
        there = pl.ds(place_of(b * BLOCK, side, length), BLOCK)
        cos, sin = cos_ref[:, there], sin_ref[:, there]
        dk = dk_scr[:, here] * SCALE
        top, bottom = rope_rows(dk[:half, :], dk[half:, :], cos, -sin)
        dk_ref[:half, there] = top.astype(BF16)
        dk_ref[half:, there] = bottom.astype(BF16)
        dv_ref[:, there] = dv_scr[:, here].astype(BF16)
    for copy in stores(group, slot):
        copy.start()

    @pl.when(group > 0)
    def _():
        for copy in stores(group - 1, 1 - slot):
            copy.wait()

    @pl.when(group == pl.num_programs(0) - 1)
    def _():
        for copy in stores(group, slot):
            copy.wait()


def attend_back(side, qkv, att, datt, lse, cos, sin, doc_q, doc_k):
    hidden, length = qkv.shape
    groups = hidden // (4 * HEAD_DIM)
    whole = lambda g, s: (0, 0)
    spec = pl.BlockSpec
    narrow = spec((2 * HEAD_DIM, length // 2), lambda g, s: (g, 0))
    source = spec((2 * HEAD_DIM, length), lambda g, s: (g, 0))
    level = spec((1, 2, length), lambda g, s: (g, 0, 0))
    anywhere = spec(memory_space=pl.ANY)
    table = spec((HEAD_DIM // 2, length), whole)
    docs = spec((DOCS, length), whole)
    tall = pltpu.VMEM((length, PAD_DIM), BF16)
    flat = pltpu.VMEM((PAD_DIM, length), BF16)
    return pl.pallas_call(
        backward_kernel,
        grid_spec=pltpu.PrefetchScalarGridSpec(
            num_scalar_prefetch=1,
            grid=(groups,),
            in_specs=group_specs(groups, length)
            + [source, narrow, narrow, level, table, table, docs, docs],
            out_specs=anywhere,
            scratch_shapes=[flat, flat, tall, flat, tall, flat]
            + [pltpu.VMEM((HEAD_DIM, length), F32)] * 2
            + [
                pltpu.VMEM((2 * HEAD_DIM, length), BF16),
                pltpu.VMEM((2, 4 * HEAD_DIM, length), BF16),
                pltpu.SemaphoreType.DMA((2, 3)),
            ],
        ),
        out_shape=jax.ShapeDtypeStruct((hidden, length), BF16),
        compiler_params=pltpu.CompilerParams(vmem_limit_bytes=32 * MIB),
        cost_estimate=FREE,
        name="attend_back",
    )(side, qkv, qkv, qkv, att, *datt, lse, cos, sin, doc_q, doc_k)


def low(weight):
    return weight.astype(BF16)


def layer(
    dp, tokens, segment_ids, positions, query_weight, key_weight, value_weight, out_weight,
    attn_gain, gate_weight, up_weight, down_weight, mlp_gain, cotangent,
):
    seqs, own_rows, model = tokens.shape
    length = segment_ids.shape[1]
    heads = query_weight.shape[1]
    ff = gate_weight.shape[1]
    side_index = lax.axis_index("tensor").astype(jnp.int32)
    side = side_index[None]
    blocks, turned = piece_blocks(dp), turn_blocks(dp)

    x_own = tokens.reshape(own_rows, model)
    e_own = cotangent.reshape(own_rows, model)
    gains = jnp.pad(jnp.stack([low(attn_gain), low(mlp_gain)], 1), ((0, 0), (0, 126)))
    order = Order(positions[0, 0] >= 0)
    first = order.done(join(query_weight, key_weight, value_weight, out_weight.T, gains))
    first = Gather(first, dp, 1280)
    x_par = swap_halves(x_own)
    first.round(order)
    first.share(order)
    places = positions.reshape(length).astype(F32)
    half = HEAD_DIM // 2
    places = jnp.where(side_index == 0, places, jnp.roll(places, length // 2))
    ladder = jnp.power(F32(ROPE_BASE), -2.0 * jnp.arange(half, dtype=F32) / HEAD_DIM)
    angles = ladder[:, None] * places[None, :]
    cos, sin = jnp.cos(angles), jnp.sin(angles)
    cos, sin = order.done(cos, sin)
    second = order.done(join(gate_weight, up_weight, down_weight.T))
    second = Gather(second, dp, 3 * ff // 2)
    for _ in range(dp // 4 - 1):
        first.next(order)
    second.share(order)
    first = first.pieces(order)
    x_first, x_par = order.done(*order.tie(x_own, x_par))
    e_par = swap_halves(order.tie(e_own))
    second.round(order)

    known = jnp.arange(DOCS, dtype=jnp.int32)[:, None] == segment_ids.reshape(1, length)
    doc_q = known.astype(BF16)
    doc_k = jnp.where(known, 0.0, -FAR).astype(BF16)

    qkv, gain_rows, a_turned, qkv_full, out_full = project(
        blocks, turned, x_first, x_par, cos, sin, first, heads
    )
    qkv = order.done(qkv)
    att, lse = attend(side, order.tie(qkv), doc_q, doc_k)
    att = order.done(att)

    own, par = slice(0, own_rows), slice(own_rows, None)
    partial = order.done(mm(att[:, par], out_full, 0, 1, BF16))
    sent = swap_halves(partial)
    e_par = order.done(e_par)
    second.next(order)
    e_turned = order.done(turn(turned, order.tie(e_own), e_par))
    partial = order.done(mm(att[:, own], order.tie(out_full), 0, 1, BF16))
    second.next(order)
    sent = order.tie(sent)
    middle, b_own = order.done(
        *by_rows(residual_kernel, (partial, sent, x_own), gain_rows, (BF16, BF16), "residual")
    )
    b_par = swap_halves(b_own)
    second.next(order)
    second = second.pieces(order)

    b_par = order.tie(b_par)
    hidden, pair, db_own, db_par, down_full = ffn(blocks, b_own, b_par, e_own, e_par, second)
    db_par = order.done(db_par)
    db_sent = swap_halves(db_par)
    b_turned = order.done(turn(turned, order.tie(b_own), b_par))
    grad_ffn = Scatter(dp, order, (e_turned, hidden, 0), (b_turned, pair, 0))
    eh_own = order.done(
        *by_rows(
            functools.partial(back_kernel, 1),
            (db_own, order.tie(db_sent), middle, e_own),
            gain_rows,
            (BF16,),
            "norm_back",
        )
    )
    eh_par = swap_halves(eh_own)
    grad_ffn.round()
    down_own, down_par = order.done(*product(order.tie(hidden), down_full))
    grad_ffn.round()
    datt_own = order.done(turned_product(order.tie(eh_own), out_full, 384))
    eh_par = order.tie(eh_par)
    datt_par = order.done(turned_product(eh_par, out_full, 384))
    down_sent = swap_halves(order.tie(down_par))
    eh_turned = order.done(turn(turned, order.tie(eh_own), eh_par))
    grad_ffn.round()
    datt = order.tie(datt_own, datt_par)
    dqkv = order.done(attend_back(side, qkv, att, datt, lse, cos, sin, doc_q, doc_k))
    down_sent = order.done(down_sent)
    da_par = order.done(turned_product(qkv_full, order.tie(dqkv), own_rows, 1, 1))
    da_sent = swap_halves(da_par)
    grad_ffn.round()
    grad_att = Scatter(dp, order, (a_turned, dqkv, 1), (eh_turned, att, 1))
    grad_att.round()
    output = (middle.astype(F32) + (down_own.astype(F32) + order.tie(down_sent).astype(F32))).astype(BF16)
    output = order.done(output)
    da_own = order.done(turned_product(qkv_full, order.tie(dqkv), own_rows, 0, 1))
    grad_ffn.arrive()
    grad_att.round()
    grad_gate, grad_up, grad_down, gain_two = grad_ffn.result(
        (
            (ff, TILE, 2 * TILE, ff // TILE),
            (ff + TILE, TILE, 2 * TILE, ff // TILE),
            (0, TILE, TILE, ff // TILE),
        ),
        (gate_weight, up_weight),
    )
    da_sent = order.done(da_sent)
    grad_att.round()
    (input_grad,) = by_rows(
        functools.partial(back_kernel, 0),
        (order.tie(da_own), da_sent, x_own, eh_own),
        gain_rows,
        (BF16,),
        "norm_back",
    )
    input_grad = order.done(input_grad)
    grad_att.round()
    kv = heads // 2
    size = kv // 3 if kv % 384 else 384
    grad_query, grad_key, grad_value, grad_out, gain_one = grad_att.result(
        (
            (0, size, size, heads // size),
            (heads, size, size, kv // size),
            (heads + kv, size, size, kv // size),
            (2 * heads, size, size, heads // size),
        ),
        (query_weight, key_weight, value_weight),
    )
    gain_grads = jnp.stack(
        [gain_one[0] / low(attn_gain).astype(F32), gain_two[0] / low(mlp_gain).astype(F32)]
    )
    gain_grads = gain_grads + swap_halves(gain_grads)
    return (
        output.reshape(seqs, own_rows, model),
        input_grad.reshape(seqs, own_rows, model),
        grad_query,
        grad_key,
        grad_value,
        grad_out.T,
        gain_grads[0],
        grad_gate,
        grad_up,
        grad_down.T,
        gain_grads[1],
    )


def solution(mesh):
    in_specs = (
        P("dp", "tensor", None),
        P("dp", None),
        P("dp", None),
        P("dp", "tensor"),
        P("dp", "tensor"),
        P("dp", "tensor"),
        P("tensor", "dp"),
        P("dp"),
        P("dp", "tensor"),
        P("dp", "tensor"),
        P("tensor", "dp"),
        P("dp"),
        P("dp", "tensor", None),
    )
    out_specs = (
        P("dp", "tensor", None),
        P("dp", "tensor", None),
        P("dp", "tensor"),
        P("dp", "tensor"),
        P("dp", "tensor"),
        P("tensor", "dp"),
        P("dp"),
        P("dp", "tensor"),
        P("dp", "tensor"),
        P("tensor", "dp"),
        P("dp"),
    )
    return jax.shard_map(
        functools.partial(layer, mesh.shape["dp"]),
        mesh=mesh,
        in_specs=in_specs,
        out_specs=out_specs,
        check_vma=False,
    )
```
